32 devices in a mesh: wide: 16 (over z, y, x), narrow: 2 (over core).
Axes of the slice: x: 2, y: 2, z: 4, core: 2. Of those that a mesh axis runs over, the one named last changes fastest.
Arguments:
- tokens: bfloat16 [2, 32, 128, 1280], P(None, ('wide', 'narrow')), may hold values from -6 to 6
- cotangent: bfloat16 [2, 32, 128, 1280], P(None, ('wide', 'narrow')), may hold values from -6 to 6
- routes: int32 [2, 32, 128, 7], P(None, ('wide', 'narrow')), may hold values from 0 to 15, all different within a row; in each aligned block of 128 rows (0 to 127, 128 to 255, ..., all dimensions but the last counted through in order) at most 64 rows name the same one
- gain_attn: bfloat16 [1280], P(('wide', 'narrow')), may hold values from 0.5 to 1.5
- gain_moe: bfloat16 [1280], P(('wide', 'narrow')), may hold values from 0.5 to 1.5
- w_query: bfloat16 [1280, 1280], P(('wide', 'narrow')), may hold values from -0.15625 to 0.15625
- w_key: bfloat16 [1280, 1280], P(('wide', 'narrow')), may hold values from -0.15625 to 0.15625
- w_value: bfloat16 [1280, 1280], P(('wide', 'narrow')), may hold values from -0.15625 to 0.15625
- attention_output_weight: bfloat16 [1280, 1280], P(('wide', 'narrow')), may hold values from -1.25 to 1.25
- router: bfloat16 [1280, 16], P(('wide', 'narrow')), may hold values from -0.078125 to 0.078125
- shared_gate: bfloat16 [1280, 896], P(('wide', 'narrow')), may hold values from -0.15625 to 0.15625
- shared_up: bfloat16 [1280, 896], P(('wide', 'narrow')), may hold values from -0.15625 to 0.15625
- shared_down: bfloat16 [896, 1280], P(None, ('wide', 'narrow')), may hold values from -0.1875 to 0.1875
- routed_gate_weight: bfloat16 [16, 1280, 896], P('wide', None, 'narrow'), may hold values from -0.15625 to 0.15625
- routed_up_weight: bfloat16 [16, 1280, 896], P('wide', None, 'narrow'), may hold values from -0.15625 to 0.15625
- routed_down_weight: bfloat16 [16, 896, 1280], P('wide', 'narrow'), may hold values from -0.1875 to 0.1875
Outputs:
- output: bfloat16 [2, 32, 128, 1280], P(None, ('wide', 'narrow'))
- grad_tokens: float32 [2, 32, 128, 1280], P(None, ('wide', 'narrow'))
- grad_gain_attn: float32 [1280], P(('wide', 'narrow'))
- grad_gain_moe: float32 [1280], P(('wide', 'narrow'))
- grad_w_query: float32 [1280, 1280], P(('wide', 'narrow'))
- grad_w_key: float32 [1280, 1280], P(('wide', 'narrow'))
- grad_w_value: float32 [1280, 1280], P(('wide', 'narrow'))
- grad_w_out: float32 [1280, 1280], P(('wide', 'narrow'))
- grad_router: float32 [1280, 16], P(('wide', 'narrow'))
- grad_shared_gate: float32 [1280, 896], P(('wide', 'narrow'))
- grad_shared_up: float32 [1280, 896], P(('wide', 'narrow'))
- grad_shared_down: float32 [896, 1280], P(None, ('wide', 'narrow'))
- grad_expert_gate: float32 [16, 1280, 896], P('wide', None, 'narrow')
- grad_expert_up: float32 [16, 1280, 896], P('wide', None, 'narrow')
- grad_expert_down: float32 [16, 896, 1280], P('wide', 'narrow')
The draws below stay inside these ranges and needn't reach their ends.
Inputs may be any that keep to these rules, and one draw needn't show every extreme that they name: `routes`: each token names 7 different experts; among the 128 tokens of one sequence no expert is named by more than 64 tokens, a bound that some block reaches.
All inputs are finite; a program needn't handle non-finite values.
Results may differ from the reference program's by a relative error of at most 0.015.
Values may be sent and summed in bfloat16 or wider, within the bound.
A program may use at most 320 MiB of HBM per device.

```python
import math
import jax
import jax.numpy as jnp
import numpy as np
from jax import lax

D = 1280
HEADS = 10
HD = 128
FFE = 896
TOP = 7
LEN = 128
MB = 2
EXPERTS = 16
NSEQ = 32
CAP = 64


def block_levels(rng, shape, pieces, smallest, largest):
    level = 1.0
    for dim, parts in pieces:
        heights = jax.random.uniform(jax.random.fold_in(jax.random.fold_in(rng, 6), dim), (parts,), jnp.float32, smallest / len(pieces), largest / len(pieces))
        level = level * jnp.repeat(jnp.exp(heights), shape[dim] // parts).reshape((-1,) + (1,) * (len(shape) - 1 - dim))
    return level


def routed_block(stream_key, own, number, rows, count, top, limit, skew):
    ranking = jax.random.permutation(stream_key, count)
    heavy_load, usual = shares(count, rows * top, limit, skew, True), shares(count, rows * top, limit, skew, False)
    places = jnp.arange(count)

    def named(tallies, offset_by):
        used = int((tallies > 0).sum())
        fixed = max(1, used // 4)
        passed = fixed + (places - fixed + offset_by * (used - fixed)) % max(1, count - fixed)
        return jnp.zeros((count,), jnp.int32).at[ranking[jnp.where(places < fixed, places, passed)]].set(jnp.asarray(tallies, jnp.int32))

    tallies = jnp.where(number % 4 == 0, named(heavy_load, number // 4), named(usual, number - number // 4 - 1))
    mixed = jax.random.permutation(jax.random.fold_in(own, 3), count)
    donor, receiver = mixed[0:count // 2 * 2:2], mixed[1:count // 2 * 2:2]
    margin = jnp.minimum(tallies[donor] - 1, limit - tallies[receiver]) // 2
    margin = jnp.where((donor == ranking[0]) | (receiver == ranking[0]) | (tallies[receiver] == 0), 0, jnp.maximum(margin, 0))
    passed = jax.random.randint(jax.random.fold_in(own, 4), (count // 2,), 0, 1 << 20) % (margin + 1)
    tallies = tallies.at[donor].add(-passed).at[receiver].add(passed)
    members = jnp.searchsorted(jnp.cumsum(tallies), jnp.arange(rows * top), side="right").astype(jnp.int32)
    grid = members.reshape(top, rows).T
    grid = grid[jax.random.permutation(jax.random.fold_in(own, 1), rows)]
    offset_by = jax.random.randint(jax.random.fold_in(own, 2), (rows, 1), 0, top)
    return jnp.take_along_axis(grid, (jnp.arange(top)[None, :] + offset_by) % top, axis=1)


def shares(number_of, total, bound, skew, full):
    weights = [(1 << 20) // math.isqrt(rank ** skew) + 1 for rank in range(1, number_of + 1)]
    largest = bound if full else min(bound, max(-(-total // number_of), total * weights[0] // sum(weights)))
    least = 1 if total - largest >= number_of - 1 else 0
    given, surplus = [largest] + [least] * (number_of - 1), total - largest - least * (number_of - 1)
    while surplus > 0:
        candidates = [i for i in range(1, number_of) if given[i] < largest] or [i for i in range(1, number_of) if given[i] < bound]
        whole, left = sum([weights[i] for i in candidates]), surplus
        for i in candidates:
            more = min(bound - given[i], max(1, left * weights[i] // whole), surplus)
            given[i] = given[i] + more
            surplus = surplus - more
    return np.array(given)


def scatter_about(key, shape, deviation, most, split=(), kind=jnp.bfloat16):
    drawn = jax.random.normal(key, shape, jnp.float32) * deviation
    if len(split) > 0:
        drawn = block_levels(key, shape, split, -0.22, 0.18) * drawn
    return jnp.clip(drawn, min=-most, max=most).astype(kind)


def setup_inputs(seed: int = 0) -> dict:
    splits = jax.random.split(jax.random.key(seed), 17)
    tokens = scatter_about(splits[0], (MB, NSEQ, LEN, D), 1.0, 6.0, ((1, 32),))
    cotangent = scatter_about(splits[1], (MB, NSEQ, LEN, D), 1.0, 6.0, ((1, 32),))
    routes_keys = jax.random.split(jax.random.fold_in(splits[2], 1), MB * NSEQ * LEN // LEN)
    routes_turns = jax.random.permutation(jax.random.fold_in(splits[2], 3), MB * NSEQ * LEN // LEN)
    routes = jax.vmap(lambda own, number: routed_block(jax.random.fold_in(splits[2], 2), own, number, LEN, EXPERTS, TOP, CAP, 1))(routes_keys, routes_turns).reshape((MB, NSEQ, LEN, TOP))
    gain_attn = jnp.clip(1.0 + 0.1 * jax.random.normal(splits[3], (D,), jnp.float32), 0.5, 1.5).astype(jnp.bfloat16)
    gain_moe = jnp.clip(1.0 + 0.1 * jax.random.normal(splits[4], (D,), jnp.float32), 0.5, 1.5).astype(jnp.bfloat16)
    w_query = scatter_about(splits[5], (D, D), D ** -0.5, 0.15625, ((0, 32),))
    w_key = scatter_about(splits[6], (D, D), D ** -0.5, 0.15625, ((0, 32),))
    w_value = scatter_about(splits[7], (D, D), D ** -0.5, 0.15625, ((0, 32),))
    attention_output_weight = scatter_about(splits[8], (D, D), (D // 64) ** -0.5, 1.25, ((0, 32),))
    router = scatter_about(splits[9], (D, EXPERTS), (4 * D) ** -0.5, 0.078125, ((0, 32),))
    shared_gate = scatter_about(splits[10], (D, FFE), D ** -0.5, 0.15625, ((0, 32),))
    shared_up = scatter_about(splits[11], (D, FFE), D ** -0.5, 0.15625, ((0, 32),))
    shared_down = scatter_about(splits[12], (FFE, D), FFE ** -0.5, 0.1875, ((1, 32),))
    routed_gate_weight = scatter_about(splits[13], (EXPERTS, D, FFE), D ** -0.5, 0.15625, ((0, 16), (2, 2)))
    routed_up_weight = scatter_about(splits[14], (EXPERTS, D, FFE), D ** -0.5, 0.15625, ((0, 16), (2, 2)))
    routed_down_weight = scatter_about(splits[15], (EXPERTS, FFE, D), FFE ** -0.5, 0.1875, ((0, 16), (1, 2)))
    return dict(tokens=tokens, cotangent=cotangent, routes=routes, gain_attn=gain_attn, gain_moe=gain_moe, w_query=w_query, w_key=w_key, w_value=w_value, attention_output_weight=attention_output_weight, router=router, shared_gate=shared_gate, shared_up=shared_up, shared_down=shared_down, routed_gate_weight=routed_gate_weight, routed_up_weight=routed_up_weight, routed_down_weight=routed_down_weight)


@jax.custom_vjp
def low(v):
    return lax.optimization_barrier(v.astype(jnp.bfloat16)).astype(jnp.float32)

@jax.custom_vjp
def reduced_backward(v):
    return v

def low_keep(v):
    return (low(v), None)

def low_pass(kept, grad):
    return (grad,)

def back_keep(v):
    return (v, None)

def back_low(kept, grad):
    return (low(grad),)
low.defvjp(low_keep, low_pass)
reduced_backward.defvjp(back_keep, back_low)
epsilon = 1e-06
greatest_accuracy = lax.Precision.HIGHEST

def angles(seq_len, head_size):
    position = jnp.arange(seq_len).astype(jnp.float32)
    exponent = jnp.arange(head_size // 2).astype(jnp.float32) * (2.0 / head_size)
    frequency = jnp.exp(-jnp.log(10000.0) * exponent)
    theta = position[:, None] * frequency[None, :]
    return (jnp.cos(theta)[:, None, :], jnp.sin(theta)[:, None, :])

def rotate(vectors, cosine_table, sine_table):
    middle = vectors.shape[-1] // 2
    first_half = vectors[..., :middle]
    second_half = vectors[..., middle:]
    return jnp.concatenate([first_half * cosine_table - second_half * sine_table, second_half * cosine_table + first_half * sine_table], axis=-1)

def norm_rows(matrix, gain):
    scale_rows = lax.rsqrt(lax.optimization_barrier(jnp.mean(matrix * matrix, axis=-1, keepdims=True)) + epsilon)
    return matrix * scale_rows * gain

def silu(pre_act):
    return pre_act * jax.nn.sigmoid(pre_act)

def layer_block(params, block_rows, block_routes):
    gain_attn, gain_moe, w_query, w_key, w_value, attention_output_weight, router, shared_gate, shared_up, shared_down, routed_gate_weight, routed_up_weight, routed_down_weight = params
    seq_count = block_rows.shape[0]
    seq_len = block_rows.shape[1]
    width_all = block_rows.shape[2]
    cosine_table, sine_table = angles(seq_len, HD)
    normalized_input = low(norm_rows(block_rows, gain_attn))

    def project(weight_matrix):
        return jnp.einsum('rpb,bx->rpx', normalized_input, weight_matrix, precision=greatest_accuracy)
    queries = low(rotate(reduced_backward(project(w_query)).reshape(seq_count, seq_len, HEADS, HD), cosine_table, sine_table))
    key_rows = low(rotate(reduced_backward(project(w_key)).reshape(seq_count, seq_len, HEADS, HD), cosine_table, sine_table))
    value_rows = low(reduced_backward(project(w_value))).reshape(seq_count, seq_len, HEADS, HD)
    scale_factor = HD ** (-0.5)
    raw_scores = reduced_backward(scale_factor * jnp.einsum('sqhd,skhd->shqk', queries, key_rows, precision=greatest_accuracy))
    causal_mask = jnp.arange(seq_len)[:, None] >= jnp.arange(seq_len)[None, :]
    masked = jnp.where(causal_mask, raw_scores, -1e+30)
    row_top = lax.optimization_barrier(jnp.max(masked, axis=-1, keepdims=True))
    exp_rows = jnp.exp(masked - row_top)
    probs = low(exp_rows / lax.optimization_barrier(jnp.sum(exp_rows, axis=-1, keepdims=True)))
    blended_output = jnp.einsum('shqk,skhd->sqhd', probs, value_rows, precision=greatest_accuracy).reshape(seq_count, seq_len, width_all)
    blended_output = reduced_backward(low(blended_output))
    attention_result = reduced_backward(jnp.einsum('rpb,bx->rpx', blended_output, attention_output_weight, precision=greatest_accuracy))
    residual = block_rows + attention_result
    normed_mid = low(norm_rows(residual, gain_moe)).reshape(seq_count * seq_len, width_all)
    token_count = seq_count * seq_len
    route_flat = block_routes.reshape(token_count, TOP).astype(jnp.int32)
    logits = reduced_backward(jnp.dot(normed_mid, router, precision=greatest_accuracy))
    picked = jnp.take_along_axis(logits, route_flat, axis=1)
    picked_top = lax.optimization_barrier(jnp.max(picked, axis=1, keepdims=True))
    gate_exp = jnp.exp(picked - picked_top)
    gates = gate_exp / lax.optimization_barrier(jnp.sum(gate_exp, axis=1, keepdims=True))
    shared_g = reduced_backward(jnp.dot(normed_mid, shared_gate, precision=greatest_accuracy))
    shared_u = reduced_backward(jnp.dot(normed_mid, shared_up, precision=greatest_accuracy))
    shared_h = low(silu(shared_g) * shared_u)
    shared_out = reduced_backward(jnp.dot(shared_h, shared_down, precision=greatest_accuracy))
    expert_ids = jnp.arange(EXPERTS).astype(jnp.int32)
    hits = route_flat[:, :, None] == expert_ids[None, None, :]
    named = jnp.any(hits, axis=1).astype(jnp.int32)
    gate_table = lax.optimization_barrier(jnp.sum(jnp.where(hits, gates[:, :, None], 0.0), axis=1))
    slot_count = seq_count * CAP
    slot_index = jnp.cumsum(named, axis=0) - named
    target = jnp.where(named > 0, expert_ids[None, :] * slot_count + slot_index, EXPERTS * slot_count).astype(jnp.int32)
    token_ids = jnp.broadcast_to(jnp.arange(token_count).astype(jnp.int32)[:, None], target.shape)
    source_rows = jnp.full((EXPERTS * slot_count,), token_count).astype(jnp.int32)
    source_rows = source_rows.at[target.reshape(-1)].set(token_ids.reshape(-1), mode='drop')
    padded_rows = jnp.concatenate([normed_mid, jnp.zeros((1, width_all), jnp.float32)], axis=0)
    expert_in = reduced_backward(padded_rows[source_rows].reshape(EXPERTS, slot_count, width_all))
    gate_padded = jnp.concatenate([gate_table, jnp.zeros((1, EXPERTS), jnp.float32)], axis=0)
    slot_gates = gate_padded[source_rows.reshape(EXPERTS, slot_count), expert_ids[:, None]]
    gate_part = reduced_backward(jnp.einsum('ogb,oby->ogy', expert_in, routed_gate_weight, precision=greatest_accuracy))
    up_portion = reduced_backward(jnp.einsum('ogb,oby->ogy', expert_in, routed_up_weight, precision=greatest_accuracy))
    hidden = low(silu(gate_part) * up_portion)
    expert_out = reduced_backward(low(jnp.einsum('erf,efd->erd', hidden, routed_down_weight, precision=greatest_accuracy)))
    weighted = slot_gates[:, :, None] * expert_out
    routed = jnp.zeros((token_count + 1, width_all), jnp.float32).at[source_rows].add(weighted.reshape(-1, width_all))[:token_count]
    combined = shared_out + routed
    return residual + combined.reshape(seq_count, seq_len, width_all)

def forward(params, rows_all, routes_all):
    total_seqs = MB * NSEQ
    per_block = max(1, 4096 // LEN)
    block_seqs = max([divisor for divisor in range(1, per_block + 1) if total_seqs % divisor == 0])
    blocks = total_seqs // block_seqs
    grouped = rows_all.reshape(blocks, block_seqs, LEN, D)
    route_groups = routes_all.reshape(blocks, block_seqs, LEN, TOP)
    run_block = jax.checkpoint(layer_block)
    results = lax.map(lambda block_pair: run_block(params, block_pair[0], block_pair[1]), (grouped, route_groups))
    return results.reshape(MB, NSEQ, LEN, D)

def reference(tokens, cotangent, routes, gain_attn, gain_moe, w_query, w_key, w_value, attention_output_weight, router, shared_gate, shared_up, shared_down, routed_gate_weight, routed_up_weight, routed_down_weight):
    params = tuple((weight_matrix.astype(jnp.float32) for weight_matrix in (gain_attn, gain_moe, w_query, w_key, w_value, attention_output_weight, router, shared_gate, shared_up, shared_down, routed_gate_weight, routed_up_weight, routed_down_weight)))
    rows_all = tokens.astype(jnp.float32)
    output, pullback = jax.vjp(lambda weights, inputs: forward(weights, inputs, routes), params, rows_all)
    weight_grads, input_grad = pullback(cotangent.astype(jnp.float32))
    return (output.astype(jnp.bfloat16), input_grad, weight_grads[0], weight_grads[1], weight_grads[2], weight_grads[3], weight_grads[4], weight_grads[5], weight_grads[6], weight_grads[7], weight_grads[8], weight_grads[9], weight_grads[10], weight_grads[11], weight_grads[12])
```

```python
import functools
import jax
import jax.numpy as jnp
from jax import lax
from jax.experimental import pallas as pl
from jax.experimental.pallas import tpu as pltpu
from jax.sharding import PartitionSpec as P

MESH = pl.DeviceIdType.MESH
HD = 128


epsilon = 1e-06


def angles(seq_len, head_size):
    position = jnp.arange(seq_len).astype(jnp.float32)
    exponent = jnp.arange(head_size // 2).astype(jnp.float32) * (2.0 / head_size)
    frequency = jnp.exp(-jnp.log(10000.0) * exponent)
    theta = position[:, None] * frequency[None, :]
    return (jnp.cos(theta)[:, None, :], jnp.sin(theta)[:, None, :])


def rotate(vectors, cosine_table, sine_table):
    middle = vectors.shape[-1] // 2
    first_half = vectors[..., :middle]
    second_half = vectors[..., middle:]
    return jnp.concatenate(
        [
            first_half * cosine_table - second_half * sine_table,
            second_half * cosine_table + first_half * sine_table,
        ],
        axis=-1,
    )


def unrotate(vectors, cosine_table, sine_table):
    middle = vectors.shape[-1] // 2
    first_half = vectors[..., :middle]
    second_half = vectors[..., middle:]
    return jnp.concatenate(
        [
            first_half * cosine_table + second_half * sine_table,
            second_half * cosine_table - first_half * sine_table,
        ],
        axis=-1,
    )


def norm_ahead(matrix, gain):
    scale_rows = lax.rsqrt(jnp.mean(matrix * matrix, axis=-1, keepdims=True) + epsilon)
    normed = matrix * scale_rows
    return ((normed * gain).astype(jnp.bfloat16), normed, scale_rows)


def norm_back(grad_rows, normed, scale_rows, gain):
    gain_grad = jnp.sum(grad_rows * normed, axis=0)
    inner = grad_rows * gain
    return (
        scale_rows * (inner - normed * jnp.mean(inner * normed, axis=-1, keepdims=True)),
        gain_grad,
    )


def silu_pair(pre_act):
    sigma = jax.nn.sigmoid(pre_act)
    return (pre_act * sigma, sigma * (1.0 + pre_act * (1.0 - sigma)))


def chip_grid(chips):
    deep = 4 if chips % 4 == 0 else 1
    rest = chips // deep
    high = max(d for d in range(1, rest + 1) if rest % d == 0 and d * d <= rest)
    return (deep, high, rest // high)

def place(dims):
    wide = lax.axis_index("wide")
    return wide // (dims[1] * dims[2]), (wide // dims[2]) % dims[1], wide % dims[2]

def greet(dims, a, b, c, core):
    deep, high, broad = dims
    barrier = pltpu.get_barrier_semaphore()
    def chip(i, j, k):
        return (i * high + j) * broad + k
    others = [(chip((a + r) % deep, b, c), core) for r in range(1, deep)]
    others += [(chip(a, (b + r) % high, c), core) for r in range(1, high)]
    others += [(chip(a, b, (c + r) % broad), core) for r in range(1, broad)]
    others += [(chip(a, b, c), 1 - core)]
    for other in others:
        pl.semaphore_signal(barrier, inc=1, device_id=other, device_id_type=MESH)
    pl.semaphore_wait(barrier, len(others))

def gather_kernel(dims, count, *refs):
    deep, high, broad = dims
    ins, outs = refs[:count], refs[count : 2 * count]
    own_sem, s1, r1, s2, r2, s3, r3, sn, rn = refs[2 * count :]
    a, b, c = place(dims)
    core = lax.axis_index("narrow")
    greet(dims, a, b, c, core)

    def chip(i, j, k):
        return (i * high + j) * broad + k

    def send(src, dst, ss, rs, to):
        copy = pltpu.make_async_remote_copy(
            src_ref=src, dst_ref=dst, send_sem=ss, recv_sem=rs, device_id=to, device_id_type=MESH
        )
        return copy

    def program(me):
        first, second = (high, broad) if me == 0 else (broad, high)

        def at2(i, r):
            if me == 0:
                return outs[i].at[:, (b - r + high) % high, c, me]
            return outs[i].at[:, b, (c - r + broad) % broad, me]

        def at3(i, r):
            if me == 0:
                return outs[i].at[:, :, (c - r + broad) % broad, me]
            return outs[i].at[:, (b - r + high) % high, :, me]

        def to2(r):
            return (chip(a, (b + r) % high, c), me) if me == 0 else (chip(a, b, (c + r) % broad), me)

        def to3(r):
            return (chip(a, b, (c + r) % broad), me) if me == 0 else (chip(a, (b + r) % high, c), me)

        mate = (chip(a, b, c), 1 - me)

        def own(i):
            return pltpu.make_async_copy(ins[i], outs[i].at[a, b, c, me], own_sem.at[i])

        def stage1(i, r):
            return send(ins[i], outs[i].at[a, b, c, me], s1.at[i, r - 1], r1.at[i, r - 1], (chip((a + r) % deep, b, c), me))

        def stage2(i, r):
            return send(at2(i, 0), at2(i, 0), s2.at[i, r - 1], r2.at[i, r - 1], to2(r))

        def stage3(i, r):
            return send(at3(i, 0), at3(i, 0), s3.at[i, r - 1], r3.at[i, r - 1], to3(r))

        def across(i, part):
            view = at2(i, 0) if part == 0 else at2(i, part) if part < first else at3(i, part - first + 1)
            return send(view, view, sn.at[i, part], rn.at[i, part], mate)

        parts = first + second - 1
        for i in range(count):
            for r in range(1, deep):
                stage1(i, r).start()
            own(i).start()
        for step in range(count + 2):
            i = step
            if i < count:
                own(i).wait()
                for r in range(1, deep):
                    stage1(i, r).wait_recv()
                for r in range(1, first):
                    stage2(i, r).start()
                across(i, 0).start()
            i = step - 1
            if 0 <= i < count:
                for r in range(1, first):
                    stage2(i, r).wait_recv()
                for r in range(1, second):
                    stage3(i, r).start()
                for r in range(1, first):
                    across(i, r).start()
            i = step - 2
            if 0 <= i < count:
                for r in range(1, second):
                    stage3(i, r).wait_recv()
                for r in range(1, second):
                    across(i, first + r - 1).start()
        for i in range(count):
            for r in range(1, deep):
                stage1(i, r).wait_send()
            for r in range(1, first):
                stage2(i, r).wait_send()
            for r in range(1, second):
                stage3(i, r).wait_send()
            for part in range(parts):
                across(i, part).wait()

    pl.when(core == 0)(lambda: program(0))
    pl.when(core == 1)(lambda: program(1))

def gather_all(dims, parts):
    count = len(parts)
    deep, high, broad = dims
    sem = pltpu.SemaphoreType.DMA
    most = max(high, broad)
    outs = pl.pallas_call(
        functools.partial(gather_kernel, dims, count),
        out_shape=[jax.ShapeDtypeStruct((deep, high, broad, 2) + p.shape, p.dtype) for p in parts],
        in_specs=[pl.BlockSpec(memory_space=pltpu.VMEM)] * count,
        out_specs=[pl.BlockSpec(memory_space=pl.ANY)] * count,
        scratch_shapes=[sem((count,))]
        + [sem((count, max(deep - 1, 1)))] * 2
        + [sem((count, max(most - 1, 1)))] * 4
        + [sem((count, high + broad - 1))] * 2,
        compiler_params=pltpu.CompilerParams(collective_id=0, has_side_effects=True),
        name="gather_dense",
    )(*parts)
    return [o.reshape((deep * high * broad * 2 * p.shape[0],) + p.shape[1:]) for o, p in zip(outs, parts)]

def scatter_kernel(dims, count, *refs):
    deep, high, broad = dims
    ins, outs = refs[:count], refs[count : 2 * count]
    held, from_mate = refs[2 * count : 3 * count], refs[3 * count : 4 * count]
    got2, got3, got4 = refs[4 * count : 5 * count], refs[5 * count : 6 * count], refs[6 * count : 7 * count]
    own_sem, sn, rn, s2, r2, s3, r3, s4, r4 = refs[7 * count :]
    a, b, c = place(dims)
    core = lax.axis_index("narrow")
    greet(dims, a, b, c, core)

    def chip(i, j, k):
        return (i * high + j) * broad + k

    def send(src, dst, ss, rs, to):
        return pltpu.make_async_remote_copy(
            src_ref=src, dst_ref=dst, send_sem=ss, recv_sem=rs, device_id=to, device_id_type=MESH
        )

    wide32 = jnp.float32

    def program(me):
        first, second = (broad, high) if me == 0 else (high, broad)
        mate = (chip(a, b, c), 1 - me)

        def own(i):
            return pltpu.make_async_copy(ins[i].at[:, :, :, me], held[i], own_sem.at[i])

        def across(i):
            return send(ins[i].at[:, :, :, 1 - me], from_mate[i], sn.at[i], rn.at[i], mate)

        def stage2(i, r):
            if me == 0:
                k = (c + r) % broad
                return send(held[i].at[:, :, k], got2[i].at[r - 1], s2.at[i, r - 1], r2.at[i, r - 1], (chip(a, b, k), me))
            j = (b + r) % high
            return send(held[i].at[:, j], got2[i].at[r - 1], s2.at[i, r - 1], r2.at[i, r - 1], (chip(a, j, c), me))

        def stage3(i, r):
            if me == 0:
                j = (b + r) % high
                return send(held[i].at[:, j, c], got3[i].at[r - 1], s3.at[i, r - 1], r3.at[i, r - 1], (chip(a, j, c), me))
            k = (c + r) % broad
            return send(held[i].at[:, b, k], got3[i].at[r - 1], s3.at[i, r - 1], r3.at[i, r - 1], (chip(a, b, k), me))

        def stage4(i, r):
            h = (a + r) % deep
            return send(held[i].at[h, b, c], got4[i].at[r - 1], s4.at[i, r - 1], r4.at[i, r - 1], (chip(h, b, c), me))

        def add_mate(i):
            for j in range(high):
                for k in range(broad):
                    @pl.loop(0, deep)
                    def _(h):
                        held[i][h, j, k] = (held[i][h, j, k].astype(wide32) + from_mate[i][h, j, k].astype(wide32)).astype(jnp.bfloat16)

        def add2(i):
            if me == 0:
                for j in range(high):
                    @pl.loop(0, deep)
                    def _(h):
                        total = held[i][h, j, c].astype(wide32)
                        for r in range(1, broad):
                            total += got2[i][r - 1, h, j].astype(wide32)
                        held[i][h, j, c] = total.astype(jnp.bfloat16)
            else:
                for k in range(broad):
                    @pl.loop(0, deep)
                    def _(h):
                        total = held[i][h, b, k].astype(wide32)
                        for r in range(1, high):
                            total += got2[i][r - 1, h, k].astype(wide32)
                        held[i][h, b, k] = total.astype(jnp.bfloat16)

        def add3(i):
            @pl.loop(0, deep)
            def _(h):
                total = held[i][h, b, c].astype(wide32)
                for r in range(1, second):
                    total += got3[i][r - 1, h].astype(wide32)
                held[i][h, b, c] = total.astype(jnp.bfloat16)

        def add4(i):
            total = held[i][a, b, c].astype(wide32)
            for r in range(1, deep):
                total += got4[i][r - 1].astype(wide32)
            outs[i][...] = total

        for i in range(count):
            across(i).start()
            own(i).start()
        for step in range(count + 3):
            i = step
            if i < count:
                own(i).wait()
                across(i).wait_recv()
                add_mate(i)
                for r in range(1, first):
                    stage2(i, r).start()
            i = step - 1
            if 0 <= i < count:
                for r in range(1, first):
                    stage2(i, r).wait_recv()
                add2(i)
                for r in range(1, second):
                    stage3(i, r).start()
            i = step - 2
            if 0 <= i < count:
                for r in range(1, second):
                    stage3(i, r).wait_recv()
                add3(i)
                for r in range(1, deep):
                    stage4(i, r).start()
            i = step - 3
            if 0 <= i < count:
                for r in range(1, deep):
                    stage4(i, r).wait_recv()
                add4(i)
        for i in range(count):
            across(i).wait_send()
            for r in range(1, first):
                stage2(i, r).wait_send()
            for r in range(1, second):
                stage3(i, r).wait_send()
            for r in range(1, deep):
                stage4(i, r).wait_send()

    pl.when(core == 0)(lambda: program(0))
    pl.when(core == 1)(lambda: program(1))

def scatter_all(dims, parts):
    count = len(parts)
    deep, high, broad = dims
    devices = deep * high * broad * 2
    blocks = [(p.shape[0] // devices, p.shape[1]) for p in parts]
    sem = pltpu.SemaphoreType.DMA
    most = max(high, broad)
    vm = lambda lead: [pltpu.VMEM(lead + blk, jnp.bfloat16) for blk in blocks]
    side = max(high, broad)
    got2 = vm((max(most - 1, 1), deep, side))
    return pl.pallas_call(
        functools.partial(scatter_kernel, dims, count),
        out_shape=[jax.ShapeDtypeStruct(blk, jnp.float32) for blk in blocks],
        in_specs=[pl.BlockSpec(memory_space=pl.ANY)] * count,
        out_specs=[pl.BlockSpec(memory_space=pltpu.VMEM)] * count,
        scratch_shapes=vm((deep, high, broad)) + vm((deep, high, broad)) + got2 + vm((max(most - 1, 1), deep)) + vm((max(deep - 1, 1),))
        + [sem((count,))] * 3
        + [sem((count, max(most - 1, 1)))] * 4
        + [sem((count, max(deep - 1, 1)))] * 2,
        compiler_params=pltpu.CompilerParams(collective_id=1, has_side_effects=True, vmem_limit_bytes=62 * 1024 * 1024),
        name="scatter_dense",
    )(*[p.reshape((deep, high, broad, 2) + blk) for p, blk in zip(parts, blocks)])


def column_pairs(dims, shift):
    deep, plane = dims[0], dims[1] * dims[2]
    return [(i * plane + p, ((i + shift) % deep) * plane + p) for i in range(deep) for p in range(plane)]


def plane_pairs(dims, offset, sign):
    deep, high, broad = dims
    up, over = (offset // broad) * sign, (offset % broad) * sign
    return [
        ((i * high + j) * broad + k, (i * high + (j + up) % high) * broad + (k + over) % broad)
        for i in range(deep)
        for j in range(high)
        for k in range(broad)
    ]


def swap_cores(rows):
    return lax.ppermute(rows, "narrow", [(0, 1), (1, 0)])


def gather_column(dims, rows):
    return jnp.stack([rows] + [lax.ppermute(rows, "wide", column_pairs(dims, k)) for k in range(1, dims[0])])


def to_experts(dims, choose, column):
    sent = jnp.einsum("kqst,ktd->qksd", choose, column, preferred_element_type=jnp.float32).astype(jnp.bfloat16)
    width = column.shape[-1]
    flat = [sent[q].reshape(-1, width) for q in range(sent.shape[0])]
    return jnp.concatenate(
        [flat[0]] + [lax.ppermute(flat[q], "wide", plane_pairs(dims, q, 1)) for q in range(1, len(flat))], axis=0
    )


def from_experts(dims, choose, rows):
    deep, offsets, slots, _ = choose.shape
    width = rows.shape[-1]
    parts = rows.reshape(offsets, deep * slots, width)
    back = jnp.stack(
        [parts[0]] + [lax.ppermute(parts[q], "wide", plane_pairs(dims, q, -1)) for q in range(1, offsets)]
    ).reshape(offsets, deep, slots, width)
    sums = jnp.einsum("kqst,qksd->ktd", choose, back, preferred_element_type=jnp.float32)
    total = sums[0]
    for k in range(1, deep):
        total = total + lax.ppermute(sums[k].astype(jnp.bfloat16), "wide", column_pairs(dims, -k)).astype(jnp.float32)
    return total


def masked_gates(logits, named):
    top = jnp.max(jnp.where(named > 0, logits, -1e30), axis=-1, keepdims=True)
    weights = jnp.where(named > 0, jnp.exp(logits - top), 0.0)
    return weights / jnp.maximum(jnp.sum(weights, axis=-1, keepdims=True), 0.5)


def f32_dot(one, two):
    return jnp.dot(one, two, preferred_element_type=jnp.float32)


def dot_t(one, two):
    return lax.dot_general(one, two, (((1,), (1,)), ((), ())), preferred_element_type=jnp.float32)


def t_dot(one, two):
    return lax.dot_general(one, two, (((0,), (0,)), ((), ())), preferred_element_type=jnp.float32)


def on_device(
    tokens,
    cotangent,
    routes,
    gain_attn,
    gain_moe,
    w_query,
    w_key,
    w_value,
    attention_output_weight,
    router,
    shared_gate,
    shared_up,
    shared_down,
    routed_gate_weight,
    routed_up_weight,
    routed_down_weight,
):
    f32, bf16 = jnp.float32, jnp.bfloat16
    micro = tokens.shape[0]
    seq_len, width_all = tokens.shape[2], tokens.shape[3]
    chosen_count = routes.shape[3]
    experts = router.shape[1]
    heads = width_all // HD
    dims = chip_grid(lax.axis_size("wide"))
    deep, high, broad = dims
    slots = 9 * seq_len * chosen_count // (8 * experts) + 1
    extra = -(-2 * experts // 128) * 128
    cosine_table, sine_table = angles(seq_len, HD)
    scale_factor = HD ** (-0.5)
    causal_mask = jnp.arange(seq_len)[:, None] >= jnp.arange(seq_len)[None, :]
    me = lax.axis_index("wide")
    own_rows = gain_attn.shape[0]

    named = jnp.any(routes[:, 0, :, :, None] == jnp.arange(experts), axis=2)
    named_wide = jnp.pad(named.astype(bf16), ((0, 0), (0, 0), (0, extra - experts)))
    d_out_rows = jnp.concatenate([cotangent[:, 0], named_wide], axis=-1)
    d_columns = [gather_column(dims, d_out_rows[m]) for m in range(micro)]

    small_width = -(-(experts + 2) // 128) * 128
    small = jnp.concatenate(
        [router, gain_attn[:, None], gain_moe[:, None], jnp.zeros((own_rows, small_width - experts - 2), bf16)], axis=1
    )
    (small_all, wq_all, wk_all, wv_all, wo_all, sgate_all, sup_all, sdown_t_all) = gather_all(
        dims,
        [small, w_query, w_key, w_value, attention_output_weight, shared_gate, shared_up, shared_down.T],
    )
    router_all = small_all[:, :experts]
    gain_one = small_all[:, experts].astype(f32)
    gain_two = small_all[:, experts + 1].astype(f32)

    chip_a, chip_b, chip_c = place(dims)
    offsets = high * broad
    step = jnp.arange(offsets)
    targets = (chip_a * high + (chip_b + step // broad) % high) * broad + (chip_c + step % broad) % broad
    is_target = (jnp.arange(experts)[:, None] == targets[None, :]).astype(bf16)
    earlier = (jnp.arange(seq_len)[:, None] > jnp.arange(seq_len)[None, :]).astype(bf16)
    choose, d_rows = [], []
    for m in range(micro):
        names = d_columns[m][:, :, width_all : width_all + experts]
        aimed = jnp.einsum("kte,eq->kqt", names, is_target, preferred_element_type=f32)
        slot = jnp.einsum("kqu,tu->kqt", aimed.astype(bf16), earlier, preferred_element_type=f32)
        hit = (slot[:, :, None, :] == jnp.arange(slots, dtype=f32)[None, None, :, None]) & (aimed[:, :, None, :] > 0.5)
        choose.append(hit.astype(bf16))
        mine = to_experts(dims, choose[m], d_columns[m])
        d_rows.append((mine, swap_cores(mine)))

    rows_in = tokens[:, 0].reshape(micro * seq_len, width_all).astype(f32)
    normalized_input, plain_in, scale_in = norm_ahead(rows_in, gain_one)
    raw_query = f32_dot(normalized_input, wq_all).reshape(micro, seq_len, heads, HD)
    raw_key = f32_dot(normalized_input, wk_all).reshape(micro, seq_len, heads, HD)
    queries = rotate(raw_query, cosine_table, sine_table).astype(bf16)
    key_rows = rotate(raw_key, cosine_table, sine_table).astype(bf16)
    value_rows = f32_dot(normalized_input, wv_all).astype(bf16).reshape(micro, seq_len, heads, HD)
    scores = scale_factor * jnp.einsum("sqhd,skhd->shqk", queries, key_rows, preferred_element_type=f32)
    scores = jnp.where(causal_mask, scores, -1e30)
    row_top = jnp.max(scores, axis=-1, keepdims=True)
    exp_rows = jnp.exp(scores - row_top)
    probs = exp_rows / jnp.sum(exp_rows, axis=-1, keepdims=True)
    probs_low = probs.astype(bf16)
    mixed = jnp.einsum("shqk,skhd->sqhd", probs_low, value_rows, preferred_element_type=f32)
    mixed = mixed.astype(bf16).reshape(micro * seq_len, width_all)
    residual = rows_in + f32_dot(mixed, wo_all)
    normed_mid, plain_mid, scale_mid = norm_ahead(residual, gain_two)

    x_rows = []
    for m in range(micro):
        column = gather_column(dims, normed_mid[m * seq_len : (m + 1) * seq_len])
        mine = to_experts(dims, choose[m], column)
        x_rows.append((mine, swap_cores(mine)))

    named_rows = named.reshape(micro * seq_len, experts)
    gates = masked_gates(f32_dot(normed_mid, router_all), named_rows)
    d_shared = cotangent[:, 0].reshape(micro * seq_len, width_all)
    d_out = d_shared.astype(f32)
    shared_g = f32_dot(normed_mid, sgate_all)
    shared_u = f32_dot(normed_mid, sup_all)
    shared_act, shared_slope = silu_pair(shared_g)
    shared_h = (shared_act * shared_u).astype(bf16)
    shared_out = dot_t(shared_h, sdown_t_all)
    d_shidden = f32_dot(d_shared, sdown_t_all)
    d_sgate = (d_shidden * shared_u * shared_slope).astype(bf16)
    d_sup = (d_shidden * shared_act).astype(bf16)
    grad_sdown_t = t_dot(d_shared, shared_h).astype(bf16)
    grad_sgate = t_dot(normed_mid, d_sgate).astype(bf16)
    grad_sup = t_dot(normed_mid, d_sup).astype(bf16)
    d_mid_near = dot_t(d_sgate, sgate_all) + dot_t(d_sup, sup_all)

    gate_w, up_w, down_w = routed_gate_weight[0], routed_up_weight[0], routed_down_weight[0]
    mine_only = jnp.arange(experts)[None, :] == me
    halves = []
    for m in range(micro):
        pair = []
        for x, d_ext in zip(x_rows[m], d_rows[m]):
            dy = d_ext[:, :width_all]
            row_gates = masked_gates(f32_dot(x, router_all), d_ext[:, width_all : width_all + experts])
            gate = jnp.sum(jnp.where(mine_only, row_gates, 0.0), axis=-1, keepdims=True)
            act, slope = silu_pair(f32_dot(x, gate_w))
            up = f32_dot(x, up_w)
            hidden = act * up
            d_plain = dot_t(dy, down_w)
            d_gate = jnp.sum(hidden * d_plain, axis=-1, keepdims=True)
            weighed = (gate * hidden).astype(bf16)
            d_hidden = gate * d_plain
            d_gate_part = (d_hidden * up * slope).astype(bf16)
            d_up = (d_hidden * act).astype(bf16)
            pair.append((x, dy, weighed, d_gate_part, d_up, d_gate))
        halves.append(pair)

    lane = jnp.arange(extra)[None, :]

    def with_d_gate(rows, d_gate):
        coarse = d_gate.astype(bf16)
        fine = (d_gate - coarse.astype(f32)).astype(bf16)
        beside = jnp.where(lane == me, coarse, jnp.where(lane == me + experts, fine, jnp.zeros((), bf16)))
        return jnp.concatenate([rows.astype(bf16), beside], axis=1)

    def d_in_of(part):
        _, _, _, d_gate_part, d_up, d_gate = part
        return dot_t(d_gate_part, gate_w) + dot_t(d_up, up_w), d_gate

    d_mid_parts, d_gate_parts = [], []
    for m in range(micro):
        theirs = swap_cores(with_d_gate(*d_in_of(halves[m][1])))
        rows, d_gate = d_in_of(halves[m][0])
        rows = rows + theirs[:, :width_all].astype(f32)
        other = jnp.sum(
            jnp.where((lane == me) | (lane == me + experts), theirs[:, width_all:].astype(f32), 0.0), axis=-1, keepdims=True
        )
        summed = from_experts(dims, choose[m], with_d_gate(rows, d_gate + other))
        d_mid_parts.append(summed[:, :width_all])
        d_gate_parts.append(summed[:, width_all : width_all + experts] + summed[:, width_all + experts : width_all + 2 * experts])
    routed_parts = []
    for m in range(micro):
        theirs = swap_cores(f32_dot(halves[m][1][2], down_w).astype(bf16))
        rows = f32_dot(halves[m][0][2], down_w) + theirs.astype(f32)
        routed_parts.append(from_experts(dims, choose[m], rows.astype(bf16)))

    def over_halves(left, right):
        return sum(t_dot(part[left], part[right]) for pair in halves for part in pair)[None]

    grad_edown = over_halves(2, 1)
    grad_egate = over_halves(0, 3)
    grad_eup = over_halves(0, 4)

    final_rows = residual + shared_out + jnp.concatenate(routed_parts, axis=0)
    output = final_rows.astype(bf16).reshape(micro, 1, seq_len, width_all)

    d_gates = jnp.concatenate(d_gate_parts, axis=0)
    d_logits = (gates * (d_gates - jnp.sum(gates * d_gates, axis=1, keepdims=True))).astype(bf16)
    d_mid = jnp.concatenate(d_mid_parts, axis=0) + d_mid_near + dot_t(d_logits, router_all)
    d_norm_two, grad_gain_two = norm_back(d_mid, plain_mid, scale_mid, gain_two)
    d_residual = d_out + d_norm_two
    d_attn = d_residual.astype(bf16)
    grad_wout = t_dot(mixed, d_attn).astype(bf16)
    d_mixed = dot_t(d_attn, wo_all).astype(bf16).reshape(micro, seq_len, heads, HD)
    d_probs = jnp.einsum("sqhd,skhd->shqk", d_mixed, value_rows, preferred_element_type=f32)
    d_value = jnp.einsum("shqk,sqhd->skhd", probs_low, d_mixed, preferred_element_type=f32)
    d_value = d_value.astype(bf16).reshape(micro * seq_len, width_all)
    d_scores = (probs * (d_probs - jnp.sum(probs * d_probs, axis=-1, keepdims=True))).astype(bf16)
    d_query = scale_factor * jnp.einsum("shqk,skhd->sqhd", d_scores, key_rows, preferred_element_type=f32)
    d_key = scale_factor * jnp.einsum("shqk,sqhd->skhd", d_scores, queries, preferred_element_type=f32)
    d_query = unrotate(d_query, cosine_table, sine_table).astype(bf16).reshape(micro * seq_len, width_all)
    d_key = unrotate(d_key, cosine_table, sine_table).astype(bf16).reshape(micro * seq_len, width_all)
    grad_wq = t_dot(normalized_input, d_query).astype(bf16)
    grad_wk = t_dot(normalized_input, d_key).astype(bf16)
    grad_wv = t_dot(normalized_input, d_value).astype(bf16)
    d_in = dot_t(d_query, wq_all) + dot_t(d_key, wk_all) + dot_t(d_value, wv_all)
    d_norm_one, grad_gain_one = norm_back(d_in, plain_in, scale_in, gain_one)
    grad_tokens = (d_residual + d_norm_one).reshape(micro, 1, seq_len, width_all)

    column = jnp.arange(small_width)[None, :]
    grad_small = t_dot(normed_mid, jnp.pad(d_logits, ((0, 0), (0, small_width - experts))))
    grad_small = jnp.where(column == experts, grad_gain_one[:, None], grad_small)
    grad_small = jnp.where(column == experts + 1, grad_gain_two[:, None], grad_small).astype(bf16)

    (g_sgate, g_sup, g_sdown_t, g_wo, g_wq, g_wk, g_wv, g_small) = scatter_all(
        dims, [grad_sgate, grad_sup, grad_sdown_t, grad_wout, grad_wq, grad_wk, grad_wv, grad_small]
    )
    return (
        output,
        grad_tokens,
        g_small[:, experts],
        g_small[:, experts + 1],
        g_wq,
        g_wk,
        g_wv,
        g_wo,
        g_small[:, :experts],
        g_sgate,
        g_sup,
        g_sdown_t.T,
        grad_egate,
        grad_eup,
        grad_edown,
    )


def solution(mesh):
    return jax.shard_map(
        on_device,
        mesh=mesh,
        in_specs=(
            P(None, ("wide", "narrow"), None, None),
            P(None, ("wide", "narrow"), None, None),
            P(None, ("wide", "narrow"), None, None),
            P(("wide", "narrow")),
            P(("wide", "narrow")),
            P(("wide", "narrow"), None),
            P(("wide", "narrow"), None),
            P(("wide", "narrow"), None),
            P(("wide", "narrow"), None),
            P(("wide", "narrow"), None),
            P(("wide", "narrow"), None),
            P(("wide", "narrow"), None),
            P(None, ("wide", "narrow")),
            P("wide", None, "narrow"),
            P("wide", None, "narrow"),
            P("wide", "narrow", None),
        ),
        out_specs=(
            P(None, ("wide", "narrow"), None, None),
            P(None, ("wide", "narrow"), None, None),
            P(("wide", "narrow")),
            P(("wide", "narrow")),
            P(("wide", "narrow"), None),
            P(("wide", "narrow"), None),
            P(("wide", "narrow"), None),
            P(("wide", "narrow"), None),
            P(("wide", "narrow"), None),
            P(("wide", "narrow"), None),
            P(("wide", "narrow"), None),
            P(None, ("wide", "narrow")),
            P("wide", None, "narrow"),
            P("wide", None, "narrow"),
            P("wide", "narrow", None),
        ),
        check_vma=False,
    )
```

```python
import functools
import jax
import jax.numpy as jnp
from jax import lax
from jax.experimental import pallas as pl
from jax.experimental.pallas import tpu as pltpu
from jax.sharding import PartitionSpec as P

MESH = pl.DeviceIdType.MESH
HD = 128


epsilon = 1e-06


def angles(seq_len, head_size):
    position = jnp.arange(seq_len).astype(jnp.float32)
    exponent = jnp.arange(head_size // 2).astype(jnp.float32) * (2.0 / head_size)
    frequency = jnp.exp(-jnp.log(10000.0) * exponent)
    theta = position[:, None] * frequency[None, :]
    return (jnp.cos(theta)[:, None, :], jnp.sin(theta)[:, None, :])


def rotate(vectors, cosine_table, sine_table):
    middle = vectors.shape[-1] // 2
    first_half = vectors[..., :middle]
    second_half = vectors[..., middle:]
    return jnp.concatenate(
        [
            first_half * cosine_table - second_half * sine_table,
            second_half * cosine_table + first_half * sine_table,
        ],
        axis=-1,
    )


def unrotate(vectors, cosine_table, sine_table):
    middle = vectors.shape[-1] // 2
    first_half = vectors[..., :middle]
    second_half = vectors[..., middle:]
    return jnp.concatenate(
        [
            first_half * cosine_table + second_half * sine_table,
            second_half * cosine_table - first_half * sine_table,
        ],
        axis=-1,
    )


def norm_ahead(matrix, gain):
    scale_rows = lax.rsqrt(jnp.mean(matrix * matrix, axis=-1, keepdims=True) + epsilon)
    normed = matrix * scale_rows
    return ((normed * gain).astype(jnp.bfloat16), normed, scale_rows)


def norm_back(grad_rows, normed, scale_rows, gain):
    gain_grad = jnp.sum(grad_rows * normed, axis=0)
    inner = grad_rows * gain
    return (
        scale_rows * (inner - normed * jnp.mean(inner * normed, axis=-1, keepdims=True)),
        gain_grad,
    )


def silu_pair(pre_act):
    sigma = jax.nn.sigmoid(pre_act)
    return (pre_act * sigma, sigma * (1.0 + pre_act * (1.0 - sigma)))


def chip_grid(chips):
    deep = 4 if chips % 4 == 0 else 1
    rest = chips // deep
    high = max(d for d in range(1, rest + 1) if rest % d == 0 and d * d <= rest)
    return (deep, high, rest // high)

def place(dims):
    wide = lax.axis_index("wide")
    return wide // (dims[1] * dims[2]), (wide // dims[2]) % dims[1], wide % dims[2]

def greet(dims, a, b, c, core):
    deep, high, broad = dims
    barrier = pltpu.get_barrier_semaphore()
    def chip(i, j, k):
        return (i * high + j) * broad + k
    others = [(chip((a + r) % deep, b, c), core) for r in range(1, deep)]
    others += [(chip(a, (b + r) % high, c), core) for r in range(1, high)]
    others += [(chip(a, b, (c + r) % broad), core) for r in range(1, broad)]
    others += [(chip(a, b, c), 1 - core)]
    for other in others:
        pl.semaphore_signal(barrier, inc=1, device_id=other, device_id_type=MESH)
    pl.semaphore_wait(barrier, len(others))

def gather_kernel(dims, count, sliced, *refs):
    deep, high, broad = dims
    ins, outs = refs[:count], refs[count + 1 : 2 * count + 1]
    rows_ref, column_ref = refs[count], refs[2 * count + 1]
    own_sem, s1, r1, s2, r2, s3, r3, sn, rn, sr, rr = refs[2 * count + 2 :]
    a, b, c = place(dims)
    core = lax.axis_index("narrow")
    greet(dims, a, b, c, core)

    def chip(i, j, k):
        return (i * high + j) * broad + k

    def send(src, dst, ss, rs, to):
        copy = pltpu.make_async_remote_copy(
            src_ref=src, dst_ref=dst, send_sem=ss, recv_sem=rs, device_id=to, device_id_type=MESH
        )
        return copy

    def program(me):
        first, second = (high, broad) if me == 0 else (broad, high)

        def at2(i, r):
            if me == 0:
                return outs[i].at[:, (b - r + high) % high, c, me]
            return outs[i].at[:, b, (c - r + broad) % broad, me]

        def at3(i, r):
            if me == 0:
                return outs[i].at[:, :, (c - r + broad) % broad, me]
            return outs[i].at[:, (b - r + high) % high, :, me]

        def to2(r):
            return (chip(a, (b + r) % high, c), me) if me == 0 else (chip(a, b, (c + r) % broad), me)

        def to3(r):
            return (chip(a, b, (c + r) % broad), me) if me == 0 else (chip(a, (b + r) % high, c), me)

        mate = (chip(a, b, c), 1 - me)

        def own(i):
            return pltpu.make_async_copy(ins[i].at[a] if sliced[i] else ins[i], outs[i].at[a, b, c, me], own_sem.at[i])

        def stage1(i, r):
            h = (a + r) % deep
            src = ins[i].at[h] if sliced[i] else ins[i]
            return send(src, outs[i].at[a, b, c, me], s1.at[i, r - 1], r1.at[i, r - 1], (chip(h, b, c), me))

        def own_rows():
            return pltpu.make_async_copy(rows_ref, column_ref.at[:, 0], own_sem.at[count])

        def column(r):
            return send(rows_ref, column_ref.at[:, r], sr.at[r - 1], rr.at[r - 1], (chip((a + r) % deep, b, c), me))

        def stage2(i, r):
            return send(at2(i, 0), at2(i, 0), s2.at[i, r - 1], r2.at[i, r - 1], to2(r))

        def stage3(i, r):
            return send(at3(i, 0), at3(i, 0), s3.at[i, r - 1], r3.at[i, r - 1], to3(r))

        def across(i, part):
            view = at2(i, 0) if part == 0 else at2(i, part) if part < first else at3(i, part - first + 1)
            return send(view, view, sn.at[i, part], rn.at[i, part], mate)

        parts = first + second - 1
        for i in range(count):
            for r in range(1, deep):
                stage1(i, r).start()
            own(i).start()
        for r in range(1, deep):
            column(r).start()
        own_rows().start()
        for step in range(count + 2):
            i = step
            if i < count:
                own(i).wait()
                for r in range(1, deep):
                    stage1(i, r).wait_recv()
                for r in range(1, first):
                    stage2(i, r).start()
                across(i, 0).start()
            i = step - 1
            if 0 <= i < count:
                for r in range(1, first):
                    stage2(i, r).wait_recv()
                for r in range(1, second):
                    stage3(i, r).start()
                for r in range(1, first):
                    across(i, r).start()
            i = step - 2
            if 0 <= i < count:
                for r in range(1, second):
                    stage3(i, r).wait_recv()
                for r in range(1, second):
                    across(i, first + r - 1).start()
        for i in range(count):
            for r in range(1, deep):
                stage1(i, r).wait_send()
            for r in range(1, first):
                stage2(i, r).wait_send()
            for r in range(1, second):
                stage3(i, r).wait_send()
            for part in range(parts):
                across(i, part).wait()
        own_rows().wait()
        for r in range(1, deep):
            column(r).wait()

    pl.when(core == 0)(lambda: program(0))
    pl.when(core == 1)(lambda: program(1))

def gather_all(dims, parts, sliced, rows):
    count = len(parts)
    deep, high, broad = dims
    sem = pltpu.SemaphoreType.DMA
    most = max(high, broad)
    shapes = [p.shape[1:] if cut else p.shape for p, cut in zip(parts, sliced)]
    vmem, anywhere = pl.BlockSpec(memory_space=pltpu.VMEM), pl.BlockSpec(memory_space=pl.ANY)
    outs = pl.pallas_call(
        functools.partial(gather_kernel, dims, count, sliced),
        out_shape=[jax.ShapeDtypeStruct((deep, high, broad, 2) + sh, p.dtype) for p, sh in zip(parts, shapes)]
        + [jax.ShapeDtypeStruct(rows.shape[:1] + (deep,) + rows.shape[1:], rows.dtype)],
        in_specs=[vmem] * (count + 1),
        out_specs=[anywhere] * (count + 1),
        scratch_shapes=[sem((count + 1,))]
        + [sem((count, max(deep - 1, 1)))] * 2
        + [sem((count, max(most - 1, 1)))] * 4
        + [sem((count, high + broad - 1))] * 2
        + [sem((max(deep - 1, 1),))] * 2,
        compiler_params=pltpu.CompilerParams(collective_id=0, has_side_effects=True),
        name="gather_dense",
    )(*parts, rows)
    return [o.reshape((-1, sh[-1])) for o, sh in zip(outs[:-1], shapes)], outs[-1]


def scatter_kernel(dims, count, sliced, *refs):
    deep, high, broad = dims
    ins, outs = refs[:count], refs[count : 2 * count]
    held, from_mate = refs[2 * count : 3 * count], refs[3 * count : 4 * count]
    got2, got3, got4 = refs[4 * count : 5 * count], refs[5 * count : 6 * count], refs[6 * count : 7 * count]
    own_sem, sn, rn, s2, r2, s3, r3, s4, r4 = refs[7 * count :]
    a, b, c = place(dims)
    core = lax.axis_index("narrow")
    greet(dims, a, b, c, core)

    def chip(i, j, k):
        return (i * high + j) * broad + k

    def send(src, dst, ss, rs, to):
        return pltpu.make_async_remote_copy(
            src_ref=src, dst_ref=dst, send_sem=ss, recv_sem=rs, device_id=to, device_id_type=MESH
        )

    wide32 = jnp.float32

    def program(me):
        first, second = (broad, high) if me == 0 else (high, broad)
        mate = (chip(a, b, c), 1 - me)

        def own(i):
            return pltpu.make_async_copy(ins[i].at[:, :, :, me], held[i], own_sem.at[i])

        def across(i):
            return send(ins[i].at[:, :, :, 1 - me], from_mate[i], sn.at[i], rn.at[i], mate)

        def stage2(i, r):
            if me == 0:
                k = (c + r) % broad
                return send(held[i].at[:, :, k], got2[i].at[r - 1], s2.at[i, r - 1], r2.at[i, r - 1], (chip(a, b, k), me))
            j = (b + r) % high
            return send(held[i].at[:, j], got2[i].at[r - 1], s2.at[i, r - 1], r2.at[i, r - 1], (chip(a, j, c), me))

        def stage3(i, r):
            if me == 0:
                j = (b + r) % high
                return send(held[i].at[:, j, c], got3[i].at[r - 1], s3.at[i, r - 1], r3.at[i, r - 1], (chip(a, j, c), me))
            k = (c + r) % broad
            return send(held[i].at[:, b, k], got3[i].at[r - 1], s3.at[i, r - 1], r3.at[i, r - 1], (chip(a, b, k), me))

        def stage4(i, r):
            h = (a + r) % deep
            return send(held[i].at[h, b, c], got4[i].at[r - 1], s4.at[i, r - 1], r4.at[i, r - 1], (chip(h, b, c), me))

        def add_mate(i):
            for j in range(high):
                for k in range(broad):
                    @pl.loop(0, deep)
                    def _(h):
                        held[i][h, j, k] = (held[i][h, j, k].astype(wide32) + from_mate[i][h, j, k].astype(wide32)).astype(jnp.bfloat16)

        def add2(i):
            if me == 0:
                for j in range(high):
                    @pl.loop(0, deep)
                    def _(h):
                        total = held[i][h, j, c].astype(wide32)
                        for r in range(1, broad):
                            total += got2[i][r - 1, h, j].astype(wide32)
                        held[i][h, j, c] = total.astype(jnp.bfloat16)
            else:
                for k in range(broad):
                    @pl.loop(0, deep)
                    def _(h):
                        total = held[i][h, b, k].astype(wide32)
                        for r in range(1, high):
                            total += got2[i][r - 1, h, k].astype(wide32)
                        held[i][h, b, k] = total.astype(jnp.bfloat16)

        def add3(i):
            @pl.loop(0, deep)
            def _(h):
                total = held[i][h, b, c].astype(wide32)
                for r in range(1, second):
                    total += got3[i][r - 1, h].astype(wide32)
                held[i][h, b, c] = total.astype(jnp.bfloat16)

        def add4(i):
            if sliced[i]:
                outs[i][a] = held[i][a, b, c].astype(wide32)
                for r in range(1, deep):
                    outs[i][(a - r + deep) % deep] = got4[i][r - 1].astype(wide32)
                return
            total = held[i][a, b, c].astype(wide32)
            for r in range(1, deep):
                total += got4[i][r - 1].astype(wide32)
            outs[i][...] = total

        for i in range(count):
            across(i).start()
            own(i).start()
        for step in range(count + 3):
            i = step
            if i < count:
                own(i).wait()
                across(i).wait_recv()
                add_mate(i)
                for r in range(1, first):
                    stage2(i, r).start()
            i = step - 1
            if 0 <= i < count:
                for r in range(1, first):
                    stage2(i, r).wait_recv()
                add2(i)
                for r in range(1, second):
                    stage3(i, r).start()
            i = step - 2
            if 0 <= i < count:
                for r in range(1, second):
                    stage3(i, r).wait_recv()
                add3(i)
                for r in range(1, deep):
                    stage4(i, r).start()
            i = step - 3
            if 0 <= i < count:
                for r in range(1, deep):
                    stage4(i, r).wait_recv()
                add4(i)
        for i in range(count):
            across(i).wait_send()
            for r in range(1, first):
                stage2(i, r).wait_send()
            for r in range(1, second):
                stage3(i, r).wait_send()
            for r in range(1, deep):
                stage4(i, r).wait_send()

    pl.when(core == 0)(lambda: program(0))
    pl.when(core == 1)(lambda: program(1))

def scatter_all(dims, parts, sliced):
    count = len(parts)
    deep, high, broad = dims
    devices = deep * high * broad * 2
    blocks = [(p.shape[0] // devices, p.shape[1]) for p in parts]
    sem = pltpu.SemaphoreType.DMA
    most = max(high, broad)
    vm = lambda lead: [pltpu.VMEM(lead + blk, jnp.bfloat16) for blk in blocks]
    side = max(high, broad)
    got2 = vm((max(most - 1, 1), deep, side))
    return pl.pallas_call(
        functools.partial(scatter_kernel, dims, count, sliced),
        out_shape=[jax.ShapeDtypeStruct(((deep,) if cut else ()) + blk, jnp.float32) for blk, cut in zip(blocks, sliced)],
        in_specs=[pl.BlockSpec(memory_space=pl.ANY)] * count,
        out_specs=[pl.BlockSpec(memory_space=pltpu.VMEM)] * count,
        scratch_shapes=vm((deep, high, broad)) + vm((deep, high, broad)) + got2 + vm((max(most - 1, 1), deep)) + vm((max(deep - 1, 1),))
        + [sem((count,))] * 3
        + [sem((count, max(most - 1, 1)))] * 4
        + [sem((count, max(deep - 1, 1)))] * 2,
        compiler_params=pltpu.CompilerParams(collective_id=1, has_side_effects=True, vmem_limit_bytes=62 * 1024 * 1024),
        name="scatter_dense",
    )(*[p.reshape((deep, high, broad, 2) + blk) for p, blk in zip(parts, blocks)])


def greet_all(dims, a, b, c, core):
    deep, high, broad = dims
    barrier = pltpu.get_barrier_semaphore()
    others = [(((a + r) % deep * high + b) * broad + c, core) for r in range(1, deep)]
    others += [
        ((a * high + (b + q // broad) % high) * broad + (c + q % broad) % broad, core) for q in range(1, high * broad)
    ]
    others += [((a * high + b) * broad + c, 1 - core)]
    for other in others:
        pl.semaphore_signal(barrier, inc=1, device_id=other, device_id_type=MESH)
    pl.semaphore_wait(barrier, len(others))


def remote(src, dst, ss, rs, to):
    return pltpu.make_async_remote_copy(
        src_ref=src, dst_ref=dst, send_sem=ss, recv_sem=rs, device_id=to, device_id_type=MESH
    )


def dispatch_kernel(dims, micro, x_ref, choose_ref, both_ref, column_ref, got, picked, scol, rcol, spl, rpl, sm, rm, sl):
    deep, high, broad = dims
    offsets = high * broad
    a, b, c = place(dims)
    core = lax.axis_index("narrow")
    greet_all(dims, a, b, c, core)
    mate = ((a * high + b) * broad + c, 1 - core)
    rows_ref, mates_ref = both_ref.at[0], both_ref.at[1]

    def column(m, k):
        return remote(x_ref.at[m], got.at[m, k], scol.at[m, k], rcol.at[m, k], (((a + k) % deep * high + b) * broad + c, core))

    def plane(m, k, q):
        to = (a * high + (b + q // broad) % high) * broad + (c + q % broad) % broad
        return remote(picked.at[m, k, q], rows_ref.at[m, q, k], spl.at[m, k, q], rpl.at[m, k, q], (to, core))

    def across(m, k, part):
        if part == 0:
            return remote(picked.at[m, k, 0], mates_ref.at[m, 0, k], sm.at[m, k, 0], rm.at[m, k, 0], mate)
        return remote(rows_ref.at[m, 1:, k], mates_ref.at[m, 1:, k], sm.at[m, k, 1], rm.at[m, k, 1], mate)

    def keep(m, k):
        return pltpu.make_async_copy(picked.at[m, k, 0], rows_ref.at[m, 0, k], sl.at[m, k, 0])

    def keep_column(m, k):
        return pltpu.make_async_copy(x_ref.at[m] if k == 0 else got.at[m, k], column_ref.at[m, k], sl.at[m, k, 1])

    order = [(m, k) for m in range(micro) for k in range(deep)]
    for m, k in order:
        if k > 0:
            column(m, k).start()
    for m, k in order:
        if k > 0:
            column(m, k).wait_recv()
        keep_column(m, k).start()
        piece = x_ref[m] if k == 0 else got[m, k]
        chosen = jnp.dot(choose_ref[m, k], piece, preferred_element_type=jnp.float32).astype(jnp.bfloat16)
        picked[m, k] = chosen.reshape(picked.shape[2:])
        for q in range(1, offsets):
            plane(m, k, q).start()
        keep(m, k).start()
        across(m, k, 0).start()
    for m, k in order:
        for q in range(1, offsets):
            plane(m, k, q).wait_recv()
        across(m, k, 1).start()
    for m, k in order:
        if k > 0:
            column(m, k).wait_send()
        keep_column(m, k).wait()
        for q in range(1, offsets):
            plane(m, k, q).wait_send()
        keep(m, k).wait()
        across(m, k, 0).wait()
        across(m, k, 1).wait()


def dispatch(dims, x, choose):
    deep, high, broad = dims
    micro, tokens, width = x.shape
    offsets = high * broad
    slots = choose.shape[2] // offsets
    sem = pltpu.SemaphoreType.DMA
    anywhere, vmem = pl.BlockSpec(memory_space=pl.ANY), pl.BlockSpec(memory_space=pltpu.VMEM)
    out = jax.ShapeDtypeStruct((2, micro, offsets, deep, slots, width), x.dtype)
    return pl.pallas_call(
        functools.partial(dispatch_kernel, dims, micro),
        out_shape=[out, jax.ShapeDtypeStruct((micro, deep, tokens, width), x.dtype)],
        in_specs=[vmem, vmem],
        out_specs=[anywhere] * 2,
        scratch_shapes=[
            pltpu.VMEM((micro, deep, tokens, width), x.dtype),
            pltpu.VMEM((micro, deep, offsets, slots, width), x.dtype),
        ]
        + [sem((micro, deep))] * 2
        + [sem((micro, deep, offsets))] * 2
        + [sem((micro, deep, 2))] * 3,
        compiler_params=pltpu.CompilerParams(collective_id=2, has_side_effects=True),
        name="dispatch_rows",
    )(x, choose)


def return_kernel(dims, micro, both_ref, choose_ref, near_ref, total_ref, held, mated, back, up, got, sl, sm, rm, spl, rpl, scol, rcol):
    deep, high, broad = dims
    offsets = high * broad
    a, b, c = place(dims)
    core = lax.axis_index("narrow")
    greet_all(dims, a, b, c, core)
    mate = ((a * high + b) * broad + c, 1 - core)
    near_width = near_ref.shape[-1]
    mine_ref, theirs_ref = both_ref.at[0], both_ref.at[1]

    def load(m, k):
        return pltpu.make_async_copy(mine_ref.at[m, :, k], held.at[m, :, k], sl.at[m, k])

    def across(m, k):
        return remote(theirs_ref.at[m, :, k], mated.at[m, :, k], sm.at[m, k], rm.at[m, k], mate)

    def plane(m, k, q):
        to = (a * high + (b - q // broad + high) % high) * broad + (c - q % broad + broad) % broad
        return remote(held.at[m, q, k], back.at[m, k, q], spl.at[m, k, q], rpl.at[m, k, q], (to, core))

    def column(m, k):
        return remote(up.at[m, k], got.at[m, k], scol.at[m, k], rcol.at[m, k], (((a - k + deep) % deep * high + b) * broad + c, core))

    order = [(m, k) for m in range(micro) for k in list(range(1, deep)) + [0]]
    for m, k in order:
        across(m, k).start()
        load(m, k).start()
    for m, k in order:
        load(m, k).wait()
        across(m, k).wait_recv()
        for q in range(1, offsets):
            held[m, q, k] = (held[m, q, k].astype(jnp.float32) + mated[m, q, k].astype(jnp.float32)).astype(jnp.bfloat16)
            plane(m, k, q).start()
        back[m, k, 0] = (held[m, 0, k].astype(jnp.float32) + mated[m, 0, k].astype(jnp.float32)).astype(jnp.bfloat16)
    for m, k in order:
        for q in range(1, offsets):
            plane(m, k, q).wait_recv()
        rows = back[m, k].reshape((-1, back.shape[-1]))
        sums = jnp.dot(choose_ref[m, k], rows, preferred_element_type=jnp.float32)
        dense = sums[:, :near_width] + near_ref[m, k].astype(jnp.float32)
        if k == 0:
            total_ref[m, :, :near_width] = dense
            if near_width < sums.shape[1]:
                total_ref[m, :, near_width:] = sums[:, near_width:]
        else:
            up[m, k, :, :near_width] = dense.astype(jnp.bfloat16)
            if near_width < sums.shape[1]:
                up[m, k, :, near_width:] = sums[:, near_width:].astype(jnp.bfloat16)
            column(m, k).start()
    for m in range(micro):
        for k in range(1, deep):
            column(m, k).wait_recv()
            total_ref[m] += got[m, k].astype(jnp.float32)
    for m, k in order:
        across(m, k).wait_send()
        for q in range(1, offsets):
            plane(m, k, q).wait_send()
        if k > 0:
            column(m, k).wait_send()


def give_back(dims, both, choose_t, near):
    deep, high, broad = dims
    _, micro, offsets, _, slots, width = both.shape
    tokens = choose_t.shape[2]
    sem = pltpu.SemaphoreType.DMA
    anywhere, vmem = pl.BlockSpec(memory_space=pl.ANY), pl.BlockSpec(memory_space=pltpu.VMEM)
    scratch = lambda *shape: pltpu.VMEM(shape, both.dtype)
    return pl.pallas_call(
        functools.partial(return_kernel, dims, micro),
        out_shape=jax.ShapeDtypeStruct((micro, tokens, width), jnp.float32),
        in_specs=[anywhere, vmem, vmem],
        out_specs=vmem,
        scratch_shapes=[
            scratch(micro, offsets, deep, slots, width),
            scratch(micro, offsets, deep, slots, width),
            scratch(micro, deep, offsets, slots, width),
            scratch(micro, deep, tokens, width),
            scratch(micro, deep, tokens, width),
        ]
        + [sem((micro, deep))] * 3
        + [sem((micro, deep, offsets))] * 2
        + [sem((micro, deep))] * 2,
        compiler_params=pltpu.CompilerParams(collective_id=3, has_side_effects=True, vmem_limit_bytes=62 * 1024 * 1024),
        name="return_rows",
    )(both, choose_t, near)


def column_pairs(dims, shift):
    deep, plane = dims[0], dims[1] * dims[2]
    return [(i * plane + p, ((i + shift) % deep) * plane + p) for i in range(deep) for p in range(plane)]


def plane_pairs(dims, offset, sign):
    deep, high, broad = dims
    up, over = (offset // broad) * sign, (offset % broad) * sign
    return [
        ((i * high + j) * broad + k, (i * high + (j + up) % high) * broad + (k + over) % broad)
        for i in range(deep)
        for j in range(high)
        for k in range(broad)
    ]


def swap_cores(rows):
    return lax.ppermute(rows, "narrow", [(0, 1), (1, 0)])


def plane_rows(dims, picked):
    return jnp.stack(
        [picked[0]] + [lax.ppermute(picked[q], "wide", plane_pairs(dims, q, 1)) for q in range(1, picked.shape[0])]
    )


def plane_back(dims, rows):
    micro, offsets, deep, slots, width = rows.shape
    return jnp.stack(
        [rows[:, 0]] + [lax.ppermute(rows[:, q], "wide", plane_pairs(dims, q, -1)) for q in range(1, offsets)], axis=2
    ).reshape(micro, deep, offsets * slots, width)


def column_sums(dims, choose, back, near):
    sums = jnp.einsum("mkst,mksd->mktd", choose, back, preferred_element_type=jnp.float32)
    return sums + near.astype(jnp.float32)


def column_back(dims, sums):
    return sums[:, 0], [
        lax.ppermute(sums[:, k].astype(jnp.bfloat16), "wide", column_pairs(dims, -k)) for k in range(1, dims[0])
    ]


def masked_gates(logits, named):
    top = jnp.max(jnp.where(named > 0, logits, -1e30), axis=-1, keepdims=True)
    weights = jnp.where(named > 0, jnp.exp(logits - top), 0.0)
    return weights / jnp.maximum(jnp.sum(weights, axis=-1, keepdims=True), 0.5)


def f32_dot(one, two):
    return jnp.dot(one, two, preferred_element_type=jnp.float32)


def dot_t(one, two):
    return lax.dot_general(one, two, (((1,), (1,)), ((), ())), preferred_element_type=jnp.float32)


def t_dot(one, two):
    return lax.dot_general(one, two, (((0,), (0,)), ((), ())), preferred_element_type=jnp.float32)


def own_gate(x, router, names, pick):
    row_gates = masked_gates(f32_dot(x, router), names.astype(jnp.float32))
    return jnp.sum(row_gates * pick[:, : row_gates.shape[1]], axis=-1, keepdims=True)


def expert_forward_kernel(half, x_ref, names_ref, mate_names_ref, router_ref, pick_ref, gate_w, up_w, down_w, out_ref, g_ref, u_ref):
    x = x_ref[...]
    names = jnp.where(pl.program_id(0) < half, names_ref[...], mate_names_ref[...])
    gate = own_gate(x, router_ref[...], names, pick_ref[0:1])
    g = f32_dot(x, gate_w[...])
    u = f32_dot(x, up_w[...])
    g_ref[...] = g
    u_ref[...] = u
    act, _ = silu_pair(g)
    out_ref[...] = f32_dot((gate * (act * u)).astype(jnp.bfloat16), down_w[...]).astype(jnp.bfloat16)


def expert_backward_kernel(
    half, width, x_ref, d_ref, mate_d_ref, router_ref, pick_ref, gate_w, up_w, down_w, g_ref, u_ref, in_ref, dg_ref, du_ref, dd_ref
):
    step = pl.program_id(0)
    x = x_ref[...]
    ext = jnp.where(step < half, d_ref[...], mate_d_ref[...])
    dy, names = ext[:, :width], ext[:, width:]
    gate = own_gate(x, router_ref[...], names, pick_ref[0:1])
    act, slope = silu_pair(g_ref[...])
    u = u_ref[...]
    d_plain = dot_t(dy, down_w[...])
    hidden = act * u
    d_gate = jnp.sum(hidden * d_plain, axis=-1, keepdims=True)
    weighed = (gate * hidden).astype(jnp.bfloat16)
    d_hidden = gate * d_plain
    d_act = (d_hidden * u * slope).astype(jnp.bfloat16)
    d_up = (d_hidden * act).astype(jnp.bfloat16)
    rows = dot_t(d_act, gate_w[...]) + dot_t(d_up, up_w[...])
    in_ref[:, :width] = rows.astype(jnp.bfloat16)
    coarse = d_gate.astype(jnp.bfloat16).astype(jnp.float32)
    beside = coarse * pick_ref[1:2] + (d_gate - coarse) * pick_ref[2:3]
    in_ref[:, width:] = beside.astype(jnp.bfloat16)

    @pl.when(step == 0)
    def _():
        dg_ref[...] = jnp.zeros_like(dg_ref)
        du_ref[...] = jnp.zeros_like(du_ref)
        dd_ref[...] = jnp.zeros_like(dd_ref)

    dg_ref[...] += t_dot(x, d_act)
    du_ref[...] += t_dot(x, d_up)
    dd_ref[...] += t_dot(weighed, dy)


def fixed(shape):
    return pl.BlockSpec(shape, lambda i: (0,) * len(shape), pipeline_mode=pl.Buffered(1))


def row_block(total):
    return max(n for n in (512, 256, 128, 64, 32, 16) if total % n == 0)


def roomy():
    return pltpu.CompilerParams(vmem_limit_bytes=60 * 1024 * 1024)


def cost(flops, moved):
    return pl.CostEstimate(flops=flops, bytes_accessed=moved, transcendentals=0)


def expert_forward(x, d_mine, d_mates, router, picks, gate_w, up_w, down_w):
    rows, width = x.shape
    hidden = gate_w.shape[1]
    block = row_block(d_mine.shape[0])
    half = d_mine.shape[0] // block
    names = d_mine.shape[1] - width
    at = width // names
    by_row = lambda w: pl.BlockSpec((block, w), lambda i: (i, 0))
    first = pl.BlockSpec((block, names), lambda i: (jnp.minimum(i, half - 1), at))
    second = pl.BlockSpec((block, names), lambda i: (jnp.maximum(i - half, 0), at))
    return pl.pallas_call(
        functools.partial(expert_forward_kernel, half),
        grid=(2 * half,),
        out_shape=[
            jax.ShapeDtypeStruct((rows, width), jnp.bfloat16),
            jax.ShapeDtypeStruct((rows, hidden), jnp.float32),
            jax.ShapeDtypeStruct((rows, hidden), jnp.float32),
        ],
        in_specs=[by_row(width), first, second, fixed(router.shape), fixed(picks.shape)]
        + [fixed(w.shape) for w in (gate_w, up_w, down_w)],
        out_specs=[by_row(width), by_row(hidden), by_row(hidden)],
        compiler_params=roomy(),
        cost_estimate=cost(6 * rows * width * hidden, rows * (4 * width + 8 * hidden)),
        name="expert_forward",
    )(x, d_mine, d_mates, router, picks, gate_w, up_w, down_w)


def expert_backward(x, d_mine, d_mates, router, picks, gate_w, up_w, down_w, g, u):
    rows, width = x.shape
    hidden = gate_w.shape[1]
    block = row_block(d_mine.shape[0])
    half = d_mine.shape[0] // block
    wide_d = d_mine.shape[1]
    by_row = lambda w: pl.BlockSpec((block, w), lambda i: (i, 0))
    first = pl.BlockSpec((block, wide_d), lambda i: (jnp.minimum(i, half - 1), 0))
    second = pl.BlockSpec((block, wide_d), lambda i: (jnp.maximum(i - half, 0), 0))
    wide_in = width + picks.shape[1]
    return pl.pallas_call(
        functools.partial(expert_backward_kernel, half, width),
        grid=(2 * half,),
        out_shape=[jax.ShapeDtypeStruct((rows, wide_in), jnp.bfloat16)]
        + [jax.ShapeDtypeStruct(w.shape, jnp.float32) for w in (gate_w, up_w, down_w)],
        in_specs=[by_row(width), first, second, fixed(router.shape), fixed(picks.shape)]
        + [fixed(w.shape) for w in (gate_w, up_w, down_w)]
        + [by_row(hidden), by_row(hidden)],
        out_specs=[by_row(wide_in)] + [fixed(w.shape) for w in (gate_w, up_w, down_w)],
        compiler_params=roomy(),
        cost_estimate=cost(12 * rows * width * hidden, rows * (6 * width + 8 * hidden)),
        name="expert_backward",
    )(x, d_mine, d_mates, router, picks, gate_w, up_w, down_w, g, u)


def shared_kernel(width, part, x_ref, d_ref, w_ref, out_ref, in_ref, grad_ref):
    x, dy = x_ref[...], d_ref[:, :width]
    gate_w, up_w, down_t = w_ref[:, :part], w_ref[:, part : 2 * part], w_ref[:, 2 * part :]
    act, slope = silu_pair(f32_dot(x, gate_w))
    u = f32_dot(x, up_w)
    hidden = (act * u).astype(jnp.bfloat16)
    out_ref[...] = dot_t(hidden, down_t).astype(jnp.bfloat16)
    d_hidden = f32_dot(dy, down_t)
    d_gate = (d_hidden * u * slope).astype(jnp.bfloat16)
    d_up = (d_hidden * act).astype(jnp.bfloat16)
    in_ref[...] = (dot_t(d_gate, gate_w) + dot_t(d_up, up_w)).astype(jnp.bfloat16)

    @pl.when(pl.program_id(0) == 0)
    def _():
        grad_ref[...] = jnp.zeros_like(grad_ref)

    grad_ref[:, :part] += t_dot(x, d_gate)
    grad_ref[:, part : 2 * part] += t_dot(x, d_up)
    grad_ref[:, 2 * part :] += t_dot(dy, hidden)


def shared_expert(x, d, weights):
    rows, width = x.shape
    part = weights.shape[1] // 3
    block = row_block(rows)
    by_row = lambda w: pl.BlockSpec((block, w), lambda i: (i, 0))
    return pl.pallas_call(
        functools.partial(shared_kernel, width, part),
        grid=(rows // block,),
        out_shape=[jax.ShapeDtypeStruct((rows, width), jnp.bfloat16)] * 2 + [jax.ShapeDtypeStruct(weights.shape, jnp.float32)],
        in_specs=[by_row(width), by_row(d.shape[1]), fixed(weights.shape)],
        out_specs=[by_row(width)] * 2 + [fixed(weights.shape)],
        compiler_params=roomy(),
        cost_estimate=cost(18 * rows * width * part, rows * 8 * width),
        name="shared_expert",
    )(x, d, weights)


def on_device(
    tokens,
    cotangent,
    routes,
    gain_attn,
    gain_moe,
    w_query,
    w_key,
    w_value,
    attention_output_weight,
    router,
    shared_gate,
    shared_up,
    shared_down,
    routed_gate_weight,
    routed_up_weight,
    routed_down_weight,
):
    f32, bf16 = jnp.float32, jnp.bfloat16
    micro = tokens.shape[0]
    seq_len, width_all = tokens.shape[2], tokens.shape[3]
    chosen_count = routes.shape[3]
    experts = router.shape[1]
    heads = width_all // HD
    dims = chip_grid(lax.axis_size("wide"))
    deep, high, broad = dims
    slots = 9 * seq_len * chosen_count // (8 * experts) + 1
    extra = -(-experts // 128) * 128
    extra_back = -(-4 * experts // 128) * 128
    cosine_table, sine_table = angles(seq_len, HD)
    scale_factor = HD ** (-0.5)
    causal_mask = jnp.arange(seq_len)[:, None] >= jnp.arange(seq_len)[None, :]
    me = lax.axis_index("wide")
    own_rows = gain_attn.shape[0]

    named = jnp.any(routes[:, 0, :, :, None] == jnp.arange(experts), axis=2)
    named_wide = jnp.pad(named.astype(bf16), ((0, 0), (0, 0), (0, extra - experts)))
    d_out_rows = jnp.concatenate([cotangent[:, 0], named_wide], axis=-1)

    small_width = -(-(experts + 2) // 128) * 128
    small = jnp.concatenate(
        [router, gain_attn[:, None], gain_moe[:, None], jnp.zeros((own_rows, small_width - experts - 2), bf16)], axis=1
    )
    hidden_all = shared_gate.shape[1]
    part = -(-hidden_all // (deep * 128)) * 128

    def cut(matrix):
        return jnp.pad(matrix, ((0, 0), (0, part * deep - hidden_all))).reshape(own_rows, deep, part).transpose(1, 0, 2)

    shared = jnp.concatenate([cut(shared_gate), cut(shared_up), cut(shared_down.T)], axis=2)
    (small_all, wq_all, wk_all, wv_all, wo_all, shared_all), d_column = gather_all(
        dims,
        [small, w_query, w_key, w_value, attention_output_weight, shared],
        [False, False, False, False, False, True],
        d_out_rows,
    )
    router_all = small_all[:, :experts]
    gain_one = small_all[:, experts].astype(f32)
    gain_two = small_all[:, experts + 1].astype(f32)

    chip_a, chip_b, chip_c = place(dims)
    offsets = high * broad
    step = jnp.arange(offsets)
    targets = (chip_a * high + (chip_b + step // broad) % high) * broad + (chip_c + step % broad) % broad
    is_target = (jnp.arange(experts)[:, None] == targets[None, :]).astype(bf16)
    earlier = (jnp.arange(seq_len)[:, None] > jnp.arange(seq_len)[None, :]).astype(bf16)
    names = d_column[..., width_all : width_all + experts]
    aimed = jnp.einsum("mkte,eq->mkqt", names, is_target, preferred_element_type=f32)
    slot = jnp.einsum("mkqu,tu->mkqt", aimed.astype(bf16), earlier, preferred_element_type=f32)
    hit = (slot[:, :, :, None, :] == jnp.arange(slots, dtype=f32)[:, None]) & (aimed[:, :, :, None, :] > 0.5)
    choose = hit.astype(bf16).reshape(micro, deep, offsets * slots, seq_len)
    choose_t = choose.transpose(0, 1, 3, 2)

    d_picked_rows = jnp.einsum("mkqst,mktd->qmksd", hit.astype(bf16), d_column, preferred_element_type=f32).astype(bf16)
    d_mine = plane_rows(dims, d_picked_rows).transpose(1, 0, 2, 3, 4).reshape(micro, -1, width_all + extra)
    d_mates = swap_cores(d_mine)

    rows_in = tokens[:, 0].reshape(micro * seq_len, width_all).astype(f32)
    normalized_input, plain_in, scale_in = norm_ahead(rows_in, gain_one)
    raw_query = f32_dot(normalized_input, wq_all).reshape(micro, seq_len, heads, HD)
    raw_key = f32_dot(normalized_input, wk_all).reshape(micro, seq_len, heads, HD)
    queries = rotate(raw_query, cosine_table, sine_table).astype(bf16)
    key_rows = rotate(raw_key, cosine_table, sine_table).astype(bf16)
    value_rows = f32_dot(normalized_input, wv_all).astype(bf16).reshape(micro, seq_len, heads, HD)
    scores = scale_factor * jnp.einsum("sqhd,skhd->shqk", queries, key_rows, preferred_element_type=f32)
    scores = jnp.where(causal_mask, scores, -1e30)
    row_top = jnp.max(scores, axis=-1, keepdims=True)
    exp_rows = jnp.exp(scores - row_top)
    probs = exp_rows / jnp.sum(exp_rows, axis=-1, keepdims=True)
    probs_low = probs.astype(bf16)
    mixed = jnp.einsum("shqk,skhd->sqhd", probs_low, value_rows, preferred_element_type=f32)
    mixed = mixed.astype(bf16).reshape(micro * seq_len, width_all)
    residual = rows_in + f32_dot(mixed, wo_all)
    normed_mid, plain_mid, scale_mid = norm_ahead(residual, gain_two)

    x_both, x_column = dispatch(dims, normed_mid.reshape(micro, seq_len, width_all), choose)
    x_rows = x_both.reshape(-1, width_all)
    d_mine, d_mates = (d.reshape(-1, width_all + extra) for d in (d_mine, d_mates))

    gate_w, up_w, down_w = routed_gate_weight[0], routed_up_weight[0], routed_down_weight[0]
    side = 2 * experts * lax.axis_index("narrow")
    places = jnp.stack([me, me + side, me + side + experts])
    picks = (jnp.arange(extra_back)[None, :] == places[:, None]).astype(f32)
    router_wide = jnp.pad(router_all, ((0, 0), (0, extra - experts)))
    expert_args = (x_rows, d_mine, d_mates, router_wide, picks, gate_w, up_w, down_w)
    out_rows, g_part, u_part = expert_forward(*expert_args)
    half = out_rows.shape[0] // 2
    theirs = swap_cores(out_rows[half:])
    routed_rows = (out_rows[:half].astype(f32) + theirs.astype(f32)).astype(bf16)
    routed_rows = routed_rows.reshape(micro, offsets, deep, slots, width_all)
    routed_back = plane_back(dims, routed_rows)

    shared_out, d_shared_in, grad_shared = shared_expert(
        x_column.reshape(-1, width_all), d_column.reshape(-1, width_all + extra), shared_all
    )
    grad_shared = grad_shared.astype(bf16)

    d_in_rows, grad_egate, grad_eup, grad_edown = expert_backward(*expert_args, g_part, u_part)
    d_total = give_back(
        dims,
        d_in_rows.reshape(2, micro, offsets, deep, slots, width_all + extra_back),
        choose_t,
        d_shared_in.reshape(x_column.shape),
    )
    choose_late, d_total = lax.optimization_barrier((choose, d_total))
    routed_sums = column_sums(dims, choose_late, routed_back, shared_out.reshape(x_column.shape))
    routed_own, routed_sent = column_back(dims, routed_sums)
    d_total = d_total.reshape(micro * seq_len, width_all + extra_back)
    d_gates = sum(d_total[:, width_all + n * experts : width_all + (n + 1) * experts] for n in range(4))

    named_rows = named.reshape(micro * seq_len, experts)
    gates = masked_gates(f32_dot(normed_mid, router_all), named_rows)
    d_out = cotangent[:, 0].reshape(micro * seq_len, width_all).astype(f32)

    d_logits = (gates * (d_gates - jnp.sum(gates * d_gates, axis=1, keepdims=True))).astype(bf16)
    d_mid = d_total[:, :width_all] + dot_t(d_logits, router_all)
    d_norm_two, grad_gain_two = norm_back(d_mid, plain_mid, scale_mid, gain_two)
    d_residual = d_out + d_norm_two
    d_attn = d_residual.astype(bf16)
    grad_wout = t_dot(mixed, d_attn).astype(bf16)
    d_mixed = dot_t(d_attn, wo_all).astype(bf16).reshape(micro, seq_len, heads, HD)
    d_probs = jnp.einsum("sqhd,skhd->shqk", d_mixed, value_rows, preferred_element_type=f32)
    d_value = jnp.einsum("shqk,sqhd->skhd", probs_low, d_mixed, preferred_element_type=f32)
    d_value = d_value.astype(bf16).reshape(micro * seq_len, width_all)
    d_scores = (probs * (d_probs - jnp.sum(probs * d_probs, axis=-1, keepdims=True))).astype(bf16)
    d_query = scale_factor * jnp.einsum("shqk,skhd->sqhd", d_scores, key_rows, preferred_element_type=f32)
    d_key = scale_factor * jnp.einsum("shqk,sqhd->skhd", d_scores, queries, preferred_element_type=f32)
    d_query = unrotate(d_query, cosine_table, sine_table).astype(bf16).reshape(micro * seq_len, width_all)
    d_key = unrotate(d_key, cosine_table, sine_table).astype(bf16).reshape(micro * seq_len, width_all)
    grad_wq = t_dot(normalized_input, d_query).astype(bf16)
    grad_wk = t_dot(normalized_input, d_key).astype(bf16)
    grad_wv = t_dot(normalized_input, d_value).astype(bf16)
    d_in = dot_t(d_query, wq_all) + dot_t(d_key, wk_all) + dot_t(d_value, wv_all)
    d_norm_one, grad_gain_one = norm_back(d_in, plain_in, scale_in, gain_one)
    grad_tokens = (d_residual + d_norm_one).reshape(micro, 1, seq_len, width_all)

    routed_sent, grad_wv = lax.optimization_barrier((routed_sent, grad_wv))
    final_rows = residual + (routed_own + sum(r.astype(f32) for r in routed_sent)).reshape(micro * seq_len, width_all)
    output = final_rows.astype(bf16).reshape(micro, 1, seq_len, width_all)

    column = jnp.arange(small_width)[None, :]
    grad_small = t_dot(normed_mid, jnp.pad(d_logits, ((0, 0), (0, small_width - experts))))
    grad_small = jnp.where(column == experts, grad_gain_one[:, None], grad_small)
    grad_small = jnp.where(column == experts + 1, grad_gain_two[:, None], grad_small).astype(bf16)

    (g_shared, g_wo, g_wq, g_wk, g_wv, g_small) = scatter_all(
        dims,
        [grad_shared, grad_wout, grad_wq, grad_wk, grad_wv, grad_small],
        [True, False, False, False, False, False],
    )

    def joined(n):
        pieces = g_shared[:, :, n * part : (n + 1) * part]
        return pieces.transpose(1, 0, 2).reshape(own_rows, deep * part)[:, :hidden_all]

    return (
        output,
        grad_tokens,
        g_small[:, experts],
        g_small[:, experts + 1],
        g_wq,
        g_wk,
        g_wv,
        g_wo,
        g_small[:, :experts],
        joined(0),
        joined(1),
        joined(2).T,
        grad_egate[None],
        grad_eup[None],
        grad_edown[None],
    )


def solution(mesh):
    return jax.shard_map(
        on_device,
        mesh=mesh,
        in_specs=(
            P(None, ("wide", "narrow"), None, None),
            P(None, ("wide", "narrow"), None, None),
            P(None, ("wide", "narrow"), None, None),
            P(("wide", "narrow")),
            P(("wide", "narrow")),
            P(("wide", "narrow"), None),
            P(("wide", "narrow"), None),
            P(("wide", "narrow"), None),
            P(("wide", "narrow"), None),
            P(("wide", "narrow"), None),
            P(("wide", "narrow"), None),
            P(("wide", "narrow"), None),
            P(None, ("wide", "narrow")),
            P("wide", None, "narrow"),
            P("wide", None, "narrow"),
            P("wide", "narrow", None),
        ),
        out_specs=(
            P(None, ("wide", "narrow"), None, None),
            P(None, ("wide", "narrow"), None, None),
            P(("wide", "narrow")),
            P(("wide", "narrow")),
            P(("wide", "narrow"), None),
            P(("wide", "narrow"), None),
            P(("wide", "narrow"), None),
            P(("wide", "narrow"), None),
            P(("wide", "narrow"), None),
            P(("wide", "narrow"), None),
            P(("wide", "narrow"), None),
            P(None, ("wide", "narrow")),
            P("wide", None, "narrow"),
            P("wide", None, "narrow"),
            P("wide", "narrow", None),
        ),
        check_vma=False,
    )
```

```python
import functools
import jax
import jax.numpy as jnp
from jax import lax
from jax.experimental import pallas as pl
from jax.experimental.pallas import tpu as pltpu
from jax.sharding import PartitionSpec as P

MESH = pl.DeviceIdType.MESH
HD = 128


epsilon = 1e-06


def angles(seq_len, head_size):
    position = jnp.arange(seq_len).astype(jnp.float32)
    exponent = jnp.arange(head_size // 2).astype(jnp.float32) * (2.0 / head_size)
    frequency = jnp.exp(-jnp.log(10000.0) * exponent)
    theta = position[:, None] * frequency[None, :]
    return (jnp.cos(theta)[:, None, :], jnp.sin(theta)[:, None, :])


def rotate(vectors, cosine_table, sine_table):
    middle = vectors.shape[-1] // 2
    first_half = vectors[..., :middle]
    second_half = vectors[..., middle:]
    return jnp.concatenate(
        [
            first_half * cosine_table - second_half * sine_table,
            second_half * cosine_table + first_half * sine_table,
        ],
        axis=-1,
    )


def unrotate(vectors, cosine_table, sine_table):
    middle = vectors.shape[-1] // 2
    first_half = vectors[..., :middle]
    second_half = vectors[..., middle:]
    return jnp.concatenate(
        [
            first_half * cosine_table + second_half * sine_table,
            second_half * cosine_table - first_half * sine_table,
        ],
        axis=-1,
    )


def norm_ahead(matrix, gain):
    scale_rows = lax.rsqrt(jnp.mean(matrix * matrix, axis=-1, keepdims=True) + epsilon)
    normed = matrix * scale_rows
    return ((normed * gain).astype(jnp.bfloat16), normed, scale_rows)


def norm_back(grad_rows, normed, scale_rows, gain):
    gain_grad = jnp.sum(grad_rows * normed, axis=0)
    inner = grad_rows * gain
    return (
        scale_rows * (inner - normed * jnp.mean(inner * normed, axis=-1, keepdims=True)),
        gain_grad,
    )


def silu_pair(pre_act):
    sigma = jax.nn.sigmoid(pre_act)
    return (pre_act * sigma, sigma * (1.0 + pre_act * (1.0 - sigma)))


def chip_grid(chips):
    deep = 4 if chips % 4 == 0 else 1
    rest = chips // deep
    high = max(d for d in range(1, rest + 1) if rest % d == 0 and d * d <= rest)
    return (deep, high, rest // high)

def place(dims):
    wide = lax.axis_index("wide")
    return wide // (dims[1] * dims[2]), (wide // dims[2]) % dims[1], wide % dims[2]

def greet(dims, a, b, c, core):
    deep, high, broad = dims
    barrier = pltpu.get_barrier_semaphore()
    def chip(i, j, k):
        return (i * high + j) * broad + k
    others = [(chip((a + r) % deep, b, c), core) for r in range(1, deep)]
    others += [(chip(a, (b + r) % high, c), core) for r in range(1, high)]
    others += [(chip(a, b, (c + r) % broad), core) for r in range(1, broad)]
    others += [(chip(a, b, c), 1 - core)]
    for other in others:
        pl.semaphore_signal(barrier, inc=1, device_id=other, device_id_type=MESH)
    pl.semaphore_wait(barrier, len(others))

def cut_columns(widths):
    pieces = []
    for n, width in enumerate(widths):
        tiles = width // 128
        middle = (tiles + 1) // 2 * 128
        pieces += [(n, 0, width)] if tiles < 6 else [(n, 0, middle), (n, middle, width)]
    return pieces


def gather_kernel(dims, arrays, pieces, sliced, *refs):
    deep, high, broad = dims
    count, ahead = len(pieces), 3
    rows_ref, column_ref = refs[arrays], refs[2 * arrays + 1]
    micro = rows_ref.shape[0]
    ins = [refs[n].at[..., lo:hi] for n, lo, hi in pieces]
    outs = [refs[arrays + 1 + n].at[..., lo:hi] for n, lo, hi in pieces]
    sliced = [sliced[n] for n, lo, hi in pieces]
    own_sem, s1, r1, s2, r2, s3, r3, sn, rn, sr, rr = refs[2 * arrays + 2 :]
    a, b, c = place(dims)
    core = lax.axis_index("narrow")
    greet(dims, a, b, c, core)

    def chip(i, j, k):
        return (i * high + j) * broad + k

    def send(src, dst, ss, rs, to):
        copy = pltpu.make_async_remote_copy(
            src_ref=src, dst_ref=dst, send_sem=ss, recv_sem=rs, device_id=to, device_id_type=MESH
        )
        return copy

    def program(me):
        first, second = (high, broad) if me == 0 else (broad, high)

        def at2(i, r):
            if me == 0:
                return outs[i].at[:, (b - r + high) % high, c, me]
            return outs[i].at[:, b, (c - r + broad) % broad, me]

        def at3(i, r):
            if me == 0:
                return outs[i].at[:, :, (c - r + broad) % broad, me]
            return outs[i].at[:, (b - r + high) % high, :, me]

        def to2(r):
            return (chip(a, (b + r) % high, c), me) if me == 0 else (chip(a, b, (c + r) % broad), me)

        def to3(r):
            return (chip(a, b, (c + r) % broad), me) if me == 0 else (chip(a, (b + r) % high, c), me)

        mate = (chip(a, b, c), 1 - me)

        def own(i):
            return pltpu.make_async_copy(ins[i].at[a] if sliced[i] else ins[i], outs[i].at[a, b, c, me], own_sem.at[i])

        def stage1(i, r):
            h = (a + r) % deep
            src = ins[i].at[h] if sliced[i] else ins[i]
            return send(src, outs[i].at[a, b, c, me], s1.at[i, r - 1], r1.at[i, r - 1], (chip(h, b, c), me))

        def own_rows():
            return pltpu.make_async_copy(rows_ref, column_ref.at[:, 0], own_sem.at[count])

        def column(m, r):
            to = (chip((a + r) % deep, b, c), me)
            return send(rows_ref.at[m], column_ref.at[m, r], sr.at[m, r - 1], rr.at[m, r - 1], to)

        def stage2(i, r):
            return send(at2(i, 0), at2(i, 0), s2.at[i, r - 1], r2.at[i, r - 1], to2(r))

        def stage3(i, r):
            return send(at3(i, 0), at3(i, 0), s3.at[i, r - 1], r3.at[i, r - 1], to3(r))

        def across(i, part):
            view = at2(i, 0) if part == 0 else at2(i, part) if part < first else at3(i, part - first + 1)
            return send(view, view, sn.at[i, part], rn.at[i, part], mate)

        parts = first + second - 1
        def begin(i):
            for r in range(1, deep):
                stage1(i, r).start()
            own(i).start()

        for i in range(min(ahead, count)):
            begin(i)
        own_rows().start()
        for step in range(count + 2):
            if step + ahead < count:
                begin(step + ahead)
            for m in range(micro):
                if step == min(2 + 2 * m, count + 1):
                    for r in range(1, deep):
                        column(m, r).start()
            i = step
            if i < count:
                own(i).wait()
                for r in range(1, deep):
                    stage1(i, r).wait_recv()
                for r in range(1, first):
                    stage2(i, r).start()
                across(i, 0).start()
            i = step - 1
            if 0 <= i < count:
                for r in range(1, first):
                    stage2(i, r).wait_recv()
                for r in range(1, second):
                    stage3(i, r).start()
                for r in range(1, first):
                    across(i, r).start()
            i = step - 2
            if 0 <= i < count:
                for r in range(1, second):
                    stage3(i, r).wait_recv()
                for r in range(1, second):
                    across(i, first + r - 1).start()
        for i in range(count):
            for r in range(1, deep):
                stage1(i, r).wait_send()
            for r in range(1, first):
                stage2(i, r).wait_send()
            for r in range(1, second):
                stage3(i, r).wait_send()
            for part in range(parts):
                across(i, part).wait()
        own_rows().wait()
        for m in range(micro):
            for r in range(1, deep):
                column(m, r).wait()

    pl.when(core == 0)(lambda: program(0))
    pl.when(core == 1)(lambda: program(1))

def gather_all(dims, parts, sliced, rows):
    arrays = len(parts)
    deep, high, broad = dims
    pieces = cut_columns([p.shape[-1] for p in parts])
    count = len(pieces)
    sem = pltpu.SemaphoreType.DMA
    most = max(high, broad)
    shapes = [p.shape[1:] if cut else p.shape for p, cut in zip(parts, sliced)]
    vmem, anywhere = pl.BlockSpec(memory_space=pltpu.VMEM), pl.BlockSpec(memory_space=pl.ANY)
    outs = pl.pallas_call(
        functools.partial(gather_kernel, dims, arrays, pieces, sliced),
        out_shape=[jax.ShapeDtypeStruct((deep, high, broad, 2) + sh, p.dtype) for p, sh in zip(parts, shapes)]
        + [jax.ShapeDtypeStruct(rows.shape[:1] + (deep,) + rows.shape[1:], rows.dtype)],
        in_specs=[vmem] * (arrays + 1),
        out_specs=[anywhere] * (arrays + 1),
        scratch_shapes=[sem((count + 1,))]
        + [sem((count, max(deep - 1, 1)))] * 2
        + [sem((count, max(most - 1, 1)))] * 4
        + [sem((count, high + broad - 1))] * 2
        + [sem((rows.shape[0], max(deep - 1, 1)))] * 2,
        compiler_params=pltpu.CompilerParams(collective_id=0, has_side_effects=True),
        name="gather_dense",
    )(*parts, rows)
    return [o.reshape((-1, sh[-1])) for o, sh in zip(outs[:-1], shapes)], outs[-1]


def scatter_kernel(dims, arrays, pieces, sliced, *refs):
    deep, high, broad = dims
    count, ahead = len(pieces), 3
    group = lambda m: [refs[m * arrays + n].at[..., lo:hi] for n, lo, hi in pieces]
    ins, outs, held, from_mate, got2, got3, got4 = [group(m) for m in range(7)]
    own_sem, sn, rn, s2, r2, s3, r3, s4, r4 = refs[7 * arrays :]
    sliced = [sliced[n] for n, lo, hi in pieces]
    a, b, c = place(dims)
    core = lax.axis_index("narrow")
    greet(dims, a, b, c, core)

    def chip(i, j, k):
        return (i * high + j) * broad + k

    def send(src, dst, ss, rs, to):
        return pltpu.make_async_remote_copy(
            src_ref=src, dst_ref=dst, send_sem=ss, recv_sem=rs, device_id=to, device_id_type=MESH
        )

    wide32 = jnp.float32

    def program(me):
        first, second = (broad, high) if me == 0 else (high, broad)
        mate = (chip(a, b, c), 1 - me)

        def own(i):
            return pltpu.make_async_copy(ins[i].at[:, :, :, me], held[i], own_sem.at[i])

        def across(i):
            return send(ins[i].at[:, :, :, 1 - me], from_mate[i], sn.at[i], rn.at[i], mate)

        def stage2(i, r):
            if me == 0:
                k = (c + r) % broad
                return send(held[i].at[:, :, k], got2[i].at[r - 1], s2.at[i, r - 1], r2.at[i, r - 1], (chip(a, b, k), me))
            j = (b + r) % high
            return send(held[i].at[:, j], got2[i].at[r - 1], s2.at[i, r - 1], r2.at[i, r - 1], (chip(a, j, c), me))

        def stage3(i, r):
            if me == 0:
                j = (b + r) % high
                return send(held[i].at[:, j, c], got3[i].at[r - 1], s3.at[i, r - 1], r3.at[i, r - 1], (chip(a, j, c), me))
            k = (c + r) % broad
            return send(held[i].at[:, b, k], got3[i].at[r - 1], s3.at[i, r - 1], r3.at[i, r - 1], (chip(a, b, k), me))

        def stage4(i, r):
            h = (a + r) % deep
            return send(held[i].at[h, b, c], got4[i].at[r - 1], s4.at[i, r - 1], r4.at[i, r - 1], (chip(h, b, c), me))

        def add_mate(i):
            for j in range(high):
                for k in range(broad):
                    @pl.loop(0, deep)
                    def _(h):
                        held[i][h, j, k] = (held[i][h, j, k].astype(wide32) + from_mate[i][h, j, k].astype(wide32)).astype(jnp.bfloat16)

        def add2(i):
            if me == 0:
                for j in range(high):
                    @pl.loop(0, deep)
                    def _(h):
                        total = held[i][h, j, c].astype(wide32)
                        for r in range(1, broad):
                            total += got2[i][r - 1, h, j].astype(wide32)
                        held[i][h, j, c] = total.astype(jnp.bfloat16)
            else:
                for k in range(broad):
                    @pl.loop(0, deep)
                    def _(h):
                        total = held[i][h, b, k].astype(wide32)
                        for r in range(1, high):
                            total += got2[i][r - 1, h, k].astype(wide32)
                        held[i][h, b, k] = total.astype(jnp.bfloat16)

        def add3(i):
            @pl.loop(0, deep)
            def _(h):
                total = held[i][h, b, c].astype(wide32)
                for r in range(1, second):
                    total += got3[i][r - 1, h].astype(wide32)
                held[i][h, b, c] = total.astype(jnp.bfloat16)

        def add4(i):
            if sliced[i]:
                outs[i][a] = held[i][a, b, c].astype(wide32)
                for r in range(1, deep):
                    outs[i][(a - r + deep) % deep] = got4[i][r - 1].astype(wide32)
                return
            total = held[i][a, b, c].astype(wide32)
            for r in range(1, deep):
                total += got4[i][r - 1].astype(wide32)
            outs[i][...] = total

        def begin(i):
            across(i).start()
            own(i).start()

        for i in range(min(ahead, count)):
            begin(i)
        for step in range(count + 3):
            if step + ahead < count:
                begin(step + ahead)
            i = step
            if i < count:
                own(i).wait()
                across(i).wait_recv()
                add_mate(i)
                for r in range(1, first):
                    stage2(i, r).start()
            i = step - 1
            if 0 <= i < count:
                for r in range(1, first):
                    stage2(i, r).wait_recv()
                add2(i)
                for r in range(1, second):
                    stage3(i, r).start()
            i = step - 2
            if 0 <= i < count:
                for r in range(1, second):
                    stage3(i, r).wait_recv()
                add3(i)
                for r in range(1, deep):
                    stage4(i, r).start()
            i = step - 3
            if 0 <= i < count:
                for r in range(1, deep):
                    stage4(i, r).wait_recv()
                add4(i)
        for i in range(count):
            across(i).wait_send()
            for r in range(1, first):
                stage2(i, r).wait_send()
            for r in range(1, second):
                stage3(i, r).wait_send()
            for r in range(1, deep):
                stage4(i, r).wait_send()

    pl.when(core == 0)(lambda: program(0))
    pl.when(core == 1)(lambda: program(1))

def scatter_all(dims, parts, sliced):
    arrays = len(parts)
    deep, high, broad = dims
    pieces = cut_columns([p.shape[-1] for p in parts])
    count = len(pieces)
    devices = deep * high * broad * 2
    blocks = [(p.shape[0] // devices, p.shape[1]) for p in parts]
    sem = pltpu.SemaphoreType.DMA
    most = max(high, broad)
    vm = lambda lead: [pltpu.VMEM(lead + blk, jnp.bfloat16) for blk in blocks]
    side = max(high, broad)
    got2 = vm((max(most - 1, 1), deep, side))
    return pl.pallas_call(
        functools.partial(scatter_kernel, dims, arrays, pieces, sliced),
        out_shape=[jax.ShapeDtypeStruct(((deep,) if cut else ()) + blk, jnp.float32) for blk, cut in zip(blocks, sliced)],
        in_specs=[pl.BlockSpec(memory_space=pl.ANY)] * arrays,
        out_specs=[pl.BlockSpec(memory_space=pltpu.VMEM)] * arrays,
        scratch_shapes=vm((deep, high, broad)) + vm((deep, high, broad)) + got2 + vm((max(most - 1, 1), deep)) + vm((max(deep - 1, 1),))
        + [sem((count,))] * 3
        + [sem((count, max(most - 1, 1)))] * 4
        + [sem((count, max(deep - 1, 1)))] * 2,
        compiler_params=pltpu.CompilerParams(collective_id=1, has_side_effects=True, vmem_limit_bytes=62 * 1024 * 1024),
        name="scatter_dense",
    )(*[p.reshape((deep, high, broad, 2) + blk) for p, blk in zip(parts, blocks)])


def greet_all(dims, a, b, c, core):
    deep, high, broad = dims
    barrier = pltpu.get_barrier_semaphore()
    others = [(((a + r) % deep * high + b) * broad + c, core) for r in range(1, deep)]
    others += [
        ((a * high + (b + q // broad) % high) * broad + (c + q % broad) % broad, core) for q in range(1, high * broad)
    ]
    others += [((a * high + b) * broad + c, 1 - core)]
    for other in others:
        pl.semaphore_signal(barrier, inc=1, device_id=other, device_id_type=MESH)
    pl.semaphore_wait(barrier, len(others))


def remote(src, dst, ss, rs, to):
    return pltpu.make_async_remote_copy(
        src_ref=src, dst_ref=dst, send_sem=ss, recv_sem=rs, device_id=to, device_id_type=MESH
    )


def dispatch_kernel(dims, micro, x_ref, choose_ref, both_ref, column_ref, got, picked, scol, rcol, spl, rpl, sm, rm, sl):
    deep, high, broad = dims
    offsets = high * broad
    a, b, c = place(dims)
    core = lax.axis_index("narrow")
    greet_all(dims, a, b, c, core)
    mate = ((a * high + b) * broad + c, 1 - core)
    rows_ref, mates_ref = both_ref.at[0], both_ref.at[1]

    def column(m, k):
        return remote(x_ref.at[m], got.at[m, k], scol.at[m, k], rcol.at[m, k], (((a + k) % deep * high + b) * broad + c, core))

    def plane(m, k, q):
        to = (a * high + (b + q // broad) % high) * broad + (c + q % broad) % broad
        return remote(picked.at[m, k, q], rows_ref.at[m, q, k], spl.at[m, k, q], rpl.at[m, k, q], (to, core))

    def across(m, k, part):
        if part == 0:
            return remote(picked.at[m, k, 0], mates_ref.at[m, 0, k], sm.at[m, k, 0], rm.at[m, k, 0], mate)
        return remote(rows_ref.at[m, 1:, k], mates_ref.at[m, 1:, k], sm.at[m, k, 1], rm.at[m, k, 1], mate)

    def keep(m, k):
        return pltpu.make_async_copy(picked.at[m, k, 0], rows_ref.at[m, 0, k], sl.at[m, k, 0])

    def keep_column(m, k):
        return pltpu.make_async_copy(x_ref.at[m] if k == 0 else got.at[m, k], column_ref.at[m, k], sl.at[m, k, 1])

    order = [(m, k) for m in range(micro) for k in range(deep)]
    for m, k in order:
        if k > 0:
            column(m, k).start()
    for m, k in order:
        if k > 0:
            column(m, k).wait_recv()
        keep_column(m, k).start()
        piece = x_ref[m] if k == 0 else got[m, k]
        chosen = jnp.dot(choose_ref[m, k], piece, preferred_element_type=jnp.float32).astype(jnp.bfloat16)
        picked[m, k] = chosen.reshape(picked.shape[2:])
        for q in range(1, offsets):
            plane(m, k, q).start()
        keep(m, k).start()
        across(m, k, 0).start()
    for m, k in order:
        for q in range(1, offsets):
            plane(m, k, q).wait_recv()
        across(m, k, 1).start()
    for m, k in order:
        if k > 0:
            column(m, k).wait_send()
        keep_column(m, k).wait()
        for q in range(1, offsets):
            plane(m, k, q).wait_send()
        keep(m, k).wait()
        across(m, k, 0).wait()
        across(m, k, 1).wait()


def dispatch(dims, x, choose):
    deep, high, broad = dims
    micro, tokens, width = x.shape
    offsets = high * broad
    slots = choose.shape[2] // offsets
    sem = pltpu.SemaphoreType.DMA
    anywhere, vmem = pl.BlockSpec(memory_space=pl.ANY), pl.BlockSpec(memory_space=pltpu.VMEM)
    out = jax.ShapeDtypeStruct((2, micro, offsets, deep, slots, width), x.dtype)
    return pl.pallas_call(
        functools.partial(dispatch_kernel, dims, micro),
        out_shape=[out, jax.ShapeDtypeStruct((micro, deep, tokens, width), x.dtype)],
        in_specs=[vmem, vmem],
        out_specs=[anywhere] * 2,
        scratch_shapes=[
            pltpu.VMEM((micro, deep, tokens, width), x.dtype),
            pltpu.VMEM((micro, deep, offsets, slots, width), x.dtype),
        ]
        + [sem((micro, deep))] * 2
        + [sem((micro, deep, offsets))] * 2
        + [sem((micro, deep, 2))] * 3,
        compiler_params=pltpu.CompilerParams(collective_id=2, has_side_effects=True),
        name="dispatch_rows",
    )(x, choose)


def return_kernel(dims, micro, both_ref, choose_ref, near_ref, total_ref, held, mated, back, up, got, sl, sm, rm, spl, rpl, scol, rcol):
    deep, high, broad = dims
    offsets = high * broad
    a, b, c = place(dims)
    core = lax.axis_index("narrow")
    greet_all(dims, a, b, c, core)
    mate = ((a * high + b) * broad + c, 1 - core)
    near_width = near_ref.shape[-1]
    mine_ref, theirs_ref = both_ref.at[0], both_ref.at[1]

    def load(m, k):
        return pltpu.make_async_copy(mine_ref.at[m, :, k], held.at[m, :, k], sl.at[m, k])

    def across(m, k):
        return remote(theirs_ref.at[m, :, k], mated.at[m, :, k], sm.at[m, k], rm.at[m, k], mate)

    def plane(m, k, q):
        to = (a * high + (b - q // broad + high) % high) * broad + (c - q % broad + broad) % broad
        return remote(held.at[m, q, k], back.at[m, k, q], spl.at[m, k, q], rpl.at[m, k, q], (to, core))

    def column(m, k):
        return remote(up.at[m, k], got.at[m, k], scol.at[m, k], rcol.at[m, k], (((a - k + deep) % deep * high + b) * broad + c, core))

    order = [(m, k) for m in range(micro) for k in list(range(1, deep)) + [0]]
    ahead = 3
    for m, k in order[:ahead]:
        across(m, k).start()
        load(m, k).start()
    for n, (m, k) in enumerate(order):
        for later in order[n + ahead : n + ahead + 1]:
            across(*later).start()
            load(*later).start()
        load(m, k).wait()
        across(m, k).wait_recv()
        for q in range(1, offsets):
            held[m, q, k] = (held[m, q, k].astype(jnp.float32) + mated[m, q, k].astype(jnp.float32)).astype(jnp.bfloat16)
            plane(m, k, q).start()
        back[m, k, 0] = (held[m, 0, k].astype(jnp.float32) + mated[m, 0, k].astype(jnp.float32)).astype(jnp.bfloat16)
    for m, k in order:
        for q in range(1, offsets):
            plane(m, k, q).wait_recv()
        rows = back[m, k].reshape((-1, back.shape[-1]))
        sums = jnp.dot(choose_ref[m, k], rows, preferred_element_type=jnp.float32)
        dense = sums[:, :near_width] + near_ref[m, k].astype(jnp.float32)
        if k == 0:
            total_ref[m, :, :near_width] = dense
            if near_width < sums.shape[1]:
                total_ref[m, :, near_width:] = sums[:, near_width:]
        else:
            up[m, k, :, :near_width] = dense.astype(jnp.bfloat16)
            if near_width < sums.shape[1]:
                up[m, k, :, near_width:] = sums[:, near_width:].astype(jnp.bfloat16)
            column(m, k).start()
    for m in range(micro):
        for k in range(1, deep):
            column(m, k).wait_recv()
            total_ref[m] += got[m, k].astype(jnp.float32)
    for m, k in order:
        across(m, k).wait_send()
        for q in range(1, offsets):
            plane(m, k, q).wait_send()
        if k > 0:
            column(m, k).wait_send()


def give_back(dims, both, choose_t, near):
    deep, high, broad = dims
    _, micro, offsets, _, slots, width = both.shape
    tokens = choose_t.shape[2]
    sem = pltpu.SemaphoreType.DMA
    anywhere, vmem = pl.BlockSpec(memory_space=pl.ANY), pl.BlockSpec(memory_space=pltpu.VMEM)
    scratch = lambda *shape: pltpu.VMEM(shape, both.dtype)
    return pl.pallas_call(
        functools.partial(return_kernel, dims, micro),
        out_shape=jax.ShapeDtypeStruct((micro, tokens, width), jnp.float32),
        in_specs=[anywhere, vmem, vmem],
        out_specs=vmem,
        scratch_shapes=[
            scratch(micro, offsets, deep, slots, width),
            scratch(micro, offsets, deep, slots, width),
            scratch(micro, deep, offsets, slots, width),
            scratch(micro, deep, tokens, width),
            scratch(micro, deep, tokens, width),
        ]
        + [sem((micro, deep))] * 3
        + [sem((micro, deep, offsets))] * 2
        + [sem((micro, deep))] * 2,
        compiler_params=pltpu.CompilerParams(collective_id=3, has_side_effects=True, vmem_limit_bytes=62 * 1024 * 1024),
        name="return_rows",
    )(both, choose_t, near)


def column_pairs(dims, shift):
    deep, plane = dims[0], dims[1] * dims[2]
    return [(i * plane + p, ((i + shift) % deep) * plane + p) for i in range(deep) for p in range(plane)]


def plane_pairs(dims, offset, sign):
    deep, high, broad = dims
    up, over = (offset // broad) * sign, (offset % broad) * sign
    return [
        ((i * high + j) * broad + k, (i * high + (j + up) % high) * broad + (k + over) % broad)
        for i in range(deep)
        for j in range(high)
        for k in range(broad)
    ]


def swap_cores(rows):
    return lax.ppermute(rows, "narrow", [(0, 1), (1, 0)])


def plane_rows(dims, picked):
    return [picked[0]] + [lax.ppermute(picked[q], "wide", plane_pairs(dims, q, 1)) for q in range(1, picked.shape[0])]


def plane_back(dims, rows):
    offsets = rows.shape[1]
    return [rows[:, 0]] + [lax.ppermute(rows[:, q], "wide", plane_pairs(dims, q, -1)) for q in range(1, offsets)]


def column_sums(dims, choose, back, near):
    sums = jnp.einsum("mkst,mksd->mktd", choose, back, preferred_element_type=jnp.float32)
    return sums + near.astype(jnp.float32)


def column_back(dims, parts):
    return [lax.ppermute(part, "wide", column_pairs(dims, -k - 1)) for k, part in enumerate(parts)]


def masked_gates(logits, named):
    top = jnp.max(jnp.where(named > 0, logits, -1e30), axis=-1, keepdims=True)
    weights = jnp.where(named > 0, jnp.exp(logits - top), 0.0)
    return weights / jnp.maximum(jnp.sum(weights, axis=-1, keepdims=True), 0.5)


def f32_dot(one, two):
    return jnp.dot(one, two, preferred_element_type=jnp.float32)


def dot_t(one, two):
    return lax.dot_general(one, two, (((1,), (1,)), ((), ())), preferred_element_type=jnp.float32)


def t_dot(one, two):
    return lax.dot_general(one, two, (((0,), (0,)), ((), ())), preferred_element_type=jnp.float32)


def own_gate(x, router, names, pick):
    row_gates = masked_gates(f32_dot(x, router), names.astype(jnp.float32))
    return jnp.sum(row_gates * pick[:, : row_gates.shape[1]], axis=-1, keepdims=True)


def expert_forward_kernel(half, x_ref, names_ref, mate_names_ref, router_ref, pick_ref, gate_w, up_w, down_w, out_ref, g_ref, u_ref):
    x = x_ref[...]
    names = jnp.where(pl.program_id(0) < half, names_ref[...], mate_names_ref[...])
    gate = own_gate(x, router_ref[...], names, pick_ref[0:1])
    g = f32_dot(x, gate_w[...])
    u = f32_dot(x, up_w[...])
    g_ref[...] = g
    u_ref[...] = u
    act, _ = silu_pair(g)
    out_ref[...] = f32_dot((gate * (act * u)).astype(jnp.bfloat16), down_w[...]).astype(jnp.bfloat16)


def expert_backward_kernel(
    half, width, x_ref, d_ref, mate_d_ref, router_ref, pick_ref, gate_w, up_w, down_w, g_ref, u_ref, in_ref, dg_ref, du_ref, dd_ref
):
    step = pl.program_id(0)
    x = x_ref[...]
    ext = jnp.where(step < half, d_ref[...], mate_d_ref[...])
    dy, names = ext[:, :width], ext[:, width:]
    gate = own_gate(x, router_ref[...], names, pick_ref[0:1])
    act, slope = silu_pair(g_ref[...])
    u = u_ref[...]
    d_plain = dot_t(dy, down_w[...])
    hidden = act * u
    d_gate = jnp.sum(hidden * d_plain, axis=-1, keepdims=True)
    weighed = (gate * hidden).astype(jnp.bfloat16)
    d_hidden = gate * d_plain
    d_act = (d_hidden * u * slope).astype(jnp.bfloat16)
    d_up = (d_hidden * act).astype(jnp.bfloat16)
    rows = dot_t(d_act, gate_w[...]) + dot_t(d_up, up_w[...])
    in_ref[:, :width] = rows.astype(jnp.bfloat16)
    coarse = d_gate.astype(jnp.bfloat16).astype(jnp.float32)
    beside = coarse * pick_ref[1:2] + (d_gate - coarse) * pick_ref[2:3]
    in_ref[:, width:] = beside.astype(jnp.bfloat16)

    @pl.when(step == 0)
    def _():
        dg_ref[...] = jnp.zeros_like(dg_ref)
        du_ref[...] = jnp.zeros_like(du_ref)
        dd_ref[...] = jnp.zeros_like(dd_ref)

    dg_ref[...] += t_dot(x, d_act)
    du_ref[...] += t_dot(x, d_up)
    dd_ref[...] += t_dot(weighed, dy)


def fixed(shape):
    return pl.BlockSpec(shape, lambda i: (0,) * len(shape), pipeline_mode=pl.Buffered(1))


def row_block(total):
    return max(n for n in (512, 256, 128, 64, 32, 16) if total % n == 0)


def roomy():
    return pltpu.CompilerParams(vmem_limit_bytes=60 * 1024 * 1024)


def cost(flops, moved):
    return pl.CostEstimate(flops=flops, bytes_accessed=moved, transcendentals=0)


def expert_forward(x, d_mine, d_mates, router, picks, gate_w, up_w, down_w):
    rows, width = x.shape
    hidden = gate_w.shape[1]
    block = row_block(d_mine.shape[0])
    half = d_mine.shape[0] // block
    names = d_mine.shape[1] - width
    at = width // names
    by_row = lambda w: pl.BlockSpec((block, w), lambda i: (i, 0))
    first = pl.BlockSpec((block, names), lambda i: (jnp.minimum(i, half - 1), at))
    second = pl.BlockSpec((block, names), lambda i: (jnp.maximum(i - half, 0), at))
    return pl.pallas_call(
        functools.partial(expert_forward_kernel, half),
        grid=(2 * half,),
        out_shape=[
            jax.ShapeDtypeStruct((rows, width), jnp.bfloat16),
            jax.ShapeDtypeStruct((rows, hidden), jnp.float32),
            jax.ShapeDtypeStruct((rows, hidden), jnp.float32),
        ],
        in_specs=[by_row(width), first, second, fixed(router.shape), fixed(picks.shape)]
        + [fixed(w.shape) for w in (gate_w, up_w, down_w)],
        out_specs=[by_row(width), by_row(hidden), by_row(hidden)],
        compiler_params=roomy(),
        cost_estimate=cost(6 * rows * width * hidden, rows * (4 * width + 8 * hidden)),
        name="expert_forward",
    )(x, d_mine, d_mates, router, picks, gate_w, up_w, down_w)


def expert_backward(x, d_mine, d_mates, router, picks, gate_w, up_w, down_w, g, u):
    rows, width = x.shape
    hidden = gate_w.shape[1]
    block = row_block(d_mine.shape[0])
    half = d_mine.shape[0] // block
    wide_d = d_mine.shape[1]
    by_row = lambda w: pl.BlockSpec((block, w), lambda i: (i, 0))
    first = pl.BlockSpec((block, wide_d), lambda i: (jnp.minimum(i, half - 1), 0))
    second = pl.BlockSpec((block, wide_d), lambda i: (jnp.maximum(i - half, 0), 0))
    wide_in = width + picks.shape[1]
    return pl.pallas_call(
        functools.partial(expert_backward_kernel, half, width),
        grid=(2 * half,),
        out_shape=[jax.ShapeDtypeStruct((rows, wide_in), jnp.bfloat16)]
        + [jax.ShapeDtypeStruct(w.shape, jnp.float32) for w in (gate_w, up_w, down_w)],
        in_specs=[by_row(width), first, second, fixed(router.shape), fixed(picks.shape)]
        + [fixed(w.shape) for w in (gate_w, up_w, down_w)]
        + [by_row(hidden), by_row(hidden)],
        out_specs=[by_row(wide_in)] + [fixed(w.shape) for w in (gate_w, up_w, down_w)],
        compiler_params=roomy(),
        cost_estimate=cost(12 * rows * width * hidden, rows * (6 * width + 8 * hidden)),
        name="expert_backward",
    )(x, d_mine, d_mates, router, picks, gate_w, up_w, down_w, g, u)


def shared_kernel(width, part, x_ref, d_ref, w_ref, out_ref, in_ref, grad_ref):
    x, dy = x_ref[...], d_ref[:, :width]
    gate_w, up_w, down_t = w_ref[:, :part], w_ref[:, part : 2 * part], w_ref[:, 2 * part :]
    act, slope = silu_pair(f32_dot(x, gate_w))
    u = f32_dot(x, up_w)
    hidden = (act * u).astype(jnp.bfloat16)
    out_ref[...] = dot_t(hidden, down_t).astype(jnp.bfloat16)
    d_hidden = f32_dot(dy, down_t)
    d_gate = (d_hidden * u * slope).astype(jnp.bfloat16)
    d_up = (d_hidden * act).astype(jnp.bfloat16)
    in_ref[...] = (dot_t(d_gate, gate_w) + dot_t(d_up, up_w)).astype(jnp.bfloat16)

    @pl.when(pl.program_id(0) == 0)
    def _():
        grad_ref[...] = jnp.zeros_like(grad_ref)

    grad_ref[:, :part] += t_dot(x, d_gate)
    grad_ref[:, part : 2 * part] += t_dot(x, d_up)
    grad_ref[:, 2 * part :] += t_dot(dy, hidden)


def shared_expert(x, d, weights):
    rows, width = x.shape
    part = weights.shape[1] // 3
    block = row_block(rows)
    by_row = lambda w: pl.BlockSpec((block, w), lambda i: (i, 0))
    return pl.pallas_call(
        functools.partial(shared_kernel, width, part),
        grid=(rows // block,),
        out_shape=[jax.ShapeDtypeStruct((rows, width), jnp.bfloat16)] * 2 + [jax.ShapeDtypeStruct(weights.shape, jnp.float32)],
        in_specs=[by_row(width), by_row(d.shape[1]), fixed(weights.shape)],
        out_specs=[by_row(width)] * 2 + [fixed(weights.shape)],
        compiler_params=roomy(),
        cost_estimate=cost(18 * rows * width * part, rows * 8 * width),
        name="shared_expert",
    )(x, d, weights)


def on_device(
    tokens,
    cotangent,
    routes,
    gain_attn,
    gain_moe,
    w_query,
    w_key,
    w_value,
    attention_output_weight,
    router,
    shared_gate,
    shared_up,
    shared_down,
    routed_gate_weight,
    routed_up_weight,
    routed_down_weight,
):
    f32, bf16 = jnp.float32, jnp.bfloat16
    micro = tokens.shape[0]
    seq_len, width_all = tokens.shape[2], tokens.shape[3]
    chosen_count = routes.shape[3]
    experts = router.shape[1]
    heads = width_all // HD
    dims = chip_grid(lax.axis_size("wide"))
    deep, high, broad = dims
    slots = 9 * seq_len * chosen_count // (8 * experts) + 1
    extra = -(-experts // 128) * 128
    extra_back = -(-4 * experts // 128) * 128
    cosine_table, sine_table = angles(seq_len, HD)
    scale_factor = HD ** (-0.5)
    causal_mask = jnp.arange(seq_len)[:, None] >= jnp.arange(seq_len)[None, :]
    me = lax.axis_index("wide")
    own_rows = gain_attn.shape[0]

    named = jnp.any(routes[:, 0, :, :, None] == jnp.arange(experts), axis=2)
    named_wide = jnp.pad(named.astype(bf16), ((0, 0), (0, 0), (0, extra - experts)))
    d_out_rows = jnp.concatenate([cotangent[:, 0], named_wide], axis=-1)

    small_width = -(-(experts + 2) // 128) * 128
    small = jnp.concatenate(
        [router, gain_attn[:, None], gain_moe[:, None], jnp.zeros((own_rows, small_width - experts - 2), bf16)], axis=1
    )
    hidden_all = shared_gate.shape[1]
    part = -(-hidden_all // (deep * 128)) * 128

    def cut(matrix):
        return jnp.pad(matrix, ((0, 0), (0, part * deep - hidden_all))).reshape(own_rows, deep, part).transpose(1, 0, 2)

    shared = jnp.concatenate([cut(shared_gate), cut(shared_up), cut(shared_down.T)], axis=2)
    (small_all, wq_all, wk_all, wv_all, wo_all, shared_all), d_column = gather_all(
        dims,
        [small, w_query, w_key, w_value, attention_output_weight, shared],
        [False, False, False, False, False, True],
        d_out_rows,
    )
    router_all = small_all[:, :experts]
    gain_one = small_all[:, experts].astype(f32)
    gain_two = small_all[:, experts + 1].astype(f32)

    chip_a, chip_b, chip_c = place(dims)
    offsets = high * broad
    step = jnp.arange(offsets)
    targets = (chip_a * high + (chip_b + step // broad) % high) * broad + (chip_c + step % broad) % broad
    is_target = (jnp.arange(experts)[:, None] == targets[None, :]).astype(bf16)
    earlier = (jnp.arange(seq_len)[:, None] > jnp.arange(seq_len)[None, :]).astype(bf16)
    names = d_column[..., width_all : width_all + experts]
    aimed = jnp.einsum("mkte,eq->mkqt", names, is_target, preferred_element_type=f32)
    slot = jnp.einsum("mkqu,tu->mkqt", aimed.astype(bf16), earlier, preferred_element_type=f32)
    hit = (slot[:, :, :, None, :] == jnp.arange(slots, dtype=f32)[:, None]) & (aimed[:, :, :, None, :] > 0.5)
    choose = hit.astype(bf16).reshape(micro, deep, offsets * slots, seq_len)
    choose_t = choose.transpose(0, 1, 3, 2)

    d_picked_rows = jnp.einsum("mkqst,mktd->qmksd", hit.astype(bf16), d_column, preferred_element_type=f32).astype(bf16)
    d_pieces = plane_rows(dims, d_picked_rows)

    rows_in = tokens[:, 0].reshape(micro * seq_len, width_all).astype(f32)
    normalized_input, plain_in, scale_in = norm_ahead(rows_in, gain_one)
    raw_query = f32_dot(normalized_input, wq_all).reshape(micro, seq_len, heads, HD)
    raw_key = f32_dot(normalized_input, wk_all).reshape(micro, seq_len, heads, HD)
    queries = rotate(raw_query, cosine_table, sine_table).astype(bf16)
    key_rows = rotate(raw_key, cosine_table, sine_table).astype(bf16)
    value_rows = f32_dot(normalized_input, wv_all).astype(bf16).reshape(micro, seq_len, heads, HD)
    scores = scale_factor * jnp.einsum("sqhd,skhd->shqk", queries, key_rows, preferred_element_type=f32)
    scores = jnp.where(causal_mask, scores, -1e30)
    row_top = jnp.max(scores, axis=-1, keepdims=True)
    exp_rows = jnp.exp(scores - row_top)
    probs = exp_rows / jnp.sum(exp_rows, axis=-1, keepdims=True)
    probs_low = probs.astype(bf16)
    mixed = jnp.einsum("shqk,skhd->sqhd", probs_low, value_rows, preferred_element_type=f32)
    mixed = mixed.astype(bf16).reshape(micro * seq_len, width_all)
    residual = rows_in + f32_dot(mixed, wo_all)
    normed_mid, plain_mid, scale_mid = norm_ahead(residual, gain_two)

    d_pieces, normed_mid = lax.optimization_barrier((d_pieces, normed_mid))
    d_mine = jnp.stack(d_pieces, axis=1).reshape(micro, -1, width_all + extra)
    d_mates = swap_cores(d_mine)

    x_both, x_column = dispatch(dims, normed_mid.reshape(micro, seq_len, width_all), choose)
    x_rows = x_both.reshape(-1, width_all)
    d_mine, d_mates = (d.reshape(-1, width_all + extra) for d in (d_mine, d_mates))

    gate_w, up_w, down_w = routed_gate_weight[0], routed_up_weight[0], routed_down_weight[0]
    side = 2 * experts * lax.axis_index("narrow")
    places = jnp.stack([me, me + side, me + side + experts])
    picks = (jnp.arange(extra_back)[None, :] == places[:, None]).astype(f32)
    router_wide = jnp.pad(router_all, ((0, 0), (0, extra - experts)))
    expert_args = (x_rows, d_mine, d_mates, router_wide, picks, gate_w, up_w, down_w)
    out_rows, g_part, u_part = expert_forward(*expert_args)
    half = out_rows.shape[0] // 2
    out_mine, out_theirs = out_rows[:half], out_rows[half:]
    theirs = swap_cores(out_theirs)

    out_mine, x_column = lax.optimization_barrier((out_mine, x_column))
    shared_out, d_shared_in, grad_shared = shared_expert(
        x_column.reshape(-1, width_all), d_column.reshape(-1, width_all + extra), shared_all
    )
    grad_shared = grad_shared.astype(bf16)
    theirs, shared_out = lax.optimization_barrier((theirs, shared_out))
    routed_rows = (out_mine.astype(f32) + theirs.astype(f32)).astype(bf16)
    routed_rows = routed_rows.reshape(micro, offsets, deep, slots, width_all)

    x_late, routed_rows = lax.optimization_barrier((x_rows, routed_rows))
    routed_pieces = plane_back(dims, routed_rows)
    d_in_rows, grad_egate, grad_eup, grad_edown = expert_backward(x_late, *expert_args[1:], g_part, u_part)
    routed_pieces, d_in_rows = lax.optimization_barrier((routed_pieces, d_in_rows))
    routed_back = jnp.stack(routed_pieces, axis=2).reshape(micro, deep, offsets * slots, width_all)
    routed_sums = column_sums(dims, choose, routed_back, shared_out.reshape(x_column.shape))
    routed_own, routed_up = routed_sums[:, 0], [routed_sums[:, k].astype(bf16) for k in range(1, deep)]
    routed_up, d_in_rows = lax.optimization_barrier((routed_up, d_in_rows))
    routed_sent = column_back(dims, routed_up)
    d_total = give_back(
        dims,
        d_in_rows.reshape(2, micro, offsets, deep, slots, width_all + extra_back),
        choose_t,
        d_shared_in.reshape(x_column.shape),
    )
    d_total = d_total.reshape(micro * seq_len, width_all + extra_back)
    d_gates = sum(d_total[:, width_all + n * experts : width_all + (n + 1) * experts] for n in range(4))

    named_rows = named.reshape(micro * seq_len, experts)
    gates = masked_gates(f32_dot(normed_mid, router_all), named_rows)
    d_out = cotangent[:, 0].reshape(micro * seq_len, width_all).astype(f32)

    d_logits = (gates * (d_gates - jnp.sum(gates * d_gates, axis=1, keepdims=True))).astype(bf16)
    d_mid = d_total[:, :width_all] + dot_t(d_logits, router_all)
    d_norm_two, grad_gain_two = norm_back(d_mid, plain_mid, scale_mid, gain_two)
    d_residual = d_out + d_norm_two
    d_attn = d_residual.astype(bf16)
    grad_wout = t_dot(mixed, d_attn).astype(bf16)
    d_mixed = dot_t(d_attn, wo_all).astype(bf16).reshape(micro, seq_len, heads, HD)
    d_probs = jnp.einsum("sqhd,skhd->shqk", d_mixed, value_rows, preferred_element_type=f32)
    d_value = jnp.einsum("shqk,sqhd->skhd", probs_low, d_mixed, preferred_element_type=f32)
    d_value = d_value.astype(bf16).reshape(micro * seq_len, width_all)
    d_scores = (probs * (d_probs - jnp.sum(probs * d_probs, axis=-1, keepdims=True))).astype(bf16)
    d_query = scale_factor * jnp.einsum("shqk,skhd->sqhd", d_scores, key_rows, preferred_element_type=f32)
    d_key = scale_factor * jnp.einsum("shqk,sqhd->skhd", d_scores, queries, preferred_element_type=f32)
    d_query = unrotate(d_query, cosine_table, sine_table).astype(bf16).reshape(micro * seq_len, width_all)
    d_key = unrotate(d_key, cosine_table, sine_table).astype(bf16).reshape(micro * seq_len, width_all)
    grad_wq = t_dot(normalized_input, d_query).astype(bf16)
    grad_wk = t_dot(normalized_input, d_key).astype(bf16)
    grad_wv = t_dot(normalized_input, d_value).astype(bf16)
    d_in = dot_t(d_query, wq_all) + dot_t(d_key, wk_all) + dot_t(d_value, wv_all)
    d_norm_one, grad_gain_one = norm_back(d_in, plain_in, scale_in, gain_one)
    grad_tokens = (d_residual + d_norm_one).reshape(micro, 1, seq_len, width_all)

    routed_sent, grad_wv = lax.optimization_barrier((routed_sent, grad_wv))
    final_rows = residual + (routed_own + sum(r.astype(f32) for r in routed_sent)).reshape(micro * seq_len, width_all)
    output = final_rows.astype(bf16).reshape(micro, 1, seq_len, width_all)

    column = jnp.arange(small_width)[None, :]
    grad_small = t_dot(normed_mid, jnp.pad(d_logits, ((0, 0), (0, small_width - experts))))
    grad_small = jnp.where(column == experts, grad_gain_one[:, None], grad_small)
    grad_small = jnp.where(column == experts + 1, grad_gain_two[:, None], grad_small).astype(bf16)

    (g_shared, g_wo, g_wq, g_wk, g_wv, g_small) = scatter_all(
        dims,
        [grad_shared, grad_wout, grad_wq, grad_wk, grad_wv, grad_small],
        [True, False, False, False, False, False],
    )

    def joined(n):
        pieces = g_shared[:, :, n * part : (n + 1) * part]
        return pieces.transpose(1, 0, 2).reshape(own_rows, deep * part)[:, :hidden_all]

    return (
        output,
        grad_tokens,
        g_small[:, experts],
        g_small[:, experts + 1],
        g_wq,
        g_wk,
        g_wv,
        g_wo,
        g_small[:, :experts],
        joined(0),
        joined(1),
        joined(2).T,
        grad_egate[None],
        grad_eup[None],
        grad_edown[None],
    )


def solution(mesh):
    return jax.shard_map(
        on_device,
        mesh=mesh,
        in_specs=(
            P(None, ("wide", "narrow"), None, None),
            P(None, ("wide", "narrow"), None, None),
            P(None, ("wide", "narrow"), None, None),
            P(("wide", "narrow")),
            P(("wide", "narrow")),
            P(("wide", "narrow"), None),
            P(("wide", "narrow"), None),
            P(("wide", "narrow"), None),
            P(("wide", "narrow"), None),
            P(("wide", "narrow"), None),
            P(("wide", "narrow"), None),
            P(("wide", "narrow"), None),
            P(None, ("wide", "narrow")),
            P("wide", None, "narrow"),
            P("wide", None, "narrow"),
            P("wide", "narrow", None),
        ),
        out_specs=(
            P(None, ("wide", "narrow"), None, None),
            P(None, ("wide", "narrow"), None, None),
            P(("wide", "narrow")),
            P(("wide", "narrow")),
            P(("wide", "narrow"), None),
            P(("wide", "narrow"), None),
            P(("wide", "narrow"), None),
            P(("wide", "narrow"), None),
            P(("wide", "narrow"), None),
            P(("wide", "narrow"), None),
            P(("wide", "narrow"), None),
            P(None, ("wide", "narrow")),
            P("wide", None, "narrow"),
            P("wide", None, "narrow"),
            P("wide", "narrow", None),
        ),
        check_vma=False,
    )
```

```python
import functools
import jax
import jax.numpy as jnp
from jax import lax
from jax.experimental import pallas as pl
from jax.experimental.pallas import tpu as pltpu
from jax.sharding import PartitionSpec as P

MESH = pl.DeviceIdType.MESH
HD = 128


epsilon = 1e-06


def angles(seq_len, head_size):
    position = jnp.arange(seq_len).astype(jnp.float32)
    exponent = jnp.arange(head_size // 2).astype(jnp.float32) * (2.0 / head_size)
    frequency = jnp.exp(-jnp.log(10000.0) * exponent)
    theta = position[:, None] * frequency[None, :]
    return (jnp.cos(theta)[:, None, :], jnp.sin(theta)[:, None, :])


def rotate(vectors, cosine_table, sine_table):
    middle = vectors.shape[-1] // 2
    first_half = vectors[..., :middle]
    second_half = vectors[..., middle:]
    return jnp.concatenate(
        [
            first_half * cosine_table - second_half * sine_table,
            second_half * cosine_table + first_half * sine_table,
        ],
        axis=-1,
    )


def unrotate(vectors, cosine_table, sine_table):
    middle = vectors.shape[-1] // 2
    first_half = vectors[..., :middle]
    second_half = vectors[..., middle:]
    return jnp.concatenate(
        [
            first_half * cosine_table + second_half * sine_table,
            second_half * cosine_table - first_half * sine_table,
        ],
        axis=-1,
    )


def norm_ahead(matrix, gain):
    scale_rows = lax.rsqrt(jnp.mean(matrix * matrix, axis=-1, keepdims=True) + epsilon)
    normed = matrix * scale_rows
    return ((normed * gain).astype(jnp.bfloat16), normed, scale_rows)


def norm_back(grad_rows, normed, scale_rows, gain):
    gain_grad = jnp.sum(grad_rows * normed, axis=0)
    inner = grad_rows * gain
    return (
        scale_rows * (inner - normed * jnp.mean(inner * normed, axis=-1, keepdims=True)),
        gain_grad,
    )


def silu_pair(pre_act):
    sigma = jax.nn.sigmoid(pre_act)
    return (pre_act * sigma, sigma * (1.0 + pre_act * (1.0 - sigma)))


def chip_grid(chips):
    deep = 4 if chips % 4 == 0 else 1
    rest = chips // deep
    high = max(d for d in range(1, rest + 1) if rest % d == 0 and d * d <= rest)
    return (deep, high, rest // high)

def place(dims):
    wide = lax.axis_index("wide")
    return wide // (dims[1] * dims[2]), (wide // dims[2]) % dims[1], wide % dims[2]

def greet(dims, a, b, c, core):
    deep, high, broad = dims
    barrier = pltpu.get_barrier_semaphore()
    def chip(i, j, k):
        return (i * high + j) * broad + k
    others = [(chip((a + r) % deep, b, c), core) for r in range(1, deep)]
    others += [(chip(a, (b + r) % high, c), core) for r in range(1, high)]
    others += [(chip(a, b, (c + r) % broad), core) for r in range(1, broad)]
    others += [(chip(a, b, c), 1 - core)]
    for other in others:
        pl.semaphore_signal(barrier, inc=1, device_id=other, device_id_type=MESH)
    pl.semaphore_wait(barrier, len(others))

def cut_columns(widths):
    pieces = []
    for n, width in enumerate(widths):
        tiles = width // 128
        middle = (tiles + 1) // 2 * 128
        pieces += [(n, 0, width)] if tiles < 6 else [(n, 0, middle), (n, middle, width)]
    return pieces


def gather_kernel(dims, arrays, pieces, sliced, *refs):
    deep, high, broad = dims
    count, ahead = len(pieces), 12
    rows_ref, column_ref = refs[arrays], refs[2 * arrays + 1]
    micro = rows_ref.shape[0]
    ins = [refs[n].at[..., lo:hi] for n, lo, hi in pieces]
    outs = [refs[arrays + 1 + n].at[..., lo:hi] for n, lo, hi in pieces]
    sliced = [sliced[n] for n, lo, hi in pieces]
    own_sem, s1, r1, s2, r2, s3, r3, sn, rn, sr, rr = refs[2 * arrays + 2 :]
    a, b, c = place(dims)
    core = lax.axis_index("narrow")
    greet(dims, a, b, c, core)

    def chip(i, j, k):
        return (i * high + j) * broad + k

    def send(src, dst, ss, rs, to):
        copy = pltpu.make_async_remote_copy(
            src_ref=src, dst_ref=dst, send_sem=ss, recv_sem=rs, device_id=to, device_id_type=MESH
        )
        return copy

    def program(me):
        first, second = (high, broad) if me == 0 else (broad, high)

        def at2(i, r):
            if me == 0:
                return outs[i].at[:, (b - r + high) % high, c, me]
            return outs[i].at[:, b, (c - r + broad) % broad, me]

        def at3(i, r):
            if me == 0:
                return outs[i].at[:, :, (c - r + broad) % broad, me]
            return outs[i].at[:, (b - r + high) % high, :, me]

        def to2(r):
            return (chip(a, (b + r) % high, c), me) if me == 0 else (chip(a, b, (c + r) % broad), me)

        def to3(r):
            return (chip(a, b, (c + r) % broad), me) if me == 0 else (chip(a, (b + r) % high, c), me)

        mate = (chip(a, b, c), 1 - me)

        def own(i):
            return pltpu.make_async_copy(ins[i].at[a] if sliced[i] else ins[i], outs[i].at[a, b, c, me], own_sem.at[i])

        def stage1(i, r):
            h = (a + r) % deep
            src = ins[i].at[h] if sliced[i] else ins[i]
            return send(src, outs[i].at[a, b, c, me], s1.at[i, r - 1], r1.at[i, r - 1], (chip(h, b, c), me))

        def own_rows():
            return pltpu.make_async_copy(rows_ref, column_ref.at[:, 0], own_sem.at[count])

        def column(m, r):
            to = (chip((a + r) % deep, b, c), me)
            return send(rows_ref.at[m], column_ref.at[m, r], sr.at[m, r - 1], rr.at[m, r - 1], to)

        def stage2(i, r):
            return send(at2(i, 0), at2(i, 0), s2.at[i, r - 1], r2.at[i, r - 1], to2(r))

        def stage3(i, r):
            return send(at3(i, 0), at3(i, 0), s3.at[i, r - 1], r3.at[i, r - 1], to3(r))

        def across(i, part):
            view = at2(i, 0) if part == 0 else at2(i, part) if part < first else at3(i, part - first + 1)
            return send(view, view, sn.at[i, part], rn.at[i, part], mate)

        parts = first + second - 1
        def begin(i):
            for r in range(1, deep):
                stage1(i, r).start()
            own(i).start()

        for i in range(min(ahead, count)):
            begin(i)
        own_rows().start()
        for step in range(count + 2):
            if step + ahead < count:
                begin(step + ahead)
            for m in range(micro):
                if step == min(2 + 2 * m, count + 1):
                    for r in range(1, deep):
                        column(m, r).start()
            i = step
            if i < count:
                own(i).wait()
                for r in range(1, deep):
                    stage1(i, r).wait_recv()
                for r in range(1, first):
                    stage2(i, r).start()
                across(i, 0).start()
            i = step - 1
            if 0 <= i < count:
                for r in range(1, first):
                    stage2(i, r).wait_recv()
                for r in range(1, second):
                    stage3(i, r).start()
                for r in range(1, first):
                    across(i, r).start()
            i = step - 2
            if 0 <= i < count:
                for r in range(1, second):
                    stage3(i, r).wait_recv()
                for r in range(1, second):
                    across(i, first + r - 1).start()
        for i in range(count):
            for r in range(1, deep):
                stage1(i, r).wait_send()
            for r in range(1, first):
                stage2(i, r).wait_send()
            for r in range(1, second):
                stage3(i, r).wait_send()
            for part in range(parts):
                across(i, part).wait()
        own_rows().wait()
        for m in range(micro):
            for r in range(1, deep):
                column(m, r).wait()

    pl.when(core == 0)(lambda: program(0))
    pl.when(core == 1)(lambda: program(1))

def gather_all(dims, parts, sliced, rows):
    arrays = len(parts)
    deep, high, broad = dims
    pieces = cut_columns([p.shape[-1] for p in parts])
    count = len(pieces)
    sem = pltpu.SemaphoreType.DMA
    most = max(high, broad)
    shapes = [p.shape[1:] if cut else p.shape for p, cut in zip(parts, sliced)]
    vmem, anywhere = pl.BlockSpec(memory_space=pltpu.VMEM), pl.BlockSpec(memory_space=pl.ANY)
    outs = pl.pallas_call(
        functools.partial(gather_kernel, dims, arrays, pieces, sliced),
        out_shape=[jax.ShapeDtypeStruct((deep, high, broad, 2) + sh, p.dtype) for p, sh in zip(parts, shapes)]
        + [jax.ShapeDtypeStruct(rows.shape[:1] + (deep,) + rows.shape[1:], rows.dtype)],
        in_specs=[vmem] * (arrays + 1),
        out_specs=[anywhere] * (arrays + 1),
        scratch_shapes=[sem((count + 1,))]
        + [sem((count, max(deep - 1, 1)))] * 2
        + [sem((count, max(most - 1, 1)))] * 4
        + [sem((count, high + broad - 1))] * 2
        + [sem((rows.shape[0], max(deep - 1, 1)))] * 2,
        compiler_params=pltpu.CompilerParams(collective_id=0, has_side_effects=True),
        name="gather_dense",
    )(*parts, rows)
    return [o.reshape((-1, sh[-1])) for o, sh in zip(outs[:-1], shapes)], outs[-1]


def scatter_kernel(dims, arrays, pieces, sliced, *refs):
    deep, high, broad = dims
    count, ahead = len(pieces), 3
    group = lambda m: [refs[m * arrays + n].at[..., lo:hi] for n, lo, hi in pieces]
    ins, outs, held, from_mate, got2, got3, got4 = [group(m) for m in range(7)]
    own_sem, sn, rn, s2, r2, s3, r3, s4, r4 = refs[7 * arrays :]
    sliced = [sliced[n] for n, lo, hi in pieces]
    a, b, c = place(dims)
    core = lax.axis_index("narrow")
    greet(dims, a, b, c, core)

    def chip(i, j, k):
        return (i * high + j) * broad + k

    def send(src, dst, ss, rs, to):
        return pltpu.make_async_remote_copy(
            src_ref=src, dst_ref=dst, send_sem=ss, recv_sem=rs, device_id=to, device_id_type=MESH
        )

    wide32 = jnp.float32

    def program(me):
        first, second = (broad, high) if me == 0 else (high, broad)
        mate = (chip(a, b, c), 1 - me)

        def own(i):
            return pltpu.make_async_copy(ins[i].at[:, :, :, me], held[i], own_sem.at[i])

        def across(i):
            return send(ins[i].at[:, :, :, 1 - me], from_mate[i], sn.at[i], rn.at[i], mate)

        def stage2(i, r):
            if me == 0:
                k = (c + r) % broad
                return send(held[i].at[:, :, k], got2[i].at[r - 1], s2.at[i, r - 1], r2.at[i, r - 1], (chip(a, b, k), me))
            j = (b + r) % high
            return send(held[i].at[:, j], got2[i].at[r - 1], s2.at[i, r - 1], r2.at[i, r - 1], (chip(a, j, c), me))

        def stage3(i, r):
            if me == 0:
                j = (b + r) % high
                return send(held[i].at[:, j, c], got3[i].at[r - 1], s3.at[i, r - 1], r3.at[i, r - 1], (chip(a, j, c), me))
            k = (c + r) % broad
            return send(held[i].at[:, b, k], got3[i].at[r - 1], s3.at[i, r - 1], r3.at[i, r - 1], (chip(a, b, k), me))

        def stage4(i, r):
            h = (a + r) % deep
            return send(held[i].at[h, b, c], got4[i].at[r - 1], s4.at[i, r - 1], r4.at[i, r - 1], (chip(h, b, c), me))

        def add_mate(i):
            for j in range(high):
                for k in range(broad):
                    @pl.loop(0, deep)
                    def _(h):
                        held[i][h, j, k] = (held[i][h, j, k].astype(wide32) + from_mate[i][h, j, k].astype(wide32)).astype(jnp.bfloat16)

        def add2(i):
            if me == 0:
                for j in range(high):
                    @pl.loop(0, deep)
                    def _(h):
                        total = held[i][h, j, c].astype(wide32)
                        for r in range(1, broad):
                            total += got2[i][r - 1, h, j].astype(wide32)
                        held[i][h, j, c] = total.astype(jnp.bfloat16)
            else:
                for k in range(broad):
                    @pl.loop(0, deep)
                    def _(h):
                        total = held[i][h, b, k].astype(wide32)
                        for r in range(1, high):
                            total += got2[i][r - 1, h, k].astype(wide32)
                        held[i][h, b, k] = total.astype(jnp.bfloat16)

        def add3(i):
            @pl.loop(0, deep)
            def _(h):
                total = held[i][h, b, c].astype(wide32)
                for r in range(1, second):
                    total += got3[i][r - 1, h].astype(wide32)
                held[i][h, b, c] = total.astype(jnp.bfloat16)

        def add4(i):
            if sliced[i]:
                outs[i][a] = held[i][a, b, c].astype(wide32)
                for r in range(1, deep):
                    outs[i][(a - r + deep) % deep] = got4[i][r - 1].astype(wide32)
                return
            total = held[i][a, b, c].astype(wide32)
            for r in range(1, deep):
                total += got4[i][r - 1].astype(wide32)
            outs[i][...] = total

        def begin(i):
            across(i).start()
            own(i).start()

        for i in range(min(ahead, count)):
            begin(i)
        for step in range(count + 3):
            if step + ahead < count:
                begin(step + ahead)
            i = step
            if i < count:
                own(i).wait()
                across(i).wait_recv()
                add_mate(i)
                for r in range(1, first):
                    stage2(i, r).start()
            i = step - 1
            if 0 <= i < count:
                for r in range(1, first):
                    stage2(i, r).wait_recv()
                add2(i)
                for r in range(1, second):
                    stage3(i, r).start()
            i = step - 2
            if 0 <= i < count:
                for r in range(1, second):
                    stage3(i, r).wait_recv()
                add3(i)
                for r in range(1, deep):
                    stage4(i, r).start()
            i = step - 3
            if 0 <= i < count:
                for r in range(1, deep):
                    stage4(i, r).wait_recv()
                add4(i)
        for i in range(count):
            across(i).wait_send()
            for r in range(1, first):
                stage2(i, r).wait_send()
            for r in range(1, second):
                stage3(i, r).wait_send()
            for r in range(1, deep):
                stage4(i, r).wait_send()

    pl.when(core == 0)(lambda: program(0))
    pl.when(core == 1)(lambda: program(1))

def scatter_all(dims, parts, sliced):
    arrays = len(parts)
    deep, high, broad = dims
    pieces = cut_columns([p.shape[-1] for p in parts])
    count = len(pieces)
    devices = deep * high * broad * 2
    blocks = [(p.shape[0] // devices, p.shape[1]) for p in parts]
    sem = pltpu.SemaphoreType.DMA
    most = max(high, broad)
    vm = lambda lead: [pltpu.VMEM(lead + blk, jnp.bfloat16) for blk in blocks]
    side = max(high, broad)
    got2 = vm((max(most - 1, 1), deep, side))
    return pl.pallas_call(
        functools.partial(scatter_kernel, dims, arrays, pieces, sliced),
        out_shape=[jax.ShapeDtypeStruct(((deep,) if cut else ()) + blk, jnp.float32) for blk, cut in zip(blocks, sliced)],
        in_specs=[pl.BlockSpec(memory_space=pl.ANY)] * arrays,
        out_specs=[pl.BlockSpec(memory_space=pltpu.VMEM)] * arrays,
        scratch_shapes=vm((deep, high, broad)) + vm((deep, high, broad)) + got2 + vm((max(most - 1, 1), deep)) + vm((max(deep - 1, 1),))
        + [sem((count,))] * 3
        + [sem((count, max(most - 1, 1)))] * 4
        + [sem((count, max(deep - 1, 1)))] * 2,
        compiler_params=pltpu.CompilerParams(collective_id=1, has_side_effects=True, vmem_limit_bytes=62 * 1024 * 1024),
        name="scatter_dense",
    )(*[p.reshape((deep, high, broad, 2) + blk) for p, blk in zip(parts, blocks)])


def greet_all(dims, a, b, c, core):
    deep, high, broad = dims
    barrier = pltpu.get_barrier_semaphore()
    others = [(((a + r) % deep * high + b) * broad + c, core) for r in range(1, deep)]
    others += [
        ((a * high + (b + q // broad) % high) * broad + (c + q % broad) % broad, core) for q in range(1, high * broad)
    ]
    others += [((a * high + b) * broad + c, 1 - core)]
    for other in others:
        pl.semaphore_signal(barrier, inc=1, device_id=other, device_id_type=MESH)
    pl.semaphore_wait(barrier, len(others))


def remote(src, dst, ss, rs, to):
    return pltpu.make_async_remote_copy(
        src_ref=src, dst_ref=dst, send_sem=ss, recv_sem=rs, device_id=to, device_id_type=MESH
    )


def dispatch_kernel(dims, micro, x_ref, choose_ref, both_ref, column_ref, got, picked, scol, rcol, spl, rpl, sm, rm, sl):
    deep, high, broad = dims
    offsets = high * broad
    a, b, c = place(dims)
    core = lax.axis_index("narrow")
    greet_all(dims, a, b, c, core)
    mate = ((a * high + b) * broad + c, 1 - core)
    rows_ref, mates_ref = both_ref.at[0], both_ref.at[1]

    def column(m, k):
        return remote(x_ref.at[m], got.at[m, k], scol.at[m, k], rcol.at[m, k], (((a + k) % deep * high + b) * broad + c, core))

    def plane(m, k, q):
        to = (a * high + (b + q // broad) % high) * broad + (c + q % broad) % broad
        return remote(picked.at[m, k, q], rows_ref.at[m, q, k], spl.at[m, k, q], rpl.at[m, k, q], (to, core))

    def across(m, k, part):
        if part == 0:
            return remote(picked.at[m, k, 0], mates_ref.at[m, 0, k], sm.at[m, k, 0], rm.at[m, k, 0], mate)
        return remote(rows_ref.at[m, 1:, k], mates_ref.at[m, 1:, k], sm.at[m, k, 1], rm.at[m, k, 1], mate)

    def keep(m, k):
        return pltpu.make_async_copy(picked.at[m, k, 0], rows_ref.at[m, 0, k], sl.at[m, k, 0])

    def keep_column(m, k):
        return pltpu.make_async_copy(x_ref.at[m] if k == 0 else got.at[m, k], column_ref.at[m, k], sl.at[m, k, 1])

    order = [(m, k) for m in range(micro) for k in range(deep)]
    for m, k in order:
        if k > 0:
            column(m, k).start()
    for m, k in order:
        if k > 0:
            column(m, k).wait_recv()
        keep_column(m, k).start()
        piece = x_ref[m] if k == 0 else got[m, k]
        chosen = jnp.dot(choose_ref[m, k], piece, preferred_element_type=jnp.float32).astype(jnp.bfloat16)
        picked[m, k] = chosen.reshape(picked.shape[2:])
        for q in range(1, offsets):
            plane(m, k, q).start()
        keep(m, k).start()
        across(m, k, 0).start()
    for m, k in order:
        for q in range(1, offsets):
            plane(m, k, q).wait_recv()
        across(m, k, 1).start()
    for m, k in order:
        if k > 0:
            column(m, k).wait_send()
        keep_column(m, k).wait()
        for q in range(1, offsets):
            plane(m, k, q).wait_send()
        keep(m, k).wait()
        across(m, k, 0).wait()
        across(m, k, 1).wait()


def dispatch(dims, x, choose):
    deep, high, broad = dims
    micro, tokens, width = x.shape
    offsets = high * broad
    slots = choose.shape[2] // offsets
    sem = pltpu.SemaphoreType.DMA
    anywhere, vmem = pl.BlockSpec(memory_space=pl.ANY), pl.BlockSpec(memory_space=pltpu.VMEM)
    out = jax.ShapeDtypeStruct((2, micro, offsets, deep, slots, width), x.dtype)
    return pl.pallas_call(
        functools.partial(dispatch_kernel, dims, micro),
        out_shape=[out, jax.ShapeDtypeStruct((micro, deep, tokens, width), x.dtype)],
        in_specs=[vmem, vmem],
        out_specs=[anywhere] * 2,
        scratch_shapes=[
            pltpu.VMEM((micro, deep, tokens, width), x.dtype),
            pltpu.VMEM((micro, deep, offsets, slots, width), x.dtype),
        ]
        + [sem((micro, deep))] * 2
        + [sem((micro, deep, offsets))] * 2
        + [sem((micro, deep, 2))] * 3,
        compiler_params=pltpu.CompilerParams(collective_id=2, has_side_effects=True),
        name="dispatch_rows",
    )(x, choose)


def return_kernel(dims, micro, both_ref, choose_ref, near_ref, total_ref, held, mated, back, up, got, sl, sm, rm, spl, rpl, scol, rcol):
    deep, high, broad = dims
    offsets = high * broad
    a, b, c = place(dims)
    core = lax.axis_index("narrow")
    greet_all(dims, a, b, c, core)
    mate = ((a * high + b) * broad + c, 1 - core)
    near_width = near_ref.shape[-1]
    mine_ref, theirs_ref = both_ref.at[0], both_ref.at[1]

    def load(m, k):
        return pltpu.make_async_copy(mine_ref.at[m, :, k], held.at[m, :, k], sl.at[m, k])

    def across(m, k):
        return remote(theirs_ref.at[m, :, k], mated.at[m, :, k], sm.at[m, k], rm.at[m, k], mate)

    def plane(m, k, q):
        to = (a * high + (b - q // broad + high) % high) * broad + (c - q % broad + broad) % broad
        return remote(held.at[m, q, k], back.at[m, k, q], spl.at[m, k, q], rpl.at[m, k, q], (to, core))

    def column(m, k):
        return remote(up.at[m, k], got.at[m, k], scol.at[m, k], rcol.at[m, k], (((a - k + deep) % deep * high + b) * broad + c, core))

    order = [(m, k) for m in range(micro) for k in list(range(1, deep)) + [0]]
    ahead = 3
    for m, k in order[:ahead]:
        across(m, k).start()
        load(m, k).start()
    for n, (m, k) in enumerate(order):
        for later in order[n + ahead : n + ahead + 1]:
            across(*later).start()
            load(*later).start()
        load(m, k).wait()
        across(m, k).wait_recv()
        for q in range(1, offsets):
            held[m, q, k] = (held[m, q, k].astype(jnp.float32) + mated[m, q, k].astype(jnp.float32)).astype(jnp.bfloat16)
            plane(m, k, q).start()
        back[m, k, 0] = (held[m, 0, k].astype(jnp.float32) + mated[m, 0, k].astype(jnp.float32)).astype(jnp.bfloat16)
    for m, k in order:
        for q in range(1, offsets):
            plane(m, k, q).wait_recv()
        rows = back[m, k].reshape((-1, back.shape[-1]))
        sums = jnp.dot(choose_ref[m, k], rows, preferred_element_type=jnp.float32)
        dense = sums[:, :near_width] + near_ref[m, k].astype(jnp.float32)
        if k == 0:
            total_ref[m, :, :near_width] = dense
            if near_width < sums.shape[1]:
                total_ref[m, :, near_width:] = sums[:, near_width:]
        else:
            up[m, k, :, :near_width] = dense.astype(jnp.bfloat16)
            if near_width < sums.shape[1]:
                up[m, k, :, near_width:] = sums[:, near_width:].astype(jnp.bfloat16)
            column(m, k).start()
    for m in range(micro):
        for k in range(1, deep):
            column(m, k).wait_recv()
            total_ref[m] += got[m, k].astype(jnp.float32)
    for m, k in order:
        across(m, k).wait_send()
        for q in range(1, offsets):
            plane(m, k, q).wait_send()
        if k > 0:
            column(m, k).wait_send()


def give_back(dims, both, choose_t, near):
    deep, high, broad = dims
    _, micro, offsets, _, slots, width = both.shape
    tokens = choose_t.shape[2]
    sem = pltpu.SemaphoreType.DMA
    anywhere, vmem = pl.BlockSpec(memory_space=pl.ANY), pl.BlockSpec(memory_space=pltpu.VMEM)
    scratch = lambda *shape: pltpu.VMEM(shape, both.dtype)
    return pl.pallas_call(
        functools.partial(return_kernel, dims, micro),
        out_shape=jax.ShapeDtypeStruct((micro, tokens, width), jnp.float32),
        in_specs=[anywhere, vmem, vmem],
        out_specs=vmem,
        scratch_shapes=[
            scratch(micro, offsets, deep, slots, width),
            scratch(micro, offsets, deep, slots, width),
            scratch(micro, deep, offsets, slots, width),
            scratch(micro, deep, tokens, width),
            scratch(micro, deep, tokens, width),
        ]
        + [sem((micro, deep))] * 3
        + [sem((micro, deep, offsets))] * 2
        + [sem((micro, deep))] * 2,
        compiler_params=pltpu.CompilerParams(collective_id=3, has_side_effects=True, vmem_limit_bytes=62 * 1024 * 1024),
        name="return_rows",
    )(both, choose_t, near)


class Line:
    def __init__(self, dims):
        deep, plane = dims[0], dims[1] * dims[2]
        self.up = [(i * plane + p, (i + 1) * plane + p) for i in range(deep - 1) for p in range(plane)]
        self.down = [(two, one) for one, two in self.up]

    def both_ways(self, one, two):
        return lax.ppermute(one, "wide", self.up), lax.ppermute(two, "wide", self.down)


def plane_pairs(dims, offset, sign):
    deep, high, broad = dims
    up, over = (offset // broad) * sign, (offset % broad) * sign
    return [
        ((i * high + j) * broad + k, (i * high + (j + up) % high) * broad + (k + over) % broad)
        for i in range(deep)
        for j in range(high)
        for k in range(broad)
    ]


def swap_cores(rows):
    return lax.ppermute(rows, "narrow", [(0, 1), (1, 0)])


def plane_rows(dims, picked):
    return [picked[0]] + [lax.ppermute(picked[q], "wide", plane_pairs(dims, q, 1)) for q in range(1, picked.shape[0])]


def plane_back(dims, rows):
    offsets = rows.shape[1]
    return [rows[:, 0]] + [lax.ppermute(rows[:, q], "wide", plane_pairs(dims, q, -1)) for q in range(1, offsets)]


def column_sums(dims, choose, back, near):
    sums = jnp.einsum("mkst,mksd->mktd", choose, back, preferred_element_type=jnp.float32)
    return sums + near.astype(jnp.float32)


def masked_gates(logits, named):
    top = jnp.max(jnp.where(named > 0, logits, -1e30), axis=-1, keepdims=True)
    weights = jnp.where(named > 0, jnp.exp(logits - top), 0.0)
    return weights / jnp.maximum(jnp.sum(weights, axis=-1, keepdims=True), 0.5)


def f32_dot(one, two):
    return jnp.dot(one, two, preferred_element_type=jnp.float32)


def dot_t(one, two):
    return lax.dot_general(one, two, (((1,), (1,)), ((), ())), preferred_element_type=jnp.float32)


def t_dot(one, two):
    return lax.dot_general(one, two, (((0,), (0,)), ((), ())), preferred_element_type=jnp.float32)


def own_gate(x, router, names, pick):
    row_gates = masked_gates(f32_dot(x, router), names.astype(jnp.float32))
    return jnp.sum(row_gates * pick[:, : row_gates.shape[1]], axis=-1, keepdims=True)


def expert_forward_kernel(width, x_ref, router_ref, pick_ref, gate_w, up_w, down_w, out_ref, g_ref, u_ref):
    x, names = x_ref[:, :width], x_ref[:, width:]
    gate = own_gate(x, router_ref[...], names, pick_ref[0:1])
    g = f32_dot(x, gate_w[...])
    u = f32_dot(x, up_w[...])
    g_ref[...] = g
    u_ref[...] = u
    act, _ = silu_pair(g)
    out_ref[...] = f32_dot((gate * (act * u)).astype(jnp.bfloat16), down_w[...]).astype(jnp.bfloat16)


def expert_backward_kernel(
    half, width, x_ref, d_ref, mate_d_ref, router_ref, pick_ref, gate_w, up_w, down_w, g_ref, u_ref, in_ref, dg_ref, du_ref, dd_ref
):
    step = pl.program_id(0)
    x, names = x_ref[:, :width], x_ref[:, width:]
    dy = jnp.where(step < half, d_ref[...], mate_d_ref[...])
    gate = own_gate(x, router_ref[...], names, pick_ref[0:1])
    act, slope = silu_pair(g_ref[...])
    u = u_ref[...]
    d_plain = dot_t(dy, down_w[...])
    hidden = act * u
    d_gate = jnp.sum(hidden * d_plain, axis=-1, keepdims=True)
    weighed = (gate * hidden).astype(jnp.bfloat16)
    d_hidden = gate * d_plain
    d_act = (d_hidden * u * slope).astype(jnp.bfloat16)
    d_up = (d_hidden * act).astype(jnp.bfloat16)
    rows = dot_t(d_act, gate_w[...]) + dot_t(d_up, up_w[...])
    in_ref[:, :width] = rows.astype(jnp.bfloat16)
    coarse = d_gate.astype(jnp.bfloat16).astype(jnp.float32)
    beside = coarse * pick_ref[1:2] + (d_gate - coarse) * pick_ref[2:3]
    in_ref[:, width:] = beside.astype(jnp.bfloat16)

    @pl.when(step == 0)
    def _():
        dg_ref[...] = jnp.zeros_like(dg_ref)
        du_ref[...] = jnp.zeros_like(du_ref)
        dd_ref[...] = jnp.zeros_like(dd_ref)

    dg_ref[...] += t_dot(x, d_act)
    du_ref[...] += t_dot(x, d_up)
    dd_ref[...] += t_dot(weighed, dy)


def fixed(shape):
    return pl.BlockSpec(shape, lambda i: (0,) * len(shape), pipeline_mode=pl.Buffered(1))


def row_block(total):
    return max(n for n in (512, 256, 128, 64, 32, 16) if total % n == 0)


def roomy():
    return pltpu.CompilerParams(vmem_limit_bytes=60 * 1024 * 1024)


def cost(flops, moved):
    return pl.CostEstimate(flops=flops, bytes_accessed=moved, transcendentals=0)


def expert_forward(x, router, picks, gate_w, up_w, down_w):
    rows, (width, hidden) = x.shape[0], gate_w.shape
    block = row_block(rows)
    by_row = lambda w: pl.BlockSpec((block, w), lambda i: (i, 0))
    return pl.pallas_call(
        functools.partial(expert_forward_kernel, width),
        grid=(rows // block,),
        out_shape=[
            jax.ShapeDtypeStruct((rows, width), jnp.bfloat16),
            jax.ShapeDtypeStruct((rows, hidden), jnp.float32),
            jax.ShapeDtypeStruct((rows, hidden), jnp.float32),
        ],
        in_specs=[by_row(x.shape[1]), fixed(router.shape), fixed(picks.shape)] + [fixed(w.shape) for w in (gate_w, up_w, down_w)],
        out_specs=[by_row(width), by_row(hidden), by_row(hidden)],
        compiler_params=roomy(),
        cost_estimate=cost(6 * rows * width * hidden, rows * (4 * width + 8 * hidden)),
        name="expert_forward",
    )(x, router, picks, gate_w, up_w, down_w)


def expert_backward(x, d_mine, d_mates, router, picks, gate_w, up_w, down_w, g, u):
    rows, (width, hidden) = x.shape[0], gate_w.shape
    block = row_block(d_mine.shape[0])
    half = d_mine.shape[0] // block
    by_row = lambda w: pl.BlockSpec((block, w), lambda i: (i, 0))
    first = pl.BlockSpec((block, width), lambda i: (jnp.minimum(i, half - 1), 0))
    second = pl.BlockSpec((block, width), lambda i: (jnp.maximum(i - half, 0), 0))
    wide_in = width + picks.shape[1]
    return pl.pallas_call(
        functools.partial(expert_backward_kernel, half, width),
        grid=(2 * half,),
        out_shape=[jax.ShapeDtypeStruct((rows, wide_in), jnp.bfloat16)]
        + [jax.ShapeDtypeStruct(w.shape, jnp.float32) for w in (gate_w, up_w, down_w)],
        in_specs=[by_row(x.shape[1]), first, second, fixed(router.shape), fixed(picks.shape)]
        + [fixed(w.shape) for w in (gate_w, up_w, down_w)]
        + [by_row(hidden), by_row(hidden)],
        out_specs=[by_row(wide_in)] + [fixed(w.shape) for w in (gate_w, up_w, down_w)],
        compiler_params=roomy(),
        cost_estimate=cost(12 * rows * width * hidden, rows * (6 * width + 8 * hidden)),
        name="expert_backward",
    )(x, d_mine, d_mates, router, picks, gate_w, up_w, down_w, g, u)


def shared_kernel(width, part, x_ref, d_ref, w_ref, out_ref, in_ref, grad_ref):
    x, dy = x_ref[:, :width], d_ref[...]
    gate_w, up_w, down_t = w_ref[:, :part], w_ref[:, part : 2 * part], w_ref[:, 2 * part :]
    act, slope = silu_pair(f32_dot(x, gate_w))
    u = f32_dot(x, up_w)
    hidden = (act * u).astype(jnp.bfloat16)
    out_ref[...] = dot_t(hidden, down_t).astype(jnp.bfloat16)
    d_hidden = f32_dot(dy, down_t)
    d_gate = (d_hidden * u * slope).astype(jnp.bfloat16)
    d_up = (d_hidden * act).astype(jnp.bfloat16)
    in_ref[...] = (dot_t(d_gate, gate_w) + dot_t(d_up, up_w)).astype(jnp.bfloat16)

    @pl.when(pl.program_id(0) == 0)
    def _():
        grad_ref[...] = jnp.zeros_like(grad_ref)

    grad_ref[:, :part] += t_dot(x, d_gate)
    grad_ref[:, part : 2 * part] += t_dot(x, d_up)
    grad_ref[:, 2 * part :] += t_dot(dy, hidden)


def shared_expert(x, d, weights):
    rows, width = d.shape
    part = weights.shape[1] // 3
    block = row_block(rows)
    by_row = lambda w: pl.BlockSpec((block, w), lambda i: (i, 0))
    return pl.pallas_call(
        functools.partial(shared_kernel, width, part),
        grid=(rows // block,),
        out_shape=[jax.ShapeDtypeStruct((rows, width), jnp.bfloat16)] * 2 + [jax.ShapeDtypeStruct(weights.shape, jnp.float32)],
        in_specs=[by_row(x.shape[1]), by_row(width), fixed(weights.shape)],
        out_specs=[by_row(width)] * 2 + [fixed(weights.shape)],
        compiler_params=roomy(),
        cost_estimate=cost(18 * rows * width * part, rows * 8 * width),
        name="shared_expert",
    )(x, d, weights)


def on_device(
    tokens,
    cotangent,
    routes,
    gain_attn,
    gain_moe,
    w_query,
    w_key,
    w_value,
    attention_output_weight,
    router,
    shared_gate,
    shared_up,
    shared_down,
    routed_gate_weight,
    routed_up_weight,
    routed_down_weight,
):
    f32, bf16 = jnp.float32, jnp.bfloat16
    micro = tokens.shape[0]
    seq_len, width_all = tokens.shape[2], tokens.shape[3]
    chosen_count = routes.shape[3]
    experts = router.shape[1]
    heads = width_all // HD
    dims = chip_grid(lax.axis_size("wide"))
    deep, high, broad = dims
    slots = 9 * seq_len * chosen_count // (8 * experts) + 1
    extra = -(-experts // 128) * 128
    extra_back = -(-4 * experts // 128) * 128
    cosine_table, sine_table = angles(seq_len, HD)
    scale_factor = HD ** (-0.5)
    causal_mask = jnp.arange(seq_len)[:, None] >= jnp.arange(seq_len)[None, :]
    me = lax.axis_index("wide")
    own_rows = gain_attn.shape[0]

    named = jnp.any(routes[:, 0, :, :, None] == jnp.arange(experts), axis=2)
    named_wide = jnp.pad(named.astype(bf16), ((0, 0), (0, 0), (0, extra - experts)))

    small_width = -(-(experts + 2) // 128) * 128
    small = jnp.concatenate(
        [router, gain_attn[:, None], gain_moe[:, None], jnp.zeros((own_rows, small_width - experts - 2), bf16)], axis=1
    )
    hidden_all = shared_gate.shape[1]
    part = -(-hidden_all // (deep * 128)) * 128

    def cut(matrix):
        return jnp.pad(matrix, ((0, 0), (0, part * deep - hidden_all))).reshape(own_rows, deep, part).transpose(1, 0, 2)

    shared = jnp.concatenate([cut(shared_gate), cut(shared_up), cut(shared_down.T)], axis=2)
    (small_all, wq_all, wk_all, wv_all, wo_all, shared_all), names_column = gather_all(
        dims,
        [small, w_query, w_key, w_value, attention_output_weight, shared],
        [False, False, False, False, False, True],
        named_wide,
    )
    line = Line(dims)
    ahead_rows, back_rows = line.both_ways(cotangent[:, 0], cotangent[:, 0])
    ahead_rows, back_rows, small_all, wq_all, wk_all = lax.optimization_barrier((ahead_rows, back_rows, small_all, wq_all, wk_all))
    from_before, from_after = [ahead_rows], [back_rows]

    def next_hop():
        if len(from_before) < deep - 1:
            one, two = line.both_ways(from_before[-1], from_after[-1])
            from_before.append(one)
            from_after.append(two)

    next_hop()
    router_all = small_all[:, :experts]
    gain_one = small_all[:, experts].astype(f32)
    gain_two = small_all[:, experts + 1].astype(f32)

    chip_a, chip_b, chip_c = place(dims)
    offsets = high * broad
    step = jnp.arange(offsets)
    targets = (chip_a * high + (chip_b + step // broad) % high) * broad + (chip_c + step % broad) % broad
    is_target = (jnp.arange(experts)[:, None] == targets[None, :]).astype(bf16)
    earlier = (jnp.arange(seq_len)[:, None] > jnp.arange(seq_len)[None, :]).astype(bf16)
    names = names_column[..., :experts]
    aimed = jnp.einsum("mkte,eq->mkqt", names, is_target, preferred_element_type=f32)
    slot = jnp.einsum("mkqu,tu->mkqt", aimed.astype(bf16), earlier, preferred_element_type=f32)
    hit = (slot[:, :, :, None, :] == jnp.arange(slots, dtype=f32)[:, None]) & (aimed[:, :, :, None, :] > 0.5)
    choose = hit.astype(bf16).reshape(micro, deep, offsets * slots, seq_len)
    choose_t = choose.transpose(0, 1, 3, 2)

    rows_in = tokens[:, 0].reshape(micro * seq_len, width_all).astype(f32)
    normalized_input, plain_in, scale_in = norm_ahead(rows_in, gain_one)
    raw_query = f32_dot(normalized_input, wq_all).reshape(micro, seq_len, heads, HD)
    raw_key = f32_dot(normalized_input, wk_all).reshape(micro, seq_len, heads, HD)
    queries = rotate(raw_query, cosine_table, sine_table).astype(bf16)
    key_rows = rotate(raw_key, cosine_table, sine_table).astype(bf16)
    value_rows = f32_dot(normalized_input, wv_all).astype(bf16).reshape(micro, seq_len, heads, HD)
    scores = scale_factor * jnp.einsum("sqhd,skhd->shqk", queries, key_rows, preferred_element_type=f32)
    scores = jnp.where(causal_mask, scores, -1e30)
    row_top = jnp.max(scores, axis=-1, keepdims=True)
    exp_rows = jnp.exp(scores - row_top)
    probs = exp_rows / jnp.sum(exp_rows, axis=-1, keepdims=True)
    probs_low = probs.astype(bf16)
    from_before[-1], from_after[-1], probs_low = lax.optimization_barrier((from_before[-1], from_after[-1], probs_low))
    next_hop()
    mixed = jnp.einsum("shqk,skhd->sqhd", probs_low, value_rows, preferred_element_type=f32)
    mixed = mixed.astype(bf16).reshape(micro * seq_len, width_all)
    residual = rows_in + f32_dot(mixed, wo_all)
    normed_mid, plain_mid, scale_mid = norm_ahead(residual, gain_two)

    from_before[-1], from_after[-1], normed_mid = lax.optimization_barrier((from_before[-1], from_after[-1], normed_mid))
    d_column = [cotangent[:, 0]] + [
        jnp.where(chip_a >= k, from_before[k - 1], from_after[deep - k - 1]) for k in range(1, deep)
    ]
    d_column = jnp.stack(d_column, axis=1)
    d_picked_rows = jnp.einsum("mkqst,mktd->qmksd", hit.astype(bf16), d_column, preferred_element_type=f32).astype(bf16)

    x_ext = jnp.concatenate([normed_mid.reshape(micro, seq_len, width_all), named_wide], axis=-1)
    x_both, x_column = dispatch(dims, x_ext, choose)
    x_both, d_picked_rows = lax.optimization_barrier((x_both, d_picked_rows))
    d_pieces = plane_rows(dims, d_picked_rows)
    x_rows = x_both.reshape(-1, width_all + extra)

    gate_w, up_w, down_w = routed_gate_weight[0], routed_up_weight[0], routed_down_weight[0]
    side = 2 * experts * lax.axis_index("narrow")
    places = jnp.stack([me, me + side, me + side + experts])
    picks = (jnp.arange(extra_back)[None, :] == places[:, None]).astype(f32)
    router_wide = jnp.pad(router_all, ((0, 0), (0, extra - experts)))
    expert_args = (router_wide, picks, gate_w, up_w, down_w)
    out_rows, g_part, u_part = expert_forward(x_rows, *expert_args)
    half = out_rows.shape[0] // 2
    out_mine, out_theirs = out_rows[:half], out_rows[half:]
    theirs = swap_cores(out_theirs)

    out_mine, x_column = lax.optimization_barrier((out_mine, x_column))
    shared_out, d_shared_in, grad_shared = shared_expert(
        x_column.reshape(-1, width_all + extra), d_column.reshape(-1, width_all), shared_all
    )
    grad_shared = grad_shared.astype(bf16)
    theirs, shared_out, d_pieces = lax.optimization_barrier((theirs, shared_out, d_pieces))
    d_mine = jnp.stack(d_pieces, axis=1).reshape(-1, width_all)
    d_mates = swap_cores(d_mine)
    routed_rows = (out_mine.astype(f32) + theirs.astype(f32)).astype(bf16)
    routed_rows = routed_rows.reshape(micro, offsets, deep, slots, width_all)

    x_late, routed_rows = lax.optimization_barrier((x_rows, routed_rows))
    routed_pieces = plane_back(dims, routed_rows)
    d_in_rows, grad_egate, grad_eup, grad_edown = expert_backward(x_late, d_mine, d_mates, *expert_args, g_part, u_part)
    routed_pieces, d_in_rows = lax.optimization_barrier((routed_pieces, d_in_rows))
    routed_back = jnp.stack(routed_pieces, axis=2).reshape(micro, deep, offsets * slots, width_all)
    routed_sums = column_sums(dims, choose, routed_back, shared_out.reshape(d_column.shape))
    routed_sums, d_in_rows = lax.optimization_barrier((routed_sums, d_in_rows))
    up_rows, down_rows = line.both_ways(routed_sums[:, 1 % deep].astype(bf16), routed_sums[:, deep - 1].astype(bf16))
    d_total = give_back(
        dims,
        d_in_rows.reshape(2, micro, offsets, deep, slots, width_all + extra_back),
        choose_t,
        d_shared_in.reshape(d_column.shape),
    )
    d_total, up_rows, down_rows = lax.optimization_barrier((d_total, up_rows, down_rows))
    hops = [1]

    def next_sum(up_rows, down_rows):
        hops[0] += 1
        if hops[0] > deep - 1:
            return up_rows, down_rows
        up_rows = up_rows.astype(f32) + routed_sums[:, hops[0]]
        down_rows = down_rows.astype(f32) + routed_sums[:, deep - hops[0]]
        return line.both_ways(up_rows.astype(bf16), down_rows.astype(bf16))

    up_rows, down_rows = next_sum(up_rows, down_rows)
    d_total = d_total.reshape(micro * seq_len, width_all + extra_back)
    d_gates = sum(d_total[:, width_all + n * experts : width_all + (n + 1) * experts] for n in range(4))

    named_rows = named.reshape(micro * seq_len, experts)
    gates = masked_gates(f32_dot(normed_mid, router_all), named_rows)
    d_out = cotangent[:, 0].reshape(micro * seq_len, width_all).astype(f32)

    d_logits = (gates * (d_gates - jnp.sum(gates * d_gates, axis=1, keepdims=True))).astype(bf16)
    d_mid = d_total[:, :width_all] + dot_t(d_logits, router_all)
    d_norm_two, grad_gain_two = norm_back(d_mid, plain_mid, scale_mid, gain_two)
    d_residual = d_out + d_norm_two
    d_attn = d_residual.astype(bf16)
    grad_wout = t_dot(mixed, d_attn).astype(bf16)
    d_mixed = dot_t(d_attn, wo_all).astype(bf16).reshape(micro, seq_len, heads, HD)
    d_probs = jnp.einsum("sqhd,skhd->shqk", d_mixed, value_rows, preferred_element_type=f32)
    d_value = jnp.einsum("shqk,sqhd->skhd", probs_low, d_mixed, preferred_element_type=f32)
    d_value = d_value.astype(bf16).reshape(micro * seq_len, width_all)
    d_scores = (probs * (d_probs - jnp.sum(probs * d_probs, axis=-1, keepdims=True))).astype(bf16)
    d_scores, up_rows, down_rows = lax.optimization_barrier((d_scores, up_rows, down_rows))
    up_rows, down_rows = next_sum(up_rows, down_rows)
    d_query = scale_factor * jnp.einsum("shqk,skhd->sqhd", d_scores, key_rows, preferred_element_type=f32)
    d_key = scale_factor * jnp.einsum("shqk,sqhd->skhd", d_scores, queries, preferred_element_type=f32)
    d_query = unrotate(d_query, cosine_table, sine_table).astype(bf16).reshape(micro * seq_len, width_all)
    d_key = unrotate(d_key, cosine_table, sine_table).astype(bf16).reshape(micro * seq_len, width_all)
    grad_wq = t_dot(normalized_input, d_query).astype(bf16)
    grad_wk = t_dot(normalized_input, d_key).astype(bf16)
    grad_wv = t_dot(normalized_input, d_value).astype(bf16)
    d_in = dot_t(d_query, wq_all) + dot_t(d_key, wk_all) + dot_t(d_value, wv_all)
    d_norm_one, grad_gain_one = norm_back(d_in, plain_in, scale_in, gain_one)
    grad_tokens = (d_residual + d_norm_one).reshape(micro, 1, seq_len, width_all)

    up_rows, down_rows, grad_wv = lax.optimization_barrier((up_rows, down_rows, grad_wv))
    routed = routed_sums[:, 0] + up_rows.astype(f32) + down_rows.astype(f32)
    final_rows = residual + routed.reshape(micro * seq_len, width_all)
    output = final_rows.astype(bf16).reshape(micro, 1, seq_len, width_all)

    column = jnp.arange(small_width)[None, :]
    grad_small = t_dot(normed_mid, jnp.pad(d_logits, ((0, 0), (0, small_width - experts))))
    grad_small = jnp.where(column == experts, grad_gain_one[:, None], grad_small)
    grad_small = jnp.where(column == experts + 1, grad_gain_two[:, None], grad_small).astype(bf16)

    (g_shared, g_wo, g_wq, g_wk, g_wv, g_small) = scatter_all(
        dims,
        [grad_shared, grad_wout, grad_wq, grad_wk, grad_wv, grad_small],
        [True, False, False, False, False, False],
    )

    def joined(n):
        pieces = g_shared[:, :, n * part : (n + 1) * part]
        return pieces.transpose(1, 0, 2).reshape(own_rows, deep * part)[:, :hidden_all]

    return (
        output,
        grad_tokens,
        g_small[:, experts],
        g_small[:, experts + 1],
        g_wq,
        g_wk,
        g_wv,
        g_wo,
        g_small[:, :experts],
        joined(0),
        joined(1),
        joined(2).T,
        grad_egate[None],
        grad_eup[None],
        grad_edown[None],
    )


def solution(mesh):
    return jax.shard_map(
        on_device,
        mesh=mesh,
        in_specs=(
            P(None, ("wide", "narrow"), None, None),
            P(None, ("wide", "narrow"), None, None),
            P(None, ("wide", "narrow"), None, None),
            P(("wide", "narrow")),
            P(("wide", "narrow")),
            P(("wide", "narrow"), None),
            P(("wide", "narrow"), None),
            P(("wide", "narrow"), None),
            P(("wide", "narrow"), None),
            P(("wide", "narrow"), None),
            P(("wide", "narrow"), None),
            P(("wide", "narrow"), None),
            P(None, ("wide", "narrow")),
            P("wide", None, "narrow"),
            P("wide", None, "narrow"),
            P("wide", "narrow", None),
        ),
        out_specs=(
            P(None, ("wide", "narrow"), None, None),
            P(None, ("wide", "narrow"), None, None),
            P(("wide", "narrow")),
            P(("wide", "narrow")),
            P(("wide", "narrow"), None),
            P(("wide", "narrow"), None),
            P(("wide", "narrow"), None),
            P(("wide", "narrow"), None),
            P(("wide", "narrow"), None),
            P(("wide", "narrow"), None),
            P(("wide", "narrow"), None),
            P(None, ("wide", "narrow")),
            P("wide", None, "narrow"),
            P("wide", None, "narrow"),
            P("wide", "narrow", None),
        ),
        check_vma=False,
    )
```

```python
import functools
import jax
import jax.numpy as jnp
from jax import lax
from jax.experimental import pallas as pl
from jax.experimental.pallas import tpu as pltpu
from jax.sharding import PartitionSpec as P

MESH = pl.DeviceIdType.MESH
HD = 128


epsilon = 1e-06


def angles(seq_len, head_size):
    position = jnp.arange(seq_len).astype(jnp.float32)
    exponent = jnp.arange(head_size // 2).astype(jnp.float32) * (2.0 / head_size)
    frequency = jnp.exp(-jnp.log(10000.0) * exponent)
    theta = position[:, None] * frequency[None, :]
    return (jnp.cos(theta)[:, None, :], jnp.sin(theta)[:, None, :])


def rotate(vectors, cosine_table, sine_table):
    middle = vectors.shape[-1] // 2
    first_half = vectors[..., :middle]
    second_half = vectors[..., middle:]
    return jnp.concatenate(
        [
            first_half * cosine_table - second_half * sine_table,
            second_half * cosine_table + first_half * sine_table,
        ],
        axis=-1,
    )


def unrotate(vectors, cosine_table, sine_table):
    middle = vectors.shape[-1] // 2
    first_half = vectors[..., :middle]
    second_half = vectors[..., middle:]
    return jnp.concatenate(
        [
            first_half * cosine_table + second_half * sine_table,
            second_half * cosine_table - first_half * sine_table,
        ],
        axis=-1,
    )


def norm_ahead(matrix, gain):
    scale_rows = lax.rsqrt(jnp.mean(matrix * matrix, axis=-1, keepdims=True) + epsilon)
    normed = matrix * scale_rows
    return ((normed * gain).astype(jnp.bfloat16), normed, scale_rows)


def norm_back(grad_rows, normed, scale_rows, gain):
    gain_grad = jnp.sum(grad_rows * normed, axis=0)
    inner = grad_rows * gain
    return (
        scale_rows * (inner - normed * jnp.mean(inner * normed, axis=-1, keepdims=True)),
        gain_grad,
    )


def silu_pair(pre_act):
    sigma = jax.nn.sigmoid(pre_act)
    return (pre_act * sigma, sigma * (1.0 + pre_act * (1.0 - sigma)))


def chip_grid(chips):
    deep = 4 if chips % 4 == 0 else 1
    rest = chips // deep
    high = max(d for d in range(1, rest + 1) if rest % d == 0 and d * d <= rest)
    return (deep, high, rest // high)

def place(dims):
    wide = lax.axis_index("wide")
    return wide // (dims[1] * dims[2]), (wide // dims[2]) % dims[1], wide % dims[2]

def greet(dims, a, b, c, core):
    deep, high, broad = dims
    barrier = pltpu.get_barrier_semaphore()
    def chip(i, j, k):
        return (i * high + j) * broad + k
    others = [(chip((a + r) % deep, b, c), core) for r in range(1, deep)]
    others += [(chip(a, (b + r) % high, c), core) for r in range(1, high)]
    others += [(chip(a, b, (c + r) % broad), core) for r in range(1, broad)]
    others += [(chip(a, b, c), 1 - core)]
    for other in others:
        pl.semaphore_signal(barrier, inc=1, device_id=other, device_id_type=MESH)
    pl.semaphore_wait(barrier, len(others))

def cut_columns(widths):
    pieces = []
    for n, width in enumerate(widths):
        tiles = width // 128
        middle = (tiles + 1) // 2 * 128
        pieces += [(n, 0, width)] if tiles < 6 else [(n, 0, middle), (n, middle, width)]
    return pieces


def gather_kernel(dims, arrays, pieces, sliced, *refs):
    deep, high, broad = dims
    count, ahead = len(pieces), 12
    rows_ref, column_ref = refs[arrays], refs[2 * arrays + 1]
    micro = rows_ref.shape[0]
    ins = [refs[n].at[..., lo:hi] for n, lo, hi in pieces]
    outs = [refs[arrays + 1 + n].at[..., lo:hi] for n, lo, hi in pieces]
    sliced = [sliced[n] for n, lo, hi in pieces]
    own_sem, s1, r1, s2, r2, s3, r3, sn, rn, sr, rr = refs[2 * arrays + 2 :]
    a, b, c = place(dims)
    core = lax.axis_index("narrow")
    greet(dims, a, b, c, core)

    def chip(i, j, k):
        return (i * high + j) * broad + k

    def send(src, dst, ss, rs, to):
        copy = pltpu.make_async_remote_copy(
            src_ref=src, dst_ref=dst, send_sem=ss, recv_sem=rs, device_id=to, device_id_type=MESH
        )
        return copy

    def program(me):
        first, second = (high, broad) if me == 0 else (broad, high)

        def at2(i, r):
            if me == 0:
                return outs[i].at[:, (b - r + high) % high, c, me]
            return outs[i].at[:, b, (c - r + broad) % broad, me]

        def at3(i, r):
            if me == 0:
                return outs[i].at[:, :, (c - r + broad) % broad, me]
            return outs[i].at[:, (b - r + high) % high, :, me]

        def to2(r):
            return (chip(a, (b + r) % high, c), me) if me == 0 else (chip(a, b, (c + r) % broad), me)

        def to3(r):
            return (chip(a, b, (c + r) % broad), me) if me == 0 else (chip(a, (b + r) % high, c), me)

        mate = (chip(a, b, c), 1 - me)

        def own(i):
            return pltpu.make_async_copy(ins[i].at[a] if sliced[i] else ins[i], outs[i].at[a, b, c, me], own_sem.at[i])

        def stage1(i, r):
            h = (a + r) % deep
            src = ins[i].at[h] if sliced[i] else ins[i]
            return send(src, outs[i].at[a, b, c, me], s1.at[i, r - 1], r1.at[i, r - 1], (chip(h, b, c), me))

        def own_rows():
            return pltpu.make_async_copy(rows_ref, column_ref.at[:, 0], own_sem.at[count])

        def column(m, r):
            to = (chip((a + r) % deep, b, c), me)
            return send(rows_ref.at[m], column_ref.at[m, r], sr.at[m, r - 1], rr.at[m, r - 1], to)

        def stage2(i, r):
            return send(at2(i, 0), at2(i, 0), s2.at[i, r - 1], r2.at[i, r - 1], to2(r))

        def stage3(i, r):
            return send(at3(i, 0), at3(i, 0), s3.at[i, r - 1], r3.at[i, r - 1], to3(r))

        def across(i, part):
            view = at2(i, 0) if part == 0 else at2(i, part) if part < first else at3(i, part - first + 1)
            return send(view, view, sn.at[i, part], rn.at[i, part], mate)

        parts = first + second - 1
        def begin(i):
            for r in range(1, deep):
                stage1(i, r).start()
            own(i).start()

        for i in range(min(ahead, count)):
            begin(i)
        own_rows().start()
        for step in range(count + 2):
            if step + ahead < count:
                begin(step + ahead)
            for m in range(micro):
                if step == min(2 + 2 * m, count + 1):
                    for r in range(1, deep):
                        column(m, r).start()
            i = step
            if i < count:
                own(i).wait()
                for r in range(1, deep):
                    stage1(i, r).wait_recv()
                for r in range(1, first):
                    stage2(i, r).start()
                across(i, 0).start()
            i = step - 1
            if 0 <= i < count:
                for r in range(1, first):
                    stage2(i, r).wait_recv()
                for r in range(1, second):
                    stage3(i, r).start()
                for r in range(1, first):
                    across(i, r).start()
            i = step - 2
            if 0 <= i < count:
                for r in range(1, second):
                    stage3(i, r).wait_recv()
                for r in range(1, second):
                    across(i, first + r - 1).start()
        for i in range(count):
            for r in range(1, deep):
                stage1(i, r).wait_send()
            for r in range(1, first):
                stage2(i, r).wait_send()
            for r in range(1, second):
                stage3(i, r).wait_send()
            for part in range(parts):
                across(i, part).wait()
        own_rows().wait()
        for m in range(micro):
            for r in range(1, deep):
                column(m, r).wait()

    pl.when(core == 0)(lambda: program(0))
    pl.when(core == 1)(lambda: program(1))

def gather_all(dims, parts, sliced, rows):
    arrays = len(parts)
    deep, high, broad = dims
    pieces = cut_columns([p.shape[-1] for p in parts])
    count = len(pieces)
    sem = pltpu.SemaphoreType.DMA
    most = max(high, broad)
    shapes = [p.shape[1:] if cut else p.shape for p, cut in zip(parts, sliced)]
    vmem, anywhere = pl.BlockSpec(memory_space=pltpu.VMEM), pl.BlockSpec(memory_space=pl.ANY)
    outs = pl.pallas_call(
        functools.partial(gather_kernel, dims, arrays, pieces, sliced),
        out_shape=[jax.ShapeDtypeStruct((deep, high, broad, 2) + sh, p.dtype) for p, sh in zip(parts, shapes)]
        + [jax.ShapeDtypeStruct(rows.shape[:1] + (deep,) + rows.shape[1:], rows.dtype)],
        in_specs=[vmem] * (arrays + 1),
        out_specs=[anywhere] * (arrays + 1),
        scratch_shapes=[sem((count + 1,))]
        + [sem((count, max(deep - 1, 1)))] * 2
        + [sem((count, max(most - 1, 1)))] * 4
        + [sem((count, high + broad - 1))] * 2
        + [sem((rows.shape[0], max(deep - 1, 1)))] * 2,
        compiler_params=pltpu.CompilerParams(collective_id=0, has_side_effects=True),
        name="gather_dense",
    )(*parts, rows)
    return [o.reshape((-1, sh[-1])) for o, sh in zip(outs[:-1], shapes)], outs[-1]


def scatter_kernel(dims, arrays, pieces, sliced, *refs):
    deep, high, broad = dims
    count, ahead = len(pieces), 3
    group = lambda m: [refs[m * arrays + n].at[..., lo:hi] for n, lo, hi in pieces]
    ins, outs, held, from_mate, got2, got3, got4 = [group(m) for m in range(7)]
    own_sem, sn, rn, s2, r2, s3, r3, s4, r4 = refs[7 * arrays :]
    sliced = [sliced[n] for n, lo, hi in pieces]
    a, b, c = place(dims)
    core = lax.axis_index("narrow")
    greet(dims, a, b, c, core)

    def chip(i, j, k):
        return (i * high + j) * broad + k

    def send(src, dst, ss, rs, to):
        return pltpu.make_async_remote_copy(
            src_ref=src, dst_ref=dst, send_sem=ss, recv_sem=rs, device_id=to, device_id_type=MESH
        )

    wide32 = jnp.float32

    def program(me):
        first, second = (broad, high) if me == 0 else (high, broad)
        mate = (chip(a, b, c), 1 - me)

        def own(i):
            return pltpu.make_async_copy(ins[i].at[:, :, :, me], held[i], own_sem.at[i])

        def across(i):
            return send(ins[i].at[:, :, :, 1 - me], from_mate[i], sn.at[i], rn.at[i], mate)

        def stage2(i, r):
            if me == 0:
                k = (c + r) % broad
                return send(held[i].at[:, :, k], got2[i].at[r - 1], s2.at[i, r - 1], r2.at[i, r - 1], (chip(a, b, k), me))
            j = (b + r) % high
            return send(held[i].at[:, j], got2[i].at[r - 1], s2.at[i, r - 1], r2.at[i, r - 1], (chip(a, j, c), me))

        def stage3(i, r):
            if me == 0:
                j = (b + r) % high
                return send(held[i].at[:, j, c], got3[i].at[r - 1], s3.at[i, r - 1], r3.at[i, r - 1], (chip(a, j, c), me))
            k = (c + r) % broad
            return send(held[i].at[:, b, k], got3[i].at[r - 1], s3.at[i, r - 1], r3.at[i, r - 1], (chip(a, b, k), me))

        def stage4(i, r):
            h = (a + r) % deep
            return send(held[i].at[h, b, c], got4[i].at[r - 1], s4.at[i, r - 1], r4.at[i, r - 1], (chip(h, b, c), me))

        def add_mate(i):
            for j in range(high):
                for k in range(broad):
                    @pl.loop(0, deep)
                    def _(h):
                        held[i][h, j, k] = (held[i][h, j, k].astype(wide32) + from_mate[i][h, j, k].astype(wide32)).astype(jnp.bfloat16)

        def add2(i):
            if me == 0:
                for j in range(high):
                    @pl.loop(0, deep)
                    def _(h):
                        total = held[i][h, j, c].astype(wide32)
                        for r in range(1, broad):
                            total += got2[i][r - 1, h, j].astype(wide32)
                        held[i][h, j, c] = total.astype(jnp.bfloat16)
            else:
                for k in range(broad):
                    @pl.loop(0, deep)
                    def _(h):
                        total = held[i][h, b, k].astype(wide32)
                        for r in range(1, high):
                            total += got2[i][r - 1, h, k].astype(wide32)
                        held[i][h, b, k] = total.astype(jnp.bfloat16)

        def add3(i):
            @pl.loop(0, deep)
            def _(h):
                total = held[i][h, b, c].astype(wide32)
                for r in range(1, second):
                    total += got3[i][r - 1, h].astype(wide32)
                held[i][h, b, c] = total.astype(jnp.bfloat16)

        def add4(i):
            if sliced[i]:
                outs[i][a] = held[i][a, b, c].astype(wide32)
                for r in range(1, deep):
                    outs[i][(a - r + deep) % deep] = got4[i][r - 1].astype(wide32)
                return
            total = held[i][a, b, c].astype(wide32)
            for r in range(1, deep):
                total += got4[i][r - 1].astype(wide32)
            outs[i][...] = total

        def begin(i):
            across(i).start()
            own(i).start()

        for i in range(min(ahead, count)):
            begin(i)
        for step in range(count + 3):
            if step + ahead < count:
                begin(step + ahead)
            i = step
            if i < count:
                own(i).wait()
                across(i).wait_recv()
                add_mate(i)
                for r in range(1, first):
                    stage2(i, r).start()
            i = step - 1
            if 0 <= i < count:
                for r in range(1, first):
                    stage2(i, r).wait_recv()
                add2(i)
                for r in range(1, second):
                    stage3(i, r).start()
            i = step - 2
            if 0 <= i < count:
                for r in range(1, second):
                    stage3(i, r).wait_recv()
                add3(i)
                for r in range(1, deep):
                    stage4(i, r).start()
            i = step - 3
            if 0 <= i < count:
                for r in range(1, deep):
                    stage4(i, r).wait_recv()
                add4(i)
        for i in range(count):
            across(i).wait_send()
            for r in range(1, first):
                stage2(i, r).wait_send()
            for r in range(1, second):
                stage3(i, r).wait_send()
            for r in range(1, deep):
                stage4(i, r).wait_send()

    pl.when(core == 0)(lambda: program(0))
    pl.when(core == 1)(lambda: program(1))

def scatter_all(dims, parts, sliced):
    arrays = len(parts)
    deep, high, broad = dims
    pieces = cut_columns([p.shape[-1] for p in parts])
    count = len(pieces)
    devices = deep * high * broad * 2
    blocks = [(p.shape[0] // devices, p.shape[1]) for p in parts]
    sem = pltpu.SemaphoreType.DMA
    most = max(high, broad)
    vm = lambda lead: [pltpu.VMEM(lead + blk, jnp.bfloat16) for blk in blocks]
    side = max(high, broad)
    got2 = vm((max(most - 1, 1), deep, side))
    return pl.pallas_call(
        functools.partial(scatter_kernel, dims, arrays, pieces, sliced),
        out_shape=[jax.ShapeDtypeStruct(((deep,) if cut else ()) + blk, jnp.float32) for blk, cut in zip(blocks, sliced)],
        in_specs=[pl.BlockSpec(memory_space=pl.ANY)] * arrays,
        out_specs=[pl.BlockSpec(memory_space=pltpu.VMEM)] * arrays,
        scratch_shapes=vm((deep, high, broad)) + vm((deep, high, broad)) + got2 + vm((max(most - 1, 1), deep)) + vm((max(deep - 1, 1),))
        + [sem((count,))] * 3
        + [sem((count, max(most - 1, 1)))] * 4
        + [sem((count, max(deep - 1, 1)))] * 2,
        compiler_params=pltpu.CompilerParams(collective_id=1, has_side_effects=True, vmem_limit_bytes=62 * 1024 * 1024),
        name="scatter_dense",
    )(*[p.reshape((deep, high, broad, 2) + blk) for p, blk in zip(parts, blocks)])


def greet_all(dims, a, b, c, core):
    deep, high, broad = dims
    barrier = pltpu.get_barrier_semaphore()
    others = [(((a + r) % deep * high + b) * broad + c, core) for r in range(1, deep)]
    others += [
        ((a * high + (b + q // broad) % high) * broad + (c + q % broad) % broad, core) for q in range(1, high * broad)
    ]
    others += [((a * high + b) * broad + c, 1 - core)]
    for other in others:
        pl.semaphore_signal(barrier, inc=1, device_id=other, device_id_type=MESH)
    pl.semaphore_wait(barrier, len(others))


def remote(src, dst, ss, rs, to):
    return pltpu.make_async_remote_copy(
        src_ref=src, dst_ref=dst, send_sem=ss, recv_sem=rs, device_id=to, device_id_type=MESH
    )


def dispatch_kernel(dims, micro, x_ref, choose_ref, both_ref, column_ref, got, picked, scol, rcol, spl, rpl, sm, rm, sl):
    deep, high, broad = dims
    offsets = high * broad
    a, b, c = place(dims)
    core = lax.axis_index("narrow")
    greet_all(dims, a, b, c, core)
    mate = ((a * high + b) * broad + c, 1 - core)
    rows_ref, mates_ref = both_ref.at[0], both_ref.at[1]

    def column(m, k):
        return remote(x_ref.at[m], got.at[m, k], scol.at[m, k], rcol.at[m, k], (((a + k) % deep * high + b) * broad + c, core))

    def plane(m, k, q):
        to = (a * high + (b + q // broad) % high) * broad + (c + q % broad) % broad
        return remote(picked.at[m, k, q], rows_ref.at[m, q, k], spl.at[m, k, q], rpl.at[m, k, q], (to, core))

    def across(m, k, part):
        if part == 0:
            return remote(picked.at[m, k, 0], mates_ref.at[m, 0, k], sm.at[m, k, 0], rm.at[m, k, 0], mate)
        return remote(rows_ref.at[m, 1:, k], mates_ref.at[m, 1:, k], sm.at[m, k, 1], rm.at[m, k, 1], mate)

    def keep(m, k):
        return pltpu.make_async_copy(picked.at[m, k, 0], rows_ref.at[m, 0, k], sl.at[m, k, 0])

    def keep_column(m, k):
        return pltpu.make_async_copy(x_ref.at[m] if k == 0 else got.at[m, k], column_ref.at[m, k], sl.at[m, k, 1])

    order = [(m, k) for m in range(micro) for k in range(deep)]
    for m, k in order:
        if k > 0:
            column(m, k).start()
    for m, k in order:
        if k > 0:
            column(m, k).wait_recv()
        keep_column(m, k).start()
        piece = x_ref[m] if k == 0 else got[m, k]
        chosen = jnp.dot(choose_ref[m, k], piece, preferred_element_type=jnp.float32).astype(jnp.bfloat16)
        picked[m, k] = chosen.reshape(picked.shape[2:])
        for q in range(1, offsets):
            plane(m, k, q).start()
        keep(m, k).start()
        across(m, k, 0).start()
    for m, k in order:
        for q in range(1, offsets):
            plane(m, k, q).wait_recv()
        across(m, k, 1).start()
    for m, k in order:
        if k > 0:
            column(m, k).wait_send()
        keep_column(m, k).wait()
        for q in range(1, offsets):
            plane(m, k, q).wait_send()
        keep(m, k).wait()
        across(m, k, 0).wait()
        across(m, k, 1).wait()


def dispatch(dims, x, choose):
    deep, high, broad = dims
    micro, tokens, width = x.shape
    offsets = high * broad
    slots = choose.shape[2] // offsets
    sem = pltpu.SemaphoreType.DMA
    anywhere, vmem = pl.BlockSpec(memory_space=pl.ANY), pl.BlockSpec(memory_space=pltpu.VMEM)
    out = jax.ShapeDtypeStruct((2, micro, offsets, deep, slots, width), x.dtype)
    return pl.pallas_call(
        functools.partial(dispatch_kernel, dims, micro),
        out_shape=[out, jax.ShapeDtypeStruct((micro, deep, tokens, width), x.dtype)],
        in_specs=[vmem, vmem],
        out_specs=[anywhere] * 2,
        scratch_shapes=[
            pltpu.VMEM((micro, deep, tokens, width), x.dtype),
            pltpu.VMEM((micro, deep, offsets, slots, width), x.dtype),
        ]
        + [sem((micro, deep))] * 2
        + [sem((micro, deep, offsets))] * 2
        + [sem((micro, deep, 2))] * 3,
        compiler_params=pltpu.CompilerParams(collective_id=2, has_side_effects=True),
        name="dispatch_rows",
    )(x, choose)


def return_kernel(dims, micro, both_ref, choose_ref, near_ref, total_ref, held, mated, back, up, got, sl, sm, rm, spl, rpl, scol, rcol):
    deep, high, broad = dims
    offsets = high * broad
    a, b, c = place(dims)
    core = lax.axis_index("narrow")
    greet_all(dims, a, b, c, core)
    mate = ((a * high + b) * broad + c, 1 - core)
    near_width = near_ref.shape[-1]
    mine_ref, theirs_ref = both_ref.at[0], both_ref.at[1]

    def load(m, k):
        return pltpu.make_async_copy(mine_ref.at[m, :, k], held.at[m, :, k], sl.at[m, k])

    def across(m, k):
        return remote(theirs_ref.at[m, :, k], mated.at[m, :, k], sm.at[m, k], rm.at[m, k], mate)

    def plane(m, k, q):
        to = (a * high + (b - q // broad + high) % high) * broad + (c - q % broad + broad) % broad
        return remote(held.at[m, q, k], back.at[m, k, q], spl.at[m, k, q], rpl.at[m, k, q], (to, core))

    def column(m, k):
        return remote(up.at[m, k], got.at[m, k], scol.at[m, k], rcol.at[m, k], (((a - k + deep) % deep * high + b) * broad + c, core))

    order = [(m, k) for m in range(micro) for k in list(range(1, deep)) + [0]]
    ahead = 3
    for m, k in order[:ahead]:
        across(m, k).start()
        load(m, k).start()
    for n, (m, k) in enumerate(order):
        for later in order[n + ahead : n + ahead + 1]:
            across(*later).start()
            load(*later).start()
        load(m, k).wait()
        across(m, k).wait_recv()
        for q in range(1, offsets):
            held[m, q, k] = (held[m, q, k].astype(jnp.float32) + mated[m, q, k].astype(jnp.float32)).astype(jnp.bfloat16)
            plane(m, k, q).start()
        back[m, k, 0] = (held[m, 0, k].astype(jnp.float32) + mated[m, 0, k].astype(jnp.float32)).astype(jnp.bfloat16)
    for m, k in order:
        for q in range(1, offsets):
            plane(m, k, q).wait_recv()
        rows = back[m, k].reshape((-1, back.shape[-1]))
        sums = jnp.dot(choose_ref[m, k], rows, preferred_element_type=jnp.float32)
        dense = sums[:, :near_width] + near_ref[m, k].astype(jnp.float32)
        if k == 0:
            total_ref[m, :, :near_width] = dense
            if near_width < sums.shape[1]:
                total_ref[m, :, near_width:] = sums[:, near_width:]
        else:
            up[m, k, :, :near_width] = dense.astype(jnp.bfloat16)
            if near_width < sums.shape[1]:
                up[m, k, :, near_width:] = sums[:, near_width:].astype(jnp.bfloat16)
            column(m, k).start()
    for m in range(micro):
        for k in range(1, deep):
            column(m, k).wait_recv()
            total_ref[m] += got[m, k].astype(jnp.float32)
    for m, k in order:
        across(m, k).wait_send()
        for q in range(1, offsets):
            plane(m, k, q).wait_send()
        if k > 0:
            column(m, k).wait_send()


def give_back(dims, both, choose_t, near):
    deep, high, broad = dims
    _, micro, offsets, _, slots, width = both.shape
    tokens = choose_t.shape[2]
    sem = pltpu.SemaphoreType.DMA
    anywhere, vmem = pl.BlockSpec(memory_space=pl.ANY), pl.BlockSpec(memory_space=pltpu.VMEM)
    scratch = lambda *shape: pltpu.VMEM(shape, both.dtype)
    return pl.pallas_call(
        functools.partial(return_kernel, dims, micro),
        out_shape=jax.ShapeDtypeStruct((micro, tokens, width), jnp.float32),
        in_specs=[anywhere, vmem, vmem],
        out_specs=vmem,
        scratch_shapes=[
            scratch(micro, offsets, deep, slots, width),
            scratch(micro, offsets, deep, slots, width),
            scratch(micro, deep, offsets, slots, width),
            scratch(micro, deep, tokens, width),
            scratch(micro, deep, tokens, width),
        ]
        + [sem((micro, deep))] * 3
        + [sem((micro, deep, offsets))] * 2
        + [sem((micro, deep))] * 2,
        compiler_params=pltpu.CompilerParams(collective_id=3, has_side_effects=True, vmem_limit_bytes=62 * 1024 * 1024),
        name="return_rows",
    )(both, choose_t, near)


class Line:
    def __init__(self, dims):
        deep, plane = dims[0], dims[1] * dims[2]
        self.up = lambda far: [(i * plane + p, (i + far) * plane + p) for i in range(deep - far) for p in range(plane)]

    def both_ways(self, one, two, far=1):
        up = self.up(far)
        return lax.ppermute(one, "wide", up), lax.ppermute(two, "wide", [(b, a) for a, b in up])


def plane_pairs(dims, offset, sign):
    deep, high, broad = dims
    up, over = (offset // broad) * sign, (offset % broad) * sign
    return [
        ((i * high + j) * broad + k, (i * high + (j + up) % high) * broad + (k + over) % broad)
        for i in range(deep)
        for j in range(high)
        for k in range(broad)
    ]


def swap_cores(rows):
    return lax.ppermute(rows, "narrow", [(0, 1), (1, 0)])


def plane_rows(dims, picked):
    return [picked[0]] + [lax.ppermute(picked[q], "wide", plane_pairs(dims, q, 1)) for q in range(1, picked.shape[0])]


def plane_back(dims, rows):
    offsets = rows.shape[1]
    return [rows[:, 0]] + [lax.ppermute(rows[:, q], "wide", plane_pairs(dims, q, -1)) for q in range(1, offsets)]


def column_sums(dims, choose, back, near):
    sums = jnp.einsum("mkst,mksd->mktd", choose, back, preferred_element_type=jnp.float32)
    return sums + near.astype(jnp.float32)


def masked_gates(logits, named):
    top = jnp.max(jnp.where(named > 0, logits, -1e30), axis=-1, keepdims=True)
    weights = jnp.where(named > 0, jnp.exp(logits - top), 0.0)
    return weights / jnp.maximum(jnp.sum(weights, axis=-1, keepdims=True), 0.5)


def f32_dot(one, two):
    return jnp.dot(one, two, preferred_element_type=jnp.float32)


def dot_t(one, two):
    return lax.dot_general(one, two, (((1,), (1,)), ((), ())), preferred_element_type=jnp.float32)


def t_dot(one, two):
    return lax.dot_general(one, two, (((0,), (0,)), ((), ())), preferred_element_type=jnp.float32)


def own_gate(x, router, names, pick):
    row_gates = masked_gates(f32_dot(x, router), names.astype(jnp.float32))
    return jnp.sum(row_gates * pick[:, : row_gates.shape[1]], axis=-1, keepdims=True)


def expert_forward_kernel(width, half, x_ref, router_ref, pick_ref, gate_w, up_w, down_w, mine_ref, theirs_ref, g_ref, u_ref):
    x, names = x_ref[:, :width], x_ref[:, width:]
    gate = own_gate(x, router_ref[...], names, pick_ref[0:1])
    g = f32_dot(x, gate_w[...])
    u = f32_dot(x, up_w[...])
    g_ref[...] = g
    u_ref[...] = u
    act, _ = silu_pair(g)
    out = f32_dot((gate * (act * u)).astype(jnp.bfloat16), down_w[...]).astype(jnp.bfloat16)

    @pl.when(pl.program_id(0) < half)
    def _():
        mine_ref[...] = out

    @pl.when(pl.program_id(0) >= half)
    def _():
        theirs_ref[...] = out


def expert_backward_kernel(
    half, width, x_ref, d_ref, mate_d_ref, router_ref, pick_ref, gate_w, up_w, down_w, g_ref, u_ref, in_ref, dg_ref, du_ref, dd_ref
):
    step = pl.program_id(0)
    x, names = x_ref[:, :width], x_ref[:, width:]
    dy = jnp.where(step < half, d_ref[...], mate_d_ref[...])
    gate = own_gate(x, router_ref[...], names, pick_ref[0:1])
    act, slope = silu_pair(g_ref[...])
    u = u_ref[...]
    d_plain = dot_t(dy, down_w[...])
    hidden = act * u
    d_gate = jnp.sum(hidden * d_plain, axis=-1, keepdims=True)
    weighed = (gate * hidden).astype(jnp.bfloat16)
    d_hidden = gate * d_plain
    d_act = (d_hidden * u * slope).astype(jnp.bfloat16)
    d_up = (d_hidden * act).astype(jnp.bfloat16)
    rows = dot_t(d_act, gate_w[...]) + dot_t(d_up, up_w[...])
    in_ref[:, :width] = rows.astype(jnp.bfloat16)
    coarse = d_gate.astype(jnp.bfloat16).astype(jnp.float32)
    beside = coarse * pick_ref[1:2] + (d_gate - coarse) * pick_ref[2:3]
    in_ref[:, width:] = beside.astype(jnp.bfloat16)

    @pl.when(step == 0)
    def _():
        dg_ref[...] = jnp.zeros_like(dg_ref)
        du_ref[...] = jnp.zeros_like(du_ref)
        dd_ref[...] = jnp.zeros_like(dd_ref)

    dg_ref[...] += t_dot(x, d_act)
    du_ref[...] += t_dot(x, d_up)
    dd_ref[...] += t_dot(weighed, dy)


def fixed(shape):
    return pl.BlockSpec(shape, lambda i: (0,) * len(shape), pipeline_mode=pl.Buffered(1))


def row_block(total):
    return max(n for n in (512, 256, 128, 64, 32, 16) if total % n == 0)


def roomy():
    return pltpu.CompilerParams(vmem_limit_bytes=60 * 1024 * 1024)


def cost(flops, moved):
    return pl.CostEstimate(flops=flops, bytes_accessed=moved, transcendentals=0)


def expert_forward(x, router, picks, gate_w, up_w, down_w):
    rows, (width, hidden) = x.shape[0], gate_w.shape
    block = row_block(rows // 2)
    half = rows // 2 // block
    by_row = lambda w: pl.BlockSpec((block, w), lambda i: (i, 0))
    return pl.pallas_call(
        functools.partial(expert_forward_kernel, width, half),
        grid=(rows // block,),
        out_shape=[
            jax.ShapeDtypeStruct((rows // 2, width), jnp.bfloat16),
            jax.ShapeDtypeStruct((rows // 2, width), jnp.bfloat16),
            jax.ShapeDtypeStruct((rows, hidden), jnp.float32),
            jax.ShapeDtypeStruct((rows, hidden), jnp.float32),
        ],
        in_specs=[by_row(x.shape[1]), fixed(router.shape), fixed(picks.shape)] + [fixed(w.shape) for w in (gate_w, up_w, down_w)],
        out_specs=[
            pl.BlockSpec((block, width), lambda i: (jnp.minimum(i, half - 1), 0)),
            pl.BlockSpec((block, width), lambda i: (jnp.maximum(i - half, 0), 0)),
            by_row(hidden),
            by_row(hidden),
        ],
        compiler_params=roomy(),
        cost_estimate=cost(6 * rows * width * hidden, rows * (4 * width + 8 * hidden)),
        name="expert_forward",
    )(x, router, picks, gate_w, up_w, down_w)


def expert_backward(x, d_mine, d_mates, router, picks, gate_w, up_w, down_w, g, u):
    rows, (width, hidden) = x.shape[0], gate_w.shape
    block = row_block(d_mine.shape[0])
    half = d_mine.shape[0] // block
    by_row = lambda w: pl.BlockSpec((block, w), lambda i: (i, 0))
    first = pl.BlockSpec((block, width), lambda i: (jnp.minimum(i, half - 1), 0))
    second = pl.BlockSpec((block, width), lambda i: (jnp.maximum(i - half, 0), 0))
    wide_in = width + picks.shape[1]
    return pl.pallas_call(
        functools.partial(expert_backward_kernel, half, width),
        grid=(2 * half,),
        out_shape=[jax.ShapeDtypeStruct((rows, wide_in), jnp.bfloat16)]
        + [jax.ShapeDtypeStruct(w.shape, jnp.float32) for w in (gate_w, up_w, down_w)],
        in_specs=[by_row(x.shape[1]), first, second, fixed(router.shape), fixed(picks.shape)]
        + [fixed(w.shape) for w in (gate_w, up_w, down_w)]
        + [by_row(hidden), by_row(hidden)],
        out_specs=[by_row(wide_in)] + [fixed(w.shape) for w in (gate_w, up_w, down_w)],
        compiler_params=roomy(),
        cost_estimate=cost(12 * rows * width * hidden, rows * (6 * width + 8 * hidden)),
        name="expert_backward",
    )(x, d_mine, d_mates, router, picks, gate_w, up_w, down_w, g, u)


def attention_kernel(
    micro, x_ref, gains_ref, cos_ref, sin_ref, wq, wk, wv, wo, q_ref, k_ref, v_ref, p_ref, mixed_ref, in_ref, residual_ref, mid_ref
):
    rows, width = x_ref.shape
    seq = rows // micro
    in_ref[...], _, _ = norm_ahead(x_ref[...].astype(jnp.float32), gains_ref[0:1])
    heads = width // HD
    group = 2 if heads % 2 == 0 else 1
    lower = lax.broadcasted_iota(jnp.int32, (seq, seq), 0) >= lax.broadcasted_iota(jnp.int32, (seq, seq), 1)

    @pl.loop(0, heads // group)
    def _(step):
        columns = pl.ds(pl.multiple_of(step * (group * HD), group * HD), group * HD)
        normed = in_ref[...]

        def turned(weights):
            raw = f32_dot(normed, weights[:, columns])
            parts = [raw[:, j * HD : (j + 1) * HD] for j in range(group)]
            parts = [p * cos_ref[...] + pltpu.roll(p, HD // 2, 1) * sin_ref[...] for p in parts]
            return jnp.concatenate(parts, axis=1).astype(jnp.bfloat16)

        q, k = turned(wq), turned(wk)
        v = f32_dot(normed, wv[:, columns]).astype(jnp.bfloat16)
        q_ref[:, columns], k_ref[:, columns], v_ref[:, columns] = q, k, v
        every = []
        for m in range(micro):
            side = []
            for j in range(group):
                one = lambda a: a[m * seq : (m + 1) * seq, j * HD : (j + 1) * HD]
                scores = HD ** (-0.5) * dot_t(one(q), one(k))
                scores = jnp.where(lower, scores, -1e30)
                weights = jnp.exp(scores - jnp.max(scores, axis=-1, keepdims=True))
                probs = weights / jnp.sum(weights, axis=-1, keepdims=True)
                p_ref[m, step * group + j] = probs
                side.append(f32_dot(probs.astype(jnp.bfloat16), one(v)))
            every.append(jnp.concatenate(side, axis=1))
        mixed_ref[:, columns] = jnp.concatenate(every, axis=0).astype(jnp.bfloat16)

    @pl.loop(0, heads // group)
    def _(step):
        columns = pl.ds(pl.multiple_of(step * (group * HD), group * HD), group * HD)
        residual_ref[:, columns] = x_ref[:, columns].astype(jnp.float32) + f32_dot(mixed_ref[...], wo[:, columns])

    mid_ref[...], _, _ = norm_ahead(residual_ref[...], gains_ref[1:2])


def attention_forward(micro, x, gains, cos, sin, wq, wk, wv, wo):
    rows, width = x.shape
    seq = rows // micro
    like = lambda kind: jax.ShapeDtypeStruct((rows, width), kind)
    return pl.pallas_call(
        functools.partial(attention_kernel, micro),
        out_shape=[like(jnp.bfloat16)] * 3
        + [jax.ShapeDtypeStruct((micro, width // HD, seq, seq), jnp.float32)]
        + [like(jnp.bfloat16)] * 2
        + [like(jnp.float32), like(jnp.bfloat16)],
        compiler_params=roomy(),
        cost_estimate=cost(32 * rows * width * width, 10 * width * width),
        name="attention_forward",
    )(x, gains, cos, sin, wq, wk, wv, wo)


def shared_kernel(width, part, x_ref, d_ref, w_ref, out_ref, in_ref, grad_ref):
    x, dy = x_ref[:, :width], d_ref[...]
    gate_w, up_w, down_t = w_ref[:, :part], w_ref[:, part : 2 * part], w_ref[:, 2 * part :]
    act, slope = silu_pair(f32_dot(x, gate_w))
    u = f32_dot(x, up_w)
    hidden = (act * u).astype(jnp.bfloat16)
    out_ref[...] = dot_t(hidden, down_t).astype(jnp.bfloat16)
    d_hidden = f32_dot(dy, down_t)
    d_gate = (d_hidden * u * slope).astype(jnp.bfloat16)
    d_up = (d_hidden * act).astype(jnp.bfloat16)
    in_ref[...] = (dot_t(d_gate, gate_w) + dot_t(d_up, up_w)).astype(jnp.bfloat16)

    @pl.when(pl.program_id(0) == 0)
    def _():
        grad_ref[...] = jnp.zeros_like(grad_ref)

    grad_ref[:, :part] += t_dot(x, d_gate)
    grad_ref[:, part : 2 * part] += t_dot(x, d_up)
    grad_ref[:, 2 * part :] += t_dot(dy, hidden)


def shared_expert(x, d, weights):
    rows, width = d.shape
    part = weights.shape[1] // 3
    block = row_block(rows)
    by_row = lambda w: pl.BlockSpec((block, w), lambda i: (i, 0))
    return pl.pallas_call(
        functools.partial(shared_kernel, width, part),
        grid=(rows // block,),
        out_shape=[jax.ShapeDtypeStruct((rows, width), jnp.bfloat16)] * 2 + [jax.ShapeDtypeStruct(weights.shape, jnp.float32)],
        in_specs=[by_row(x.shape[1]), by_row(width), fixed(weights.shape)],
        out_specs=[by_row(width)] * 2 + [fixed(weights.shape)],
        compiler_params=roomy(),
        cost_estimate=cost(18 * rows * width * part, rows * 8 * width),
        name="shared_expert",
    )(x, d, weights)


def on_device(
    tokens,
    cotangent,
    routes,
    gain_attn,
    gain_moe,
    w_query,
    w_key,
    w_value,
    attention_output_weight,
    router,
    shared_gate,
    shared_up,
    shared_down,
    routed_gate_weight,
    routed_up_weight,
    routed_down_weight,
):
    f32, bf16 = jnp.float32, jnp.bfloat16
    micro = tokens.shape[0]
    seq_len, width_all = tokens.shape[2], tokens.shape[3]
    chosen_count = routes.shape[3]
    experts = router.shape[1]
    heads = width_all // HD
    dims = chip_grid(lax.axis_size("wide"))
    deep, high, broad = dims
    slots = 9 * seq_len * chosen_count // (8 * experts) + 1
    extra = -(-experts // 128) * 128
    extra_back = -(-4 * experts // 128) * 128
    cosine_table, sine_table = angles(seq_len, HD)
    scale_factor = HD ** (-0.5)
    causal_mask = jnp.arange(seq_len)[:, None] >= jnp.arange(seq_len)[None, :]
    me = lax.axis_index("wide")
    own_rows = gain_attn.shape[0]

    named = jnp.any(routes[:, 0, :, :, None] == jnp.arange(experts), axis=2)
    named_wide = jnp.pad(named.astype(bf16), ((0, 0), (0, 0), (0, extra - experts)))

    small_width = -(-(experts + 2) // 128) * 128
    small = jnp.concatenate(
        [router, gain_attn[:, None], gain_moe[:, None], jnp.zeros((own_rows, small_width - experts - 2), bf16)], axis=1
    )
    hidden_all = shared_gate.shape[1]
    part = -(-hidden_all // (deep * 128)) * 128

    def cut(matrix):
        return jnp.pad(matrix, ((0, 0), (0, part * deep - hidden_all))).reshape(own_rows, deep, part).transpose(1, 0, 2)

    shared = jnp.concatenate([cut(shared_gate), cut(shared_up), cut(shared_down.T)], axis=2)
    (small_all, wq_all, wk_all, wv_all, wo_all, shared_all), names_column = gather_all(
        dims,
        [small, w_query, w_key, w_value, attention_output_weight, shared],
        [False, False, False, False, False, True],
        named_wide,
    )
    line = Line(dims)
    ahead_rows, back_rows = line.both_ways(cotangent[:, 0], cotangent[:, 0])
    ahead_rows, back_rows, small_all, wq_all, wk_all = lax.optimization_barrier((ahead_rows, back_rows, small_all, wq_all, wk_all))
    from_before, from_after = [ahead_rows], [back_rows]

    if deep > 2:
        one, two = line.both_ways(ahead_rows, back_rows)
        from_before, from_after = from_before + [one], from_after + [two]
    for far in range(3, deep):
        one, two = line.both_ways(cotangent[:, 0], cotangent[:, 0], far)
        from_before, from_after = from_before + [one], from_after + [two]
    router_all = small_all[:, :experts]
    gain_one = small_all[:, experts].astype(f32)
    gain_two = small_all[:, experts + 1].astype(f32)

    chip_a, chip_b, chip_c = place(dims)
    offsets = high * broad
    step = jnp.arange(offsets)
    targets = (chip_a * high + (chip_b + step // broad) % high) * broad + (chip_c + step % broad) % broad
    is_target = (jnp.arange(experts)[:, None] == targets[None, :]).astype(bf16)
    earlier = (jnp.arange(seq_len)[:, None] > jnp.arange(seq_len)[None, :]).astype(bf16)
    names = names_column[..., :experts]
    aimed = jnp.einsum("mkte,eq->mkqt", names, is_target, preferred_element_type=f32)
    slot = jnp.einsum("mkqu,tu->mkqt", aimed.astype(bf16), earlier, preferred_element_type=f32)
    hit = (slot[:, :, :, None, :] == jnp.arange(slots, dtype=f32)[:, None]) & (aimed[:, :, :, None, :] > 0.5)
    choose = hit.astype(bf16).reshape(micro, deep, offsets * slots, seq_len)
    choose_t = choose.transpose(0, 1, 3, 2)

    rows_low = tokens[:, 0].reshape(micro * seq_len, width_all)
    rows_in = rows_low.astype(f32)
    cos_row, sin_row = cosine_table[:, 0], sine_table[:, 0]
    queries, key_rows, value_rows, probs, mixed, normalized_input, residual, normed_mid = attention_forward(
        micro,
        rows_low,
        jnp.stack([gain_one, gain_two]),
        jnp.tile(jnp.concatenate([cos_row, cos_row], axis=1), (micro, 1)),
        jnp.tile(jnp.concatenate([-sin_row, sin_row], axis=1), (micro, 1)),
        wq_all,
        wk_all,
        wv_all,
        wo_all,
    )
    queries, key_rows, value_rows = (a.reshape(micro, seq_len, heads, HD) for a in (queries, key_rows, value_rows))
    probs_low = probs.astype(bf16)
    _, plain_in, scale_in = norm_ahead(rows_in, gain_one)
    _, plain_mid, scale_mid = norm_ahead(residual, gain_two)

    from_before, from_after, normed_mid = lax.optimization_barrier((from_before, from_after, normed_mid))
    d_column = [cotangent[:, 0]] + [
        jnp.where(chip_a >= k, from_before[k - 1], from_after[deep - k - 1]) for k in range(1, deep)
    ]
    d_column = jnp.stack(d_column, axis=1)
    d_picked_rows = jnp.einsum("mkqst,mktd->qmksd", hit.astype(bf16), d_column, preferred_element_type=f32).astype(bf16)

    x_ext = jnp.concatenate([normed_mid.reshape(micro, seq_len, width_all), named_wide], axis=-1)
    x_both, x_column = dispatch(dims, x_ext, choose)
    x_both, d_picked_rows = lax.optimization_barrier((x_both, d_picked_rows))
    d_pieces = plane_rows(dims, d_picked_rows)
    x_rows = x_both.reshape(-1, width_all + extra)

    shared_out, d_shared_in, grad_shared = shared_expert(
        x_column.reshape(-1, width_all + extra), d_column.reshape(-1, width_all), shared_all
    )
    grad_shared = grad_shared.astype(bf16)
    x_rows, shared_out = lax.optimization_barrier((x_rows, shared_out))

    gate_w, up_w, down_w = routed_gate_weight[0], routed_up_weight[0], routed_down_weight[0]
    side = 2 * experts * lax.axis_index("narrow")
    places = jnp.stack([me, me + side, me + side + experts])
    picks = (jnp.arange(extra_back)[None, :] == places[:, None]).astype(f32)
    router_wide = jnp.pad(router_all, ((0, 0), (0, extra - experts)))
    expert_args = (router_wide, picks, gate_w, up_w, down_w)
    out_mine, out_theirs, g_part, u_part = expert_forward(x_rows, *expert_args)
    d_pieces, out_mine, out_theirs = lax.optimization_barrier((d_pieces, out_mine, out_theirs))
    theirs = swap_cores(out_theirs)
    d_mine = jnp.stack(d_pieces, axis=1).reshape(-1, width_all)
    d_mates = swap_cores(d_mine)
    routed_rows = (out_mine.astype(f32) + theirs.astype(f32)).astype(bf16)
    routed_rows = routed_rows.reshape(micro, offsets, deep, slots, width_all)

    x_late, routed_rows = lax.optimization_barrier((x_rows, routed_rows))
    routed_pieces = plane_back(dims, routed_rows)
    d_in_rows, grad_egate, grad_eup, grad_edown = expert_backward(x_late, d_mine, d_mates, *expert_args, g_part, u_part)
    routed_pieces, d_in_rows = lax.optimization_barrier((routed_pieces, d_in_rows))
    routed_back = jnp.stack(routed_pieces, axis=2).reshape(micro, deep, offsets * slots, width_all)
    routed_sums = column_sums(dims, choose, routed_back, shared_out.reshape(d_column.shape))
    routed_sums, d_in_rows = lax.optimization_barrier((routed_sums, d_in_rows))
    up_rows, down_rows = line.both_ways(routed_sums[:, 1 % deep].astype(bf16), routed_sums[:, deep - 1].astype(bf16))
    d_total = give_back(
        dims,
        d_in_rows.reshape(2, micro, offsets, deep, slots, width_all + extra_back),
        choose_t,
        d_shared_in.reshape(d_column.shape),
    )
    d_total, up_rows, down_rows = lax.optimization_barrier((d_total, up_rows, down_rows))
    hops = [1]

    def next_sum(up_rows, down_rows):
        hops[0] += 1
        if hops[0] > deep - 1:
            return up_rows, down_rows
        up_rows = up_rows.astype(f32) + routed_sums[:, hops[0]]
        down_rows = down_rows.astype(f32) + routed_sums[:, deep - hops[0]]
        return line.both_ways(up_rows.astype(bf16), down_rows.astype(bf16))

    up_rows, down_rows = next_sum(up_rows, down_rows)
    d_total = d_total.reshape(micro * seq_len, width_all + extra_back)
    d_gates = sum(d_total[:, width_all + n * experts : width_all + (n + 1) * experts] for n in range(4))

    named_rows = named.reshape(micro * seq_len, experts)
    gates = masked_gates(f32_dot(normed_mid, router_all), named_rows)
    d_out = cotangent[:, 0].reshape(micro * seq_len, width_all).astype(f32)

    d_logits = (gates * (d_gates - jnp.sum(gates * d_gates, axis=1, keepdims=True))).astype(bf16)
    d_mid = d_total[:, :width_all] + dot_t(d_logits, router_all)
    d_norm_two, grad_gain_two = norm_back(d_mid, plain_mid, scale_mid, gain_two)
    d_residual = d_out + d_norm_two
    d_attn = d_residual.astype(bf16)
    grad_wout = t_dot(mixed, d_attn).astype(bf16)
    d_mixed = dot_t(d_attn, wo_all).astype(bf16).reshape(micro, seq_len, heads, HD)
    d_probs = jnp.einsum("sqhd,skhd->shqk", d_mixed, value_rows, preferred_element_type=f32)
    d_value = jnp.einsum("shqk,sqhd->skhd", probs_low, d_mixed, preferred_element_type=f32)
    d_value = d_value.astype(bf16).reshape(micro * seq_len, width_all)
    d_scores = (probs * (d_probs - jnp.sum(probs * d_probs, axis=-1, keepdims=True))).astype(bf16)
    d_scores, up_rows, down_rows = lax.optimization_barrier((d_scores, up_rows, down_rows))
    up_rows, down_rows = next_sum(up_rows, down_rows)
    d_query = scale_factor * jnp.einsum("shqk,skhd->sqhd", d_scores, key_rows, preferred_element_type=f32)
    d_key = scale_factor * jnp.einsum("shqk,sqhd->skhd", d_scores, queries, preferred_element_type=f32)
    d_query = unrotate(d_query, cosine_table, sine_table).astype(bf16).reshape(micro * seq_len, width_all)
    d_key = unrotate(d_key, cosine_table, sine_table).astype(bf16).reshape(micro * seq_len, width_all)
    grad_wq = t_dot(normalized_input, d_query).astype(bf16)
    grad_wk = t_dot(normalized_input, d_key).astype(bf16)
    grad_wv = t_dot(normalized_input, d_value).astype(bf16)
    d_in = dot_t(d_query, wq_all) + dot_t(d_key, wk_all) + dot_t(d_value, wv_all)
    d_norm_one, grad_gain_one = norm_back(d_in, plain_in, scale_in, gain_one)
    grad_tokens = (d_residual + d_norm_one).reshape(micro, 1, seq_len, width_all)

    up_rows, down_rows, grad_wv = lax.optimization_barrier((up_rows, down_rows, grad_wv))
    routed = routed_sums[:, 0] + up_rows.astype(f32) + down_rows.astype(f32)
    final_rows = residual + routed.reshape(micro * seq_len, width_all)
    output = final_rows.astype(bf16).reshape(micro, 1, seq_len, width_all)

    column = jnp.arange(small_width)[None, :]
    grad_small = t_dot(normed_mid, jnp.pad(d_logits, ((0, 0), (0, small_width - experts))))
    grad_small = jnp.where(column == experts, grad_gain_one[:, None], grad_small)
    grad_small = jnp.where(column == experts + 1, grad_gain_two[:, None], grad_small).astype(bf16)

    (g_shared, g_wo, g_wq, g_wk, g_wv, g_small) = scatter_all(
        dims,
        [grad_shared, grad_wout, grad_wq, grad_wk, grad_wv, grad_small],
        [True, False, False, False, False, False],
    )

    def joined(n):
        pieces = g_shared[:, :, n * part : (n + 1) * part]
        return pieces.transpose(1, 0, 2).reshape(own_rows, deep * part)[:, :hidden_all]

    return (
        output,
        grad_tokens,
        g_small[:, experts],
        g_small[:, experts + 1],
        g_wq,
        g_wk,
        g_wv,
        g_wo,
        g_small[:, :experts],
        joined(0),
        joined(1),
        joined(2).T,
        grad_egate[None],
        grad_eup[None],
        grad_edown[None],
    )


def solution(mesh):
    return jax.shard_map(
        on_device,
        mesh=mesh,
        in_specs=(
            P(None, ("wide", "narrow"), None, None),
            P(None, ("wide", "narrow"), None, None),
            P(None, ("wide", "narrow"), None, None),
            P(("wide", "narrow")),
            P(("wide", "narrow")),
            P(("wide", "narrow"), None),
            P(("wide", "narrow"), None),
            P(("wide", "narrow"), None),
            P(("wide", "narrow"), None),
            P(("wide", "narrow"), None),
            P(("wide", "narrow"), None),
            P(("wide", "narrow"), None),
            P(None, ("wide", "narrow")),
            P("wide", None, "narrow"),
            P("wide", None, "narrow"),
            P("wide", "narrow", None),
        ),
        out_specs=(
            P(None, ("wide", "narrow"), None, None),
            P(None, ("wide", "narrow"), None, None),
            P(("wide", "narrow")),
            P(("wide", "narrow")),
            P(("wide", "narrow"), None),
            P(("wide", "narrow"), None),
            P(("wide", "narrow"), None),
            P(("wide", "narrow"), None),
            P(("wide", "narrow"), None),
            P(("wide", "narrow"), None),
            P(("wide", "narrow"), None),
            P(None, ("wide", "narrow")),
            P("wide", None, "narrow"),
            P("wide", None, "narrow"),
            P("wide", "narrow", None),
        ),
        check_vma=False,
    )
```

```python
import functools
import jax
import jax.numpy as jnp
from jax import lax
from jax.experimental import pallas as pl
from jax.experimental.pallas import tpu as pltpu
from jax.sharding import PartitionSpec as P

MESH = pl.DeviceIdType.MESH
HD = 128


epsilon = 1e-06


def angles(seq_len, head_size):
    position = jnp.arange(seq_len).astype(jnp.float32)
    exponent = jnp.arange(head_size // 2).astype(jnp.float32) * (2.0 / head_size)
    frequency = jnp.exp(-jnp.log(10000.0) * exponent)
    theta = position[:, None] * frequency[None, :]
    return (jnp.cos(theta)[:, None, :], jnp.sin(theta)[:, None, :])


def rotate(vectors, cosine_table, sine_table):
    middle = vectors.shape[-1] // 2
    first_half = vectors[..., :middle]
    second_half = vectors[..., middle:]
    return jnp.concatenate(
        [
            first_half * cosine_table - second_half * sine_table,
            second_half * cosine_table + first_half * sine_table,
        ],
        axis=-1,
    )


def unrotate(vectors, cosine_table, sine_table):
    middle = vectors.shape[-1] // 2
    first_half = vectors[..., :middle]
    second_half = vectors[..., middle:]
    return jnp.concatenate(
        [
            first_half * cosine_table + second_half * sine_table,
            second_half * cosine_table - first_half * sine_table,
        ],
        axis=-1,
    )


def norm_ahead(matrix, gain):
    scale_rows = lax.rsqrt(jnp.mean(matrix * matrix, axis=-1, keepdims=True) + epsilon)
    normed = matrix * scale_rows
    return ((normed * gain).astype(jnp.bfloat16), normed, scale_rows)


def norm_back(grad_rows, normed, scale_rows, gain):
    gain_grad = jnp.sum(grad_rows * normed, axis=0)
    inner = grad_rows * gain
    return (
        scale_rows * (inner - normed * jnp.mean(inner * normed, axis=-1, keepdims=True)),
        gain_grad,
    )


def silu_pair(pre_act):
    sigma = jax.nn.sigmoid(pre_act)
    return (pre_act * sigma, sigma * (1.0 + pre_act * (1.0 - sigma)))


def chip_grid(chips):
    deep = 4 if chips % 4 == 0 else 1
    rest = chips // deep
    high = max(d for d in range(1, rest + 1) if rest % d == 0 and d * d <= rest)
    return (deep, high, rest // high)

def place(dims):
    wide = lax.axis_index("wide")
    return wide // (dims[1] * dims[2]), (wide // dims[2]) % dims[1], wide % dims[2]

def greet(dims, a, b, c, core):
    deep, high, broad = dims
    barrier = pltpu.get_barrier_semaphore()
    def chip(i, j, k):
        return (i * high + j) * broad + k
    others = [(chip((a + r) % deep, b, c), core) for r in range(1, deep)]
    others += [(chip(a, (b + r) % high, c), core) for r in range(1, high)]
    others += [(chip(a, b, (c + r) % broad), core) for r in range(1, broad)]
    others += [(chip(a, b, c), 1 - core)]
    for other in others:
        pl.semaphore_signal(barrier, inc=1, device_id=other, device_id_type=MESH)
    pl.semaphore_wait(barrier, len(others))

def near_first(dims, a):
    deep = dims[0]
    if deep != 4:
        return list(range(deep))
    one = 1 + 2 * (1 - 2 * a // deep)
    inner = (a + 1) // 2 % 2
    other = deep - one
    return [0, one, 2 + inner * (other - 2), other + inner * (2 - other)]


def pass_on(deep, a, k, up, down, act):
    if isinstance(k, int) and k == 0:
        pl.when(a + 1 < deep)(lambda: act(up(k)))
        pl.when(a >= 1)(lambda: act(down(k)))
    else:
        pl.when((k <= a) & (a + 1 < deep))(lambda: act(up(k)))
        pl.when((k > a) & (a >= 1))(lambda: act(down(k)))


def cut_columns(widths):
    pieces = []
    for n, width in enumerate(widths):
        tiles = width // 128
        middle = (tiles + 1) // 2 * 128
        pieces += [(n, 0, width)] if tiles < 6 else [(n, 0, middle), (n, middle, width)]
    return pieces


def gather_kernel(dims, arrays, beside, pieces, sliced, *refs):
    deep, high, broad = dims
    count, ahead = len(pieces), 12
    first_out = arrays + beside
    rows_refs, column_refs = refs[arrays:first_out], refs[first_out + arrays : 2 * first_out]
    ins = [refs[n].at[..., lo:hi] for n, lo, hi in pieces]
    outs = [refs[first_out + n].at[..., lo:hi] for n, lo, hi in pieces]
    sliced = [sliced[n] for n, lo, hi in pieces]
    own_sem, s1, r1, s2, r2, s3, r3, sn, rn, su, sd, rr = refs[2 * first_out :]
    a, b, c = place(dims)
    core = lax.axis_index("narrow")
    greet(dims, a, b, c, core)

    def chip(i, j, k):
        return (i * high + j) * broad + k

    def send(src, dst, ss, rs, to):
        copy = pltpu.make_async_remote_copy(
            src_ref=src, dst_ref=dst, send_sem=ss, recv_sem=rs, device_id=to, device_id_type=MESH
        )
        return copy

    def program(me):
        first, second = (high, broad) if me == 0 else (broad, high)

        def at2(i, r):
            if me == 0:
                return outs[i].at[:, (b - r + high) % high, c, me]
            return outs[i].at[:, b, (c - r + broad) % broad, me]

        def at3(i, r):
            if me == 0:
                return outs[i].at[:, :, (c - r + broad) % broad, me]
            return outs[i].at[:, (b - r + high) % high, :, me]

        def to2(r):
            return (chip(a, (b + r) % high, c), me) if me == 0 else (chip(a, b, (c + r) % broad), me)

        def to3(r):
            return (chip(a, b, (c + r) % broad), me) if me == 0 else (chip(a, (b + r) % high, c), me)

        mate = (chip(a, b, c), 1 - me)

        def own(i):
            return pltpu.make_async_copy(ins[i].at[a] if sliced[i] else ins[i], outs[i].at[a, b, c, me], own_sem.at[i])

        def stage1(i, r):
            h = (a + r) % deep
            src = ins[i].at[h] if sliced[i] else ins[i]
            return send(src, outs[i].at[a, b, c, me], s1.at[i, r - 1], r1.at[i, r - 1], (chip(h, b, c), me))

        def own_rows(n):
            return pltpu.make_async_copy(rows_refs[n], column_refs[n].at[:, 0], own_sem.at[count + n])

        def block(n, k):
            return rows_refs[n] if isinstance(k, int) and k == 0 else column_refs[n].at[:, k]

        def arrival(n, k):
            view = column_refs[n].at[:, k]
            return send(view, view, su.at[n, k], rr.at[n, k], (chip(a, b, c), 1 - me))

        def relay(n, k, act):
            def up(k):
                return send(block(n, k), column_refs[n].at[:, k + 1], su.at[n, k], rr.at[n, k + 1], (chip(a + 1, b, c), me))

            def down(k):
                to = (k + deep - 1) % deep
                return send(block(n, k), column_refs[n].at[:, to], sd.at[n, k], rr.at[n, to], (chip(a - 1, b, c), me))

            pass_on(deep, a, k, up, down, act)

        order = near_first(dims, a)
        hop_steps = [min(3 + 3 * p, count + 1) for p in range(deep)]

        def stage2(i, r):
            return send(at2(i, 0), at2(i, 0), s2.at[i, r - 1], r2.at[i, r - 1], to2(r))

        def stage3(i, r):
            return send(at3(i, 0), at3(i, 0), s3.at[i, r - 1], r3.at[i, r - 1], to3(r))

        def across(i, part):
            view = at2(i, 0) if part == 0 else at2(i, part) if part < first else at3(i, part - first + 1)
            return send(view, view, sn.at[i, part], rn.at[i, part], mate)

        parts = first + second - 1
        def begin(i):
            for r in range(1, deep):
                stage1(i, r).start()
            own(i).start()

        for i in range(min(ahead, count)):
            begin(i)
        for n in range(beside):
            relay(n, 0, lambda copy: copy.start())
            own_rows(n).start()
        for step in range(count + 2):
            if step + ahead < count:
                begin(step + ahead)
            for p in range(1, deep):
                if step == hop_steps[p - 1]:
                    for n in range(beside):
                        arrival(n, order[p]).wait_recv()
                        relay(n, order[p], lambda copy: copy.start())
            i = step
            if i < count:
                own(i).wait()
                for r in range(1, deep):
                    stage1(i, r).wait_recv()
                for r in range(1, first):
                    stage2(i, r).start()
                across(i, 0).start()
            i = step - 1
            if 0 <= i < count:
                for r in range(1, first):
                    stage2(i, r).wait_recv()
                for r in range(1, second):
                    stage3(i, r).start()
                for r in range(1, first):
                    across(i, r).start()
            i = step - 2
            if 0 <= i < count:
                for r in range(1, second):
                    stage3(i, r).wait_recv()
                for r in range(1, second):
                    across(i, first + r - 1).start()
        for i in range(count):
            for r in range(1, deep):
                stage1(i, r).wait_send()
            for r in range(1, first):
                stage2(i, r).wait_send()
            for r in range(1, second):
                stage3(i, r).wait_send()
            for part in range(parts):
                across(i, part).wait()
        for n in range(beside):
            own_rows(n).wait()
            for k in order:
                relay(n, k, lambda copy: copy.wait_send())

    pl.when(core == 0)(lambda: program(0))
    pl.when(core == 1)(lambda: program(1))

def gather_all(dims, parts, sliced, rows):
    arrays, beside = len(parts), len(rows)
    deep, high, broad = dims
    pieces = cut_columns([p.shape[-1] for p in parts])
    count = len(pieces)
    sem = pltpu.SemaphoreType.DMA
    most = max(high, broad)
    shapes = [p.shape[1:] if cut else p.shape for p, cut in zip(parts, sliced)]
    vmem, anywhere = pl.BlockSpec(memory_space=pltpu.VMEM), pl.BlockSpec(memory_space=pl.ANY)
    outs = pl.pallas_call(
        functools.partial(gather_kernel, dims, arrays, beside, pieces, sliced),
        out_shape=[jax.ShapeDtypeStruct((deep, high, broad, 2) + sh, p.dtype) for p, sh in zip(parts, shapes)]
        + [jax.ShapeDtypeStruct(p.shape[:1] + (deep,) + p.shape[1:], p.dtype) for p in rows],
        in_specs=[vmem] * (arrays + beside),
        out_specs=[anywhere] * (arrays + beside),
        scratch_shapes=[sem((count + beside,))]
        + [sem((count, max(deep - 1, 1)))] * 2
        + [sem((count, max(most - 1, 1)))] * 4
        + [sem((count, high + broad - 1))] * 2
        + [sem((beside, deep))] * 3,
        compiler_params=pltpu.CompilerParams(collective_id=0, has_side_effects=True),
        name="gather_dense",
    )(*parts, *rows)
    return [o.reshape((-1, sh[-1])) for o, sh in zip(outs[:arrays], shapes)], outs[arrays:]


def scatter_kernel(dims, arrays, pieces, sliced, *refs):
    deep, high, broad = dims
    count, ahead = len(pieces), 3
    group = lambda m: [refs[m * arrays + n].at[..., lo:hi] for n, lo, hi in pieces]
    ins, outs, held, from_mate, got2, got3, got4 = [group(m) for m in range(7)]
    own_sem, sn, rn, s2, r2, s3, r3, s4, r4 = refs[7 * arrays :]
    sliced = [sliced[n] for n, lo, hi in pieces]
    a, b, c = place(dims)
    core = lax.axis_index("narrow")
    greet(dims, a, b, c, core)

    def chip(i, j, k):
        return (i * high + j) * broad + k

    def send(src, dst, ss, rs, to):
        return pltpu.make_async_remote_copy(
            src_ref=src, dst_ref=dst, send_sem=ss, recv_sem=rs, device_id=to, device_id_type=MESH
        )

    wide32 = jnp.float32

    def program(me):
        first, second = (broad, high) if me == 0 else (high, broad)
        mate = (chip(a, b, c), 1 - me)

        def own(i):
            return pltpu.make_async_copy(ins[i].at[:, :, :, me], held[i], own_sem.at[i])

        def across(i):
            return send(ins[i].at[:, :, :, 1 - me], from_mate[i], sn.at[i], rn.at[i], mate)

        def stage2(i, r):
            if me == 0:
                k = (c + r) % broad
                return send(held[i].at[:, :, k], got2[i].at[r - 1], s2.at[i, r - 1], r2.at[i, r - 1], (chip(a, b, k), me))
            j = (b + r) % high
            return send(held[i].at[:, j], got2[i].at[r - 1], s2.at[i, r - 1], r2.at[i, r - 1], (chip(a, j, c), me))

        def stage3(i, r):
            if me == 0:
                j = (b + r) % high
                return send(held[i].at[:, j, c], got3[i].at[r - 1], s3.at[i, r - 1], r3.at[i, r - 1], (chip(a, j, c), me))
            k = (c + r) % broad
            return send(held[i].at[:, b, k], got3[i].at[r - 1], s3.at[i, r - 1], r3.at[i, r - 1], (chip(a, b, k), me))

        def stage4(i, r):
            h = (a + r) % deep
            return send(held[i].at[h, b, c], got4[i].at[r - 1], s4.at[i, r - 1], r4.at[i, r - 1], (chip(h, b, c), me))

        def add_mate(i):
            for j in range(high):
                for k in range(broad):
                    @pl.loop(0, deep)
                    def _(h):
                        held[i][h, j, k] = (held[i][h, j, k].astype(wide32) + from_mate[i][h, j, k].astype(wide32)).astype(jnp.bfloat16)

        def add2(i):
            if me == 0:
                for j in range(high):
                    @pl.loop(0, deep)
                    def _(h):
                        total = held[i][h, j, c].astype(wide32)
                        for r in range(1, broad):
                            total += got2[i][r - 1, h, j].astype(wide32)
                        held[i][h, j, c] = total.astype(jnp.bfloat16)
            else:
                for k in range(broad):
                    @pl.loop(0, deep)
                    def _(h):
                        total = held[i][h, b, k].astype(wide32)
                        for r in range(1, high):
                            total += got2[i][r - 1, h, k].astype(wide32)
                        held[i][h, b, k] = total.astype(jnp.bfloat16)

        def add3(i):
            @pl.loop(0, deep)
            def _(h):
                total = held[i][h, b, c].astype(wide32)
                for r in range(1, second):
                    total += got3[i][r - 1, h].astype(wide32)
                held[i][h, b, c] = total.astype(jnp.bfloat16)

        def add4(i):
            if sliced[i]:
                outs[i][a] = held[i][a, b, c].astype(wide32)
                for r in range(1, deep):
                    outs[i][(a - r + deep) % deep] = got4[i][r - 1].astype(wide32)
                return
            total = held[i][a, b, c].astype(wide32)
            for r in range(1, deep):
                total += got4[i][r - 1].astype(wide32)
            outs[i][...] = total

        def begin(i):
            across(i).start()
            own(i).start()

        for i in range(min(ahead, count)):
            begin(i)
        for step in range(count + 3):
            if step + ahead < count:
                begin(step + ahead)
            i = step
            if i < count:
                own(i).wait()
                across(i).wait_recv()
                add_mate(i)
                for r in range(1, first):
                    stage2(i, r).start()
            i = step - 1
            if 0 <= i < count:
                for r in range(1, first):
                    stage2(i, r).wait_recv()
                add2(i)
                for r in range(1, second):
                    stage3(i, r).start()
            i = step - 2
            if 0 <= i < count:
                for r in range(1, second):
                    stage3(i, r).wait_recv()
                add3(i)
                for r in range(1, deep):
                    stage4(i, r).start()
            i = step - 3
            if 0 <= i < count:
                for r in range(1, deep):
                    stage4(i, r).wait_recv()
                add4(i)
        for i in range(count):
            across(i).wait_send()
            for r in range(1, first):
                stage2(i, r).wait_send()
            for r in range(1, second):
                stage3(i, r).wait_send()
            for r in range(1, deep):
                stage4(i, r).wait_send()

    pl.when(core == 0)(lambda: program(0))
    pl.when(core == 1)(lambda: program(1))

def scatter_all(dims, parts, sliced):
    arrays = len(parts)
    deep, high, broad = dims
    pieces = cut_columns([p.shape[-1] for p in parts])
    count = len(pieces)
    devices = deep * high * broad * 2
    blocks = [(p.shape[0] // devices, p.shape[1]) for p in parts]
    sem = pltpu.SemaphoreType.DMA
    most = max(high, broad)
    vm = lambda lead: [pltpu.VMEM(lead + blk, jnp.bfloat16) for blk in blocks]
    side = max(high, broad)
    got2 = vm((max(most - 1, 1), deep, side))
    return pl.pallas_call(
        functools.partial(scatter_kernel, dims, arrays, pieces, sliced),
        out_shape=[jax.ShapeDtypeStruct(((deep,) if cut else ()) + blk, jnp.float32) for blk, cut in zip(blocks, sliced)],
        in_specs=[pl.BlockSpec(memory_space=pl.ANY)] * arrays,
        out_specs=[pl.BlockSpec(memory_space=pltpu.VMEM)] * arrays,
        scratch_shapes=vm((deep, high, broad)) + vm((deep, high, broad)) + got2 + vm((max(most - 1, 1), deep)) + vm((max(deep - 1, 1),))
        + [sem((count,))] * 3
        + [sem((count, max(most - 1, 1)))] * 4
        + [sem((count, max(deep - 1, 1)))] * 2,
        compiler_params=pltpu.CompilerParams(collective_id=1, has_side_effects=True, vmem_limit_bytes=62 * 1024 * 1024),
        name="scatter_dense",
    )(*[p.reshape((deep, high, broad, 2) + blk) for p, blk in zip(parts, blocks)])


def greet_all(dims, a, b, c, core):
    deep, high, broad = dims
    barrier = pltpu.get_barrier_semaphore()
    others = [(((a + r) % deep * high + b) * broad + c, core) for r in range(1, deep)]
    others += [
        ((a * high + (b + q // broad) % high) * broad + (c + q % broad) % broad, core) for q in range(1, high * broad)
    ]
    others += [((a * high + b) * broad + c, 1 - core)]
    for other in others:
        pl.semaphore_signal(barrier, inc=1, device_id=other, device_id_type=MESH)
    pl.semaphore_wait(barrier, len(others))


def remote(src, dst, ss, rs, to):
    return pltpu.make_async_remote_copy(
        src_ref=src, dst_ref=dst, send_sem=ss, recv_sem=rs, device_id=to, device_id_type=MESH
    )


def dispatch_kernel(dims, micro, x_ref, choose_ref, both_ref, column_ref, got, picked, sup, sdown, rcol, spl, rpl, sm, rm, sl):
    deep, high, broad = dims
    offsets = high * broad
    a, b, c = place(dims)
    core = lax.axis_index("narrow")
    greet_all(dims, a, b, c, core)
    mate = ((a * high + b) * broad + c, 1 - core)
    rows_ref, mates_ref = both_ref.at[0], both_ref.at[1]

    def block(m, k):
        return x_ref.at[m] if isinstance(k, int) and k == 0 else got.at[m, k]

    def arrival(m, k):
        return remote(got.at[m, k], got.at[m, k], sup.at[m, k], rcol.at[m, k], mate)

    def relay(m, k, act):
        def up(k):
            to = ((a + 1) * high + b) * broad + c
            return remote(block(m, k), got.at[m, k + 1], sup.at[m, k], rcol.at[m, k + 1], (to, core))

        def down(k):
            to, there = ((a - 1) * high + b) * broad + c, (k + deep - 1) % deep
            return remote(block(m, k), got.at[m, there], sdown.at[m, k], rcol.at[m, there], (to, core))

        pass_on(deep, a, k, up, down, act)

    def plane(m, k, q):
        to = (a * high + (b + q // broad) % high) * broad + (c + q % broad) % broad
        return remote(picked.at[m, k, q], rows_ref.at[m, q, k], spl.at[m, k, q], rpl.at[m, k, q], (to, core))

    def across(m, k, part):
        if part == 0:
            return remote(picked.at[m, k, 0], mates_ref.at[m, 0, k], sm.at[m, k, 0], rm.at[m, k, 0], mate)
        return remote(rows_ref.at[m, 1:, k], mates_ref.at[m, 1:, k], sm.at[m, k, 1], rm.at[m, k, 1], mate)

    def keep(m, k):
        return pltpu.make_async_copy(picked.at[m, k, 0], rows_ref.at[m, 0, k], sl.at[m, k, 0])

    def keep_column(m, k):
        return pltpu.make_async_copy(block(m, k), column_ref.at[m, k], sl.at[m, k, 1])

    order = [(m, k) for k in near_first(dims, a) for m in range(micro)]
    for m in range(micro):
        relay(m, 0, lambda copy: copy.start())
    for n, (m, k) in enumerate(order):
        if n >= micro:
            arrival(m, k).wait_recv()
            relay(m, k, lambda copy: copy.start())
        keep_column(m, k).start()
        piece = block(m, k)[...]
        chosen = jnp.dot(choose_ref[m, k], piece, preferred_element_type=jnp.float32).astype(jnp.bfloat16)
        picked[m, k] = chosen.reshape(picked.shape[2:])
        for q in range(1, offsets):
            plane(m, k, q).start()
        keep(m, k).start()
        across(m, k, 0).start()
    for m, k in order:
        for q in range(1, offsets):
            plane(m, k, q).wait_recv()
        across(m, k, 1).start()
    for m, k in order:
        relay(m, k, lambda copy: copy.wait_send())
        keep_column(m, k).wait()
        for q in range(1, offsets):
            plane(m, k, q).wait_send()
        keep(m, k).wait()
        across(m, k, 0).wait()
        across(m, k, 1).wait()


def dispatch(dims, x, choose):
    deep, high, broad = dims
    micro, tokens, width = x.shape
    offsets = high * broad
    slots = choose.shape[2] // offsets
    sem = pltpu.SemaphoreType.DMA
    anywhere, vmem = pl.BlockSpec(memory_space=pl.ANY), pl.BlockSpec(memory_space=pltpu.VMEM)
    out = jax.ShapeDtypeStruct((2, micro, offsets, deep, slots, width), x.dtype)
    return pl.pallas_call(
        functools.partial(dispatch_kernel, dims, micro),
        out_shape=[out, jax.ShapeDtypeStruct((micro, deep, tokens, width), x.dtype)],
        in_specs=[vmem, vmem],
        out_specs=[anywhere] * 2,
        scratch_shapes=[
            pltpu.VMEM((micro, deep, tokens, width), x.dtype),
            pltpu.VMEM((micro, deep, offsets, slots, width), x.dtype),
        ]
        + [sem((micro, deep))] * 3
        + [sem((micro, deep, offsets))] * 2
        + [sem((micro, deep, 2))] * 3,
        compiler_params=pltpu.CompilerParams(collective_id=2, has_side_effects=True),
        name="dispatch_rows",
    )(x, choose)


def return_kernel(dims, micro, both_ref, choose_ref, near_ref, total_ref, held, mated, back, up, got, sl, sm, rm, spl, rpl, scol, rcol):
    deep, high, broad = dims
    offsets = high * broad
    a, b, c = place(dims)
    core = lax.axis_index("narrow")
    greet_all(dims, a, b, c, core)
    mate = ((a * high + b) * broad + c, 1 - core)
    near_width = near_ref.shape[-1]
    mine_ref, theirs_ref = both_ref.at[0], both_ref.at[1]

    def load(m, k):
        return pltpu.make_async_copy(mine_ref.at[m, :, k], held.at[m, :, k], sl.at[m, k])

    def across(m, k):
        return remote(theirs_ref.at[m, :, k], mated.at[m, :, k], sm.at[m, k], rm.at[m, k], mate)

    def plane(m, k, q):
        to = (a * high + (b - q // broad + high) % high) * broad + (c - q % broad + broad) % broad
        return remote(held.at[m, q, k], back.at[m, k, q], spl.at[m, k, q], rpl.at[m, k, q], (to, core))

    def column(m, k):
        return remote(up.at[m, k], got.at[m, k], scol.at[m, k], rcol.at[m, k], (((a - k + deep) % deep * high + b) * broad + c, core))

    order = [(m, k) for m in range(micro) for k in list(range(1, deep)) + [0]]
    ahead = 3
    for m, k in order[:ahead]:
        across(m, k).start()
        load(m, k).start()
    for n, (m, k) in enumerate(order):
        for later in order[n + ahead : n + ahead + 1]:
            across(*later).start()
            load(*later).start()
        load(m, k).wait()
        across(m, k).wait_recv()
        for q in range(1, offsets):
            held[m, q, k] = (held[m, q, k].astype(jnp.float32) + mated[m, q, k].astype(jnp.float32)).astype(jnp.bfloat16)
            plane(m, k, q).start()
        back[m, k, 0] = (held[m, 0, k].astype(jnp.float32) + mated[m, 0, k].astype(jnp.float32)).astype(jnp.bfloat16)
    for m, k in order:
        for q in range(1, offsets):
            plane(m, k, q).wait_recv()
        rows = back[m, k].reshape((-1, back.shape[-1]))
        sums = jnp.dot(choose_ref[m, k], rows, preferred_element_type=jnp.float32)
        dense = sums[:, :near_width] + near_ref[m, k].astype(jnp.float32)
        if k == 0:
            total_ref[m, :, :near_width] = dense
            if near_width < sums.shape[1]:
                total_ref[m, :, near_width:] = sums[:, near_width:]
        else:
            up[m, k, :, :near_width] = dense.astype(jnp.bfloat16)
            if near_width < sums.shape[1]:
                up[m, k, :, near_width:] = sums[:, near_width:].astype(jnp.bfloat16)
            column(m, k).start()
    for m in range(micro):
        for k in range(1, deep):
            column(m, k).wait_recv()
            total_ref[m] += got[m, k].astype(jnp.float32)
    for m, k in order:
        across(m, k).wait_send()
        for q in range(1, offsets):
            plane(m, k, q).wait_send()
        if k > 0:
            column(m, k).wait_send()


def give_back(dims, both, choose_t, near):
    deep, high, broad = dims
    _, micro, offsets, _, slots, width = both.shape
    tokens = choose_t.shape[2]
    sem = pltpu.SemaphoreType.DMA
    anywhere, vmem = pl.BlockSpec(memory_space=pl.ANY), pl.BlockSpec(memory_space=pltpu.VMEM)
    scratch = lambda *shape: pltpu.VMEM(shape, both.dtype)
    return pl.pallas_call(
        functools.partial(return_kernel, dims, micro),
        out_shape=jax.ShapeDtypeStruct((micro, tokens, width), jnp.float32),
        in_specs=[anywhere, vmem, vmem],
        out_specs=vmem,
        scratch_shapes=[
            scratch(micro, offsets, deep, slots, width),
            scratch(micro, offsets, deep, slots, width),
            scratch(micro, deep, offsets, slots, width),
            scratch(micro, deep, tokens, width),
            scratch(micro, deep, tokens, width),
        ]
        + [sem((micro, deep))] * 3
        + [sem((micro, deep, offsets))] * 2
        + [sem((micro, deep))] * 2,
        compiler_params=pltpu.CompilerParams(collective_id=3, has_side_effects=True, vmem_limit_bytes=62 * 1024 * 1024),
        name="return_rows",
    )(both, choose_t, near)


class Line:
    def __init__(self, dims):
        deep, plane = dims[0], dims[1] * dims[2]
        self.up = lambda far: [(i * plane + p, (i + far) * plane + p) for i in range(deep - far) for p in range(plane)]

    def both_ways(self, one, two, far=1):
        up = self.up(far)
        return lax.ppermute(one, "wide", up), lax.ppermute(two, "wide", [(b, a) for a, b in up])


def plane_pairs(dims, offset, sign):
    deep, high, broad = dims
    up, over = (offset // broad) * sign, (offset % broad) * sign
    return [
        ((i * high + j) * broad + k, (i * high + (j + up) % high) * broad + (k + over) % broad)
        for i in range(deep)
        for j in range(high)
        for k in range(broad)
    ]


def swap_cores(rows):
    return lax.ppermute(rows, "narrow", [(0, 1), (1, 0)])


def plane_rows(dims, picked):
    return [picked[0]] + [lax.ppermute(picked[q], "wide", plane_pairs(dims, q, 1)) for q in range(1, picked.shape[0])]


def plane_back(dims, rows):
    offsets = rows.shape[1]
    return [rows[:, 0]] + [lax.ppermute(rows[:, q], "wide", plane_pairs(dims, q, -1)) for q in range(1, offsets)]


def column_sums(dims, choose, back, near):
    sums = jnp.einsum("mkst,mksd->mktd", choose, back, preferred_element_type=jnp.float32)
    return sums + near.astype(jnp.float32)


def masked_gates(logits, named):
    top = jnp.max(jnp.where(named > 0, logits, -1e30), axis=-1, keepdims=True)
    weights = jnp.where(named > 0, jnp.exp(logits - top), 0.0)
    return weights / jnp.maximum(jnp.sum(weights, axis=-1, keepdims=True), 0.5)


def f32_dot(one, two):
    return jnp.dot(one, two, preferred_element_type=jnp.float32)


def dot_t(one, two):
    return lax.dot_general(one, two, (((1,), (1,)), ((), ())), preferred_element_type=jnp.float32)


def t_dot(one, two):
    return lax.dot_general(one, two, (((0,), (0,)), ((), ())), preferred_element_type=jnp.float32)


def own_gate(x, router, names, pick):
    row_gates = masked_gates(f32_dot(x, router), names.astype(jnp.float32))
    return jnp.sum(row_gates * pick[:, : row_gates.shape[1]], axis=-1, keepdims=True)


def expert_forward_kernel(width, half, x_ref, router_ref, pick_ref, gate_w, up_w, down_w, mine_ref, theirs_ref, g_ref, u_ref):
    x, names = x_ref[:, :width], x_ref[:, width:]
    gate = own_gate(x, router_ref[...], names, pick_ref[0:1])
    g = f32_dot(x, gate_w[...])
    u = f32_dot(x, up_w[...])
    g_ref[...] = g
    u_ref[...] = u
    act, _ = silu_pair(g)
    out = f32_dot((gate * (act * u)).astype(jnp.bfloat16), down_w[...]).astype(jnp.bfloat16)

    @pl.when(pl.program_id(0) < half)
    def _():
        mine_ref[...] = out

    @pl.when(pl.program_id(0) >= half)
    def _():
        theirs_ref[...] = out


def expert_backward_kernel(
    half, width, x_ref, d_ref, mate_d_ref, router_ref, pick_ref, gate_w, up_w, down_w, g_ref, u_ref, in_ref, dg_ref, du_ref, dd_ref
):
    step = pl.program_id(0)
    x, names = x_ref[:, :width], x_ref[:, width:]
    dy = jnp.where(step < half, d_ref[...], mate_d_ref[...])
    gate = own_gate(x, router_ref[...], names, pick_ref[0:1])
    act, slope = silu_pair(g_ref[...])
    u = u_ref[...]
    d_plain = dot_t(dy, down_w[...])
    hidden = act * u
    d_gate = jnp.sum(hidden * d_plain, axis=-1, keepdims=True)
    weighed = (gate * hidden).astype(jnp.bfloat16)
    d_hidden = gate * d_plain
    d_act = (d_hidden * u * slope).astype(jnp.bfloat16)
    d_up = (d_hidden * act).astype(jnp.bfloat16)
    rows = dot_t(d_act, gate_w[...]) + dot_t(d_up, up_w[...])
    in_ref[:, :width] = rows.astype(jnp.bfloat16)
    coarse = d_gate.astype(jnp.bfloat16).astype(jnp.float32)
    beside = coarse * pick_ref[1:2] + (d_gate - coarse) * pick_ref[2:3]
    in_ref[:, width:] = beside.astype(jnp.bfloat16)

    @pl.when(step == 0)
    def _():
        dg_ref[...] = jnp.zeros_like(dg_ref)
        du_ref[...] = jnp.zeros_like(du_ref)
        dd_ref[...] = jnp.zeros_like(dd_ref)

    dg_ref[...] += t_dot(x, d_act)
    du_ref[...] += t_dot(x, d_up)
    dd_ref[...] += t_dot(weighed, dy)


def fixed(shape):
    return pl.BlockSpec(shape, lambda i: (0,) * len(shape), pipeline_mode=pl.Buffered(1))


def row_block(total):
    return max(n for n in (512, 256, 128, 64, 32, 16) if total % n == 0)


def roomy():
    return pltpu.CompilerParams(vmem_limit_bytes=60 * 1024 * 1024)


def cost(flops, moved):
    return pl.CostEstimate(flops=flops, bytes_accessed=moved, transcendentals=0)


def expert_forward(x, router, picks, gate_w, up_w, down_w):
    rows, (width, hidden) = x.shape[0], gate_w.shape
    block = row_block(rows // 2)
    half = rows // 2 // block
    by_row = lambda w: pl.BlockSpec((block, w), lambda i: (i, 0))
    return pl.pallas_call(
        functools.partial(expert_forward_kernel, width, half),
        grid=(rows // block,),
        out_shape=[
            jax.ShapeDtypeStruct((rows // 2, width), jnp.bfloat16),
            jax.ShapeDtypeStruct((rows // 2, width), jnp.bfloat16),
            jax.ShapeDtypeStruct((rows, hidden), jnp.float32),
            jax.ShapeDtypeStruct((rows, hidden), jnp.float32),
        ],
        in_specs=[by_row(x.shape[1]), fixed(router.shape), fixed(picks.shape)] + [fixed(w.shape) for w in (gate_w, up_w, down_w)],
        out_specs=[
            pl.BlockSpec((block, width), lambda i: (jnp.minimum(i, half - 1), 0)),
            pl.BlockSpec((block, width), lambda i: (jnp.maximum(i - half, 0), 0)),
            by_row(hidden),
            by_row(hidden),
        ],
        compiler_params=roomy(),
        cost_estimate=cost(6 * rows * width * hidden, rows * (4 * width + 8 * hidden)),
        name="expert_forward",
    )(x, router, picks, gate_w, up_w, down_w)


def expert_backward(x, d_mine, d_mates, router, picks, gate_w, up_w, down_w, g, u):
    rows, (width, hidden) = x.shape[0], gate_w.shape
    block = row_block(d_mine.shape[0])
    half = d_mine.shape[0] // block
    by_row = lambda w: pl.BlockSpec((block, w), lambda i: (i, 0))
    first = pl.BlockSpec((block, width), lambda i: (jnp.minimum(i, half - 1), 0))
    second = pl.BlockSpec((block, width), lambda i: (jnp.maximum(i - half, 0), 0))
    wide_in = width + picks.shape[1]
    return pl.pallas_call(
        functools.partial(expert_backward_kernel, half, width),
        grid=(2 * half,),
        out_shape=[jax.ShapeDtypeStruct((rows, wide_in), jnp.bfloat16)]
        + [jax.ShapeDtypeStruct(w.shape, jnp.float32) for w in (gate_w, up_w, down_w)],
        in_specs=[by_row(x.shape[1]), first, second, fixed(router.shape), fixed(picks.shape)]
        + [fixed(w.shape) for w in (gate_w, up_w, down_w)]
        + [by_row(hidden), by_row(hidden)],
        out_specs=[by_row(wide_in)] + [fixed(w.shape) for w in (gate_w, up_w, down_w)],
        compiler_params=roomy(),
        cost_estimate=cost(12 * rows * width * hidden, rows * (6 * width + 8 * hidden)),
        name="expert_backward",
    )(x, d_mine, d_mates, router, picks, gate_w, up_w, down_w, g, u)


def attention_kernel(
    micro, x_ref, gains_ref, cos_ref, sin_ref, wq, wk, wv, wo, q_ref, k_ref, v_ref, p_ref, mixed_ref, in_ref, residual_ref, mid_ref
):
    rows, width = x_ref.shape
    seq = rows // micro
    in_ref[...], _, _ = norm_ahead(x_ref[...].astype(jnp.float32), gains_ref[0:1])
    heads = width // HD
    group = 2 if heads % 2 == 0 else 1
    lower = lax.broadcasted_iota(jnp.int32, (seq, seq), 0) >= lax.broadcasted_iota(jnp.int32, (seq, seq), 1)

    @pl.loop(0, heads // group)
    def _(step):
        columns = pl.ds(pl.multiple_of(step * (group * HD), group * HD), group * HD)
        normed = in_ref[...]

        def turned(weights):
            raw = f32_dot(normed, weights[:, columns])
            parts = [raw[:, j * HD : (j + 1) * HD] for j in range(group)]
            parts = [p * cos_ref[...] + pltpu.roll(p, HD // 2, 1) * sin_ref[...] for p in parts]
            return jnp.concatenate(parts, axis=1).astype(jnp.bfloat16)

        q, k = turned(wq), turned(wk)
        v = f32_dot(normed, wv[:, columns]).astype(jnp.bfloat16)
        q_ref[:, columns], k_ref[:, columns], v_ref[:, columns] = q, k, v
        every = []
        for m in range(micro):
            side = []
            for j in range(group):
                one = lambda a: a[m * seq : (m + 1) * seq, j * HD : (j + 1) * HD]
                scores = HD ** (-0.5) * dot_t(one(q), one(k))
                scores = jnp.where(lower, scores, -1e30)
                weights = jnp.exp(scores - jnp.max(scores, axis=-1, keepdims=True))
                probs = weights / jnp.sum(weights, axis=-1, keepdims=True)
                p_ref[m, step * group + j] = probs
                side.append(f32_dot(probs.astype(jnp.bfloat16), one(v)))
            every.append(jnp.concatenate(side, axis=1))
        mixed_ref[:, columns] = jnp.concatenate(every, axis=0).astype(jnp.bfloat16)

    @pl.loop(0, heads // group)
    def _(step):
        columns = pl.ds(pl.multiple_of(step * (group * HD), group * HD), group * HD)
        residual_ref[:, columns] = x_ref[:, columns].astype(jnp.float32) + f32_dot(mixed_ref[...], wo[:, columns])

    mid_ref[...], _, _ = norm_ahead(residual_ref[...], gains_ref[1:2])


def attention_forward(micro, x, gains, cos, sin, wq, wk, wv, wo):
    rows, width = x.shape
    seq = rows // micro
    like = lambda kind: jax.ShapeDtypeStruct((rows, width), kind)
    return pl.pallas_call(
        functools.partial(attention_kernel, micro),
        out_shape=[like(jnp.bfloat16)] * 3
        + [jax.ShapeDtypeStruct((micro, width // HD, seq, seq), jnp.float32)]
        + [like(jnp.bfloat16)] * 2
        + [like(jnp.float32), like(jnp.bfloat16)],
        compiler_params=roomy(),
        cost_estimate=cost(32 * rows * width * width, 10 * width * width),
        name="attention_forward",
    )(x, gains, cos, sin, wq, wk, wv, wo)


def shared_kernel(width, part, x_ref, d_ref, w_ref, out_ref, in_ref, grad_ref):
    x, dy = x_ref[:, :width], d_ref[...]
    gate_w, up_w, down_t = w_ref[:, :part], w_ref[:, part : 2 * part], w_ref[:, 2 * part :]
    act, slope = silu_pair(f32_dot(x, gate_w))
    u = f32_dot(x, up_w)
    hidden = (act * u).astype(jnp.bfloat16)
    out_ref[...] = dot_t(hidden, down_t).astype(jnp.bfloat16)
    d_hidden = f32_dot(dy, down_t)
    d_gate = (d_hidden * u * slope).astype(jnp.bfloat16)
    d_up = (d_hidden * act).astype(jnp.bfloat16)
    in_ref[...] = (dot_t(d_gate, gate_w) + dot_t(d_up, up_w)).astype(jnp.bfloat16)

    @pl.when(pl.program_id(0) == 0)
    def _():
        grad_ref[...] = jnp.zeros_like(grad_ref)

    grad_ref[:, :part] += t_dot(x, d_gate)
    grad_ref[:, part : 2 * part] += t_dot(x, d_up)
    grad_ref[:, 2 * part :] += t_dot(dy, hidden)


def shared_expert(x, d, weights):
    rows, width = d.shape
    part = weights.shape[1] // 3
    block = row_block(rows)
    by_row = lambda w: pl.BlockSpec((block, w), lambda i: (i, 0))
    return pl.pallas_call(
        functools.partial(shared_kernel, width, part),
        grid=(rows // block,),
        out_shape=[jax.ShapeDtypeStruct((rows, width), jnp.bfloat16)] * 2 + [jax.ShapeDtypeStruct(weights.shape, jnp.float32)],
        in_specs=[by_row(x.shape[1]), by_row(width), fixed(weights.shape)],
        out_specs=[by_row(width)] * 2 + [fixed(weights.shape)],
        compiler_params=roomy(),
        cost_estimate=cost(18 * rows * width * part, rows * 8 * width),
        name="shared_expert",
    )(x, d, weights)


def on_device(
    tokens,
    cotangent,
    routes,
    gain_attn,
    gain_moe,
    w_query,
    w_key,
    w_value,
    attention_output_weight,
    router,
    shared_gate,
    shared_up,
    shared_down,
    routed_gate_weight,
    routed_up_weight,
    routed_down_weight,
):
    f32, bf16 = jnp.float32, jnp.bfloat16
    micro = tokens.shape[0]
    seq_len, width_all = tokens.shape[2], tokens.shape[3]
    chosen_count = routes.shape[3]
    experts = router.shape[1]
    heads = width_all // HD
    dims = chip_grid(lax.axis_size("wide"))
    deep, high, broad = dims
    slots = 9 * seq_len * chosen_count // (8 * experts) + 1
    extra = -(-experts // 128) * 128
    extra_back = -(-4 * experts // 128) * 128
    cosine_table, sine_table = angles(seq_len, HD)
    scale_factor = HD ** (-0.5)
    causal_mask = jnp.arange(seq_len)[:, None] >= jnp.arange(seq_len)[None, :]
    me = lax.axis_index("wide")
    own_rows = gain_attn.shape[0]

    named = jnp.any(routes[:, 0, :, :, None] == jnp.arange(experts), axis=2)
    named_wide = jnp.pad(named.astype(bf16), ((0, 0), (0, 0), (0, extra - experts)))

    small_width = -(-(experts + 2) // 128) * 128
    small = jnp.concatenate(
        [router, gain_attn[:, None], gain_moe[:, None], jnp.zeros((own_rows, small_width - experts - 2), bf16)], axis=1
    )
    hidden_all = shared_gate.shape[1]
    part = -(-hidden_all // (deep * 128)) * 128

    def cut(matrix):
        return jnp.pad(matrix, ((0, 0), (0, part * deep - hidden_all))).reshape(own_rows, deep, part).transpose(1, 0, 2)

    shared = jnp.concatenate([cut(shared_gate), cut(shared_up), cut(shared_down.T)], axis=2)
    (small_all, wq_all, wk_all, wv_all, wo_all, shared_all), (d_column, names_column) = gather_all(
        dims,
        [small, w_query, w_key, w_value, attention_output_weight, shared],
        [False, False, False, False, False, True],
        [cotangent[:, 0], named_wide],
    )
    line = Line(dims)
    router_all = small_all[:, :experts]
    gain_one = small_all[:, experts].astype(f32)
    gain_two = small_all[:, experts + 1].astype(f32)

    chip_a, chip_b, chip_c = place(dims)
    offsets = high * broad
    step = jnp.arange(offsets)
    targets = (chip_a * high + (chip_b + step // broad) % high) * broad + (chip_c + step % broad) % broad
    is_target = (jnp.arange(experts)[:, None] == targets[None, :]).astype(bf16)
    earlier = (jnp.arange(seq_len)[:, None] > jnp.arange(seq_len)[None, :]).astype(bf16)
    names = names_column[..., :experts]
    aimed = jnp.einsum("mkte,eq->mkqt", names, is_target, preferred_element_type=f32)
    slot = jnp.einsum("mkqu,tu->mkqt", aimed.astype(bf16), earlier, preferred_element_type=f32)
    hit = (slot[:, :, :, None, :] == jnp.arange(slots, dtype=f32)[:, None]) & (aimed[:, :, :, None, :] > 0.5)
    choose = hit.astype(bf16).reshape(micro, deep, offsets * slots, seq_len)
    choose_t = choose.transpose(0, 1, 3, 2)

    rows_low = tokens[:, 0].reshape(micro * seq_len, width_all)
    rows_in = rows_low.astype(f32)
    cos_row, sin_row = cosine_table[:, 0], sine_table[:, 0]
    queries, key_rows, value_rows, probs, mixed, normalized_input, residual, normed_mid = attention_forward(
        micro,
        rows_low,
        jnp.stack([gain_one, gain_two]),
        jnp.tile(jnp.concatenate([cos_row, cos_row], axis=1), (micro, 1)),
        jnp.tile(jnp.concatenate([-sin_row, sin_row], axis=1), (micro, 1)),
        wq_all,
        wk_all,
        wv_all,
        wo_all,
    )
    queries, key_rows, value_rows = (a.reshape(micro, seq_len, heads, HD) for a in (queries, key_rows, value_rows))
    probs_low = probs.astype(bf16)
    _, plain_in, scale_in = norm_ahead(rows_in, gain_one)
    _, plain_mid, scale_mid = norm_ahead(residual, gain_two)

    d_picked_rows = jnp.einsum("mkqst,mktd->qmksd", hit.astype(bf16), d_column, preferred_element_type=f32).astype(bf16)

    x_ext = jnp.concatenate([normed_mid.reshape(micro, seq_len, width_all), named_wide], axis=-1)
    x_both, x_column = dispatch(dims, x_ext, choose)
    x_both, d_picked_rows = lax.optimization_barrier((x_both, d_picked_rows))
    d_pieces = plane_rows(dims, d_picked_rows)
    x_rows = x_both.reshape(-1, width_all + extra)

    shared_out, d_shared_in, grad_shared = shared_expert(
        x_column.reshape(-1, width_all + extra), d_column.reshape(-1, width_all), shared_all
    )
    grad_shared = grad_shared.astype(bf16)
    x_rows, shared_out = lax.optimization_barrier((x_rows, shared_out))

    gate_w, up_w, down_w = routed_gate_weight[0], routed_up_weight[0], routed_down_weight[0]
    side = 2 * experts * lax.axis_index("narrow")
    places = jnp.stack([me, me + side, me + side + experts])
    picks = (jnp.arange(extra_back)[None, :] == places[:, None]).astype(f32)
    router_wide = jnp.pad(router_all, ((0, 0), (0, extra - experts)))
    expert_args = (router_wide, picks, gate_w, up_w, down_w)
    out_mine, out_theirs, g_part, u_part = expert_forward(x_rows, *expert_args)
    d_pieces, out_mine, out_theirs = lax.optimization_barrier((d_pieces, out_mine, out_theirs))
    theirs = swap_cores(out_theirs)
    d_mine = jnp.stack(d_pieces, axis=1).reshape(-1, width_all)
    d_mates = swap_cores(d_mine)
    routed_rows = (out_mine.astype(f32) + theirs.astype(f32)).astype(bf16)
    routed_rows = routed_rows.reshape(micro, offsets, deep, slots, width_all)

    x_late, routed_rows = lax.optimization_barrier((x_rows, routed_rows))
    routed_pieces = plane_back(dims, routed_rows)
    d_in_rows, grad_egate, grad_eup, grad_edown = expert_backward(x_late, d_mine, d_mates, *expert_args, g_part, u_part)
    routed_pieces, d_in_rows = lax.optimization_barrier((routed_pieces, d_in_rows))
    routed_back = jnp.stack(routed_pieces, axis=2).reshape(micro, deep, offsets * slots, width_all)
    routed_sums = column_sums(dims, choose, routed_back, shared_out.reshape(d_column.shape))
    routed_sums, d_in_rows = lax.optimization_barrier((routed_sums, d_in_rows))
    up_rows, down_rows = line.both_ways(routed_sums[:, 1 % deep].astype(bf16), routed_sums[:, deep - 1].astype(bf16))
    d_total = give_back(
        dims,
        d_in_rows.reshape(2, micro, offsets, deep, slots, width_all + extra_back),
        choose_t,
        d_shared_in.reshape(d_column.shape),
    )
    d_total, up_rows, down_rows = lax.optimization_barrier((d_total, up_rows, down_rows))
    hops = [1]

    def next_sum(up_rows, down_rows):
        hops[0] += 1
        if hops[0] > deep - 1:
            return up_rows, down_rows
        up_rows = up_rows.astype(f32) + routed_sums[:, hops[0]]
        down_rows = down_rows.astype(f32) + routed_sums[:, deep - hops[0]]
        return line.both_ways(up_rows.astype(bf16), down_rows.astype(bf16))

    up_rows, down_rows = next_sum(up_rows, down_rows)
    d_total = d_total.reshape(micro * seq_len, width_all + extra_back)
    d_gates = sum(d_total[:, width_all + n * experts : width_all + (n + 1) * experts] for n in range(4))

    named_rows = named.reshape(micro * seq_len, experts)
    gates = masked_gates(f32_dot(normed_mid, router_all), named_rows)
    d_out = cotangent[:, 0].reshape(micro * seq_len, width_all).astype(f32)

    d_logits = (gates * (d_gates - jnp.sum(gates * d_gates, axis=1, keepdims=True))).astype(bf16)
    d_mid = d_total[:, :width_all] + dot_t(d_logits, router_all)
    d_norm_two, grad_gain_two = norm_back(d_mid, plain_mid, scale_mid, gain_two)
    d_residual = d_out + d_norm_two
    d_attn = d_residual.astype(bf16)
    grad_wout = t_dot(mixed, d_attn).astype(bf16)
    d_mixed = dot_t(d_attn, wo_all).astype(bf16).reshape(micro, seq_len, heads, HD)
    d_probs = jnp.einsum("sqhd,skhd->shqk", d_mixed, value_rows, preferred_element_type=f32)
    d_value = jnp.einsum("shqk,sqhd->skhd", probs_low, d_mixed, preferred_element_type=f32)
    d_value = d_value.astype(bf16).reshape(micro * seq_len, width_all)
    d_scores = (probs * (d_probs - jnp.sum(probs * d_probs, axis=-1, keepdims=True))).astype(bf16)
    d_scores, up_rows, down_rows = lax.optimization_barrier((d_scores, up_rows, down_rows))
    up_rows, down_rows = next_sum(up_rows, down_rows)
    d_query = scale_factor * jnp.einsum("shqk,skhd->sqhd", d_scores, key_rows, preferred_element_type=f32)
    d_key = scale_factor * jnp.einsum("shqk,sqhd->skhd", d_scores, queries, preferred_element_type=f32)
    d_query = unrotate(d_query, cosine_table, sine_table).astype(bf16).reshape(micro * seq_len, width_all)
    d_key = unrotate(d_key, cosine_table, sine_table).astype(bf16).reshape(micro * seq_len, width_all)
    grad_wq = t_dot(normalized_input, d_query).astype(bf16)
    grad_wk = t_dot(normalized_input, d_key).astype(bf16)
    grad_wv = t_dot(normalized_input, d_value).astype(bf16)
    d_in = dot_t(d_query, wq_all) + dot_t(d_key, wk_all) + dot_t(d_value, wv_all)
    d_norm_one, grad_gain_one = norm_back(d_in, plain_in, scale_in, gain_one)
    grad_tokens = (d_residual + d_norm_one).reshape(micro, 1, seq_len, width_all)

    up_rows, down_rows, grad_wv = lax.optimization_barrier((up_rows, down_rows, grad_wv))
    routed = routed_sums[:, 0] + up_rows.astype(f32) + down_rows.astype(f32)
    final_rows = residual + routed.reshape(micro * seq_len, width_all)
    output = final_rows.astype(bf16).reshape(micro, 1, seq_len, width_all)

    column = jnp.arange(small_width)[None, :]
    grad_small = t_dot(normed_mid, jnp.pad(d_logits, ((0, 0), (0, small_width - experts))))
    grad_small = jnp.where(column == experts, grad_gain_one[:, None], grad_small)
    grad_small = jnp.where(column == experts + 1, grad_gain_two[:, None], grad_small).astype(bf16)

    (g_shared, g_wo, g_wq, g_wk, g_wv, g_small) = scatter_all(
        dims,
        [grad_shared, grad_wout, grad_wq, grad_wk, grad_wv, grad_small],
        [True, False, False, False, False, False],
    )

    def joined(n):
        pieces = g_shared[:, :, n * part : (n + 1) * part]
        return pieces.transpose(1, 0, 2).reshape(own_rows, deep * part)[:, :hidden_all]

    return (
        output,
        grad_tokens,
        g_small[:, experts],
        g_small[:, experts + 1],
        g_wq,
        g_wk,
        g_wv,
        g_wo,
        g_small[:, :experts],
        joined(0),
        joined(1),
        joined(2).T,
        grad_egate[None],
        grad_eup[None],
        grad_edown[None],
    )


def solution(mesh):
    return jax.shard_map(
        on_device,
        mesh=mesh,
        in_specs=(
            P(None, ("wide", "narrow"), None, None),
            P(None, ("wide", "narrow"), None, None),
            P(None, ("wide", "narrow"), None, None),
            P(("wide", "narrow")),
            P(("wide", "narrow")),
            P(("wide", "narrow"), None),
            P(("wide", "narrow"), None),
            P(("wide", "narrow"), None),
            P(("wide", "narrow"), None),
            P(("wide", "narrow"), None),
            P(("wide", "narrow"), None),
            P(("wide", "narrow"), None),
            P(None, ("wide", "narrow")),
            P("wide", None, "narrow"),
            P("wide", None, "narrow"),
            P("wide", "narrow", None),
        ),
        out_specs=(
            P(None, ("wide", "narrow"), None, None),
            P(None, ("wide", "narrow"), None, None),
            P(("wide", "narrow")),
            P(("wide", "narrow")),
            P(("wide", "narrow"), None),
            P(("wide", "narrow"), None),
            P(("wide", "narrow"), None),
            P(("wide", "narrow"), None),
            P(("wide", "narrow"), None),
            P(("wide", "narrow"), None),
            P(("wide", "narrow"), None),
            P(None, ("wide", "narrow")),
            P("wide", None, "narrow"),
            P("wide", None, "narrow"),
            P("wide", "narrow", None),
        ),
        check_vma=False,
    )
```

```python
import functools
import jax
import jax.numpy as jnp
from jax import lax
from jax.experimental import pallas as pl
from jax.experimental.pallas import tpu as pltpu
from jax.sharding import PartitionSpec as P

MESH = pl.DeviceIdType.MESH
HD = 128


epsilon = 1e-06


def angles(seq_len, head_size):
    position = jnp.arange(seq_len).astype(jnp.float32)
    exponent = jnp.arange(head_size // 2).astype(jnp.float32) * (2.0 / head_size)
    frequency = jnp.exp(-jnp.log(10000.0) * exponent)
    theta = position[:, None] * frequency[None, :]
    return (jnp.cos(theta)[:, None, :], jnp.sin(theta)[:, None, :])


def rotate(vectors, cosine_table, sine_table):
    middle = vectors.shape[-1] // 2
    first_half = vectors[..., :middle]
    second_half = vectors[..., middle:]
    return jnp.concatenate(
        [
            first_half * cosine_table - second_half * sine_table,
            second_half * cosine_table + first_half * sine_table,
        ],
        axis=-1,
    )


def unrotate(vectors, cosine_table, sine_table):
    middle = vectors.shape[-1] // 2
    first_half = vectors[..., :middle]
    second_half = vectors[..., middle:]
    return jnp.concatenate(
        [
            first_half * cosine_table + second_half * sine_table,
            second_half * cosine_table - first_half * sine_table,
        ],
        axis=-1,
    )


def norm_ahead(matrix, gain):
    scale_rows = lax.rsqrt(jnp.mean(matrix * matrix, axis=-1, keepdims=True) + epsilon)
    normed = matrix * scale_rows
    return ((normed * gain).astype(jnp.bfloat16), normed, scale_rows)


def norm_back(grad_rows, normed, scale_rows, gain):
    gain_grad = jnp.sum(grad_rows * normed, axis=0)
    inner = grad_rows * gain
    return (
        scale_rows * (inner - normed * jnp.mean(inner * normed, axis=-1, keepdims=True)),
        gain_grad,
    )


def silu_pair(pre_act):
    sigma = jax.nn.sigmoid(pre_act)
    return (pre_act * sigma, sigma * (1.0 + pre_act * (1.0 - sigma)))


def chip_grid(chips):
    deep = 4 if chips % 4 == 0 else 1
    rest = chips // deep
    high = max(d for d in range(1, rest + 1) if rest % d == 0 and d * d <= rest)
    return (deep, high, rest // high)

def place(dims):
    wide = lax.axis_index("wide")
    return wide // (dims[1] * dims[2]), (wide // dims[2]) % dims[1], wide % dims[2]

def greet(dims, a, b, c, core):
    deep, high, broad = dims
    barrier = pltpu.get_barrier_semaphore()
    def chip(i, j, k):
        return (i * high + j) * broad + k
    others = [(chip((a + r) % deep, b, c), core) for r in range(1, deep)]
    others += [(chip(a, (b + r) % high, c), core) for r in range(1, high)]
    others += [(chip(a, b, (c + r) % broad), core) for r in range(1, broad)]
    others += [(chip(a, b, c), 1 - core)]
    for other in others:
        pl.semaphore_signal(barrier, inc=1, device_id=other, device_id_type=MESH)
    pl.semaphore_wait(barrier, len(others))

def near_first(dims, a):
    deep = dims[0]
    if deep != 4:
        return list(range(deep))
    one = 1 + 2 * (1 - 2 * a // deep)
    inner = (a + 1) // 2 % 2
    other = deep - one
    return [0, one, 2 + inner * (other - 2), other + inner * (2 - other)]


def pass_on(deep, a, k, up, down, act):
    if isinstance(k, int) and k == 0:
        pl.when(a + 1 < deep)(lambda: act(up(k)))
        pl.when(a >= 1)(lambda: act(down(k)))
    else:
        pl.when((k <= a) & (a + 1 < deep))(lambda: act(up(k)))
        pl.when((k > a) & (a >= 1))(lambda: act(down(k)))


def cut_columns(widths):
    pieces = []
    for n, width in enumerate(widths):
        tiles = width // 128
        middle = (tiles + 1) // 2 * 128
        pieces += [(n, 0, width)] if tiles < 6 else [(n, 0, middle), (n, middle, width)]
    return pieces


def gather_kernel(dims, arrays, pieces, sliced, *refs):
    deep, high, broad = dims
    count, ahead = len(pieces), 12
    rows_ref, column_ref = refs[arrays], refs[2 * arrays + 1]
    micro = rows_ref.shape[0]
    ins = [refs[n].at[..., lo:hi] for n, lo, hi in pieces]
    outs = [refs[arrays + 1 + n].at[..., lo:hi] for n, lo, hi in pieces]
    sliced = [sliced[n] for n, lo, hi in pieces]
    own_sem, s1, r1, s2, r2, s3, r3, sn, rn, sr, rr = refs[2 * arrays + 2 :]
    a, b, c = place(dims)
    core = lax.axis_index("narrow")
    greet(dims, a, b, c, core)

    def chip(i, j, k):
        return (i * high + j) * broad + k

    def send(src, dst, ss, rs, to):
        copy = pltpu.make_async_remote_copy(
            src_ref=src, dst_ref=dst, send_sem=ss, recv_sem=rs, device_id=to, device_id_type=MESH
        )
        return copy

    def program(me):
        first, second = (high, broad) if me == 0 else (broad, high)

        def at2(i, r):
            if me == 0:
                return outs[i].at[:, (b - r + high) % high, c, me]
            return outs[i].at[:, b, (c - r + broad) % broad, me]

        def at3(i, r):
            if me == 0:
                return outs[i].at[:, :, (c - r + broad) % broad, me]
            return outs[i].at[:, (b - r + high) % high, :, me]

        def to2(r):
            return (chip(a, (b + r) % high, c), me) if me == 0 else (chip(a, b, (c + r) % broad), me)

        def to3(r):
            return (chip(a, b, (c + r) % broad), me) if me == 0 else (chip(a, (b + r) % high, c), me)

        mate = (chip(a, b, c), 1 - me)

        def own(i):
            return pltpu.make_async_copy(ins[i].at[a] if sliced[i] else ins[i], outs[i].at[a, b, c, me], own_sem.at[i])

        def stage1(i, r):
            h = (a + r) % deep
            src = ins[i].at[h] if sliced[i] else ins[i]
            return send(src, outs[i].at[a, b, c, me], s1.at[i, r - 1], r1.at[i, r - 1], (chip(h, b, c), me))

        def own_rows():
            return pltpu.make_async_copy(rows_ref, column_ref.at[:, 0], own_sem.at[count])

        def column(m, r):
            to = (chip((a + r) % deep, b, c), me)
            return send(rows_ref.at[m], column_ref.at[m, r], sr.at[m, r - 1], rr.at[m, r - 1], to)

        def stage2(i, r):
            return send(at2(i, 0), at2(i, 0), s2.at[i, r - 1], r2.at[i, r - 1], to2(r))

        def stage3(i, r):
            return send(at3(i, 0), at3(i, 0), s3.at[i, r - 1], r3.at[i, r - 1], to3(r))

        def across(i, part):
            view = at2(i, 0) if part == 0 else at2(i, part) if part < first else at3(i, part - first + 1)
            return send(view, view, sn.at[i, part], rn.at[i, part], mate)

        parts = first + second - 1
        def begin(i):
            for r in range(1, deep):
                stage1(i, r).start()
            own(i).start()

        for i in range(min(ahead, count)):
            begin(i)
        own_rows().start()
        for step in range(count + 2):
            if step + ahead < count:
                begin(step + ahead)
            for m in range(micro):
                if step == min(2 + 2 * m, count + 1):
                    for r in range(1, deep):
                        column(m, r).start()
            i = step
            if i < count:
                own(i).wait()
                for r in range(1, deep):
                    stage1(i, r).wait_recv()
                for r in range(1, first):
                    stage2(i, r).start()
                across(i, 0).start()
            i = step - 1
            if 0 <= i < count:
                for r in range(1, first):
                    stage2(i, r).wait_recv()
                for r in range(1, second):
                    stage3(i, r).start()
                for r in range(1, first):
                    across(i, r).start()
            i = step - 2
            if 0 <= i < count:
                for r in range(1, second):
                    stage3(i, r).wait_recv()
                for r in range(1, second):
                    across(i, first + r - 1).start()
        for i in range(count):
            for r in range(1, deep):
                stage1(i, r).wait_send()
            for r in range(1, first):
                stage2(i, r).wait_send()
            for r in range(1, second):
                stage3(i, r).wait_send()
            for part in range(parts):
                across(i, part).wait()
        own_rows().wait()
        for m in range(micro):
            for r in range(1, deep):
                column(m, r).wait()

    pl.when(core == 0)(lambda: program(0))
    pl.when(core == 1)(lambda: program(1))

def gather_all(dims, parts, sliced, rows):
    arrays = len(parts)
    deep, high, broad = dims
    pieces = cut_columns([p.shape[-1] for p in parts])
    count = len(pieces)
    sem = pltpu.SemaphoreType.DMA
    most = max(high, broad)
    shapes = [p.shape[1:] if cut else p.shape for p, cut in zip(parts, sliced)]
    vmem, anywhere = pl.BlockSpec(memory_space=pltpu.VMEM), pl.BlockSpec(memory_space=pl.ANY)
    outs = pl.pallas_call(
        functools.partial(gather_kernel, dims, arrays, pieces, sliced),
        out_shape=[jax.ShapeDtypeStruct((deep, high, broad, 2) + sh, p.dtype) for p, sh in zip(parts, shapes)]
        + [jax.ShapeDtypeStruct(rows.shape[:1] + (deep,) + rows.shape[1:], rows.dtype)],
        in_specs=[vmem] * (arrays + 1),
        out_specs=[anywhere] * (arrays + 1),
        scratch_shapes=[sem((count + 1,))]
        + [sem((count, max(deep - 1, 1)))] * 2
        + [sem((count, max(most - 1, 1)))] * 4
        + [sem((count, high + broad - 1))] * 2
        + [sem((rows.shape[0], max(deep - 1, 1)))] * 2,
        compiler_params=pltpu.CompilerParams(collective_id=0, has_side_effects=True),
        name="gather_dense",
    )(*parts, rows)
    return [o.reshape((-1, sh[-1])) for o, sh in zip(outs[:-1], shapes)], outs[-1]


def scatter_kernel(dims, arrays, pieces, sliced, *refs):
    deep, high, broad = dims
    count, ahead = len(pieces), 3
    group = lambda m: [refs[m * arrays + n].at[..., lo:hi] for n, lo, hi in pieces]
    ins, outs, held, from_mate, got2, got3, got4 = [group(m) for m in range(7)]
    own_sem, sn, rn, s2, r2, s3, r3, s4, r4 = refs[7 * arrays :]
    sliced = [sliced[n] for n, lo, hi in pieces]
    a, b, c = place(dims)
    core = lax.axis_index("narrow")
    greet(dims, a, b, c, core)

    def chip(i, j, k):
        return (i * high + j) * broad + k

    def send(src, dst, ss, rs, to):
        return pltpu.make_async_remote_copy(
            src_ref=src, dst_ref=dst, send_sem=ss, recv_sem=rs, device_id=to, device_id_type=MESH
        )

    wide32 = jnp.float32

    def program(me):
        first, second = (broad, high) if me == 0 else (high, broad)
        mate = (chip(a, b, c), 1 - me)

        def own(i):
            return pltpu.make_async_copy(ins[i].at[:, :, :, me], held[i], own_sem.at[i])

        def across(i):
            return send(ins[i].at[:, :, :, 1 - me], from_mate[i], sn.at[i], rn.at[i], mate)

        def stage2(i, r):
            if me == 0:
                k = (c + r) % broad
                return send(held[i].at[:, :, k], got2[i].at[r - 1], s2.at[i, r - 1], r2.at[i, r - 1], (chip(a, b, k), me))
            j = (b + r) % high
            return send(held[i].at[:, j], got2[i].at[r - 1], s2.at[i, r - 1], r2.at[i, r - 1], (chip(a, j, c), me))

        def stage3(i, r):
            if me == 0:
                j = (b + r) % high
                return send(held[i].at[:, j, c], got3[i].at[r - 1], s3.at[i, r - 1], r3.at[i, r - 1], (chip(a, j, c), me))
            k = (c + r) % broad
            return send(held[i].at[:, b, k], got3[i].at[r - 1], s3.at[i, r - 1], r3.at[i, r - 1], (chip(a, b, k), me))

        def stage4(i, r):
            h = (a + r) % deep
            return send(held[i].at[h, b, c], got4[i].at[r - 1], s4.at[i, r - 1], r4.at[i, r - 1], (chip(h, b, c), me))

        def add_mate(i):
            for j in range(high):
                for k in range(broad):
                    @pl.loop(0, deep)
                    def _(h):
                        held[i][h, j, k] = (held[i][h, j, k].astype(wide32) + from_mate[i][h, j, k].astype(wide32)).astype(jnp.bfloat16)

        def add2(i):
            if me == 0:
                for j in range(high):
                    @pl.loop(0, deep)
                    def _(h):
                        total = held[i][h, j, c].astype(wide32)
                        for r in range(1, broad):
                            total += got2[i][r - 1, h, j].astype(wide32)
                        held[i][h, j, c] = total.astype(jnp.bfloat16)
            else:
                for k in range(broad):
                    @pl.loop(0, deep)
                    def _(h):
                        total = held[i][h, b, k].astype(wide32)
                        for r in range(1, high):
                            total += got2[i][r - 1, h, k].astype(wide32)
                        held[i][h, b, k] = total.astype(jnp.bfloat16)

        def add3(i):
            @pl.loop(0, deep)
            def _(h):
                total = held[i][h, b, c].astype(wide32)
                for r in range(1, second):
                    total += got3[i][r - 1, h].astype(wide32)
                held[i][h, b, c] = total.astype(jnp.bfloat16)

        def add4(i):
            if sliced[i]:
                outs[i][a] = held[i][a, b, c].astype(wide32)
                for r in range(1, deep):
                    outs[i][(a - r + deep) % deep] = got4[i][r - 1].astype(wide32)
                return
            total = held[i][a, b, c].astype(wide32)
            for r in range(1, deep):
                total += got4[i][r - 1].astype(wide32)
            outs[i][...] = total

        def begin(i):
            across(i).start()
            own(i).start()

        for i in range(min(ahead, count)):
            begin(i)
        for step in range(count + 3):
            if step + ahead < count:
                begin(step + ahead)
            i = step
            if i < count:
                own(i).wait()
                across(i).wait_recv()
                add_mate(i)
                for r in range(1, first):
                    stage2(i, r).start()
            i = step - 1
            if 0 <= i < count:
                for r in range(1, first):
                    stage2(i, r).wait_recv()
                add2(i)
                for r in range(1, second):
                    stage3(i, r).start()
            i = step - 2
            if 0 <= i < count:
                for r in range(1, second):
                    stage3(i, r).wait_recv()
                add3(i)
                for r in range(1, deep):
                    stage4(i, r).start()
            i = step - 3
            if 0 <= i < count:
                for r in range(1, deep):
                    stage4(i, r).wait_recv()
                add4(i)
        for i in range(count):
            across(i).wait_send()
            for r in range(1, first):
                stage2(i, r).wait_send()
            for r in range(1, second):
                stage3(i, r).wait_send()
            for r in range(1, deep):
                stage4(i, r).wait_send()

    pl.when(core == 0)(lambda: program(0))
    pl.when(core == 1)(lambda: program(1))

def scatter_all(dims, parts, sliced):
    arrays = len(parts)
    deep, high, broad = dims
    pieces = cut_columns([p.shape[-1] for p in parts])
    count = len(pieces)
    devices = deep * high * broad * 2
    blocks = [(p.shape[0] // devices, p.shape[1]) for p in parts]
    sem = pltpu.SemaphoreType.DMA
    most = max(high, broad)
    vm = lambda lead: [pltpu.VMEM(lead + blk, jnp.bfloat16) for blk in blocks]
    side = max(high, broad)
    got2 = vm((max(most - 1, 1), deep, side))
    return pl.pallas_call(
        functools.partial(scatter_kernel, dims, arrays, pieces, sliced),
        out_shape=[jax.ShapeDtypeStruct(((deep,) if cut else ()) + blk, jnp.float32) for blk, cut in zip(blocks, sliced)],
        in_specs=[pl.BlockSpec(memory_space=pl.ANY)] * arrays,
        out_specs=[pl.BlockSpec(memory_space=pltpu.VMEM)] * arrays,
        scratch_shapes=vm((deep, high, broad)) + vm((deep, high, broad)) + got2 + vm((max(most - 1, 1), deep)) + vm((max(deep - 1, 1),))
        + [sem((count,))] * 3
        + [sem((count, max(most - 1, 1)))] * 4
        + [sem((count, max(deep - 1, 1)))] * 2,
        compiler_params=pltpu.CompilerParams(collective_id=1, has_side_effects=True, vmem_limit_bytes=62 * 1024 * 1024),
        name="scatter_dense",
    )(*[p.reshape((deep, high, broad, 2) + blk) for p, blk in zip(parts, blocks)])


def greet_all(dims, a, b, c, core):
    deep, high, broad = dims
    barrier = pltpu.get_barrier_semaphore()
    others = [(((a + r) % deep * high + b) * broad + c, core) for r in range(1, deep)]
    others += [
        ((a * high + (b + q // broad) % high) * broad + (c + q % broad) % broad, core) for q in range(1, high * broad)
    ]
    others += [((a * high + b) * broad + c, 1 - core)]
    for other in others:
        pl.semaphore_signal(barrier, inc=1, device_id=other, device_id_type=MESH)
    pl.semaphore_wait(barrier, len(others))


def remote(src, dst, ss, rs, to):
    return pltpu.make_async_remote_copy(
        src_ref=src, dst_ref=dst, send_sem=ss, recv_sem=rs, device_id=to, device_id_type=MESH
    )


def dispatch_kernel(dims, micro, x_ref, choose_ref, both_ref, column_ref, got, picked, sup, sdown, rcol, spl, rpl, sm, rm, sl):
    deep, high, broad = dims
    offsets = high * broad
    a, b, c = place(dims)
    core = lax.axis_index("narrow")
    greet_all(dims, a, b, c, core)
    mate = ((a * high + b) * broad + c, 1 - core)
    rows_ref, mates_ref = both_ref.at[0], both_ref.at[1]

    def block(m, k):
        return x_ref.at[m] if isinstance(k, int) and k == 0 else got.at[m, k]

    def arrival(m, k):
        return remote(got.at[m, k], got.at[m, k], sup.at[m, k], rcol.at[m, k], mate)

    def relay(m, k, act):
        def up(k):
            to = ((a + 1) * high + b) * broad + c
            return remote(block(m, k), got.at[m, k + 1], sup.at[m, k], rcol.at[m, k + 1], (to, core))

        def down(k):
            to, there = ((a - 1) * high + b) * broad + c, (k + deep - 1) % deep
            return remote(block(m, k), got.at[m, there], sdown.at[m, k], rcol.at[m, there], (to, core))

        pass_on(deep, a, k, up, down, act)

    def plane(m, k, q):
        to = (a * high + (b + q // broad) % high) * broad + (c + q % broad) % broad
        return remote(picked.at[m, k, q], rows_ref.at[m, q, k], spl.at[m, k, q], rpl.at[m, k, q], (to, core))

    def across(m, k, part):
        if part == 0:
            return remote(picked.at[m, k, 0], mates_ref.at[m, 0, k], sm.at[m, k, 0], rm.at[m, k, 0], mate)
        return remote(rows_ref.at[m, 1:, k], mates_ref.at[m, 1:, k], sm.at[m, k, 1], rm.at[m, k, 1], mate)

    def keep(m, k):
        return pltpu.make_async_copy(picked.at[m, k, 0], rows_ref.at[m, 0, k], sl.at[m, k, 0])

    def keep_column(m, k):
        return pltpu.make_async_copy(block(m, k), column_ref.at[m, k], sl.at[m, k, 1])

    order = [(m, k) for k in near_first(dims, a) for m in range(micro)]
    for m in range(micro):
        relay(m, 0, lambda copy: copy.start())
    for n, (m, k) in enumerate(order):
        if n >= micro:
            arrival(m, k).wait_recv()
            relay(m, k, lambda copy: copy.start())
        keep_column(m, k).start()
        piece = block(m, k)[...]
        chosen = jnp.dot(choose_ref[m, k], piece, preferred_element_type=jnp.float32).astype(jnp.bfloat16)
        picked[m, k] = chosen.reshape(picked.shape[2:])
        for q in range(1, offsets):
            plane(m, k, q).start()
        keep(m, k).start()
        across(m, k, 0).start()
    for m, k in order:
        for q in range(1, offsets):
            plane(m, k, q).wait_recv()
        across(m, k, 1).start()
    for m, k in order:
        relay(m, k, lambda copy: copy.wait_send())
        keep_column(m, k).wait()
        for q in range(1, offsets):
            plane(m, k, q).wait_send()
        keep(m, k).wait()
        across(m, k, 0).wait()
        across(m, k, 1).wait()


def dispatch(dims, x, choose):
    deep, high, broad = dims
    micro, tokens, width = x.shape
    offsets = high * broad
    slots = choose.shape[2] // offsets
    sem = pltpu.SemaphoreType.DMA
    anywhere, vmem = pl.BlockSpec(memory_space=pl.ANY), pl.BlockSpec(memory_space=pltpu.VMEM)
    out = jax.ShapeDtypeStruct((2, micro, offsets, deep, slots, width), x.dtype)
    return pl.pallas_call(
        functools.partial(dispatch_kernel, dims, micro),
        out_shape=[out, jax.ShapeDtypeStruct((micro, deep, tokens, width), x.dtype)],
        in_specs=[vmem, vmem],
        out_specs=[anywhere] * 2,
        scratch_shapes=[
            pltpu.VMEM((micro, deep, tokens, width), x.dtype),
            pltpu.VMEM((micro, deep, offsets, slots, width), x.dtype),
        ]
        + [sem((micro, deep))] * 3
        + [sem((micro, deep, offsets))] * 2
        + [sem((micro, deep, 2))] * 3,
        compiler_params=pltpu.CompilerParams(collective_id=2, has_side_effects=True),
        name="dispatch_rows",
    )(x, choose)


def return_kernel(dims, micro, both_ref, choose_ref, near_ref, total_ref, held, mated, back, up, got, sl, sm, rm, spl, rpl, scol, rcol):
    deep, high, broad = dims
    offsets = high * broad
    a, b, c = place(dims)
    core = lax.axis_index("narrow")
    greet_all(dims, a, b, c, core)
    mate = ((a * high + b) * broad + c, 1 - core)
    near_width = near_ref.shape[-1]
    mine_ref, theirs_ref = both_ref.at[0], both_ref.at[1]

    def load(m, k):
        return pltpu.make_async_copy(mine_ref.at[m, :, k], held.at[m, :, k], sl.at[m, k])

    def across(m, k):
        return remote(theirs_ref.at[m, :, k], mated.at[m, :, k], sm.at[m, k], rm.at[m, k], mate)

    def plane(m, k, q):
        to = (a * high + (b - q // broad + high) % high) * broad + (c - q % broad + broad) % broad
        return remote(held.at[m, q, k], back.at[m, k, q], spl.at[m, k, q], rpl.at[m, k, q], (to, core))

    def column(m, k):
        return remote(up.at[m, k], got.at[m, k], scol.at[m, k], rcol.at[m, k], (((a - k + deep) % deep * high + b) * broad + c, core))

    order = [(m, k) for m in range(micro) for k in list(range(1, deep)) + [0]]
    ahead = 3
    for m, k in order[:ahead]:
        across(m, k).start()
        load(m, k).start()
    for n, (m, k) in enumerate(order):
        for later in order[n + ahead : n + ahead + 1]:
            across(*later).start()
            load(*later).start()
        load(m, k).wait()
        across(m, k).wait_recv()
        for q in range(1, offsets):
            held[m, q, k] = (held[m, q, k].astype(jnp.float32) + mated[m, q, k].astype(jnp.float32)).astype(jnp.bfloat16)
            plane(m, k, q).start()
        back[m, k, 0] = (held[m, 0, k].astype(jnp.float32) + mated[m, 0, k].astype(jnp.float32)).astype(jnp.bfloat16)
    for m, k in order:
        for q in range(1, offsets):
            plane(m, k, q).wait_recv()
        rows = back[m, k].reshape((-1, back.shape[-1]))
        sums = jnp.dot(choose_ref[m, k], rows, preferred_element_type=jnp.float32)
        dense = sums[:, :near_width] + near_ref[m, k].astype(jnp.float32)
        if k == 0:
            total_ref[m, :, :near_width] = dense
            if near_width < sums.shape[1]:
                total_ref[m, :, near_width:] = sums[:, near_width:]
        else:
            up[m, k, :, :near_width] = dense.astype(jnp.bfloat16)
            if near_width < sums.shape[1]:
                up[m, k, :, near_width:] = sums[:, near_width:].astype(jnp.bfloat16)
            column(m, k).start()
    for m in range(micro):
        for k in range(1, deep):
            column(m, k).wait_recv()
            total_ref[m] += got[m, k].astype(jnp.float32)
    for m, k in order:
        across(m, k).wait_send()
        for q in range(1, offsets):
            plane(m, k, q).wait_send()
        if k > 0:
            column(m, k).wait_send()


def give_back(dims, both, choose_t, near):
    deep, high, broad = dims
    _, micro, offsets, _, slots, width = both.shape
    tokens = choose_t.shape[2]
    sem = pltpu.SemaphoreType.DMA
    anywhere, vmem = pl.BlockSpec(memory_space=pl.ANY), pl.BlockSpec(memory_space=pltpu.VMEM)
    scratch = lambda *shape: pltpu.VMEM(shape, both.dtype)
    return pl.pallas_call(
        functools.partial(return_kernel, dims, micro),
        out_shape=jax.ShapeDtypeStruct((micro, tokens, width), jnp.float32),
        in_specs=[anywhere, vmem, vmem],
        out_specs=vmem,
        scratch_shapes=[
            scratch(micro, offsets, deep, slots, width),
            scratch(micro, offsets, deep, slots, width),
            scratch(micro, deep, offsets, slots, width),
            scratch(micro, deep, tokens, width),
            scratch(micro, deep, tokens, width),
        ]
        + [sem((micro, deep))] * 3
        + [sem((micro, deep, offsets))] * 2
        + [sem((micro, deep))] * 2,
        compiler_params=pltpu.CompilerParams(collective_id=3, has_side_effects=True, vmem_limit_bytes=62 * 1024 * 1024),
        name="return_rows",
    )(both, choose_t, near)


class Line:
    def __init__(self, dims):
        deep, plane = dims[0], dims[1] * dims[2]
        self.up = lambda far: [(i * plane + p, (i + far) * plane + p) for i in range(deep - far) for p in range(plane)]

    def both_ways(self, one, two, far=1):
        up = self.up(far)
        return lax.ppermute(one, "wide", up), lax.ppermute(two, "wide", [(b, a) for a, b in up])


def plane_pairs(dims, offset, sign):
    deep, high, broad = dims
    up, over = (offset // broad) * sign, (offset % broad) * sign
    return [
        ((i * high + j) * broad + k, (i * high + (j + up) % high) * broad + (k + over) % broad)
        for i in range(deep)
        for j in range(high)
        for k in range(broad)
    ]


def swap_cores(rows):
    return lax.ppermute(rows, "narrow", [(0, 1), (1, 0)])


def plane_rows(dims, picked):
    return [picked[0]] + [lax.ppermute(picked[q], "wide", plane_pairs(dims, q, 1)) for q in range(1, picked.shape[0])]


def plane_back(dims, rows):
    offsets = rows.shape[1]
    return [rows[:, 0]] + [lax.ppermute(rows[:, q], "wide", plane_pairs(dims, q, -1)) for q in range(1, offsets)]


def column_sums(dims, choose, back, near):
    sums = jnp.einsum("mkst,mksd->mktd", choose, back, preferred_element_type=jnp.float32)
    return sums + near.astype(jnp.float32)


def masked_gates(logits, named):
    top = jnp.max(jnp.where(named > 0, logits, -1e30), axis=-1, keepdims=True)
    weights = jnp.where(named > 0, jnp.exp(logits - top), 0.0)
    return weights / jnp.maximum(jnp.sum(weights, axis=-1, keepdims=True), 0.5)


def f32_dot(one, two):
    return jnp.dot(one, two, preferred_element_type=jnp.float32)


def dot_t(one, two):
    return lax.dot_general(one, two, (((1,), (1,)), ((), ())), preferred_element_type=jnp.float32)


def t_dot(one, two):
    return lax.dot_general(one, two, (((0,), (0,)), ((), ())), preferred_element_type=jnp.float32)


def own_gate(x, router, names, pick):
    row_gates = masked_gates(f32_dot(x, router), names.astype(jnp.float32))
    return jnp.sum(row_gates * pick[:, : row_gates.shape[1]], axis=-1, keepdims=True)


def expert_forward_kernel(width, half, x_ref, router_ref, pick_ref, gate_w, up_w, down_w, mine_ref, theirs_ref, g_ref, u_ref):
    x, names = x_ref[:, :width], x_ref[:, width:]
    gate = own_gate(x, router_ref[...], names, pick_ref[0:1])
    g = f32_dot(x, gate_w[...])
    u = f32_dot(x, up_w[...])
    g_ref[...] = g
    u_ref[...] = u
    act, _ = silu_pair(g)
    out = f32_dot((gate * (act * u)).astype(jnp.bfloat16), down_w[...]).astype(jnp.bfloat16)

    @pl.when(pl.program_id(0) < half)
    def _():
        mine_ref[...] = out

    @pl.when(pl.program_id(0) >= half)
    def _():
        theirs_ref[...] = out


def expert_backward_kernel(
    half, width, x_ref, d_ref, mate_d_ref, router_ref, pick_ref, gate_w, up_w, down_w, g_ref, u_ref, in_ref, dg_ref, du_ref, dd_ref
):
    step = pl.program_id(0)
    x, names = x_ref[:, :width], x_ref[:, width:]
    dy = jnp.where(step < half, d_ref[...], mate_d_ref[...])
    gate = own_gate(x, router_ref[...], names, pick_ref[0:1])
    act, slope = silu_pair(g_ref[...])
    u = u_ref[...]
    d_plain = dot_t(dy, down_w[...])
    hidden = act * u
    d_gate = jnp.sum(hidden * d_plain, axis=-1, keepdims=True)
    weighed = (gate * hidden).astype(jnp.bfloat16)
    d_hidden = gate * d_plain
    d_act = (d_hidden * u * slope).astype(jnp.bfloat16)
    d_up = (d_hidden * act).astype(jnp.bfloat16)
    rows = dot_t(d_act, gate_w[...]) + dot_t(d_up, up_w[...])
    in_ref[:, :width] = rows.astype(jnp.bfloat16)
    coarse = d_gate.astype(jnp.bfloat16).astype(jnp.float32)
    beside = coarse * pick_ref[1:2] + (d_gate - coarse) * pick_ref[2:3]
    in_ref[:, width:] = beside.astype(jnp.bfloat16)

    @pl.when(step == 0)
    def _():
        dg_ref[...] = jnp.zeros_like(dg_ref)
        du_ref[...] = jnp.zeros_like(du_ref)
        dd_ref[...] = jnp.zeros_like(dd_ref)

    dg_ref[...] += t_dot(x, d_act)
    du_ref[...] += t_dot(x, d_up)
    dd_ref[...] += t_dot(weighed, dy)


def fixed(shape):
    return pl.BlockSpec(shape, lambda i: (0,) * len(shape), pipeline_mode=pl.Buffered(1))


def row_block(total):
    return max(n for n in (512, 256, 128, 64, 32, 16) if total % n == 0)


def roomy():
    return pltpu.CompilerParams(vmem_limit_bytes=60 * 1024 * 1024)


def cost(flops, moved):
    return pl.CostEstimate(flops=flops, bytes_accessed=moved, transcendentals=0)


def expert_forward(x, router, picks, gate_w, up_w, down_w):
    rows, (width, hidden) = x.shape[0], gate_w.shape
    block = row_block(rows // 2)
    half = rows // 2 // block
    by_row = lambda w: pl.BlockSpec((block, w), lambda i: (i, 0))
    return pl.pallas_call(
        functools.partial(expert_forward_kernel, width, half),
        grid=(rows // block,),
        out_shape=[
            jax.ShapeDtypeStruct((rows // 2, width), jnp.bfloat16),
            jax.ShapeDtypeStruct((rows // 2, width), jnp.bfloat16),
            jax.ShapeDtypeStruct((rows, hidden), jnp.float32),
            jax.ShapeDtypeStruct((rows, hidden), jnp.float32),
        ],
        in_specs=[by_row(x.shape[1]), fixed(router.shape), fixed(picks.shape)] + [fixed(w.shape) for w in (gate_w, up_w, down_w)],
        out_specs=[
            pl.BlockSpec((block, width), lambda i: (jnp.minimum(i, half - 1), 0)),
            pl.BlockSpec((block, width), lambda i: (jnp.maximum(i - half, 0), 0)),
            by_row(hidden),
            by_row(hidden),
        ],
        compiler_params=roomy(),
        cost_estimate=cost(6 * rows * width * hidden, rows * (4 * width + 8 * hidden)),
        name="expert_forward",
    )(x, router, picks, gate_w, up_w, down_w)


def expert_backward(x, d_mine, d_mates, router, picks, gate_w, up_w, down_w, g, u):
    rows, (width, hidden) = x.shape[0], gate_w.shape
    block = row_block(d_mine.shape[0])
    half = d_mine.shape[0] // block
    by_row = lambda w: pl.BlockSpec((block, w), lambda i: (i, 0))
    first = pl.BlockSpec((block, width), lambda i: (jnp.minimum(i, half - 1), 0))
    second = pl.BlockSpec((block, width), lambda i: (jnp.maximum(i - half, 0), 0))
    wide_in = width + picks.shape[1]
    return pl.pallas_call(
        functools.partial(expert_backward_kernel, half, width),
        grid=(2 * half,),
        out_shape=[jax.ShapeDtypeStruct((rows, wide_in), jnp.bfloat16)]
        + [jax.ShapeDtypeStruct(w.shape, jnp.float32) for w in (gate_w, up_w, down_w)],
        in_specs=[by_row(x.shape[1]), first, second, fixed(router.shape), fixed(picks.shape)]
        + [fixed(w.shape) for w in (gate_w, up_w, down_w)]
        + [by_row(hidden), by_row(hidden)],
        out_specs=[by_row(wide_in)] + [fixed(w.shape) for w in (gate_w, up_w, down_w)],
        compiler_params=roomy(),
        cost_estimate=cost(12 * rows * width * hidden, rows * (6 * width + 8 * hidden)),
        name="expert_backward",
    )(x, d_mine, d_mates, router, picks, gate_w, up_w, down_w, g, u)


def attention_kernel(
    micro, x_ref, gains_ref, cos_ref, sin_ref, wq, wk, wv, wo, q_ref, k_ref, v_ref, p_ref, mixed_ref, in_ref, residual_ref, mid_ref
):
    rows, width = x_ref.shape
    seq = rows // micro
    in_ref[...], _, _ = norm_ahead(x_ref[...].astype(jnp.float32), gains_ref[0:1])
    heads = width // HD
    group = 2 if heads % 2 == 0 else 1
    lower = lax.broadcasted_iota(jnp.int32, (seq, seq), 0) >= lax.broadcasted_iota(jnp.int32, (seq, seq), 1)

    @pl.loop(0, heads // group)
    def _(step):
        columns = pl.ds(pl.multiple_of(step * (group * HD), group * HD), group * HD)
        normed = in_ref[...]

        def turned(weights):
            raw = f32_dot(normed, weights[:, columns])
            parts = [raw[:, j * HD : (j + 1) * HD] for j in range(group)]
            parts = [p * cos_ref[...] + pltpu.roll(p, HD // 2, 1) * sin_ref[...] for p in parts]
            return jnp.concatenate(parts, axis=1).astype(jnp.bfloat16)

        q, k = turned(wq), turned(wk)
        v = f32_dot(normed, wv[:, columns]).astype(jnp.bfloat16)
        q_ref[:, columns], k_ref[:, columns], v_ref[:, columns] = q, k, v
        every = []
        for m in range(micro):
            side = []
            for j in range(group):
                one = lambda a: a[m * seq : (m + 1) * seq, j * HD : (j + 1) * HD]
                scores = HD ** (-0.5) * dot_t(one(q), one(k))
                scores = jnp.where(lower, scores, -1e30)
                weights = jnp.exp(scores - jnp.max(scores, axis=-1, keepdims=True))
                probs = weights / jnp.sum(weights, axis=-1, keepdims=True)
                p_ref[m, step * group + j] = probs
                side.append(f32_dot(probs.astype(jnp.bfloat16), one(v)))
            every.append(jnp.concatenate(side, axis=1))
        mixed_ref[:, columns] = jnp.concatenate(every, axis=0).astype(jnp.bfloat16)

    @pl.loop(0, heads // group)
    def _(step):
        columns = pl.ds(pl.multiple_of(step * (group * HD), group * HD), group * HD)
        residual_ref[:, columns] = x_ref[:, columns].astype(jnp.float32) + f32_dot(mixed_ref[...], wo[:, columns])

    mid_ref[...], _, _ = norm_ahead(residual_ref[...], gains_ref[1:2])


def attention_forward(micro, x, gains, cos, sin, wq, wk, wv, wo):
    rows, width = x.shape
    seq = rows // micro
    like = lambda kind: jax.ShapeDtypeStruct((rows, width), kind)
    return pl.pallas_call(
        functools.partial(attention_kernel, micro),
        out_shape=[like(jnp.bfloat16)] * 3
        + [jax.ShapeDtypeStruct((micro, width // HD, seq, seq), jnp.float32)]
        + [like(jnp.bfloat16)] * 2
        + [like(jnp.float32), like(jnp.bfloat16)],
        compiler_params=roomy(),
        cost_estimate=cost(32 * rows * width * width, 10 * width * width),
        name="attention_forward",
    )(x, gains, cos, sin, wq, wk, wv, wo)


def shared_kernel(width, part, x_ref, d_ref, w_ref, out_ref, in_ref, grad_ref):
    x, dy = x_ref[:, :width], d_ref[...]
    gate_w, up_w, down_t = w_ref[:, :part], w_ref[:, part : 2 * part], w_ref[:, 2 * part :]
    act, slope = silu_pair(f32_dot(x, gate_w))
    u = f32_dot(x, up_w)
    hidden = (act * u).astype(jnp.bfloat16)
    out_ref[...] = dot_t(hidden, down_t).astype(jnp.bfloat16)
    d_hidden = f32_dot(dy, down_t)
    d_gate = (d_hidden * u * slope).astype(jnp.bfloat16)
    d_up = (d_hidden * act).astype(jnp.bfloat16)
    in_ref[...] = (dot_t(d_gate, gate_w) + dot_t(d_up, up_w)).astype(jnp.bfloat16)

    @pl.when(pl.program_id(0) == 0)
    def _():
        grad_ref[...] = jnp.zeros_like(grad_ref)

    grad_ref[:, :part] += t_dot(x, d_gate)
    grad_ref[:, part : 2 * part] += t_dot(x, d_up)
    grad_ref[:, 2 * part :] += t_dot(dy, hidden)


def shared_expert(x, d, weights):
    rows, width = d.shape
    part = weights.shape[1] // 3
    block = row_block(rows)
    by_row = lambda w: pl.BlockSpec((block, w), lambda i: (i, 0))
    return pl.pallas_call(
        functools.partial(shared_kernel, width, part),
        grid=(rows // block,),
        out_shape=[jax.ShapeDtypeStruct((rows, width), jnp.bfloat16)] * 2 + [jax.ShapeDtypeStruct(weights.shape, jnp.float32)],
        in_specs=[by_row(x.shape[1]), by_row(width), fixed(weights.shape)],
        out_specs=[by_row(width)] * 2 + [fixed(weights.shape)],
        compiler_params=roomy(),
        cost_estimate=cost(18 * rows * width * part, rows * 8 * width),
        name="shared_expert",
    )(x, d, weights)


def on_device(
    tokens,
    cotangent,
    routes,
    gain_attn,
    gain_moe,
    w_query,
    w_key,
    w_value,
    attention_output_weight,
    router,
    shared_gate,
    shared_up,
    shared_down,
    routed_gate_weight,
    routed_up_weight,
    routed_down_weight,
):
    f32, bf16 = jnp.float32, jnp.bfloat16
    micro = tokens.shape[0]
    seq_len, width_all = tokens.shape[2], tokens.shape[3]
    chosen_count = routes.shape[3]
    experts = router.shape[1]
    heads = width_all // HD
    dims = chip_grid(lax.axis_size("wide"))
    deep, high, broad = dims
    slots = 9 * seq_len * chosen_count // (8 * experts) + 1
    extra = -(-experts // 128) * 128
    extra_back = -(-4 * experts // 128) * 128
    cosine_table, sine_table = angles(seq_len, HD)
    scale_factor = HD ** (-0.5)
    causal_mask = jnp.arange(seq_len)[:, None] >= jnp.arange(seq_len)[None, :]
    me = lax.axis_index("wide")
    own_rows = gain_attn.shape[0]

    named = jnp.any(routes[:, 0, :, :, None] == jnp.arange(experts), axis=2)
    named_wide = jnp.pad(named.astype(bf16), ((0, 0), (0, 0), (0, extra - experts)))

    small_width = -(-(experts + 2) // 128) * 128
    small = jnp.concatenate(
        [router, gain_attn[:, None], gain_moe[:, None], jnp.zeros((own_rows, small_width - experts - 2), bf16)], axis=1
    )
    hidden_all = shared_gate.shape[1]
    part = -(-hidden_all // (deep * 128)) * 128

    def cut(matrix):
        return jnp.pad(matrix, ((0, 0), (0, part * deep - hidden_all))).reshape(own_rows, deep, part).transpose(1, 0, 2)

    shared = jnp.concatenate([cut(shared_gate), cut(shared_up), cut(shared_down.T)], axis=2)
    (small_all, wq_all, wk_all, wv_all, wo_all, shared_all), names_column = gather_all(
        dims,
        [small, w_query, w_key, w_value, attention_output_weight, shared],
        [False, False, False, False, False, True],
        named_wide,
    )
    line = Line(dims)
    ahead_rows, back_rows = line.both_ways(cotangent[:, 0], cotangent[:, 0])
    ahead_rows, back_rows, small_all, wq_all, wk_all = lax.optimization_barrier((ahead_rows, back_rows, small_all, wq_all, wk_all))
    from_before, from_after = [ahead_rows], [back_rows]

    if deep > 2:
        one, two = line.both_ways(ahead_rows, back_rows)
        from_before, from_after = from_before + [one], from_after + [two]
    for far in range(3, deep):
        one, two = line.both_ways(cotangent[:, 0], cotangent[:, 0], far)
        from_before, from_after = from_before + [one], from_after + [two]
    router_all = small_all[:, :experts]
    gain_one = small_all[:, experts].astype(f32)
    gain_two = small_all[:, experts + 1].astype(f32)

    chip_a, chip_b, chip_c = place(dims)
    offsets = high * broad
    step = jnp.arange(offsets)
    targets = (chip_a * high + (chip_b + step // broad) % high) * broad + (chip_c + step % broad) % broad
    is_target = (jnp.arange(experts)[:, None] == targets[None, :]).astype(bf16)
    earlier = (jnp.arange(seq_len)[:, None] > jnp.arange(seq_len)[None, :]).astype(bf16)
    names = names_column[..., :experts]
    aimed = jnp.einsum("mkte,eq->mkqt", names, is_target, preferred_element_type=f32)
    slot = jnp.einsum("mkqu,tu->mkqt", aimed.astype(bf16), earlier, preferred_element_type=f32)
    hit = (slot[:, :, :, None, :] == jnp.arange(slots, dtype=f32)[:, None]) & (aimed[:, :, :, None, :] > 0.5)
    choose = hit.astype(bf16).reshape(micro, deep, offsets * slots, seq_len)
    choose_t = choose.transpose(0, 1, 3, 2)

    rows_low = tokens[:, 0].reshape(micro * seq_len, width_all)
    rows_in = rows_low.astype(f32)
    cos_row, sin_row = cosine_table[:, 0], sine_table[:, 0]
    queries, key_rows, value_rows, probs, mixed, normalized_input, residual, normed_mid = attention_forward(
        micro,
        rows_low,
        jnp.stack([gain_one, gain_two]),
        jnp.tile(jnp.concatenate([cos_row, cos_row], axis=1), (micro, 1)),
        jnp.tile(jnp.concatenate([-sin_row, sin_row], axis=1), (micro, 1)),
        wq_all,
        wk_all,
        wv_all,
        wo_all,
    )
    queries, key_rows, value_rows = (a.reshape(micro, seq_len, heads, HD) for a in (queries, key_rows, value_rows))
    probs_low = probs.astype(bf16)
    _, plain_in, scale_in = norm_ahead(rows_in, gain_one)
    _, plain_mid, scale_mid = norm_ahead(residual, gain_two)

    from_before, from_after, normed_mid = lax.optimization_barrier((from_before, from_after, normed_mid))
    d_column = [cotangent[:, 0]] + [
        jnp.where(chip_a >= k, from_before[k - 1], from_after[deep - k - 1]) for k in range(1, deep)
    ]
    d_column = jnp.stack(d_column, axis=1)
    d_picked_rows = jnp.einsum("mkqst,mktd->qmksd", hit.astype(bf16), d_column, preferred_element_type=f32).astype(bf16)

    x_ext = jnp.concatenate([normed_mid.reshape(micro, seq_len, width_all), named_wide], axis=-1)
    x_both, x_column = dispatch(dims, x_ext, choose)
    x_both, d_picked_rows = lax.optimization_barrier((x_both, d_picked_rows))
    d_pieces = plane_rows(dims, d_picked_rows)
    x_rows = x_both.reshape(-1, width_all + extra)

    shared_out, d_shared_in, grad_shared = shared_expert(
        x_column.reshape(-1, width_all + extra), d_column.reshape(-1, width_all), shared_all
    )
    grad_shared = grad_shared.astype(bf16)
    x_rows, shared_out = lax.optimization_barrier((x_rows, shared_out))

    gate_w, up_w, down_w = routed_gate_weight[0], routed_up_weight[0], routed_down_weight[0]
    side = 2 * experts * lax.axis_index("narrow")
    places = jnp.stack([me, me + side, me + side + experts])
    picks = (jnp.arange(extra_back)[None, :] == places[:, None]).astype(f32)
    router_wide = jnp.pad(router_all, ((0, 0), (0, extra - experts)))
    expert_args = (router_wide, picks, gate_w, up_w, down_w)
    out_mine, out_theirs, g_part, u_part = expert_forward(x_rows, *expert_args)
    d_pieces, out_mine, out_theirs = lax.optimization_barrier((d_pieces, out_mine, out_theirs))
    theirs = swap_cores(out_theirs)
    d_mine = jnp.stack(d_pieces, axis=1).reshape(-1, width_all)
    d_mates = swap_cores(d_mine)
    routed_rows = (out_mine.astype(f32) + theirs.astype(f32)).astype(bf16)
    routed_rows = routed_rows.reshape(micro, offsets, deep, slots, width_all)

    x_late, routed_rows = lax.optimization_barrier((x_rows, routed_rows))
    routed_pieces = plane_back(dims, routed_rows)
    d_in_rows, grad_egate, grad_eup, grad_edown = expert_backward(x_late, d_mine, d_mates, *expert_args, g_part, u_part)
    routed_pieces, d_in_rows = lax.optimization_barrier((routed_pieces, d_in_rows))
    routed_back = jnp.stack(routed_pieces, axis=2).reshape(micro, deep, offsets * slots, width_all)
    routed_sums = column_sums(dims, choose, routed_back, shared_out.reshape(d_column.shape))
    routed_sums, d_in_rows = lax.optimization_barrier((routed_sums, d_in_rows))
    up_rows, down_rows = line.both_ways(routed_sums[:, 1 % deep].astype(bf16), routed_sums[:, deep - 1].astype(bf16))
    d_total = give_back(
        dims,
        d_in_rows.reshape(2, micro, offsets, deep, slots, width_all + extra_back),
        choose_t,
        d_shared_in.reshape(d_column.shape),
    )
    d_total, up_rows, down_rows = lax.optimization_barrier((d_total, up_rows, down_rows))
    hops = [1]

    def next_sum(up_rows, down_rows):
        hops[0] += 1
        if hops[0] > deep - 1:
            return up_rows, down_rows
        up_rows = up_rows.astype(f32) + routed_sums[:, hops[0]]
        down_rows = down_rows.astype(f32) + routed_sums[:, deep - hops[0]]
        return line.both_ways(up_rows.astype(bf16), down_rows.astype(bf16))

    up_rows, down_rows = next_sum(up_rows, down_rows)
    d_total = d_total.reshape(micro * seq_len, width_all + extra_back)
    d_gates = sum(d_total[:, width_all + n * experts : width_all + (n + 1) * experts] for n in range(4))

    named_rows = named.reshape(micro * seq_len, experts)
    gates = masked_gates(f32_dot(normed_mid, router_all), named_rows)
    d_out = cotangent[:, 0].reshape(micro * seq_len, width_all).astype(f32)

    d_logits = (gates * (d_gates - jnp.sum(gates * d_gates, axis=1, keepdims=True))).astype(bf16)
    d_mid = d_total[:, :width_all] + dot_t(d_logits, router_all)
    d_norm_two, grad_gain_two = norm_back(d_mid, plain_mid, scale_mid, gain_two)
    d_residual = d_out + d_norm_two
    d_attn = d_residual.astype(bf16)
    grad_wout = t_dot(mixed, d_attn).astype(bf16)
    d_mixed = dot_t(d_attn, wo_all).astype(bf16).reshape(micro, seq_len, heads, HD)
    d_probs = jnp.einsum("sqhd,skhd->shqk", d_mixed, value_rows, preferred_element_type=f32)
    d_value = jnp.einsum("shqk,sqhd->skhd", probs_low, d_mixed, preferred_element_type=f32)
    d_value = d_value.astype(bf16).reshape(micro * seq_len, width_all)
    d_scores = (probs * (d_probs - jnp.sum(probs * d_probs, axis=-1, keepdims=True))).astype(bf16)
    d_scores, up_rows, down_rows = lax.optimization_barrier((d_scores, up_rows, down_rows))
    up_rows, down_rows = next_sum(up_rows, down_rows)
    d_query = scale_factor * jnp.einsum("shqk,skhd->sqhd", d_scores, key_rows, preferred_element_type=f32)
    d_key = scale_factor * jnp.einsum("shqk,sqhd->skhd", d_scores, queries, preferred_element_type=f32)
    d_query = unrotate(d_query, cosine_table, sine_table).astype(bf16).reshape(micro * seq_len, width_all)
    d_key = unrotate(d_key, cosine_table, sine_table).astype(bf16).reshape(micro * seq_len, width_all)
    grad_wq = t_dot(normalized_input, d_query).astype(bf16)
    grad_wk = t_dot(normalized_input, d_key).astype(bf16)
    grad_wv = t_dot(normalized_input, d_value).astype(bf16)
    d_in = dot_t(d_query, wq_all) + dot_t(d_key, wk_all) + dot_t(d_value, wv_all)
    d_norm_one, grad_gain_one = norm_back(d_in, plain_in, scale_in, gain_one)
    grad_tokens = (d_residual + d_norm_one).reshape(micro, 1, seq_len, width_all)

    up_rows, down_rows, grad_wv = lax.optimization_barrier((up_rows, down_rows, grad_wv))
    routed = routed_sums[:, 0] + up_rows.astype(f32) + down_rows.astype(f32)
    final_rows = residual + routed.reshape(micro * seq_len, width_all)
    output = final_rows.astype(bf16).reshape(micro, 1, seq_len, width_all)

    column = jnp.arange(small_width)[None, :]
    grad_small = t_dot(normed_mid, jnp.pad(d_logits, ((0, 0), (0, small_width - experts))))
    grad_small = jnp.where(column == experts, grad_gain_one[:, None], grad_small)
    grad_small = jnp.where(column == experts + 1, grad_gain_two[:, None], grad_small).astype(bf16)

    (g_shared, g_wo, g_wq, g_wk, g_wv, g_small) = scatter_all(
        dims,
        [grad_shared, grad_wout, grad_wq, grad_wk, grad_wv, grad_small],
        [True, False, False, False, False, False],
    )

    def joined(n):
        pieces = g_shared[:, :, n * part : (n + 1) * part]
        return pieces.transpose(1, 0, 2).reshape(own_rows, deep * part)[:, :hidden_all]

    return (
        output,
        grad_tokens,
        g_small[:, experts],
        g_small[:, experts + 1],
        g_wq,
        g_wk,
        g_wv,
        g_wo,
        g_small[:, :experts],
        joined(0),
        joined(1),
        joined(2).T,
        grad_egate[None],
        grad_eup[None],
        grad_edown[None],
    )


def solution(mesh):
    return jax.shard_map(
        on_device,
        mesh=mesh,
        in_specs=(
            P(None, ("wide", "narrow"), None, None),
            P(None, ("wide", "narrow"), None, None),
            P(None, ("wide", "narrow"), None, None),
            P(("wide", "narrow")),
            P(("wide", "narrow")),
            P(("wide", "narrow"), None),
            P(("wide", "narrow"), None),
            P(("wide", "narrow"), None),
            P(("wide", "narrow"), None),
            P(("wide", "narrow"), None),
            P(("wide", "narrow"), None),
            P(("wide", "narrow"), None),
            P(None, ("wide", "narrow")),
            P("wide", None, "narrow"),
            P("wide", None, "narrow"),
            P("wide", "narrow", None),
        ),
        out_specs=(
            P(None, ("wide", "narrow"), None, None),
            P(None, ("wide", "narrow"), None, None),
            P(("wide", "narrow")),
            P(("wide", "narrow")),
            P(("wide", "narrow"), None),
            P(("wide", "narrow"), None),
            P(("wide", "narrow"), None),
            P(("wide", "narrow"), None),
            P(("wide", "narrow"), None),
            P(("wide", "narrow"), None),
            P(("wide", "narrow"), None),
            P(None, ("wide", "narrow")),
            P("wide", None, "narrow"),
            P("wide", None, "narrow"),
            P("wide", "narrow", None),
        ),
        check_vma=False,
    )
```

```python
import functools
import jax
import jax.numpy as jnp
from jax import lax
from jax.experimental import pallas as pl
from jax.experimental.pallas import tpu as pltpu
from jax.sharding import PartitionSpec as P

MESH = pl.DeviceIdType.MESH
HD = 128


epsilon = 1e-06


def angles(seq_len, head_size):
    position = jnp.arange(seq_len).astype(jnp.float32)
    exponent = jnp.arange(head_size // 2).astype(jnp.float32) * (2.0 / head_size)
    frequency = jnp.exp(-jnp.log(10000.0) * exponent)
    theta = position[:, None] * frequency[None, :]
    return (jnp.cos(theta)[:, None, :], jnp.sin(theta)[:, None, :])


def rotate(vectors, cosine_table, sine_table):
    middle = vectors.shape[-1] // 2
    first_half = vectors[..., :middle]
    second_half = vectors[..., middle:]
    return jnp.concatenate(
        [
            first_half * cosine_table - second_half * sine_table,
            second_half * cosine_table + first_half * sine_table,
        ],
        axis=-1,
    )


def unrotate(vectors, cosine_table, sine_table):
    middle = vectors.shape[-1] // 2
    first_half = vectors[..., :middle]
    second_half = vectors[..., middle:]
    return jnp.concatenate(
        [
            first_half * cosine_table + second_half * sine_table,
            second_half * cosine_table - first_half * sine_table,
        ],
        axis=-1,
    )


def norm_ahead(matrix, gain):
    scale_rows = lax.rsqrt(jnp.mean(matrix * matrix, axis=-1, keepdims=True) + epsilon)
    normed = matrix * scale_rows
    return ((normed * gain).astype(jnp.bfloat16), normed, scale_rows)


def norm_back(grad_rows, normed, scale_rows, gain):
    gain_grad = jnp.sum(grad_rows * normed, axis=0)
    inner = grad_rows * gain
    return (
        scale_rows * (inner - normed * jnp.mean(inner * normed, axis=-1, keepdims=True)),
        gain_grad,
    )


def silu_pair(pre_act):
    sigma = jax.nn.sigmoid(pre_act)
    return (pre_act * sigma, sigma * (1.0 + pre_act * (1.0 - sigma)))


def chip_grid(chips):
    deep = 4 if chips % 4 == 0 else 1
    rest = chips // deep
    high = max(d for d in range(1, rest + 1) if rest % d == 0 and d * d <= rest)
    return (deep, high, rest // high)

def place(dims):
    wide = lax.axis_index("wide")
    return wide // (dims[1] * dims[2]), (wide // dims[2]) % dims[1], wide % dims[2]

def greet(dims, a, b, c, core):
    deep, high, broad = dims
    barrier = pltpu.get_barrier_semaphore()
    def chip(i, j, k):
        return (i * high + j) * broad + k
    others = [(chip((a + r) % deep, b, c), core) for r in range(1, deep)]
    others += [(chip(a, (b + r) % high, c), core) for r in range(1, high)]
    others += [(chip(a, b, (c + r) % broad), core) for r in range(1, broad)]
    others += [(chip(a, b, c), 1 - core)]
    for other in others:
        pl.semaphore_signal(barrier, inc=1, device_id=other, device_id_type=MESH)
    pl.semaphore_wait(barrier, len(others))

def near_first(dims, a):
    deep = dims[0]
    if deep != 4:
        return list(range(deep))
    one = 1 + 2 * (1 - 2 * a // deep)
    inner = (a + 1) // 2 % 2
    other = deep - one
    return [0, one, 2 + inner * (other - 2), other + inner * (2 - other)]


def pass_on(deep, a, k, up, down, act):
    if isinstance(k, int) and k == 0:
        pl.when(a + 1 < deep)(lambda: act(up(k)))
        pl.when(a >= 1)(lambda: act(down(k)))
    else:
        pl.when((k <= a) & (a + 1 < deep))(lambda: act(up(k)))
        pl.when((k > a) & (a >= 1))(lambda: act(down(k)))


def cut_columns(widths):
    pieces = []
    for n, width in enumerate(widths):
        tiles = width // 128
        middle = (tiles + 1) // 2 * 128
        pieces += [(n, 0, width)] if tiles < 6 else [(n, 0, middle), (n, middle, width)]
    return pieces


def gather_kernel(dims, arrays, pieces, sliced, *refs):
    deep, high, broad = dims
    count, ahead = len(pieces), 12
    rows_ref, column_ref = refs[arrays], refs[2 * arrays + 1]
    micro = rows_ref.shape[0]
    ins = [refs[n].at[..., lo:hi] for n, lo, hi in pieces]
    outs = [refs[arrays + 1 + n].at[..., lo:hi] for n, lo, hi in pieces]
    sliced = [sliced[n] for n, lo, hi in pieces]
    own_sem, s1, r1, s2, r2, s3, r3, sn, rn, sr, rr = refs[2 * arrays + 2 :]
    a, b, c = place(dims)
    core = lax.axis_index("narrow")
    greet(dims, a, b, c, core)

    def chip(i, j, k):
        return (i * high + j) * broad + k

    def send(src, dst, ss, rs, to):
        copy = pltpu.make_async_remote_copy(
            src_ref=src, dst_ref=dst, send_sem=ss, recv_sem=rs, device_id=to, device_id_type=MESH
        )
        return copy

    def program(me):
        first, second = (high, broad) if me == 0 else (broad, high)

        def at2(i, r):
            if me == 0:
                return outs[i].at[:, (b - r + high) % high, c, me]
            return outs[i].at[:, b, (c - r + broad) % broad, me]

        def at3(i, r):
            if me == 0:
                return outs[i].at[:, :, (c - r + broad) % broad, me]
            return outs[i].at[:, (b - r + high) % high, :, me]

        def to2(r):
            return (chip(a, (b + r) % high, c), me) if me == 0 else (chip(a, b, (c + r) % broad), me)

        def to3(r):
            return (chip(a, b, (c + r) % broad), me) if me == 0 else (chip(a, (b + r) % high, c), me)

        mate = (chip(a, b, c), 1 - me)

        def own(i):
            return pltpu.make_async_copy(ins[i].at[a] if sliced[i] else ins[i], outs[i].at[a, b, c, me], own_sem.at[i])

        def stage1(i, r):
            h = (a + r) % deep
            src = ins[i].at[h] if sliced[i] else ins[i]
            return send(src, outs[i].at[a, b, c, me], s1.at[i, r - 1], r1.at[i, r - 1], (chip(h, b, c), me))

        def own_rows():
            return pltpu.make_async_copy(rows_ref, column_ref.at[:, 0], own_sem.at[count])

        def column(m, r):
            to = (chip((a + r) % deep, b, c), me)
            return send(rows_ref.at[m], column_ref.at[m, r], sr.at[m, r - 1], rr.at[m, r - 1], to)

        def stage2(i, r):
            return send(at2(i, 0), at2(i, 0), s2.at[i, r - 1], r2.at[i, r - 1], to2(r))

        def stage3(i, r):
            return send(at3(i, 0), at3(i, 0), s3.at[i, r - 1], r3.at[i, r - 1], to3(r))

        def across(i, part):
            view = at2(i, 0) if part == 0 else at2(i, part) if part < first else at3(i, part - first + 1)
            return send(view, view, sn.at[i, part], rn.at[i, part], mate)

        parts = first + second - 1
        def begin(i):
            for r in range(1, deep):
                stage1(i, r).start()
            own(i).start()

        for i in range(min(ahead, count)):
            begin(i)
        own_rows().start()
        for step in range(count + 2):
            if step + ahead < count:
                begin(step + ahead)
            for m in range(micro):
                if step == min(2 + 2 * m, count + 1):
                    for r in range(1, deep):
                        column(m, r).start()
            i = step
            if i < count:
                own(i).wait()
                for r in range(1, deep):
                    stage1(i, r).wait_recv()
                for r in range(1, first):
                    stage2(i, r).start()
                across(i, 0).start()
            i = step - 1
            if 0 <= i < count:
                for r in range(1, first):
                    stage2(i, r).wait_recv()
                for r in range(1, second):
                    stage3(i, r).start()
                for r in range(1, first):
                    across(i, r).start()
            i = step - 2
            if 0 <= i < count:
                for r in range(1, second):
                    stage3(i, r).wait_recv()
                for r in range(1, second):
                    across(i, first + r - 1).start()
        for i in range(count):
            for r in range(1, deep):
                stage1(i, r).wait_send()
            for r in range(1, first):
                stage2(i, r).wait_send()
            for r in range(1, second):
                stage3(i, r).wait_send()
            for part in range(parts):
                across(i, part).wait()
        own_rows().wait()
        for m in range(micro):
            for r in range(1, deep):
                column(m, r).wait()

    pl.when(core == 0)(lambda: program(0))
    pl.when(core == 1)(lambda: program(1))

def gather_all(dims, parts, sliced, rows):
    arrays = len(parts)
    deep, high, broad = dims
    pieces = cut_columns([p.shape[-1] for p in parts])
    count = len(pieces)
    sem = pltpu.SemaphoreType.DMA
    most = max(high, broad)
    shapes = [p.shape[1:] if cut else p.shape for p, cut in zip(parts, sliced)]
    vmem, anywhere = pl.BlockSpec(memory_space=pltpu.VMEM), pl.BlockSpec(memory_space=pl.ANY)
    outs = pl.pallas_call(
        functools.partial(gather_kernel, dims, arrays, pieces, sliced),
        out_shape=[jax.ShapeDtypeStruct((deep, high, broad, 2) + sh, p.dtype) for p, sh in zip(parts, shapes)]
        + [jax.ShapeDtypeStruct(rows.shape[:1] + (deep,) + rows.shape[1:], rows.dtype)],
        in_specs=[vmem] * (arrays + 1),
        out_specs=[anywhere] * (arrays + 1),
        scratch_shapes=[sem((count + 1,))]
        + [sem((count, max(deep - 1, 1)))] * 2
        + [sem((count, max(most - 1, 1)))] * 4
        + [sem((count, high + broad - 1))] * 2
        + [sem((rows.shape[0], max(deep - 1, 1)))] * 2,
        compiler_params=pltpu.CompilerParams(collective_id=0, has_side_effects=True),
        name="gather_dense",
    )(*parts, rows)
    return [o.reshape((-1, sh[-1])) for o, sh in zip(outs[:-1], shapes)], outs[-1]


def scatter_kernel(dims, arrays, pieces, sliced, *refs):
    deep, high, broad = dims
    count, ahead = len(pieces), 3
    group = lambda m: [refs[m * arrays + n].at[..., lo:hi] for n, lo, hi in pieces]
    ins, outs, held, from_mate, got2, got3, got4 = [group(m) for m in range(7)]
    own_sem, sn, rn, s2, r2, s3, r3, s4, r4 = refs[7 * arrays :]
    sliced = [sliced[n] for n, lo, hi in pieces]
    a, b, c = place(dims)
    core = lax.axis_index("narrow")
    greet(dims, a, b, c, core)

    def chip(i, j, k):
        return (i * high + j) * broad + k

    def send(src, dst, ss, rs, to):
        return pltpu.make_async_remote_copy(
            src_ref=src, dst_ref=dst, send_sem=ss, recv_sem=rs, device_id=to, device_id_type=MESH
        )

    wide32 = jnp.float32

    def program(me):
        first, second = (broad, high) if me == 0 else (high, broad)
        mate = (chip(a, b, c), 1 - me)

        def own(i):
            return pltpu.make_async_copy(ins[i].at[:, :, :, me], held[i], own_sem.at[i])

        def across(i):
            return send(ins[i].at[:, :, :, 1 - me], from_mate[i], sn.at[i], rn.at[i], mate)

        def stage2(i, r):
            if me == 0:
                k = (c + r) % broad
                return send(held[i].at[:, :, k], got2[i].at[r - 1], s2.at[i, r - 1], r2.at[i, r - 1], (chip(a, b, k), me))
            j = (b + r) % high
            return send(held[i].at[:, j], got2[i].at[r - 1], s2.at[i, r - 1], r2.at[i, r - 1], (chip(a, j, c), me))

        def stage3(i, r):
            if me == 0:
                j = (b + r) % high
                return send(held[i].at[:, j, c], got3[i].at[r - 1], s3.at[i, r - 1], r3.at[i, r - 1], (chip(a, j, c), me))
            k = (c + r) % broad
            return send(held[i].at[:, b, k], got3[i].at[r - 1], s3.at[i, r - 1], r3.at[i, r - 1], (chip(a, b, k), me))

        def stage4(i, r):
            h = (a + r) % deep
            return send(held[i].at[h, b, c], got4[i].at[r - 1], s4.at[i, r - 1], r4.at[i, r - 1], (chip(h, b, c), me))

        def add_mate(i):
            for j in range(high):
                for k in range(broad):
                    @pl.loop(0, deep)
                    def _(h):
                        held[i][h, j, k] = (held[i][h, j, k].astype(wide32) + from_mate[i][h, j, k].astype(wide32)).astype(jnp.bfloat16)

        def add2(i):
            if me == 0:
                for j in range(high):
                    @pl.loop(0, deep)
                    def _(h):
                        total = held[i][h, j, c].astype(wide32)
                        for r in range(1, broad):
                            total += got2[i][r - 1, h, j].astype(wide32)
                        held[i][h, j, c] = total.astype(jnp.bfloat16)
            else:
                for k in range(broad):
                    @pl.loop(0, deep)
                    def _(h):
                        total = held[i][h, b, k].astype(wide32)
                        for r in range(1, high):
                            total += got2[i][r - 1, h, k].astype(wide32)
                        held[i][h, b, k] = total.astype(jnp.bfloat16)

        def add3(i):
            @pl.loop(0, deep)
            def _(h):
                total = held[i][h, b, c].astype(wide32)
                for r in range(1, second):
                    total += got3[i][r - 1, h].astype(wide32)
                held[i][h, b, c] = total.astype(jnp.bfloat16)

        def add4(i):
            if sliced[i]:
                outs[i][a] = held[i][a, b, c].astype(wide32)
                for r in range(1, deep):
                    outs[i][(a - r + deep) % deep] = got4[i][r - 1].astype(wide32)
                return
            total = held[i][a, b, c].astype(wide32)
            for r in range(1, deep):
                total += got4[i][r - 1].astype(wide32)
            outs[i][...] = total

        def begin(i):
            across(i).start()
            own(i).start()

        for i in range(min(ahead, count)):
            begin(i)
        for step in range(count + 3):
            if step + ahead < count:
                begin(step + ahead)
            i = step
            if i < count:
                own(i).wait()
                across(i).wait_recv()
                add_mate(i)
                for r in range(1, first):
                    stage2(i, r).start()
            i = step - 1
            if 0 <= i < count:
                for r in range(1, first):
                    stage2(i, r).wait_recv()
                add2(i)
                for r in range(1, second):
                    stage3(i, r).start()
            i = step - 2
            if 0 <= i < count:
                for r in range(1, second):
                    stage3(i, r).wait_recv()
                add3(i)
                for r in range(1, deep):
                    stage4(i, r).start()
            i = step - 3
            if 0 <= i < count:
                for r in range(1, deep):
                    stage4(i, r).wait_recv()
                add4(i)
        for i in range(count):
            across(i).wait_send()
            for r in range(1, first):
                stage2(i, r).wait_send()
            for r in range(1, second):
                stage3(i, r).wait_send()
            for r in range(1, deep):
                stage4(i, r).wait_send()

    pl.when(core == 0)(lambda: program(0))
    pl.when(core == 1)(lambda: program(1))

def scatter_all(dims, parts, sliced):
    arrays = len(parts)
    deep, high, broad = dims
    pieces = cut_columns([p.shape[-1] for p in parts])
    count = len(pieces)
    devices = deep * high * broad * 2
    blocks = [(p.shape[0] // devices, p.shape[1]) for p in parts]
    sem = pltpu.SemaphoreType.DMA
    most = max(high, broad)
    vm = lambda lead: [pltpu.VMEM(lead + blk, jnp.bfloat16) for blk in blocks]
    side = max(high, broad)
    got2 = vm((max(most - 1, 1), deep, side))
    return pl.pallas_call(
        functools.partial(scatter_kernel, dims, arrays, pieces, sliced),
        out_shape=[jax.ShapeDtypeStruct(((deep,) if cut else ()) + blk, jnp.float32) for blk, cut in zip(blocks, sliced)],
        in_specs=[pl.BlockSpec(memory_space=pl.ANY)] * arrays,
        out_specs=[pl.BlockSpec(memory_space=pltpu.VMEM)] * arrays,
        scratch_shapes=vm((deep, high, broad)) + vm((deep, high, broad)) + got2 + vm((max(most - 1, 1), deep)) + vm((max(deep - 1, 1),))
        + [sem((count,))] * 3
        + [sem((count, max(most - 1, 1)))] * 4
        + [sem((count, max(deep - 1, 1)))] * 2,
        compiler_params=pltpu.CompilerParams(collective_id=1, has_side_effects=True, vmem_limit_bytes=62 * 1024 * 1024),
        name="scatter_dense",
    )(*[p.reshape((deep, high, broad, 2) + blk) for p, blk in zip(parts, blocks)])


def greet_all(dims, a, b, c, core):
    deep, high, broad = dims
    barrier = pltpu.get_barrier_semaphore()
    others = [(((a + r) % deep * high + b) * broad + c, core) for r in range(1, deep)]
    others += [
        ((a * high + (b + q // broad) % high) * broad + (c + q % broad) % broad, core) for q in range(1, high * broad)
    ]
    others += [((a * high + b) * broad + c, 1 - core)]
    for other in others:
        pl.semaphore_signal(barrier, inc=1, device_id=other, device_id_type=MESH)
    pl.semaphore_wait(barrier, len(others))


def remote(src, dst, ss, rs, to):
    return pltpu.make_async_remote_copy(
        src_ref=src, dst_ref=dst, send_sem=ss, recv_sem=rs, device_id=to, device_id_type=MESH
    )


def dispatch_kernel(dims, micro, x_ref, choose_ref, both_ref, column_ref, got, picked, sup, sdown, rcol, spl, rpl, sm, rm, sl):
    deep, high, broad = dims
    offsets = high * broad
    a, b, c = place(dims)
    core = lax.axis_index("narrow")
    greet_all(dims, a, b, c, core)
    mate = ((a * high + b) * broad + c, 1 - core)
    rows_ref, mates_ref = both_ref.at[0], both_ref.at[1]

    def block(m, k):
        return x_ref.at[m] if isinstance(k, int) and k == 0 else got.at[m, k]

    def arrival(m, k):
        return remote(got.at[m, k], got.at[m, k], sup.at[m, k], rcol.at[m, k], mate)

    def relay(m, k, act):
        def up(k):
            to = ((a + 1) * high + b) * broad + c
            return remote(block(m, k), got.at[m, k + 1], sup.at[m, k], rcol.at[m, k + 1], (to, core))

        def down(k):
            to, there = ((a - 1) * high + b) * broad + c, (k + deep - 1) % deep
            return remote(block(m, k), got.at[m, there], sdown.at[m, k], rcol.at[m, there], (to, core))

        pass_on(deep, a, k, up, down, act)

    def plane(m, k, q):
        to = (a * high + (b + q // broad) % high) * broad + (c + q % broad) % broad
        return remote(picked.at[m, k, q], rows_ref.at[m, q, k], spl.at[m, k, q], rpl.at[m, k, q], (to, core))

    def across(m, k, part):
        if part == 0:
            return remote(picked.at[m, k, 0], mates_ref.at[m, 0, k], sm.at[m, k, 0], rm.at[m, k, 0], mate)
        return remote(rows_ref.at[m, 1:, k], mates_ref.at[m, 1:, k], sm.at[m, k, 1], rm.at[m, k, 1], mate)

    def keep(m, k):
        return pltpu.make_async_copy(picked.at[m, k, 0], rows_ref.at[m, 0, k], sl.at[m, k, 0])

    def keep_column(m, k):
        return pltpu.make_async_copy(block(m, k), column_ref.at[m, k], sl.at[m, k, 1])

    order = [(m, k) for k in near_first(dims, a) for m in range(micro)]
    for m in range(micro):
        relay(m, 0, lambda copy: copy.start())
    for n, (m, k) in enumerate(order):
        if n >= micro:
            arrival(m, k).wait_recv()
            relay(m, k, lambda copy: copy.start())
        keep_column(m, k).start()
        piece = block(m, k)[...]
        chosen = jnp.dot(choose_ref[m, k], piece, preferred_element_type=jnp.float32).astype(jnp.bfloat16)
        picked[m, k] = chosen.reshape(picked.shape[2:])
        for q in range(1, offsets):
            plane(m, k, q).start()
        keep(m, k).start()
        across(m, k, 0).start()
    for m, k in order:
        for q in range(1, offsets):
            plane(m, k, q).wait_recv()
        across(m, k, 1).start()
    for m, k in order:
        relay(m, k, lambda copy: copy.wait_send())
        keep_column(m, k).wait()
        for q in range(1, offsets):
            plane(m, k, q).wait_send()
        keep(m, k).wait()
        across(m, k, 0).wait()
        across(m, k, 1).wait()


def dispatch(dims, x, choose):
    deep, high, broad = dims
    micro, tokens, width = x.shape
    offsets = high * broad
    slots = choose.shape[2] // offsets
    sem = pltpu.SemaphoreType.DMA
    anywhere, vmem = pl.BlockSpec(memory_space=pl.ANY), pl.BlockSpec(memory_space=pltpu.VMEM)
    out = jax.ShapeDtypeStruct((2, micro, offsets, deep, slots, width), x.dtype)
    return pl.pallas_call(
        functools.partial(dispatch_kernel, dims, micro),
        out_shape=[out, jax.ShapeDtypeStruct((micro, deep, tokens, width), x.dtype)],
        in_specs=[vmem, vmem],
        out_specs=[anywhere] * 2,
        scratch_shapes=[
            pltpu.VMEM((micro, deep, tokens, width), x.dtype),
            pltpu.VMEM((micro, deep, offsets, slots, width), x.dtype),
        ]
        + [sem((micro, deep))] * 3
        + [sem((micro, deep, offsets))] * 2
        + [sem((micro, deep, 2))] * 3,
        compiler_params=pltpu.CompilerParams(collective_id=2, has_side_effects=True),
        name="dispatch_rows",
    )(x, choose)


def return_kernel(dims, micro, both_ref, choose_ref, near_ref, total_ref, held, mated, back, up, got, sl, sm, rm, spl, rpl, scol, rcol):
    deep, high, broad = dims
    offsets = high * broad
    a, b, c = place(dims)
    core = lax.axis_index("narrow")
    greet_all(dims, a, b, c, core)
    mate = ((a * high + b) * broad + c, 1 - core)
    near_width = near_ref.shape[-1]
    mine_ref, theirs_ref = both_ref.at[0], both_ref.at[1]

    def load(m, k):
        return pltpu.make_async_copy(mine_ref.at[m, :, k], held.at[m, :, k], sl.at[m, k])

    def across(m, k):
        return remote(theirs_ref.at[m, :, k], mated.at[m, :, k], sm.at[m, k], rm.at[m, k], mate)

    def plane(m, k, q):
        to = (a * high + (b - q // broad + high) % high) * broad + (c - q % broad + broad) % broad
        return remote(held.at[m, q, k], back.at[m, k, q], spl.at[m, k, q], rpl.at[m, k, q], (to, core))

    def column(m, k):
        return remote(up.at[m, k], got.at[m, k], scol.at[m, k], rcol.at[m, k], (((a - k + deep) % deep * high + b) * broad + c, core))

    order = [(m, k) for m in range(micro) for k in list(range(1, deep)) + [0]]
    ahead = 3
    for m, k in order[:ahead]:
        across(m, k).start()
        load(m, k).start()
    for n, (m, k) in enumerate(order):
        for later in order[n + ahead : n + ahead + 1]:
            across(*later).start()
            load(*later).start()
        load(m, k).wait()
        across(m, k).wait_recv()
        for q in range(1, offsets):
            held[m, q, k] = (held[m, q, k].astype(jnp.float32) + mated[m, q, k].astype(jnp.float32)).astype(jnp.bfloat16)
            plane(m, k, q).start()
        back[m, k, 0] = (held[m, 0, k].astype(jnp.float32) + mated[m, 0, k].astype(jnp.float32)).astype(jnp.bfloat16)
    for m, k in order:
        for q in range(1, offsets):
            plane(m, k, q).wait_recv()
        rows = back[m, k].reshape((-1, back.shape[-1]))
        sums = jnp.dot(choose_ref[m, k], rows, preferred_element_type=jnp.float32)
        dense = sums[:, :near_width] + near_ref[m, k].astype(jnp.float32)
        if k == 0:
            total_ref[m, :, :near_width] = dense
            if near_width < sums.shape[1]:
                total_ref[m, :, near_width:] = sums[:, near_width:]
        else:
            up[m, k, :, :near_width] = dense.astype(jnp.bfloat16)
            if near_width < sums.shape[1]:
                up[m, k, :, near_width:] = sums[:, near_width:].astype(jnp.bfloat16)
            column(m, k).start()
    for m in range(micro):
        for k in range(1, deep):
            column(m, k).wait_recv()
            total_ref[m] += got[m, k].astype(jnp.float32)
    for m, k in order:
        across(m, k).wait_send()
        for q in range(1, offsets):
            plane(m, k, q).wait_send()
        if k > 0:
            column(m, k).wait_send()


def give_back(dims, both, choose_t, near):
    deep, high, broad = dims
    _, micro, offsets, _, slots, width = both.shape
    tokens = choose_t.shape[2]
    sem = pltpu.SemaphoreType.DMA
    anywhere, vmem = pl.BlockSpec(memory_space=pl.ANY), pl.BlockSpec(memory_space=pltpu.VMEM)
    scratch = lambda *shape: pltpu.VMEM(shape, both.dtype)
    return pl.pallas_call(
        functools.partial(return_kernel, dims, micro),
        out_shape=jax.ShapeDtypeStruct((micro, tokens, width), jnp.float32),
        in_specs=[anywhere, vmem, vmem],
        out_specs=vmem,
        scratch_shapes=[
            scratch(micro, offsets, deep, slots, width),
            scratch(micro, offsets, deep, slots, width),
            scratch(micro, deep, offsets, slots, width),
            scratch(micro, deep, tokens, width),
            scratch(micro, deep, tokens, width),
        ]
        + [sem((micro, deep))] * 3
        + [sem((micro, deep, offsets))] * 2
        + [sem((micro, deep))] * 2,
        compiler_params=pltpu.CompilerParams(collective_id=3, has_side_effects=True, vmem_limit_bytes=62 * 1024 * 1024),
        name="return_rows",
    )(both, choose_t, near)


class Line:
    def __init__(self, dims):
        deep, plane = dims[0], dims[1] * dims[2]
        self.up = lambda far: [(i * plane + p, (i + far) * plane + p) for i in range(deep - far) for p in range(plane)]

    def both_ways(self, one, two, far=1):
        up = self.up(far)
        return lax.ppermute(one, "wide", up), lax.ppermute(two, "wide", [(b, a) for a, b in up])


def plane_pairs(dims, offset, sign):
    deep, high, broad = dims
    up, over = (offset // broad) * sign, (offset % broad) * sign
    return [
        ((i * high + j) * broad + k, (i * high + (j + up) % high) * broad + (k + over) % broad)
        for i in range(deep)
        for j in range(high)
        for k in range(broad)
    ]


def swap_cores(rows):
    return lax.ppermute(rows, "narrow", [(0, 1), (1, 0)])


def plane_rows(dims, picked):
    return [picked[0]] + [lax.ppermute(picked[q], "wide", plane_pairs(dims, q, 1)) for q in range(1, picked.shape[0])]


def plane_back(dims, rows):
    offsets = rows.shape[1]
    return [rows[:, 0]] + [lax.ppermute(rows[:, q], "wide", plane_pairs(dims, q, -1)) for q in range(1, offsets)]


def column_sums(dims, choose, back, near):
    sums = jnp.einsum("mkst,mksd->mktd", choose, back, preferred_element_type=jnp.float32)
    return sums + near.astype(jnp.float32)


def masked_gates(logits, named):
    top = jnp.max(jnp.where(named > 0, logits, -1e30), axis=-1, keepdims=True)
    weights = jnp.where(named > 0, jnp.exp(logits - top), 0.0)
    return weights / jnp.maximum(jnp.sum(weights, axis=-1, keepdims=True), 0.5)


def f32_dot(one, two):
    return jnp.dot(one, two, preferred_element_type=jnp.float32)


def dot_t(one, two):
    return lax.dot_general(one, two, (((1,), (1,)), ((), ())), preferred_element_type=jnp.float32)


def t_dot(one, two):
    return lax.dot_general(one, two, (((0,), (0,)), ((), ())), preferred_element_type=jnp.float32)


def own_gate(x, router, names, pick):
    row_gates = masked_gates(f32_dot(x, router), names.astype(jnp.float32))
    return jnp.sum(row_gates * pick[:, : row_gates.shape[1]], axis=-1, keepdims=True)


def expert_forward_kernel(width, half, x_ref, router_ref, pick_ref, gate_w, up_w, down_w, mine_ref, theirs_ref, g_ref, u_ref):
    x, names = x_ref[:, :width], x_ref[:, width:]
    gate = own_gate(x, router_ref[...], names, pick_ref[0:1])
    g = dot_t(x, gate_w[...])
    u = dot_t(x, up_w[...])
    g_ref[...] = g
    u_ref[...] = u
    act, _ = silu_pair(g)
    out = f32_dot((gate * (act * u)).astype(jnp.bfloat16), down_w[...]).astype(jnp.bfloat16)

    @pl.when(pl.program_id(0) < half)
    def _():
        mine_ref[...] = out

    @pl.when(pl.program_id(0) >= half)
    def _():
        theirs_ref[...] = out


def expert_backward_kernel(
    half, width, x_ref, d_ref, mate_d_ref, router_ref, pick_ref, gate_w, up_w, down_w, g_ref, u_ref, in_ref, dg_ref, du_ref, dd_ref
):
    step = pl.program_id(0)
    x, names = x_ref[:, :width], x_ref[:, width:]
    dy = jnp.where(step < half, d_ref[...], mate_d_ref[...])
    gate = own_gate(x, router_ref[...], names, pick_ref[0:1])
    act, slope = silu_pair(g_ref[...])
    u = u_ref[...]
    d_plain = dot_t(dy, down_w[...])
    hidden = act * u
    d_gate = jnp.sum(hidden * d_plain, axis=-1, keepdims=True)
    weighed = (gate * hidden).astype(jnp.bfloat16)
    d_hidden = gate * d_plain
    d_act = (d_hidden * u * slope).astype(jnp.bfloat16)
    d_up = (d_hidden * act).astype(jnp.bfloat16)
    rows = f32_dot(d_act, gate_w[...]) + f32_dot(d_up, up_w[...])
    in_ref[:, :width] = rows.astype(jnp.bfloat16)
    coarse = d_gate.astype(jnp.bfloat16).astype(jnp.float32)
    beside = coarse * pick_ref[1:2] + (d_gate - coarse) * pick_ref[2:3]
    in_ref[:, width:] = beside.astype(jnp.bfloat16)

    @pl.when(step == 0)
    def _():
        dg_ref[...] = jnp.zeros_like(dg_ref)
        du_ref[...] = jnp.zeros_like(du_ref)
        dd_ref[...] = jnp.zeros_like(dd_ref)

    dg_ref[...] += t_dot(d_act, x)
    du_ref[...] += t_dot(d_up, x)
    dd_ref[...] += t_dot(weighed, dy)


def fixed(shape):
    return pl.BlockSpec(shape, lambda i: (0,) * len(shape), pipeline_mode=pl.Buffered(1))


def row_block(total):
    return max(n for n in (512, 256, 128, 64, 32, 16) if total % n == 0)


def roomy():
    return pltpu.CompilerParams(vmem_limit_bytes=60 * 1024 * 1024)


def cost(flops, moved):
    return pl.CostEstimate(flops=flops, bytes_accessed=moved, transcendentals=0)


def expert_forward(x, router, picks, gate_w, up_w, down_w):
    rows, (hidden, width) = x.shape[0], gate_w.shape
    block = row_block(rows // 2)
    half = rows // 2 // block
    by_row = lambda w: pl.BlockSpec((block, w), lambda i: (i, 0))
    return pl.pallas_call(
        functools.partial(expert_forward_kernel, width, half),
        grid=(rows // block,),
        out_shape=[
            jax.ShapeDtypeStruct((rows // 2, width), jnp.bfloat16),
            jax.ShapeDtypeStruct((rows // 2, width), jnp.bfloat16),
            jax.ShapeDtypeStruct((rows, hidden), jnp.float32),
            jax.ShapeDtypeStruct((rows, hidden), jnp.float32),
        ],
        in_specs=[by_row(x.shape[1]), fixed(router.shape), fixed(picks.shape)] + [fixed(w.shape) for w in (gate_w, up_w, down_w)],
        out_specs=[
            pl.BlockSpec((block, width), lambda i: (jnp.minimum(i, half - 1), 0)),
            pl.BlockSpec((block, width), lambda i: (jnp.maximum(i - half, 0), 0)),
            by_row(hidden),
            by_row(hidden),
        ],
        compiler_params=roomy(),
        cost_estimate=cost(6 * rows * width * hidden, rows * (4 * width + 8 * hidden)),
        name="expert_forward",
    )(x, router, picks, gate_w, up_w, down_w)


def expert_backward(x, d_mine, d_mates, router, picks, gate_w, up_w, down_w, g, u):
    rows, (hidden, width) = x.shape[0], gate_w.shape
    block = row_block(d_mine.shape[0])
    half = d_mine.shape[0] // block
    by_row = lambda w: pl.BlockSpec((block, w), lambda i: (i, 0))
    first = pl.BlockSpec((block, width), lambda i: (jnp.minimum(i, half - 1), 0))
    second = pl.BlockSpec((block, width), lambda i: (jnp.maximum(i - half, 0), 0))
    wide_in = width + picks.shape[1]
    return pl.pallas_call(
        functools.partial(expert_backward_kernel, half, width),
        grid=(2 * half,),
        out_shape=[jax.ShapeDtypeStruct((rows, wide_in), jnp.bfloat16)]
        + [jax.ShapeDtypeStruct(w.shape, jnp.float32) for w in (gate_w, up_w, down_w)],
        in_specs=[by_row(x.shape[1]), first, second, fixed(router.shape), fixed(picks.shape)]
        + [fixed(w.shape) for w in (gate_w, up_w, down_w)]
        + [by_row(hidden), by_row(hidden)],
        out_specs=[by_row(wide_in)] + [fixed(w.shape) for w in (gate_w, up_w, down_w)],
        compiler_params=roomy(),
        cost_estimate=cost(12 * rows * width * hidden, rows * (6 * width + 8 * hidden)),
        name="expert_backward",
    )(x, d_mine, d_mates, router, picks, gate_w, up_w, down_w, g, u)


def attention_kernel(
    micro, x_ref, gains_ref, cos_ref, sin_ref, wq, wk, wv, wo, q_ref, k_ref, v_ref, p_ref, mixed_ref, in_ref, residual_ref, mid_ref
):
    rows, width = x_ref.shape
    seq = rows // micro
    in_ref[...], _, _ = norm_ahead(x_ref[...].astype(jnp.float32), gains_ref[0:1])
    heads = width // HD
    group = 2 if heads % 2 == 0 else 1
    lower = lax.broadcasted_iota(jnp.int32, (seq, seq), 0) >= lax.broadcasted_iota(jnp.int32, (seq, seq), 1)

    @pl.loop(0, heads // group)
    def _(step):
        columns = pl.ds(pl.multiple_of(step * (group * HD), group * HD), group * HD)
        normed = in_ref[...]

        def turned(weights):
            raw = f32_dot(normed, weights[:, columns])
            parts = [raw[:, j * HD : (j + 1) * HD] for j in range(group)]
            parts = [p * cos_ref[...] + pltpu.roll(p, HD // 2, 1) * sin_ref[...] for p in parts]
            return jnp.concatenate(parts, axis=1).astype(jnp.bfloat16)

        q, k = turned(wq), turned(wk)
        v = f32_dot(normed, wv[:, columns]).astype(jnp.bfloat16)
        q_ref[:, columns], k_ref[:, columns], v_ref[:, columns] = q, k, v
        every = []
        for m in range(micro):
            side = []
            for j in range(group):
                one = lambda a: a[m * seq : (m + 1) * seq, j * HD : (j + 1) * HD]
                scores = HD ** (-0.5) * dot_t(one(q), one(k))
                scores = jnp.where(lower, scores, -1e30)
                weights = jnp.exp(scores - jnp.max(scores, axis=-1, keepdims=True))
                probs = weights / jnp.sum(weights, axis=-1, keepdims=True)
                p_ref[m, step * group + j] = probs
                side.append(f32_dot(probs.astype(jnp.bfloat16), one(v)))
            every.append(jnp.concatenate(side, axis=1))
        mixed_ref[:, columns] = jnp.concatenate(every, axis=0).astype(jnp.bfloat16)

    @pl.loop(0, heads // group)
    def _(step):
        columns = pl.ds(pl.multiple_of(step * (group * HD), group * HD), group * HD)
        residual_ref[:, columns] = x_ref[:, columns].astype(jnp.float32) + f32_dot(mixed_ref[...], wo[:, columns])

    mid_ref[...], _, _ = norm_ahead(residual_ref[...], gains_ref[1:2])


def attention_forward(micro, x, gains, cos, sin, wq, wk, wv, wo):
    rows, width = x.shape
    seq = rows // micro
    like = lambda kind: jax.ShapeDtypeStruct((rows, width), kind)
    return pl.pallas_call(
        functools.partial(attention_kernel, micro),
        out_shape=[like(jnp.bfloat16)] * 3
        + [jax.ShapeDtypeStruct((micro, width // HD, seq, seq), jnp.float32)]
        + [like(jnp.bfloat16)] * 2
        + [like(jnp.float32), like(jnp.bfloat16)],
        compiler_params=roomy(),
        cost_estimate=cost(32 * rows * width * width, 10 * width * width),
        name="attention_forward",
    )(x, gains, cos, sin, wq, wk, wv, wo)


def shared_kernel(width, part, x_ref, d_ref, w_ref, out_ref, in_ref, grad_ref):
    x, dy = x_ref[:, :width], d_ref[...]
    gate_w, up_w, down_t = w_ref[:, :part], w_ref[:, part : 2 * part], w_ref[:, 2 * part :]
    act, slope = silu_pair(f32_dot(x, gate_w))
    u = f32_dot(x, up_w)
    hidden = (act * u).astype(jnp.bfloat16)
    out_ref[...] = dot_t(hidden, down_t).astype(jnp.bfloat16)
    d_hidden = f32_dot(dy, down_t)
    d_gate = (d_hidden * u * slope).astype(jnp.bfloat16)
    d_up = (d_hidden * act).astype(jnp.bfloat16)
    in_ref[...] = (dot_t(d_gate, gate_w) + dot_t(d_up, up_w)).astype(jnp.bfloat16)

    @pl.when(pl.program_id(0) == 0)
    def _():
        grad_ref[...] = jnp.zeros_like(grad_ref)

    grad_ref[:, :part] += t_dot(x, d_gate)
    grad_ref[:, part : 2 * part] += t_dot(x, d_up)
    grad_ref[:, 2 * part :] += t_dot(dy, hidden)


def shared_expert(x, d, weights):
    rows, width = d.shape
    part = weights.shape[1] // 3
    block = row_block(rows)
    by_row = lambda w: pl.BlockSpec((block, w), lambda i: (i, 0))
    return pl.pallas_call(
        functools.partial(shared_kernel, width, part),
        grid=(rows // block,),
        out_shape=[jax.ShapeDtypeStruct((rows, width), jnp.bfloat16)] * 2 + [jax.ShapeDtypeStruct(weights.shape, jnp.float32)],
        in_specs=[by_row(x.shape[1]), by_row(width), fixed(weights.shape)],
        out_specs=[by_row(width)] * 2 + [fixed(weights.shape)],
        compiler_params=roomy(),
        cost_estimate=cost(18 * rows * width * part, rows * 8 * width),
        name="shared_expert",
    )(x, d, weights)


def on_device(
    tokens,
    cotangent,
    routes,
    gain_attn,
    gain_moe,
    w_query,
    w_key,
    w_value,
    attention_output_weight,
    router,
    shared_gate,
    shared_up,
    shared_down,
    routed_gate_weight,
    routed_up_weight,
    routed_down_weight,
):
    f32, bf16 = jnp.float32, jnp.bfloat16
    micro = tokens.shape[0]
    seq_len, width_all = tokens.shape[2], tokens.shape[3]
    chosen_count = routes.shape[3]
    experts = router.shape[1]
    heads = width_all // HD
    dims = chip_grid(lax.axis_size("wide"))
    deep, high, broad = dims
    slots = 9 * seq_len * chosen_count // (8 * experts) + 1
    extra = -(-experts // 128) * 128
    extra_back = -(-4 * experts // 128) * 128
    cosine_table, sine_table = angles(seq_len, HD)
    scale_factor = HD ** (-0.5)
    causal_mask = jnp.arange(seq_len)[:, None] >= jnp.arange(seq_len)[None, :]
    me = lax.axis_index("wide")
    own_rows = gain_attn.shape[0]

    named = jnp.any(routes[:, 0, :, :, None] == jnp.arange(experts), axis=2)
    named_wide = jnp.pad(named.astype(bf16), ((0, 0), (0, 0), (0, extra - experts)))

    small_width = -(-(experts + 2) // 128) * 128
    small = jnp.concatenate(
        [router, gain_attn[:, None], gain_moe[:, None], jnp.zeros((own_rows, small_width - experts - 2), bf16)], axis=1
    )
    hidden_all = shared_gate.shape[1]
    part = -(-hidden_all // (deep * 128)) * 128

    def cut(matrix):
        return jnp.pad(matrix, ((0, 0), (0, part * deep - hidden_all))).reshape(own_rows, deep, part).transpose(1, 0, 2)

    shared = jnp.concatenate([cut(shared_gate), cut(shared_up), cut(shared_down.T)], axis=2)
    (small_all, wq_all, wk_all, wv_all, wo_all, shared_all), names_column = gather_all(
        dims,
        [small, w_query, w_key, w_value, attention_output_weight, shared],
        [False, False, False, False, False, True],
        named_wide,
    )
    line = Line(dims)
    ahead_rows, back_rows = line.both_ways(cotangent[:, 0], cotangent[:, 0])
    ahead_rows, back_rows, small_all, wq_all, wk_all = lax.optimization_barrier((ahead_rows, back_rows, small_all, wq_all, wk_all))
    from_before, from_after = [ahead_rows], [back_rows]

    if deep > 2:
        one, two = line.both_ways(ahead_rows, back_rows)
        from_before, from_after = from_before + [one], from_after + [two]
    for far in range(3, deep):
        one, two = line.both_ways(cotangent[:, 0], cotangent[:, 0], far)
        from_before, from_after = from_before + [one], from_after + [two]
    router_all = small_all[:, :experts]
    gain_one = small_all[:, experts].astype(f32)
    gain_two = small_all[:, experts + 1].astype(f32)

    chip_a, chip_b, chip_c = place(dims)
    offsets = high * broad
    step = jnp.arange(offsets)
    targets = (chip_a * high + (chip_b + step // broad) % high) * broad + (chip_c + step % broad) % broad
    is_target = (jnp.arange(experts)[:, None] == targets[None, :]).astype(bf16)
    earlier = (jnp.arange(seq_len)[:, None] > jnp.arange(seq_len)[None, :]).astype(bf16)
    names = names_column[..., :experts]
    aimed = jnp.einsum("mkte,eq->mkqt", names, is_target, preferred_element_type=f32)
    slot = jnp.einsum("mkqu,tu->mkqt", aimed.astype(bf16), earlier, preferred_element_type=f32)
    hit = (slot[:, :, :, None, :] == jnp.arange(slots, dtype=f32)[:, None]) & (aimed[:, :, :, None, :] > 0.5)
    choose = hit.astype(bf16).reshape(micro, deep, offsets * slots, seq_len)
    choose_t = choose.transpose(0, 1, 3, 2)

    rows_low = tokens[:, 0].reshape(micro * seq_len, width_all)
    rows_in = rows_low.astype(f32)
    cos_row, sin_row = cosine_table[:, 0], sine_table[:, 0]
    queries, key_rows, value_rows, probs, mixed, normalized_input, residual, normed_mid = attention_forward(
        micro,
        rows_low,
        jnp.stack([gain_one, gain_two]),
        jnp.tile(jnp.concatenate([cos_row, cos_row], axis=1), (micro, 1)),
        jnp.tile(jnp.concatenate([-sin_row, sin_row], axis=1), (micro, 1)),
        wq_all,
        wk_all,
        wv_all,
        wo_all,
    )
    queries, key_rows, value_rows = (a.reshape(micro, seq_len, heads, HD) for a in (queries, key_rows, value_rows))
    probs_low = probs.astype(bf16)
    _, plain_in, scale_in = norm_ahead(rows_in, gain_one)
    _, plain_mid, scale_mid = norm_ahead(residual, gain_two)

    from_before, from_after, normed_mid = lax.optimization_barrier((from_before, from_after, normed_mid))
    d_column = [cotangent[:, 0]] + [
        jnp.where(chip_a >= k, from_before[k - 1], from_after[deep - k - 1]) for k in range(1, deep)
    ]
    d_column = jnp.stack(d_column, axis=1)
    d_picked_rows = jnp.einsum("mkqst,mktd->qmksd", hit.astype(bf16), d_column, preferred_element_type=f32).astype(bf16)

    x_ext = jnp.concatenate([normed_mid.reshape(micro, seq_len, width_all), named_wide], axis=-1)
    x_both, x_column = dispatch(dims, x_ext, choose)
    x_both, d_picked_rows = lax.optimization_barrier((x_both, d_picked_rows))
    d_pieces = plane_rows(dims, d_picked_rows)
    x_rows = x_both.reshape(-1, width_all + extra)

    shared_out, d_shared_in, grad_shared = shared_expert(
        x_column.reshape(-1, width_all + extra), d_column.reshape(-1, width_all), shared_all
    )
    grad_shared = grad_shared.astype(bf16)
    x_rows, shared_out = lax.optimization_barrier((x_rows, shared_out))

    gate_w, up_w, down_w = routed_gate_weight[0].T, routed_up_weight[0].T, routed_down_weight[0]
    side = 2 * experts * lax.axis_index("narrow")
    places = jnp.stack([me, me + side, me + side + experts])
    picks = (jnp.arange(extra_back)[None, :] == places[:, None]).astype(f32)
    router_wide = jnp.pad(router_all, ((0, 0), (0, extra - experts)))
    expert_args = (router_wide, picks, gate_w, up_w, down_w)
    out_mine, out_theirs, g_part, u_part = expert_forward(x_rows, *expert_args)
    d_pieces, out_mine, out_theirs = lax.optimization_barrier((d_pieces, out_mine, out_theirs))
    theirs = swap_cores(out_theirs)
    d_mine = jnp.stack(d_pieces, axis=1).reshape(-1, width_all)
    d_mates = swap_cores(d_mine)
    routed_rows = (out_mine.astype(f32) + theirs.astype(f32)).astype(bf16)
    routed_rows = routed_rows.reshape(micro, offsets, deep, slots, width_all)

    x_late, routed_rows = lax.optimization_barrier((x_rows, routed_rows))
    routed_pieces = plane_back(dims, routed_rows)
    d_in_rows, grad_egate, grad_eup, grad_edown = expert_backward(x_late, d_mine, d_mates, *expert_args, g_part, u_part)
    routed_pieces, d_in_rows = lax.optimization_barrier((routed_pieces, d_in_rows))
    routed_back = jnp.stack(routed_pieces, axis=2).reshape(micro, deep, offsets * slots, width_all)
    routed_sums = column_sums(dims, choose, routed_back, shared_out.reshape(d_column.shape))
    routed_sums, d_in_rows = lax.optimization_barrier((routed_sums, d_in_rows))
    up_rows, down_rows = line.both_ways(routed_sums[:, 1 % deep].astype(bf16), routed_sums[:, deep - 1].astype(bf16))
    d_total = give_back(
        dims,
        d_in_rows.reshape(2, micro, offsets, deep, slots, width_all + extra_back),
        choose_t,
        d_shared_in.reshape(d_column.shape),
    )
    d_total, up_rows, down_rows = lax.optimization_barrier((d_total, up_rows, down_rows))
    hops = [1]

    def next_sum(up_rows, down_rows):
        hops[0] += 1
        if hops[0] > deep - 1:
            return up_rows, down_rows
        up_rows = up_rows.astype(f32) + routed_sums[:, hops[0]]
        down_rows = down_rows.astype(f32) + routed_sums[:, deep - hops[0]]
        return line.both_ways(up_rows.astype(bf16), down_rows.astype(bf16))

    up_rows, down_rows = next_sum(up_rows, down_rows)
    d_total = d_total.reshape(micro * seq_len, width_all + extra_back)
    d_gates = sum(d_total[:, width_all + n * experts : width_all + (n + 1) * experts] for n in range(4))

    named_rows = named.reshape(micro * seq_len, experts)
    gates = masked_gates(f32_dot(normed_mid, router_all), named_rows)
    d_out = cotangent[:, 0].reshape(micro * seq_len, width_all).astype(f32)

    d_logits = (gates * (d_gates - jnp.sum(gates * d_gates, axis=1, keepdims=True))).astype(bf16)
    d_mid = d_total[:, :width_all] + dot_t(d_logits, router_all)
    d_norm_two, grad_gain_two = norm_back(d_mid, plain_mid, scale_mid, gain_two)
    d_residual = d_out + d_norm_two
    d_attn = d_residual.astype(bf16)
    grad_wout = t_dot(mixed, d_attn).astype(bf16)
    d_mixed = dot_t(d_attn, wo_all).astype(bf16).reshape(micro, seq_len, heads, HD)
    d_probs = jnp.einsum("sqhd,skhd->shqk", d_mixed, value_rows, preferred_element_type=f32)
    d_value = jnp.einsum("shqk,sqhd->skhd", probs_low, d_mixed, preferred_element_type=f32)
    d_value = d_value.astype(bf16).reshape(micro * seq_len, width_all)
    d_scores = (probs * (d_probs - jnp.sum(probs * d_probs, axis=-1, keepdims=True))).astype(bf16)
    d_scores, up_rows, down_rows = lax.optimization_barrier((d_scores, up_rows, down_rows))
    up_rows, down_rows = next_sum(up_rows, down_rows)
    d_query = scale_factor * jnp.einsum("shqk,skhd->sqhd", d_scores, key_rows, preferred_element_type=f32)
    d_key = scale_factor * jnp.einsum("shqk,sqhd->skhd", d_scores, queries, preferred_element_type=f32)
    d_query = unrotate(d_query, cosine_table, sine_table).astype(bf16).reshape(micro * seq_len, width_all)
    d_key = unrotate(d_key, cosine_table, sine_table).astype(bf16).reshape(micro * seq_len, width_all)
    grad_wq = t_dot(normalized_input, d_query).astype(bf16)
    grad_wk = t_dot(normalized_input, d_key).astype(bf16)
    grad_wv = t_dot(normalized_input, d_value).astype(bf16)
    d_in = dot_t(d_query, wq_all) + dot_t(d_key, wk_all) + dot_t(d_value, wv_all)
    d_norm_one, grad_gain_one = norm_back(d_in, plain_in, scale_in, gain_one)
    grad_tokens = (d_residual + d_norm_one).reshape(micro, 1, seq_len, width_all)

    up_rows, down_rows, grad_wv = lax.optimization_barrier((up_rows, down_rows, grad_wv))
    routed = routed_sums[:, 0] + up_rows.astype(f32) + down_rows.astype(f32)
    final_rows = residual + routed.reshape(micro * seq_len, width_all)
    output = final_rows.astype(bf16).reshape(micro, 1, seq_len, width_all)

    column = jnp.arange(small_width)[None, :]
    grad_small = t_dot(normed_mid, jnp.pad(d_logits, ((0, 0), (0, small_width - experts))))
    grad_small = jnp.where(column == experts, grad_gain_one[:, None], grad_small)
    grad_small = jnp.where(column == experts + 1, grad_gain_two[:, None], grad_small).astype(bf16)

    (g_shared, g_wo, g_wq, g_wk, g_wv, g_small) = scatter_all(
        dims,
        [grad_shared, grad_wout, grad_wq, grad_wk, grad_wv, grad_small],
        [True, False, False, False, False, False],
    )

    def joined(n):
        pieces = g_shared[:, :, n * part : (n + 1) * part]
        return pieces.transpose(1, 0, 2).reshape(own_rows, deep * part)[:, :hidden_all]

    return (
        output,
        grad_tokens,
        g_small[:, experts],
        g_small[:, experts + 1],
        g_wq,
        g_wk,
        g_wv,
        g_wo,
        g_small[:, :experts],
        joined(0),
        joined(1),
        joined(2).T,
        grad_egate.T[None],
        grad_eup.T[None],
        grad_edown[None],
    )


def solution(mesh):
    return jax.shard_map(
        on_device,
        mesh=mesh,
        in_specs=(
            P(None, ("wide", "narrow"), None, None),
            P(None, ("wide", "narrow"), None, None),
            P(None, ("wide", "narrow"), None, None),
            P(("wide", "narrow")),
            P(("wide", "narrow")),
            P(("wide", "narrow"), None),
            P(("wide", "narrow"), None),
            P(("wide", "narrow"), None),
            P(("wide", "narrow"), None),
            P(("wide", "narrow"), None),
            P(("wide", "narrow"), None),
            P(("wide", "narrow"), None),
            P(None, ("wide", "narrow")),
            P("wide", None, "narrow"),
            P("wide", None, "narrow"),
            P("wide", "narrow", None),
        ),
        out_specs=(
            P(None, ("wide", "narrow"), None, None),
            P(None, ("wide", "narrow"), None, None),
            P(("wide", "narrow")),
            P(("wide", "narrow")),
            P(("wide", "narrow"), None),
            P(("wide", "narrow"), None),
            P(("wide", "narrow"), None),
            P(("wide", "narrow"), None),
            P(("wide", "narrow"), None),
            P(("wide", "narrow"), None),
            P(("wide", "narrow"), None),
            P(None, ("wide", "narrow")),
            P("wide", None, "narrow"),
            P("wide", None, "narrow"),
            P("wide", "narrow", None),
        ),
        check_vma=False,
    )
```
